512 devices in a mesh: row: 32 (over x, z_lo), col: 16 (over y, z_hi, core).
Axes of the slice: x: 4, y: 4, z: 16 (z_hi: 2, z_lo: 8; z = z_hi * 8 + z_lo), core: 2. Of those that a mesh axis runs over, the one named last changes fastest.
Arguments:
- traces: bfloat16 [32, 2048, 2048], P(None, 'row', 'col'), may hold values from -6 to 6
- source_pos: int32 [2048], P('row'), may hold values from 0 to 16383
- receiver_pos: int32 [2048], replicated, may hold values from 0 to 16383
- aperture_list: int32 [128, 1024], P('row'), may hold values from 0 to 2047, as said below
- band_index: int32 [16384], P('row'), may hold values from 0 to 31
- weight_tiles: bfloat16 [32, 2, 128], replicated, may hold values from -4 to 4
Outputs:
- primaries: bfloat16 [32, 2048, 2048], P(None, 'row', 'col')
- image: float32 [2048, 16384], P('col', 'row')
The draws below stay inside these ranges and needn't reach their ends.
Inputs may be any that keep to these rules, and one draw needn't show every extreme that they name: `aperture_list`: the 1024 receivers listed for one tile are distinct.
All inputs are finite; a program needn't handle non-finite values.
Results may differ from the reference program's by a relative error of at most 0.012.
Values may be sent and summed in bfloat16 or wider, within the bound.
A program may use at most 64 MiB of HBM per device.

```python
import math
import jax
import jax.numpy as jnp
from jax import lax

SRC_DEV = 64
NPOS = 2048
TW = 32
NFFT = 4096
NF = 4
TP = 2
IX_DEV = 512
DEPTH_BAND_CELLS = 128
NXI = 16384
NZI = 2048
TX = 128
APER = 1024
KT = 32
HALF = 4096
N_ROW = 32
N_COL = 16


def draw_aperture_list(key, part):
    tile_keys = jax.random.split(jax.random.fold_in(key, 11), NXI // TX)

    def one_tile(tile_key):
        return jax.random.permutation(tile_key, NPOS)[:APER]
    return jax.vmap(one_tile)(tile_keys).astype(jnp.int32)


def set_ends(array, key, smallest, largest):
    longest = array.shape.index(max(array.shape))
    spots = []
    for shift in (0, 1):
        where = [jax.random.randint(jax.random.fold_in(key, axis), (), 0, length) for axis, length in enumerate(array.shape)]
        where[longest] = (where[longest] + shift) % array.shape[longest]
        spots.append(tuple(where))
    return array.at[spots[0]].set(smallest).at[spots[1]].set(largest)


def block_scale(stream_key, dims, cuts, least, high):
    gain, own = 1.0, jax.random.fold_in(stream_key, 6)
    for axis_at, blocks in cuts:
        steps = jnp.exp(jax.random.uniform(jax.random.fold_in(own, axis_at), (blocks,), jnp.float32, least / len(cuts), high / len(cuts)))
        gain = gain * jnp.repeat(steps, dims[axis_at] // blocks).reshape([-1 if axis == axis_at else 1 for axis in range(len(dims))])
    return gain


def gaussian(key, shape, spread, reach, pieces=(), held_as=jnp.bfloat16):
    entries = spread * jax.random.normal(key, shape, jnp.float32)
    if pieces:
        entries = entries * block_scale(key, shape, pieces, -0.22, 0.18)
    return jnp.clip(entries, -reach, reach).astype(held_as)


def setup_inputs(seed: int = 0) -> dict:
    arg_keys = jax.random.split(jax.random.key(seed), 7)
    traces = gaussian(arg_keys[0], (TW, NPOS, NPOS), 1.0, 6.0, ((1, 32), (2, 16)))
    source_pos = set_ends(jax.random.randint(arg_keys[1], (NPOS,), 0, NXI), jax.random.fold_in(arg_keys[1], 1), 0, NXI - 1).astype(jnp.int32)
    receiver_pos = set_ends(jax.random.randint(arg_keys[2], (NPOS,), 0, NXI), jax.random.fold_in(arg_keys[2], 1), 0, NXI - 1).astype(jnp.int32)
    aperture_list = draw_aperture_list(jax.random.fold_in(arg_keys[6], 71), 0)
    band_index = set_ends(jax.random.randint(arg_keys[4], (NXI,), 0, KT), jax.random.fold_in(arg_keys[4], 1), 0, KT - 1).astype(jnp.int32)
    weight_tiles = gaussian(arg_keys[5], (KT, TP, DEPTH_BAND_CELLS), TP ** -0.5, 4.0)
    return dict(traces=traces, source_pos=source_pos, receiver_pos=receiver_pos, aperture_list=aperture_list, band_index=band_index, weight_tiles=weight_tiles)


def phase_tables(samples):
    freq_bins = (2 * jnp.arange(NF, dtype=jnp.int32) + 1) * (NFFT // (4 * NF))
    sample_ticks = jnp.arange(samples, dtype=jnp.int32)
    phase_turns = freq_bins[:, None] * sample_ticks[None, :] % NFFT
    phase_angle = phase_turns.astype(jnp.float32) * (2.0 * math.pi / NFFT)
    return (jnp.cos(phase_angle), jnp.sin(phase_angle))

def aperture_matrix(tile_index_lists, positions, columns, first_row, row_count, spread_len):
    tile_count, listed = tile_index_lists.shape
    col_width = columns.shape[0]
    inside = (tile_index_lists >= first_row) & (tile_index_lists < first_row + row_count)
    local_index = jnp.where(inside, tile_index_lists - first_row, row_count)
    tile_rows = jnp.broadcast_to(jnp.arange(tile_count, dtype=jnp.int32)[:, None], tile_index_lists.shape)
    member = jnp.zeros((tile_count, row_count), jnp.float32).at[tile_rows, local_index].add(1.0, mode='drop')
    widened = jnp.repeat(member.T, col_width // tile_count, axis=1)
    offset = (positions[:, None] - columns[None, :]).astype(jnp.float32) / spread_len
    taper_weight = 1.0 / (1.0 + offset * offset)
    return (widened * taper_weight * (2.0 / math.sqrt(listed))).astype(jnp.bfloat16)

def shot_weights(positions, columns, spread_len):
    offset = (positions[:, None] - columns[None, :]).astype(jnp.float32) / spread_len
    return 1.0 / (1.0 + offset * offset)

def reference(traces, source_pos, receiver_pos, aperture_list, band_index, weight_tiles):
    cosine, sine_table = phase_tables(TW)
    forward = (jnp.concatenate([cosine, -sine_table], 0) / math.sqrt(TW)).astype(jnp.bfloat16)
    inverse = jnp.concatenate([cosine, -sine_table], 0).T / math.sqrt(NF)

    def spectra_block(block_index):
        trace_block = lax.dynamic_slice_in_dim(traces, block_index * SRC_DEV, SRC_DEV, 1)
        result = jnp.dot(forward.astype(jnp.float32), trace_block.reshape(TW, SRC_DEV * NPOS).astype(jnp.float32), preferred_element_type=jnp.float32)
        return result.astype(jnp.bfloat16).reshape(2 * NF, SRC_DEV, NPOS)
    blocks_out = lax.map(spectra_block, jnp.arange(N_ROW, dtype=jnp.int32))
    spectra = jnp.moveaxis(blocks_out, 0, 1).reshape(2, NF, NPOS, NPOS)

    def predict(spectrum_pair):
        real_part = spectrum_pair[0].astype(jnp.float32)
        imag_part = spectrum_pair[1].astype(jnp.float32)
        real_real = jnp.dot(real_part, real_part, preferred_element_type=jnp.float32)
        imag_imag = jnp.dot(imag_part, imag_part, preferred_element_type=jnp.float32)
        real_imag = jnp.dot(real_part, imag_part, preferred_element_type=jnp.float32)
        imag_real = jnp.dot(imag_part, real_part, preferred_element_type=jnp.float32)
        return -jnp.stack([real_real - imag_imag, real_imag + imag_real]) / math.sqrt(NPOS)
    multiples = jnp.moveaxis(lax.map(predict, jnp.moveaxis(spectra, 1, 0)), 0, 1)

    def panel_work(block_index):
        first_shot = block_index * SRC_DEV
        trace_block = lax.dynamic_slice_in_dim(traces, first_shot, SRC_DEV, 1)
        mult_block = lax.dynamic_slice_in_dim(multiples, first_shot, SRC_DEV, 2).reshape(2 * NF, SRC_DEV * NPOS)
        wave_field = jnp.dot(inverse, mult_block, precision=lax.Precision.HIGHEST, preferred_element_type=jnp.float32)
        primary_block = (trace_block.astype(jnp.float32) - wave_field.reshape(TW, SRC_DEV, NPOS)).astype(jnp.bfloat16)
        columns = block_index * IX_DEV + jnp.arange(IX_DEV, dtype=jnp.int32)
        tile_index_lists = lax.dynamic_slice_in_dim(aperture_list, block_index * (IX_DEV // TX), IX_DEV // TX, 0)
        aperture = aperture_matrix(tile_index_lists, receiver_pos, columns, 0, NPOS, HALF)
        shot_pos = lax.dynamic_slice_in_dim(source_pos, first_shot, SRC_DEV, 0)
        stacking_weights = shot_weights(shot_pos, columns, HALF)
        stacked = jnp.dot(primary_block.reshape(TW * SRC_DEV, NPOS).astype(jnp.float32), aperture.astype(jnp.float32), preferred_element_type=jnp.float32).reshape(TW, SRC_DEV, IX_DEV)
        column_stack = (lax.optimization_barrier(jnp.sum(stacked * stacking_weights[None], axis=1)) / math.sqrt(SRC_DEV)).astype(jnp.bfloat16)
        band_rows = lax.dynamic_slice_in_dim(band_index, block_index * IX_DEV, IX_DEV, 0)
        select = band_rows[None, :] == jnp.arange(KT, dtype=jnp.int32)[:, None]
        slab_stacks = column_stack.reshape(N_COL, TP, IX_DEV)
        widened = jnp.where(select[None, :, None, :], slab_stacks[:, None], jnp.zeros((), jnp.bfloat16))
        image_panel = jnp.einsum('kz,qkx->qzx', weight_tiles.reshape(KT * TP, DEPTH_BAND_CELLS).astype(jnp.float32), widened.reshape(N_COL, KT * TP, IX_DEV).astype(jnp.float32))
        return (primary_block, image_panel.reshape(N_COL * DEPTH_BAND_CELLS, IX_DEV))
    primary_blocks, image_panels = lax.map(panel_work, jnp.arange(N_ROW, dtype=jnp.int32))
    primaries = jnp.moveaxis(primary_blocks, 0, 1).reshape(TW, NPOS, NPOS)
    image_out = jnp.moveaxis(image_panels, 0, 1).reshape(NZI, NXI)
    return (primaries, image_out)
```

```python
import math

import jax
import jax.numpy as jnp
from jax import lax
from jax.sharding import Mesh
from jax.sharding import PartitionSpec as P

NFFT = 4096
NF = 4

ROW = ("x", "zl")
COL = ("y", "zh", "c")


def phase_tables(samples):
    freq_bins = (2 * jnp.arange(NF, dtype=jnp.int32) + 1) * (NFFT // (4 * NF))
    sample_ticks = jnp.arange(samples, dtype=jnp.int32)
    phase_turns = freq_bins[:, None] * sample_ticks[None, :] % NFFT
    phase_angle = phase_turns.astype(jnp.float32) * (2.0 * math.pi / NFFT)
    return (jnp.cos(phase_angle), jnp.sin(phase_angle))


def aperture_rows(tile_index_lists, positions, columns, first_row, row_count, spread_len):
    tile_count, listed = tile_index_lists.shape
    col_width = columns.shape[0]
    rows = first_row + jnp.arange(row_count, dtype=jnp.int32)
    hits = (tile_index_lists[:, :, None] == rows[None, None, :]).astype(jnp.float32)
    member = jnp.sum(hits, axis=1)
    widened = jnp.repeat(member.T, col_width // tile_count, axis=1)
    offset = (positions[:, None] - columns[None, :]).astype(jnp.float32) / spread_len
    taper_weight = 1.0 / (1.0 + offset * offset)
    return (widened * taper_weight * (2.0 / math.sqrt(listed))).astype(jnp.bfloat16)


def shot_weights(positions, columns, spread_len):
    offset = (positions[:, None] - columns[None, :]).astype(jnp.float32) / spread_len
    return 1.0 / (1.0 + offset * offset)


def complex_product(left_section, right_section):
    real_real = jnp.einsum(
        "qju,quy->qjy", left_section[0], right_section[0], preferred_element_type=jnp.float32
    )
    imag_imag = jnp.einsum(
        "qju,quy->qjy", left_section[1], right_section[1], preferred_element_type=jnp.float32
    )
    real_imag = jnp.einsum(
        "qju,quy->qjy", left_section[0], right_section[1], preferred_element_type=jnp.float32
    )
    imag_real = jnp.einsum(
        "qju,quy->qjy", left_section[1], right_section[0], preferred_element_type=jnp.float32
    )
    return jnp.stack([real_real - imag_imag, real_imag + imag_real])


def axis_pos(names):
    index = 0
    for name in names:
        index = index * lax.axis_size(name) + lax.axis_index(name)
    return index


def axis_count(names):
    count = 1
    for name in names:
        count *= lax.axis_size(name)
    return count


def per_device(traces, source_pos, receiver_pos, aperture_list, band_index, weight_tiles):
    samples, shot_count, recv_count = traces.shape
    col_count = axis_count(COL)
    row_count = axis_count(ROW)
    surface_count = recv_count * col_count
    image_panel_width = band_index.shape[0]
    depth_slab_samples = samples // col_count
    cosine, sine_table = phase_tables(samples)
    forward = (jnp.concatenate([cosine, -sine_table], 0) / math.sqrt(samples)).astype(jnp.bfloat16)
    spectra = jnp.dot(
        forward,
        traces.reshape(samples, shot_count * recv_count),
        preferred_element_type=jnp.float32,
    )
    spectra = spectra.astype(jnp.bfloat16).reshape(2, NF, shot_count, recv_count)

    columns_whole = lax.all_gather(spectra, "zl", axis=2, tiled=True)
    columns_whole = lax.all_gather(columns_whole, "x", axis=2, tiled=True)
    row_parts = lax.all_gather(spectra, "zh", axis=0)
    row_parts = lax.all_gather(row_parts, "c", axis=0)
    row_parts = lax.all_gather(row_parts, "y", axis=0)
    rows_whole = jnp.transpose(row_parts, (3, 4, 5, 0, 2, 1, 6)).reshape(
        2, NF, shot_count, surface_count
    )

    col_pos = axis_pos(COL)
    row_pos = axis_pos(ROW)
    columns = row_pos * image_panel_width + jnp.arange(image_panel_width, dtype=jnp.int32)
    spread_len = image_panel_width * row_count // 4
    stacking_weights = shot_weights(source_pos, columns, spread_len)
    my_receivers = lax.dynamic_slice_in_dim(receiver_pos, col_pos * recv_count, recv_count, 0)
    aperture = aperture_rows(
        aperture_list, my_receivers, columns, col_pos * recv_count, recv_count, spread_len
    )
    rows_whole, columns_whole, aperture, stacking_weights = lax.optimization_barrier(
        (rows_whole, columns_whole, aperture, stacking_weights)
    )

    summed = complex_product(rows_whole, columns_whole)
    multiples = -summed / math.sqrt(surface_count)
    inverse = jnp.concatenate([cosine, -sine_table], 0).T / math.sqrt(NF)
    wave_field = jnp.dot(
        inverse,
        multiples.reshape(2 * NF, shot_count * recv_count),
        precision=lax.Precision.HIGHEST,
        preferred_element_type=jnp.float32,
    )
    primaries = (
        traces.astype(jnp.float32) - wave_field.reshape(samples, shot_count, recv_count)
    ).astype(jnp.bfloat16)

    partial = jnp.dot(
        primaries.reshape(samples * shot_count, recv_count),
        aperture,
        preferred_element_type=jnp.float32,
    ).reshape(samples, shot_count, image_panel_width)
    partial = jnp.sum(partial * stacking_weights[None], axis=1)
    stacked = lax.psum_scatter(partial, COL, scatter_dimension=0, tiled=True)
    column_stack = (stacked / math.sqrt(shot_count)).astype(jnp.bfloat16)

    tile_kinds = weight_tiles.shape[0]
    select = band_index[None, :] == jnp.arange(tile_kinds, dtype=jnp.int32)[:, None]
    widened = jnp.where(select[:, None, :], column_stack[None], jnp.zeros((), jnp.bfloat16))
    image_out = jnp.einsum(
        "kz,kx->zx",
        weight_tiles.reshape(tile_kinds * depth_slab_samples, weight_tiles.shape[2]),
        widened.reshape(tile_kinds * depth_slab_samples, image_panel_width),
        preferred_element_type=jnp.float32,
    )
    return (primaries, image_out)


def solution(mesh):
    n_row = mesh.shape["row"]
    n_col = mesh.shape["col"]
    fine = Mesh(
        mesh.devices.reshape(4, n_row // 4, 4, n_col // 8, 2), ("x", "zl", "y", "zh", "c")
    )
    placed = (P(None, ROW, COL), P(ROW), P(), P(ROW, None), P(ROW), P())
    return jax.shard_map(
        per_device,
        mesh=fine,
        in_specs=placed,
        out_specs=(P(None, ROW, COL), P(COL, ROW)),
        check_vma=False,
    )
```

```python
import math

import jax
import jax.numpy as jnp
from jax import lax
from jax.experimental import pallas as pl
from jax.experimental.pallas import tpu as pltpu
from jax.sharding import Mesh
from jax.sharding import PartitionSpec as P

NFFT = 4096
NF = 4

ROW = ("x", "zl")
COL = ("y", "zh", "c")


def phase_tables(samples):
    freq_bins = (2 * jnp.arange(NF, dtype=jnp.int32) + 1) * (NFFT // (4 * NF))
    sample_ticks = jnp.arange(samples, dtype=jnp.int32)
    phase_turns = freq_bins[:, None] * sample_ticks[None, :] % NFFT
    phase_angle = phase_turns.astype(jnp.float32) * (2.0 * math.pi / NFFT)
    return (jnp.cos(phase_angle), jnp.sin(phase_angle))


def aperture_rows(tile_index_lists, positions, columns, first_row, row_count, spread_len):
    tile_count, listed = tile_index_lists.shape
    col_width = columns.shape[0]
    rows = first_row + jnp.arange(row_count, dtype=jnp.int32)
    hits = (tile_index_lists[:, :, None] == rows[None, None, :]).astype(jnp.float32)
    member = jnp.sum(hits, axis=1)
    widened = jnp.repeat(member.T, col_width // tile_count, axis=1)
    offset = (positions[:, None] - columns[None, :]).astype(jnp.float32) / spread_len
    taper_weight = 1.0 / (1.0 + offset * offset)
    return (widened * taper_weight * (2.0 / math.sqrt(listed))).astype(jnp.bfloat16)


def shot_weights(positions, columns, spread_len):
    offset = (positions[:, None] - columns[None, :]).astype(jnp.float32) / spread_len
    return 1.0 / (1.0 + offset * offset)


def complex_product(left_section, right_section):
    real_real = jnp.einsum(
        "qju,quy->qjy", left_section[0], right_section[0], preferred_element_type=jnp.float32
    )
    imag_imag = jnp.einsum(
        "qju,quy->qjy", left_section[1], right_section[1], preferred_element_type=jnp.float32
    )
    real_imag = jnp.einsum(
        "qju,quy->qjy", left_section[0], right_section[1], preferred_element_type=jnp.float32
    )
    imag_real = jnp.einsum(
        "qju,quy->qjy", left_section[1], right_section[0], preferred_element_type=jnp.float32
    )
    return jnp.stack([real_real - imag_imag, real_imag + imag_real])


def axis_pos(names):
    index = 0
    for name in names:
        index = index * lax.axis_size(name) + lax.axis_index(name)
    return index


def axis_count(names):
    count = 1
    for name in names:
        count *= lax.axis_size(name)
    return count


MESH_ID = pl.DeviceIdType.MESH
NX, NZ, NY = 4, 8, 4


def gather_kernel(spec_ref, colw_ref, roww_ref, recv_row, recv_col, send_row, send_col):
    x = lax.axis_index("x")
    z = lax.axis_index("zl")
    y = lax.axis_index("y")
    h = lax.axis_index("zh")
    c = lax.axis_index("c")
    xp = lax.rem(x + 1, NX)
    xm = lax.rem(x + NX - 1, NX)
    yp = lax.rem(y + 1, NY)
    ym = lax.rem(y + NY - 1, NY)
    me_row = x * NZ + z
    me_col = (y * 2 + h) * 2 + c

    barrier = pltpu.get_barrier_semaphore()
    for peer in ({"x": xp}, {"x": xm}, {"y": yp}, {"y": ym}, {"zh": 1 - h}, {"c": 1 - c}):
        pl.semaphore_signal(barrier, 1, device_id=peer, device_id_type=MESH_ID)

    @pl.when(z > 0)
    def _():
        pl.semaphore_signal(barrier, 1, device_id={"zl": z - 1}, device_id_type=MESH_ID)

    @pl.when(z < NZ - 1)
    def _():
        pl.semaphore_signal(barrier, 1, device_id={"zl": z + 1}, device_id_type=MESH_ID)

    ends = jnp.logical_or(z == 0, z == NZ - 1)
    pl.when(ends)(lambda: pl.semaphore_wait(barrier, 7))
    pl.when(jnp.logical_not(ends))(lambda: pl.semaphore_wait(barrier, 8))

    started = []

    def row_copy(b, d, peer, own=False):
        src = spec_ref if own else colw_ref.at[b]
        return pltpu.make_async_remote_copy(
            src, colw_ref.at[b], send_row.at[b, d], recv_row.at[b],
            device_id=peer, device_id_type=MESH_ID,
        )

    def col_copy(j, d, peer, own=False):
        src = spec_ref if own else roww_ref.at[j]
        return pltpu.make_async_remote_copy(
            src, roww_ref.at[j], send_col.at[j, d], recv_col.at[j],
            device_id=peer, device_id_type=MESH_ID,
        )

    def start(desc, cond=None):
        if cond is None:
            desc.start()
        else:
            pl.when(cond)(desc.start)
        started.append((desc, cond))

    def wait_row(b, cond=None):
        desc = row_copy(b, 0, {"x": x})
        if cond is None:
            desc.wait_recv()
        else:
            pl.when(cond)(desc.wait_recv)

    def wait_col(j, cond=None):
        desc = col_copy(j, 0, {"y": y})
        if cond is None:
            desc.wait_recv()
        else:
            pl.when(cond)(desc.wait_recv)

    start(col_copy(me_col, 0, {"c": 1 - c}, own=True))
    start(col_copy(me_col, 1, {"zh": 1 - h}, own=True))
    start(row_copy(me_row, 0, {"zl": z + 1}, own=True), z < NZ - 1)
    start(row_copy(me_row, 1, {"zl": z - 1}, own=True), z > 0)
    start(row_copy(me_row, 2, {"x": xp}, own=True))
    start(row_copy(me_row, 3, {"x": xm}, own=True))
    start(col_copy(me_col, 2, {"y": yp}, own=True))
    start(col_copy(me_col, 3, {"y": ym}, own=True))
    colw_ref[me_row] = spec_ref[...]
    roww_ref[me_col] = spec_ref[...]

    j_h = (y * 2 + 1 - h) * 2 + c
    j_c = (y * 2 + h) * 2 + 1 - c
    j_hc = (y * 2 + 1 - h) * 2 + 1 - c
    wait_col(j_h)
    start(col_copy(j_h, 0, {"c": 1 - c}))
    start(col_copy(j_h, 2, {"y": yp}))
    start(col_copy(j_h, 3, {"y": ym}))
    wait_col(j_c)
    start(col_copy(j_c, 2, {"y": yp}))
    start(col_copy(j_c, 3, {"y": ym}))

    def x_forward(zsrc, cond):
        even = lax.rem(zsrc, 2) == 0
        b_left = xm * NZ + zsrc
        b_right = xp * NZ + zsrc
        wait_row(b_left, jnp.logical_and(cond, even))
        start(row_copy(b_left, 2, {"x": xp}), jnp.logical_and(cond, even))
        odd = jnp.logical_not(even)
        wait_row(b_right, jnp.logical_and(cond, odd))
        start(row_copy(b_right, 3, {"x": xm}), jnp.logical_and(cond, odd))

    for k in range(1, NZ):
        lo = z >= k
        b = x * NZ + z - k
        wait_row(b, lo)
        start(row_copy(b, 0, {"zl": z + 1}), jnp.logical_and(lo, z < NZ - 1))
        start(row_copy(b, 2, {"x": xp}), lo)
        start(row_copy(b, 3, {"x": xm}), lo)
        hi = z + k < NZ
        b = x * NZ + z + k
        wait_row(b, hi)
        start(row_copy(b, 1, {"zl": z - 1}), jnp.logical_and(hi, z > 0))
        start(row_copy(b, 2, {"x": xp}), hi)
        start(row_copy(b, 3, {"x": xm}), hi)
        if k == 1:
            x_forward(z, True)
            wait_col(j_hc)
            start(col_copy(j_hc, 2, {"y": yp}))
            start(col_copy(j_hc, 3, {"y": ym}))
            for cc in range(2):
                jl = (ym * 2 + 0) * 2 + cc
                wait_col(jl)
                start(col_copy(jl, 2, {"y": yp}))
                jr = (yp * 2 + 1) * 2 + cc
                wait_col(jr)
                start(col_copy(jr, 3, {"y": ym}))
        else:
            x_forward(z - (k - 1), z >= k - 1)
            x_forward(z + (k - 1), z + (k - 1) < NZ)
    x_forward(z - (NZ - 1), z >= NZ - 1)
    x_forward(z + (NZ - 1), z + (NZ - 1) < NZ)

    x2 = lax.rem(x + 2, NX)
    for zz in range(NZ):
        if zz % 2 == 1:
            wait_row(xm * NZ + zz)
        else:
            wait_row(xp * NZ + zz)
        wait_row(x2 * NZ + zz)
    y2 = lax.rem(y + 2, NY)
    for cc in range(2):
        wait_col((ym * 2 + 1) * 2 + cc)
        wait_col((yp * 2 + 0) * 2 + cc)
        for hh in range(2):
            wait_col((y2 * 2 + hh) * 2 + cc)
    for desc, cond in started:
        if cond is None:
            desc.wait_send()
        else:
            pl.when(cond)(desc.wait_send)


def gather_spectra(spectra_planes, row_count, col_count):
    planes = spectra_planes.shape
    return pl.pallas_call(
        gather_kernel,
        out_shape=(
            jax.ShapeDtypeStruct((row_count,) + planes, spectra_planes.dtype),
            jax.ShapeDtypeStruct((col_count,) + planes, spectra_planes.dtype),
        ),
        in_specs=[pl.BlockSpec(memory_space=pltpu.VMEM)],
        out_specs=(pl.BlockSpec(memory_space=pltpu.VMEM), pl.BlockSpec(memory_space=pltpu.VMEM)),
        scratch_shapes=[
            pltpu.SemaphoreType.DMA((row_count,)),
            pltpu.SemaphoreType.DMA((col_count,)),
            pltpu.SemaphoreType.DMA((row_count, 4)),
            pltpu.SemaphoreType.DMA((col_count, 4)),
        ],
        compiler_params=pltpu.CompilerParams(collective_id=0, has_side_effects=True),
    )(spectra_planes)


def reduce_kernel(part_ref, out_ref, slots, recv_sem, send_sem):
    y = lax.axis_index("y")
    h = lax.axis_index("zh")
    c = lax.axis_index("c")
    me = (y * 2 + h) * 2 + c
    peers = []
    for yy in range(NY):
        for hh in range(2):
            for cc in range(2):
                peers.append(((yy * 2 + hh) * 2 + cc, {"y": yy, "zh": hh, "c": cc}))
    barrier = pltpu.get_barrier_semaphore()
    for j, peer in peers:
        pl.when(j != me)(
            lambda peer=peer: pl.semaphore_signal(
                barrier, 1, device_id=peer, device_id_type=MESH_ID
            )
        )
    pl.semaphore_wait(barrier, len(peers) - 1)
    copies = []
    for j, peer in peers:
        desc = pltpu.make_async_remote_copy(
            part_ref.at[j], slots.at[me], send_sem.at[j], recv_sem.at[me],
            device_id=peer, device_id_type=MESH_ID,
        )
        pl.when(j != me)(desc.start)
        copies.append((j, desc))
    slots[me] = part_ref[me]
    for j, desc in copies:
        recv = pltpu.make_async_remote_copy(
            part_ref.at[j], slots.at[j], send_sem.at[j], recv_sem.at[j],
            device_id={"y": y}, device_id_type=MESH_ID,
        )
        pl.when(j != me)(recv.wait_recv)
    total = slots[0]
    for j in range(1, len(peers)):
        total = total + slots[j]
    out_ref[...] = total
    for j, desc in copies:
        pl.when(j != me)(desc.wait_send)


def reduce_bands(partial, col_count):
    rows, width = partial.shape
    band = rows // col_count
    parts = partial.reshape(col_count, band, width)
    return pl.pallas_call(
        reduce_kernel,
        out_shape=jax.ShapeDtypeStruct((band, width), partial.dtype),
        in_specs=[pl.BlockSpec(memory_space=pltpu.VMEM)],
        out_specs=pl.BlockSpec(memory_space=pltpu.VMEM),
        scratch_shapes=[
            pltpu.VMEM((col_count, band, width), partial.dtype),
            pltpu.SemaphoreType.DMA((col_count,)),
            pltpu.SemaphoreType.DMA((col_count,)),
        ],
        compiler_params=pltpu.CompilerParams(collective_id=1, has_side_effects=True),
    )(parts)


def per_device(traces, source_pos, receiver_pos, aperture_list, band_index, weight_tiles):
    samples, shot_count, recv_count = traces.shape
    col_count = axis_count(COL)
    row_count = axis_count(ROW)
    surface_count = recv_count * col_count
    image_panel_width = band_index.shape[0]
    depth_slab_samples = samples // col_count
    cosine, sine_table = phase_tables(samples)
    forward = (jnp.concatenate([cosine, -sine_table], 0) / math.sqrt(samples)).astype(jnp.bfloat16)
    spectra = jnp.dot(
        forward,
        traces.reshape(samples, shot_count * recv_count),
        preferred_element_type=jnp.float32,
    )
    spectra = spectra.astype(jnp.bfloat16).reshape(2, NF, shot_count, recv_count)

    colw, roww = gather_spectra(
        spectra.reshape(2 * NF, shot_count, recv_count), row_count, col_count
    )
    columns_whole = jnp.transpose(colw, (1, 0, 2, 3)).reshape(2, NF, row_count * shot_count, recv_count)
    rows_whole = jnp.transpose(roww, (1, 2, 0, 3)).reshape(2, NF, shot_count, surface_count)

    col_pos = axis_pos(COL)
    row_pos = axis_pos(ROW)
    columns = row_pos * image_panel_width + jnp.arange(image_panel_width, dtype=jnp.int32)
    spread_len = image_panel_width * row_count // 4
    stacking_weights = shot_weights(source_pos, columns, spread_len)
    my_receivers = lax.dynamic_slice_in_dim(receiver_pos, col_pos * recv_count, recv_count, 0)
    aperture = aperture_rows(
        aperture_list, my_receivers, columns, col_pos * recv_count, recv_count, spread_len
    )
    rows_whole, columns_whole, aperture, stacking_weights = lax.optimization_barrier(
        (rows_whole, columns_whole, aperture, stacking_weights)
    )

    summed = complex_product(rows_whole, columns_whole)
    multiples = -summed / math.sqrt(surface_count)
    inverse = jnp.concatenate([cosine, -sine_table], 0).T / math.sqrt(NF)
    wave_field = jnp.dot(
        inverse,
        multiples.reshape(2 * NF, shot_count * recv_count),
        precision=lax.Precision.HIGHEST,
        preferred_element_type=jnp.float32,
    )
    primaries = (
        traces.astype(jnp.float32) - wave_field.reshape(samples, shot_count, recv_count)
    ).astype(jnp.bfloat16)

    partial = jnp.dot(
        primaries.reshape(samples * shot_count, recv_count),
        aperture,
        preferred_element_type=jnp.float32,
    ).reshape(samples, shot_count, image_panel_width)
    partial = jnp.sum(partial * stacking_weights[None], axis=1)
    stacked = reduce_bands(partial, col_count)
    column_stack = (stacked / math.sqrt(shot_count)).astype(jnp.bfloat16)

    tile_kinds = weight_tiles.shape[0]
    select = band_index[None, :] == jnp.arange(tile_kinds, dtype=jnp.int32)[:, None]
    widened = jnp.where(select[:, None, :], column_stack[None], jnp.zeros((), jnp.bfloat16))
    image_out = jnp.einsum(
        "kz,kx->zx",
        weight_tiles.reshape(tile_kinds * depth_slab_samples, weight_tiles.shape[2]),
        widened.reshape(tile_kinds * depth_slab_samples, image_panel_width),
        preferred_element_type=jnp.float32,
    )
    return (primaries, image_out)


def solution(mesh):
    n_row = mesh.shape["row"]
    n_col = mesh.shape["col"]
    fine = Mesh(
        mesh.devices.reshape(4, n_row // 4, 4, n_col // 8, 2), ("x", "zl", "y", "zh", "c")
    )
    placed = (P(None, ROW, COL), P(ROW), P(), P(ROW, None), P(ROW), P())
    return jax.shard_map(
        per_device,
        mesh=fine,
        in_specs=placed,
        out_specs=(P(None, ROW, COL), P(COL, ROW)),
        check_vma=False,
    )
```

```python
import math

import jax
import jax.numpy as jnp
from jax import lax
from jax.experimental import pallas as pl
from jax.experimental.pallas import tpu as pltpu
from jax.sharding import Mesh
from jax.sharding import PartitionSpec as P

NFFT = 4096
NF = 4

ROW = ("x", "zl")
COL = ("y", "zh", "c")


def phase_tables(samples):
    freq_bins = (2 * jnp.arange(NF, dtype=jnp.int32) + 1) * (NFFT // (4 * NF))
    sample_ticks = jnp.arange(samples, dtype=jnp.int32)
    phase_turns = freq_bins[:, None] * sample_ticks[None, :] % NFFT
    phase_angle = phase_turns.astype(jnp.float32) * (2.0 * math.pi / NFFT)
    return (jnp.cos(phase_angle), jnp.sin(phase_angle))


def aperture_rows(tile_index_lists, positions, columns, first_row, row_count, spread_len):
    tile_count, listed = tile_index_lists.shape
    col_width = columns.shape[0]
    rows = first_row + jnp.arange(row_count, dtype=jnp.int32)
    hits = (tile_index_lists[:, :, None] == rows[None, None, :]).astype(jnp.float32)
    member = jnp.sum(hits, axis=1)
    widened = jnp.repeat(member.T, col_width // tile_count, axis=1)
    offset = (positions[:, None] - columns[None, :]).astype(jnp.float32) / spread_len
    taper_weight = 1.0 / (1.0 + offset * offset)
    return (widened * taper_weight * (2.0 / math.sqrt(listed))).astype(jnp.bfloat16)


def shot_weights(positions, columns, spread_len):
    offset = (positions[:, None] - columns[None, :]).astype(jnp.float32) / spread_len
    return 1.0 / (1.0 + offset * offset)


def complex_product(left_section, right_section):
    real_real = jnp.einsum(
        "qju,quy->qjy", left_section[0], right_section[0], preferred_element_type=jnp.float32
    )
    imag_imag = jnp.einsum(
        "qju,quy->qjy", left_section[1], right_section[1], preferred_element_type=jnp.float32
    )
    real_imag = jnp.einsum(
        "qju,quy->qjy", left_section[0], right_section[1], preferred_element_type=jnp.float32
    )
    imag_real = jnp.einsum(
        "qju,quy->qjy", left_section[1], right_section[0], preferred_element_type=jnp.float32
    )
    return jnp.stack([real_real - imag_imag, real_imag + imag_real])


def axis_pos(names):
    index = 0
    for name in names:
        index = index * lax.axis_size(name) + lax.axis_index(name)
    return index


def axis_count(names):
    count = 1
    for name in names:
        count *= lax.axis_size(name)
    return count


MESH_ID = pl.DeviceIdType.MESH
NX, NZ, NY = 4, 8, 4


def gather_kernel(spec_ref, colw_ref, roww_ref, recv_row, recv_col, send_row, send_col):
    x = lax.axis_index("x")
    z = lax.axis_index("zl")
    y = lax.axis_index("y")
    h = lax.axis_index("zh")
    c = lax.axis_index("c")
    xp = lax.rem(x + 1, NX)
    xm = lax.rem(x + NX - 1, NX)
    yp = lax.rem(y + 1, NY)
    ym = lax.rem(y + NY - 1, NY)
    me_row = x * NZ + z
    me_col = (y * 2 + h) * 2 + c

    barrier = pltpu.get_barrier_semaphore()
    for peer in ({"x": xp}, {"x": xm}, {"y": yp}, {"y": ym}, {"zh": 1 - h}, {"c": 1 - c}):
        pl.semaphore_signal(barrier, 1, device_id=peer, device_id_type=MESH_ID)

    @pl.when(z > 0)
    def _():
        pl.semaphore_signal(barrier, 1, device_id={"zl": z - 1}, device_id_type=MESH_ID)

    @pl.when(z < NZ - 1)
    def _():
        pl.semaphore_signal(barrier, 1, device_id={"zl": z + 1}, device_id_type=MESH_ID)

    ends = jnp.logical_or(z == 0, z == NZ - 1)
    pl.when(ends)(lambda: pl.semaphore_wait(barrier, 7))
    pl.when(jnp.logical_not(ends))(lambda: pl.semaphore_wait(barrier, 8))

    started = []

    shots = spec_ref.shape[1]
    recvs = spec_ref.shape[2]

    def colw_blk(b):
        return colw_ref.at[:, pl.ds(pl.multiple_of(b * shots, shots), shots), :]

    def roww_blk(j):
        return roww_ref.at[:, :, pl.ds(pl.multiple_of(j * recvs, recvs), recvs)]

    def row_copy(b, d, peer, own=False):
        src = spec_ref if own else colw_blk(b)
        return pltpu.make_async_remote_copy(
            src, colw_blk(b), send_row.at[b, d], recv_row.at[b],
            device_id=peer, device_id_type=MESH_ID,
        )

    def col_copy(j, d, peer, own=False):
        src = spec_ref if own else roww_blk(j)
        return pltpu.make_async_remote_copy(
            src, roww_blk(j), send_col.at[j, d], recv_col.at[j],
            device_id=peer, device_id_type=MESH_ID,
        )

    def start(desc, cond=None):
        if cond is None:
            desc.start()
        else:
            pl.when(cond)(desc.start)
        started.append((desc, cond))

    def wait_row(b, cond=None):
        desc = row_copy(b, 0, {"x": x})
        if cond is None:
            desc.wait_recv()
        else:
            pl.when(cond)(desc.wait_recv)

    def wait_col(j, cond=None):
        desc = col_copy(j, 0, {"y": y})
        if cond is None:
            desc.wait_recv()
        else:
            pl.when(cond)(desc.wait_recv)

    start(col_copy(me_col, 0, {"c": 1 - c}, own=True))
    start(col_copy(me_col, 1, {"zh": 1 - h}, own=True))
    start(row_copy(me_row, 0, {"zl": z + 1}, own=True), z < NZ - 1)
    start(row_copy(me_row, 1, {"zl": z - 1}, own=True), z > 0)
    start(row_copy(me_row, 2, {"x": xp}, own=True))
    start(row_copy(me_row, 3, {"x": xm}, own=True))
    start(col_copy(me_col, 2, {"y": yp}, own=True))
    start(col_copy(me_col, 3, {"y": ym}, own=True))
    colw_ref[:, pl.ds(pl.multiple_of(me_row * shots, shots), shots), :] = spec_ref[...]
    roww_ref[:, :, pl.ds(pl.multiple_of(me_col * recvs, recvs), recvs)] = spec_ref[...]

    j_h = (y * 2 + 1 - h) * 2 + c
    j_c = (y * 2 + h) * 2 + 1 - c
    j_hc = (y * 2 + 1 - h) * 2 + 1 - c
    wait_col(j_h)
    start(col_copy(j_h, 0, {"c": 1 - c}))
    start(col_copy(j_h, 2, {"y": yp}))
    start(col_copy(j_h, 3, {"y": ym}))
    wait_col(j_c)
    start(col_copy(j_c, 2, {"y": yp}))
    start(col_copy(j_c, 3, {"y": ym}))

    def x_forward(zsrc, cond):
        even = lax.rem(zsrc, 2) == 0
        b_left = xm * NZ + zsrc
        b_right = xp * NZ + zsrc
        wait_row(b_left, jnp.logical_and(cond, even))
        start(row_copy(b_left, 2, {"x": xp}), jnp.logical_and(cond, even))
        odd = jnp.logical_not(even)
        wait_row(b_right, jnp.logical_and(cond, odd))
        start(row_copy(b_right, 3, {"x": xm}), jnp.logical_and(cond, odd))

    for k in range(1, NZ):
        lo = z >= k
        b = x * NZ + z - k
        wait_row(b, lo)
        start(row_copy(b, 0, {"zl": z + 1}), jnp.logical_and(lo, z < NZ - 1))
        start(row_copy(b, 2, {"x": xp}), lo)
        start(row_copy(b, 3, {"x": xm}), lo)
        hi = z + k < NZ
        b = x * NZ + z + k
        wait_row(b, hi)
        start(row_copy(b, 1, {"zl": z - 1}), jnp.logical_and(hi, z > 0))
        start(row_copy(b, 2, {"x": xp}), hi)
        start(row_copy(b, 3, {"x": xm}), hi)
        if k == 1:
            x_forward(z, True)
            wait_col(j_hc)
            start(col_copy(j_hc, 2, {"y": yp}))
            start(col_copy(j_hc, 3, {"y": ym}))
            for cc in range(2):
                jl = (ym * 2 + 0) * 2 + cc
                wait_col(jl)
                start(col_copy(jl, 2, {"y": yp}))
                jr = (yp * 2 + 1) * 2 + cc
                wait_col(jr)
                start(col_copy(jr, 3, {"y": ym}))
        else:
            x_forward(z - (k - 1), z >= k - 1)
            x_forward(z + (k - 1), z + (k - 1) < NZ)
    x_forward(z - (NZ - 1), z >= NZ - 1)
    x_forward(z + (NZ - 1), z + (NZ - 1) < NZ)

    x2 = lax.rem(x + 2, NX)
    for zz in range(NZ):
        if zz % 2 == 1:
            wait_row(xm * NZ + zz)
        else:
            wait_row(xp * NZ + zz)
        wait_row(x2 * NZ + zz)
    y2 = lax.rem(y + 2, NY)
    for cc in range(2):
        wait_col((ym * 2 + 1) * 2 + cc)
        wait_col((yp * 2 + 0) * 2 + cc)
        for hh in range(2):
            wait_col((y2 * 2 + hh) * 2 + cc)
    for desc, cond in started:
        if cond is None:
            desc.wait_send()
        else:
            pl.when(cond)(desc.wait_send)


def gather_spectra(spectra_planes, row_count, col_count):
    planes, shots, recvs = spectra_planes.shape
    return pl.pallas_call(
        gather_kernel,
        out_shape=(
            jax.ShapeDtypeStruct((planes, row_count * shots, recvs), spectra_planes.dtype),
            jax.ShapeDtypeStruct((planes, shots, col_count * recvs), spectra_planes.dtype),
        ),
        in_specs=[pl.BlockSpec(memory_space=pltpu.VMEM)],
        out_specs=(pl.BlockSpec(memory_space=pltpu.VMEM), pl.BlockSpec(memory_space=pltpu.VMEM)),
        scratch_shapes=[
            pltpu.SemaphoreType.DMA((row_count,)),
            pltpu.SemaphoreType.DMA((col_count,)),
            pltpu.SemaphoreType.DMA((row_count, 4)),
            pltpu.SemaphoreType.DMA((col_count, 4)),
        ],
        compiler_params=pltpu.CompilerParams(collective_id=0, has_side_effects=True),
    )(spectra_planes)


def reduce_kernel(part_ref, out_ref, slots, recv_sem, send_sem):
    y = lax.axis_index("y")
    h = lax.axis_index("zh")
    c = lax.axis_index("c")
    me = (y * 2 + h) * 2 + c
    peers = []
    for yy in range(NY):
        for hh in range(2):
            for cc in range(2):
                peers.append(((yy * 2 + hh) * 2 + cc, {"y": yy, "zh": hh, "c": cc}))
    barrier = pltpu.get_barrier_semaphore()
    for j, peer in peers:
        pl.when(j != me)(
            lambda peer=peer: pl.semaphore_signal(
                barrier, 1, device_id=peer, device_id_type=MESH_ID
            )
        )
    pl.semaphore_wait(barrier, len(peers) - 1)
    copies = []
    for j, peer in peers:
        desc = pltpu.make_async_remote_copy(
            part_ref.at[j], slots.at[me], send_sem.at[j], recv_sem.at[me],
            device_id=peer, device_id_type=MESH_ID,
        )
        pl.when(j != me)(desc.start)
        copies.append((j, desc))
    slots[me] = part_ref[me]
    for j, desc in copies:
        recv = pltpu.make_async_remote_copy(
            part_ref.at[j], slots.at[j], send_sem.at[j], recv_sem.at[j],
            device_id={"y": y}, device_id_type=MESH_ID,
        )
        pl.when(j != me)(recv.wait_recv)
    total = slots[0]
    for j in range(1, len(peers)):
        total = total + slots[j]
    out_ref[...] = total
    for j, desc in copies:
        pl.when(j != me)(desc.wait_send)


def reduce_bands(partial, col_count):
    rows, width = partial.shape
    band = rows // col_count
    parts = partial.reshape(col_count, band, width)
    return pl.pallas_call(
        reduce_kernel,
        out_shape=jax.ShapeDtypeStruct((band, width), partial.dtype),
        in_specs=[pl.BlockSpec(memory_space=pltpu.VMEM)],
        out_specs=pl.BlockSpec(memory_space=pltpu.VMEM),
        scratch_shapes=[
            pltpu.VMEM((col_count, band, width), partial.dtype),
            pltpu.SemaphoreType.DMA((col_count,)),
            pltpu.SemaphoreType.DMA((col_count,)),
        ],
        compiler_params=pltpu.CompilerParams(collective_id=1, has_side_effects=True),
    )(parts)


def per_device(traces, source_pos, receiver_pos, aperture_list, band_index, weight_tiles):
    samples, shot_count, recv_count = traces.shape
    col_count = axis_count(COL)
    row_count = axis_count(ROW)
    surface_count = recv_count * col_count
    image_panel_width = band_index.shape[0]
    depth_slab_samples = samples // col_count
    cosine, sine_table = phase_tables(samples)
    forward = (jnp.concatenate([cosine, -sine_table], 0) / math.sqrt(samples)).astype(jnp.bfloat16)
    spectra = jnp.dot(
        forward,
        traces.reshape(samples, shot_count * recv_count),
        preferred_element_type=jnp.float32,
    )
    spectra = spectra.astype(jnp.bfloat16).reshape(2, NF, shot_count, recv_count)

    colw, roww = gather_spectra(
        spectra.reshape(2 * NF, shot_count, recv_count), row_count, col_count
    )
    columns_whole = colw.reshape(2, NF, row_count * shot_count, recv_count)
    rows_whole = roww.reshape(2, NF, shot_count, surface_count)

    col_pos = axis_pos(COL)
    row_pos = axis_pos(ROW)
    columns = row_pos * image_panel_width + jnp.arange(image_panel_width, dtype=jnp.int32)
    spread_len = image_panel_width * row_count // 4
    stacking_weights = shot_weights(source_pos, columns, spread_len)
    my_receivers = lax.dynamic_slice_in_dim(receiver_pos, col_pos * recv_count, recv_count, 0)
    aperture = aperture_rows(
        aperture_list, my_receivers, columns, col_pos * recv_count, recv_count, spread_len
    )
    rows_whole, columns_whole, aperture, stacking_weights = lax.optimization_barrier(
        (rows_whole, columns_whole, aperture, stacking_weights)
    )

    summed = complex_product(rows_whole, columns_whole)
    multiples = -summed / math.sqrt(surface_count)
    inverse = jnp.concatenate([cosine, -sine_table], 0).T / math.sqrt(NF)
    wave_field = jnp.dot(
        inverse,
        multiples.reshape(2 * NF, shot_count * recv_count),
        precision=lax.Precision.HIGHEST,
        preferred_element_type=jnp.float32,
    )
    primaries = (
        traces.astype(jnp.float32) - wave_field.reshape(samples, shot_count, recv_count)
    ).astype(jnp.bfloat16)

    partial = jnp.dot(
        primaries.reshape(samples * shot_count, recv_count),
        aperture,
        preferred_element_type=jnp.float32,
    ).reshape(samples, shot_count, image_panel_width)
    partial = jnp.sum(partial * stacking_weights[None], axis=1)
    stacked = reduce_bands(partial, col_count)
    column_stack = (stacked / math.sqrt(shot_count)).astype(jnp.bfloat16)

    tile_kinds = weight_tiles.shape[0]
    select = band_index[None, :] == jnp.arange(tile_kinds, dtype=jnp.int32)[:, None]
    widened = jnp.where(select[:, None, :], column_stack[None], jnp.zeros((), jnp.bfloat16))
    image_out = jnp.einsum(
        "kz,kx->zx",
        weight_tiles.reshape(tile_kinds * depth_slab_samples, weight_tiles.shape[2]),
        widened.reshape(tile_kinds * depth_slab_samples, image_panel_width),
        preferred_element_type=jnp.float32,
    )
    return (primaries, image_out)


def solution(mesh):
    n_row = mesh.shape["row"]
    n_col = mesh.shape["col"]
    fine = Mesh(
        mesh.devices.reshape(4, n_row // 4, 4, n_col // 8, 2), ("x", "zl", "y", "zh", "c")
    )
    placed = (P(None, ROW, COL), P(ROW), P(), P(ROW, None), P(ROW), P())
    return jax.shard_map(
        per_device,
        mesh=fine,
        in_specs=placed,
        out_specs=(P(None, ROW, COL), P(COL, ROW)),
        check_vma=False,
    )
```

```python
import math

import jax
import jax.numpy as jnp
from jax import lax
from jax.experimental import pallas as pl
from jax.experimental.pallas import tpu as pltpu
from jax.sharding import Mesh
from jax.sharding import PartitionSpec as P

NFFT = 4096
NF = 4

ROW = ("x", "zl")
COL = ("y", "zh", "c")


def phase_tables(samples):
    freq_bins = (2 * jnp.arange(NF, dtype=jnp.int32) + 1) * (NFFT // (4 * NF))
    sample_ticks = jnp.arange(samples, dtype=jnp.int32)
    phase_turns = freq_bins[:, None] * sample_ticks[None, :] % NFFT
    phase_angle = phase_turns.astype(jnp.float32) * (2.0 * math.pi / NFFT)
    return (jnp.cos(phase_angle), jnp.sin(phase_angle))


def aperture_rows(tile_index_lists, positions, columns, first_row, row_count, spread_len):
    tile_count, listed = tile_index_lists.shape
    col_width = columns.shape[0]
    rows = first_row + jnp.arange(row_count, dtype=jnp.int32)
    hits = (tile_index_lists[:, :, None] == rows[None, None, :]).astype(jnp.float32)
    member = jnp.sum(hits, axis=1)
    widened = jnp.repeat(member.T, col_width // tile_count, axis=1)
    offset = (positions[:, None] - columns[None, :]).astype(jnp.float32) / spread_len
    taper_weight = 1.0 / (1.0 + offset * offset)
    return (widened * taper_weight * (2.0 / math.sqrt(listed))).astype(jnp.bfloat16)


def shot_weights(positions, columns, spread_len):
    offset = (positions[:, None] - columns[None, :]).astype(jnp.float32) / spread_len
    return 1.0 / (1.0 + offset * offset)


def complex_product(left_section, right_section):
    real_real = jnp.einsum(
        "qju,quy->qjy", left_section[0], right_section[0], preferred_element_type=jnp.float32
    )
    imag_imag = jnp.einsum(
        "qju,quy->qjy", left_section[1], right_section[1], preferred_element_type=jnp.float32
    )
    real_imag = jnp.einsum(
        "qju,quy->qjy", left_section[0], right_section[1], preferred_element_type=jnp.float32
    )
    imag_real = jnp.einsum(
        "qju,quy->qjy", left_section[1], right_section[0], preferred_element_type=jnp.float32
    )
    return jnp.stack([real_real - imag_imag, real_imag + imag_real])


def axis_pos(names):
    index = 0
    for name in names:
        index = index * lax.axis_size(name) + lax.axis_index(name)
    return index


def axis_count(names):
    count = 1
    for name in names:
        count *= lax.axis_size(name)
    return count


MESH_ID = pl.DeviceIdType.MESH
NX, NZ, NY = 4, 8, 4


def gather_kernel(spec_ref, colw_ref, roww_ref, recv_row, recv_col, send_row, send_col):
    x = lax.axis_index("x")
    z = lax.axis_index("zl")
    y = lax.axis_index("y")
    h = lax.axis_index("zh")
    c = lax.axis_index("c")
    xp = lax.rem(x + 1, NX)
    xm = lax.rem(x + NX - 1, NX)
    yp = lax.rem(y + 1, NY)
    ym = lax.rem(y + NY - 1, NY)
    me_row = x * NZ + z
    me_col = (y * 2 + h) * 2 + c

    barrier = pltpu.get_barrier_semaphore()
    for peer in ({"x": xp}, {"x": xm}, {"y": yp}, {"y": ym}, {"zh": 1 - h}, {"c": 1 - c}):
        pl.semaphore_signal(barrier, 1, device_id=peer, device_id_type=MESH_ID)

    @pl.when(z > 0)
    def _():
        pl.semaphore_signal(barrier, 1, device_id={"zl": z - 1}, device_id_type=MESH_ID)

    @pl.when(z < NZ - 1)
    def _():
        pl.semaphore_signal(barrier, 1, device_id={"zl": z + 1}, device_id_type=MESH_ID)

    ends = jnp.logical_or(z == 0, z == NZ - 1)
    pl.when(ends)(lambda: pl.semaphore_wait(barrier, 7))
    pl.when(jnp.logical_not(ends))(lambda: pl.semaphore_wait(barrier, 8))

    started = []
    shots = spec_ref.shape[1]
    recvs = spec_ref.shape[2]
    half = spec_ref.shape[0] // 2
    parts = (0, 1)

    def planes(part):
        return pl.ds(part * half, half)

    def colw_blk(b, part):
        return colw_ref.at[planes(part), pl.ds(pl.multiple_of(b * shots, shots), shots), :]

    def roww_blk(j, part):
        return roww_ref.at[planes(part), :, pl.ds(pl.multiple_of(j * recvs, recvs), recvs)]

    def row_copy(b, part, d, peer, own=False):
        src = spec_ref.at[planes(part)] if own else colw_blk(b, part)
        return pltpu.make_async_remote_copy(
            src, colw_blk(b, part), send_row.at[b, part, d], recv_row.at[b, part],
            device_id=peer, device_id_type=MESH_ID,
        )

    def col_copy(j, part, d, peer, own=False):
        src = spec_ref.at[planes(part)] if own else roww_blk(j, part)
        return pltpu.make_async_remote_copy(
            src, roww_blk(j, part), send_col.at[j, part, d], recv_col.at[j, part],
            device_id=peer, device_id_type=MESH_ID,
        )

    def start(desc, cond=None):
        if cond is None:
            desc.start()
        else:
            pl.when(cond)(desc.start)
        started.append((desc, cond))

    def when(cond, fn):
        if cond is None:
            fn()
        else:
            pl.when(cond)(fn)

    def row_relay(b, sends, cond=None):
        for part in parts:
            when(cond, row_copy(b, part, 0, {"x": x}).wait_recv)
            for d, peer, extra in sends:
                c2 = cond if extra is None else (extra if cond is None else jnp.logical_and(cond, extra))
                start(row_copy(b, part, d, peer), c2)

    def col_relay(j, sends, cond=None):
        for part in parts:
            when(cond, col_copy(j, part, 0, {"y": y}).wait_recv)
            for d, peer in sends:
                start(col_copy(j, part, d, peer), cond)

    for part in parts:
        start(col_copy(me_col, part, 0, {"c": 1 - c}, own=True))
        start(col_copy(me_col, part, 1, {"zh": 1 - h}, own=True))
        start(row_copy(me_row, part, 0, {"zl": z + 1}, own=True), z < NZ - 1)
        start(row_copy(me_row, part, 1, {"zl": z - 1}, own=True), z > 0)
        start(row_copy(me_row, part, 2, {"x": xp}, own=True))
        start(row_copy(me_row, part, 3, {"x": xm}, own=True))
        start(col_copy(me_col, part, 2, {"y": yp}, own=True))
        start(col_copy(me_col, part, 3, {"y": ym}, own=True))
    colw_ref[:, pl.ds(pl.multiple_of(me_row * shots, shots), shots), :] = spec_ref[...]
    roww_ref[:, :, pl.ds(pl.multiple_of(me_col * recvs, recvs), recvs)] = spec_ref[...]

    j_h = (y * 2 + 1 - h) * 2 + c
    j_c = (y * 2 + h) * 2 + 1 - c
    j_hc = (y * 2 + 1 - h) * 2 + 1 - c
    y_sends = ((2, {"y": yp}), (3, {"y": ym}))
    col_relay(j_h, ((0, {"c": 1 - c}),) + y_sends)
    col_relay(j_c, y_sends)

    def x_forward(zsrc, cond):
        even = lax.rem(zsrc, 2) == 0
        row_relay(xm * NZ + zsrc, ((2, {"x": xp}, None),), jnp.logical_and(cond, even))
        odd = jnp.logical_not(even)
        row_relay(xp * NZ + zsrc, ((3, {"x": xm}, None),), jnp.logical_and(cond, odd))

    x_sends = ((2, {"x": xp}, None), (3, {"x": xm}, None))
    for k in range(1, NZ):
        row_relay(x * NZ + z - k, ((0, {"zl": z + 1}, z < NZ - 1),) + x_sends, z >= k)
        row_relay(x * NZ + z + k, ((1, {"zl": z - 1}, z > 0),) + x_sends, z + k < NZ)
        if k == 1:
            x_forward(z, True)
            col_relay(j_hc, y_sends)
            for cc in range(2):
                col_relay((ym * 2 + 0) * 2 + cc, ((2, {"y": yp}),))
                col_relay((yp * 2 + 1) * 2 + cc, ((3, {"y": ym}),))
        else:
            x_forward(z - (k - 1), z >= k - 1)
            x_forward(z + (k - 1), z + (k - 1) < NZ)
    x_forward(z - (NZ - 1), z >= NZ - 1)
    x_forward(z + (NZ - 1), z + (NZ - 1) < NZ)

    x2 = lax.rem(x + 2, NX)
    for zz in range(NZ):
        row_relay(xm * NZ + zz if zz % 2 == 1 else xp * NZ + zz, ())
        row_relay(x2 * NZ + zz, ())
    y2 = lax.rem(y + 2, NY)
    for cc in range(2):
        col_relay((ym * 2 + 1) * 2 + cc, ())
        col_relay((yp * 2 + 0) * 2 + cc, ())
        for hh in range(2):
            col_relay((y2 * 2 + hh) * 2 + cc, ())
    for desc, cond in started:
        when(cond, desc.wait_send)


def gather_spectra(spectra_planes, row_count, col_count):
    planes, shots, recvs = spectra_planes.shape
    return pl.pallas_call(
        gather_kernel,
        out_shape=(
            jax.ShapeDtypeStruct((planes, row_count * shots, recvs), spectra_planes.dtype),
            jax.ShapeDtypeStruct((planes, shots, col_count * recvs), spectra_planes.dtype),
        ),
        in_specs=[pl.BlockSpec(memory_space=pltpu.VMEM)],
        out_specs=(pl.BlockSpec(memory_space=pltpu.VMEM), pl.BlockSpec(memory_space=pltpu.VMEM)),
        scratch_shapes=[
            pltpu.SemaphoreType.DMA((row_count, 2)),
            pltpu.SemaphoreType.DMA((col_count, 2)),
            pltpu.SemaphoreType.DMA((row_count, 2, 4)),
            pltpu.SemaphoreType.DMA((col_count, 2, 4)),
        ],
        compiler_params=pltpu.CompilerParams(collective_id=0, has_side_effects=True),
    )(spectra_planes)


def reduce_kernel(part_ref, out_ref, slots, recv_sem, send_sem):
    y = lax.axis_index("y")
    h = lax.axis_index("zh")
    c = lax.axis_index("c")
    me = (y * 2 + h) * 2 + c
    peers = []
    for yy in range(NY):
        for hh in range(2):
            for cc in range(2):
                peers.append(((yy * 2 + hh) * 2 + cc, {"y": yy, "zh": hh, "c": cc}))
    barrier = pltpu.get_barrier_semaphore()
    for j, peer in peers:
        pl.when(j != me)(
            lambda peer=peer: pl.semaphore_signal(
                barrier, 1, device_id=peer, device_id_type=MESH_ID
            )
        )
    pl.semaphore_wait(barrier, len(peers) - 1)
    copies = []
    for j, peer in peers:
        desc = pltpu.make_async_remote_copy(
            part_ref.at[j], slots.at[me], send_sem.at[j], recv_sem.at[me],
            device_id=peer, device_id_type=MESH_ID,
        )
        pl.when(j != me)(desc.start)
        copies.append((j, desc))
    slots[me] = part_ref[me]
    for j, desc in copies:
        recv = pltpu.make_async_remote_copy(
            part_ref.at[j], slots.at[j], send_sem.at[j], recv_sem.at[j],
            device_id={"y": y}, device_id_type=MESH_ID,
        )
        pl.when(j != me)(recv.wait_recv)
    total = slots[0]
    for j in range(1, len(peers)):
        total = total + slots[j]
    out_ref[...] = total
    for j, desc in copies:
        pl.when(j != me)(desc.wait_send)


def reduce_bands(partial, col_count):
    rows, width = partial.shape
    band = rows // col_count
    parts = partial.reshape(col_count, band, width)
    return pl.pallas_call(
        reduce_kernel,
        out_shape=jax.ShapeDtypeStruct((band, width), partial.dtype),
        in_specs=[pl.BlockSpec(memory_space=pltpu.VMEM)],
        out_specs=pl.BlockSpec(memory_space=pltpu.VMEM),
        scratch_shapes=[
            pltpu.VMEM((col_count, band, width), partial.dtype),
            pltpu.SemaphoreType.DMA((col_count,)),
            pltpu.SemaphoreType.DMA((col_count,)),
        ],
        compiler_params=pltpu.CompilerParams(collective_id=1, has_side_effects=True),
    )(parts)


def per_device(traces, source_pos, receiver_pos, aperture_list, band_index, weight_tiles):
    samples, shot_count, recv_count = traces.shape
    col_count = axis_count(COL)
    row_count = axis_count(ROW)
    surface_count = recv_count * col_count
    image_panel_width = band_index.shape[0]
    depth_slab_samples = samples // col_count
    cosine, sine_table = phase_tables(samples)
    forward = (jnp.concatenate([cosine, -sine_table], 0) / math.sqrt(samples)).astype(jnp.bfloat16)
    spectra = jnp.dot(
        forward,
        traces.reshape(samples, shot_count * recv_count),
        preferred_element_type=jnp.float32,
    )
    spectra = spectra.astype(jnp.bfloat16).reshape(2, NF, shot_count, recv_count)

    colw, roww = gather_spectra(
        spectra.reshape(2 * NF, shot_count, recv_count), row_count, col_count
    )
    columns_whole = colw.reshape(2, NF, row_count * shot_count, recv_count)
    rows_whole = roww.reshape(2, NF, shot_count, surface_count)

    col_pos = axis_pos(COL)
    row_pos = axis_pos(ROW)
    columns = row_pos * image_panel_width + jnp.arange(image_panel_width, dtype=jnp.int32)
    spread_len = image_panel_width * row_count // 4
    stacking_weights = shot_weights(source_pos, columns, spread_len)
    my_receivers = lax.dynamic_slice_in_dim(receiver_pos, col_pos * recv_count, recv_count, 0)
    aperture = aperture_rows(
        aperture_list, my_receivers, columns, col_pos * recv_count, recv_count, spread_len
    )
    rows_whole, columns_whole, aperture, stacking_weights = lax.optimization_barrier(
        (rows_whole, columns_whole, aperture, stacking_weights)
    )

    summed = complex_product(rows_whole, columns_whole)
    multiples = -summed / math.sqrt(surface_count)
    inverse = jnp.concatenate([cosine, -sine_table], 0).T / math.sqrt(NF)
    wave_field = jnp.dot(
        inverse,
        multiples.reshape(2 * NF, shot_count * recv_count),
        precision=lax.Precision.HIGHEST,
        preferred_element_type=jnp.float32,
    )
    primaries = (
        traces.astype(jnp.float32) - wave_field.reshape(samples, shot_count, recv_count)
    ).astype(jnp.bfloat16)

    partial = jnp.dot(
        primaries.reshape(samples * shot_count, recv_count),
        aperture,
        preferred_element_type=jnp.float32,
    ).reshape(samples, shot_count, image_panel_width)
    partial = jnp.sum(partial * stacking_weights[None], axis=1)
    stacked = reduce_bands(partial, col_count)
    column_stack = (stacked / math.sqrt(shot_count)).astype(jnp.bfloat16)

    tile_kinds = weight_tiles.shape[0]
    select = band_index[None, :] == jnp.arange(tile_kinds, dtype=jnp.int32)[:, None]
    widened = jnp.where(select[:, None, :], column_stack[None], jnp.zeros((), jnp.bfloat16))
    image_out = jnp.einsum(
        "kz,kx->zx",
        weight_tiles.reshape(tile_kinds * depth_slab_samples, weight_tiles.shape[2]),
        widened.reshape(tile_kinds * depth_slab_samples, image_panel_width),
        preferred_element_type=jnp.float32,
    )
    return (primaries, image_out)


def solution(mesh):
    n_row = mesh.shape["row"]
    n_col = mesh.shape["col"]
    fine = Mesh(
        mesh.devices.reshape(4, n_row // 4, 4, n_col // 8, 2), ("x", "zl", "y", "zh", "c")
    )
    placed = (P(None, ROW, COL), P(ROW), P(), P(ROW, None), P(ROW), P())
    return jax.shard_map(
        per_device,
        mesh=fine,
        in_specs=placed,
        out_specs=(P(None, ROW, COL), P(COL, ROW)),
        check_vma=False,
    )
```

```python
import math

import jax
import jax.numpy as jnp
from jax import lax
from jax.experimental import pallas as pl
from jax.experimental.pallas import tpu as pltpu
from jax.sharding import Mesh
from jax.sharding import PartitionSpec as P

NFFT = 4096
NF = 4

ROW = ("x", "zl")
COL = ("y", "zh", "c")


def phase_tables(samples):
    freq_bins = (2 * jnp.arange(NF, dtype=jnp.int32) + 1) * (NFFT // (4 * NF))
    sample_ticks = jnp.arange(samples, dtype=jnp.int32)
    phase_turns = freq_bins[:, None] * sample_ticks[None, :] % NFFT
    phase_angle = phase_turns.astype(jnp.float32) * (2.0 * math.pi / NFFT)
    return (jnp.cos(phase_angle), jnp.sin(phase_angle))


def aperture_rows(tile_index_lists, positions, columns, first_row, row_count, spread_len):
    tile_count, listed = tile_index_lists.shape
    col_width = columns.shape[0]
    rows = first_row + jnp.arange(row_count, dtype=jnp.int32)
    hits = (tile_index_lists[:, :, None] == rows[None, None, :]).astype(jnp.float32)
    member = jnp.sum(hits, axis=1)
    widened = jnp.repeat(member.T, col_width // tile_count, axis=1)
    offset = (positions[:, None] - columns[None, :]).astype(jnp.float32) / spread_len
    taper_weight = 1.0 / (1.0 + offset * offset)
    return (widened * taper_weight * (2.0 / math.sqrt(listed))).astype(jnp.bfloat16)


def shot_weights(positions, columns, spread_len):
    offset = (positions[:, None] - columns[None, :]).astype(jnp.float32) / spread_len
    return 1.0 / (1.0 + offset * offset)


def complex_product(left_section, right_section):
    real_real = jnp.einsum(
        "qju,quy->qjy", left_section[0], right_section[0], preferred_element_type=jnp.float32
    )
    imag_imag = jnp.einsum(
        "qju,quy->qjy", left_section[1], right_section[1], preferred_element_type=jnp.float32
    )
    real_imag = jnp.einsum(
        "qju,quy->qjy", left_section[0], right_section[1], preferred_element_type=jnp.float32
    )
    imag_real = jnp.einsum(
        "qju,quy->qjy", left_section[1], right_section[0], preferred_element_type=jnp.float32
    )
    return jnp.stack([real_real - imag_imag, real_imag + imag_real])


def axis_pos(names):
    index = 0
    for name in names:
        index = index * lax.axis_size(name) + lax.axis_index(name)
    return index


def axis_count(names):
    count = 1
    for name in names:
        count *= lax.axis_size(name)
    return count


MESH_ID = pl.DeviceIdType.MESH
NX, NZ, NY = 4, 8, 4


def gather_kernel(spec_ref, colw_ref, roww_ref, recv_row, recv_col, send_row, send_col):
    x = lax.axis_index("x")
    z = lax.axis_index("zl")
    y = lax.axis_index("y")
    h = lax.axis_index("zh")
    c = lax.axis_index("c")
    xp = lax.rem(x + 1, NX)
    xm = lax.rem(x + NX - 1, NX)
    yp = lax.rem(y + 1, NY)
    ym = lax.rem(y + NY - 1, NY)
    me_row = x * NZ + z
    me_col = (y * 2 + h) * 2 + c

    barrier = pltpu.get_barrier_semaphore()
    for peer in ({"x": xp}, {"x": xm}, {"y": yp}, {"y": ym}, {"zh": 1 - h}, {"c": 1 - c}):
        pl.semaphore_signal(barrier, 1, device_id=peer, device_id_type=MESH_ID)

    @pl.when(z > 0)
    def _():
        pl.semaphore_signal(barrier, 1, device_id={"zl": z - 1}, device_id_type=MESH_ID)

    @pl.when(z < NZ - 1)
    def _():
        pl.semaphore_signal(barrier, 1, device_id={"zl": z + 1}, device_id_type=MESH_ID)

    ends = jnp.logical_or(z == 0, z == NZ - 1)
    pl.when(ends)(lambda: pl.semaphore_wait(barrier, 7))
    pl.when(jnp.logical_not(ends))(lambda: pl.semaphore_wait(barrier, 8))

    started = []
    shots = spec_ref.shape[1]
    recvs = spec_ref.shape[2]
    half = spec_ref.shape[0] // 2
    parts = (0, 1)

    def planes(part):
        return pl.ds(part * half, half)

    def colw_blk(b, part):
        return colw_ref.at[planes(part), pl.ds(pl.multiple_of(b * shots, shots), shots), :]

    def roww_blk(j, part):
        return roww_ref.at[planes(part), :, pl.ds(pl.multiple_of(j * recvs, recvs), recvs)]

    def row_copy(b, part, d, peer, own=False):
        src = spec_ref.at[planes(part)] if own else colw_blk(b, part)
        return pltpu.make_async_remote_copy(
            src, colw_blk(b, part), send_row.at[b, part, d], recv_row.at[b, part],
            device_id=peer, device_id_type=MESH_ID,
        )

    def col_copy(j, part, d, peer, own=False):
        src = spec_ref.at[planes(part)] if own else roww_blk(j, part)
        return pltpu.make_async_remote_copy(
            src, roww_blk(j, part), send_col.at[j, part, d], recv_col.at[j, part],
            device_id=peer, device_id_type=MESH_ID,
        )

    def start(desc, cond=None):
        if cond is None:
            desc.start()
        else:
            pl.when(cond)(desc.start)
        started.append((desc, cond))

    def when(cond, fn):
        if cond is None:
            fn()
        else:
            pl.when(cond)(fn)

    def row_relay(b, sends, cond=None):
        for part in parts:
            when(cond, row_copy(b, part, 0, {"x": x}).wait_recv)
            for d, peer, extra in sends:
                c2 = cond if extra is None else (extra if cond is None else jnp.logical_and(cond, extra))
                start(row_copy(b, part, d, peer), c2)

    def col_relay(j, sends, cond=None):
        for part in parts:
            when(cond, col_copy(j, part, 0, {"y": y}).wait_recv)
            for d, peer in sends:
                start(col_copy(j, part, d, peer), cond)

    for part in parts:
        start(col_copy(me_col, part, 0, {"c": 1 - c}, own=True))
        start(col_copy(me_col, part, 1, {"zh": 1 - h}, own=True))
        start(row_copy(me_row, part, 0, {"zl": z + 1}, own=True), z < NZ - 1)
        start(row_copy(me_row, part, 1, {"zl": z - 1}, own=True), z > 0)
        start(row_copy(me_row, part, 2, {"x": xp}, own=True))
        start(row_copy(me_row, part, 3, {"x": xm}, own=True))
        start(col_copy(me_col, part, 2, {"y": yp}, own=True))
        start(col_copy(me_col, part, 3, {"y": ym}, own=True))
    colw_ref[:, pl.ds(pl.multiple_of(me_row * shots, shots), shots), :] = spec_ref[...]
    roww_ref[:, :, pl.ds(pl.multiple_of(me_col * recvs, recvs), recvs)] = spec_ref[...]

    j_h = (y * 2 + 1 - h) * 2 + c
    j_c = (y * 2 + h) * 2 + 1 - c
    j_hc = (y * 2 + 1 - h) * 2 + 1 - c
    y_sends = ((2, {"y": yp}), (3, {"y": ym}))
    col_relay(j_c, y_sends)

    def x_forward(zsrc, cond):
        even = lax.rem(zsrc, 2) == 0
        row_relay(xm * NZ + zsrc, ((2, {"x": xp}, None),), jnp.logical_and(cond, even))
        odd = jnp.logical_not(even)
        row_relay(xp * NZ + zsrc, ((3, {"x": xm}, None),), jnp.logical_and(cond, odd))

    def x_forward_at(dist):
        if dist == 0:
            x_forward(z, True)
        else:
            x_forward(z - dist, z >= dist)
            x_forward(z + dist, z + dist < NZ)

    lag = 2
    x_sends = ((2, {"x": xp}, None), (3, {"x": xm}, None))
    for k in range(1, NZ):
        row_relay(x * NZ + z - k, ((0, {"zl": z + 1}, z < NZ - 1),) + x_sends, z >= k)
        row_relay(x * NZ + z + k, ((1, {"zl": z - 1}, z > 0),) + x_sends, z + k < NZ)
        if k - lag >= 0:
            x_forward_at(k - lag)
        if k == 2:
            col_relay(j_h, ((0, {"c": 1 - c}),) + y_sends)
        if k == 3:
            col_relay(j_hc, y_sends)
        if k == 4:
            for cc in range(2):
                col_relay((ym * 2 + 0) * 2 + cc, ((2, {"y": yp}),))
                col_relay((yp * 2 + 1) * 2 + cc, ((3, {"y": ym}),))
    for dist in range(NZ - lag, NZ):
        x_forward_at(dist)

    x2 = lax.rem(x + 2, NX)
    for zz in range(NZ):
        row_relay(xm * NZ + zz if zz % 2 == 1 else xp * NZ + zz, ())
        row_relay(x2 * NZ + zz, ())
    y2 = lax.rem(y + 2, NY)
    for cc in range(2):
        col_relay((ym * 2 + 1) * 2 + cc, ())
        col_relay((yp * 2 + 0) * 2 + cc, ())
        for hh in range(2):
            col_relay((y2 * 2 + hh) * 2 + cc, ())
    for desc, cond in started:
        when(cond, desc.wait_send)


def gather_spectra(spectra_planes, row_count, col_count):
    planes, shots, recvs = spectra_planes.shape
    return pl.pallas_call(
        gather_kernel,
        out_shape=(
            jax.ShapeDtypeStruct((planes, row_count * shots, recvs), spectra_planes.dtype),
            jax.ShapeDtypeStruct((planes, shots, col_count * recvs), spectra_planes.dtype),
        ),
        in_specs=[pl.BlockSpec(memory_space=pltpu.VMEM)],
        out_specs=(pl.BlockSpec(memory_space=pltpu.VMEM), pl.BlockSpec(memory_space=pltpu.VMEM)),
        scratch_shapes=[
            pltpu.SemaphoreType.DMA((row_count, 2)),
            pltpu.SemaphoreType.DMA((col_count, 2)),
            pltpu.SemaphoreType.DMA((row_count, 2, 4)),
            pltpu.SemaphoreType.DMA((col_count, 2, 4)),
        ],
        compiler_params=pltpu.CompilerParams(collective_id=0, has_side_effects=True),
    )(spectra_planes)


def reduce_kernel(part_ref, out_ref, slots, recv_sem, send_sem):
    y = lax.axis_index("y")
    h = lax.axis_index("zh")
    c = lax.axis_index("c")
    me = (y * 2 + h) * 2 + c
    peers = []
    for yy in range(NY):
        for hh in range(2):
            for cc in range(2):
                peers.append(((yy * 2 + hh) * 2 + cc, {"y": yy, "zh": hh, "c": cc}))
    barrier = pltpu.get_barrier_semaphore()
    for j, peer in peers:
        pl.when(j != me)(
            lambda peer=peer: pl.semaphore_signal(
                barrier, 1, device_id=peer, device_id_type=MESH_ID
            )
        )
    pl.semaphore_wait(barrier, len(peers) - 1)
    copies = []
    for j, peer in peers:
        desc = pltpu.make_async_remote_copy(
            part_ref.at[j], slots.at[me], send_sem.at[j], recv_sem.at[me],
            device_id=peer, device_id_type=MESH_ID,
        )
        pl.when(j != me)(desc.start)
        copies.append((j, desc))
    slots[me] = part_ref[me]
    for j, desc in copies:
        recv = pltpu.make_async_remote_copy(
            part_ref.at[j], slots.at[j], send_sem.at[j], recv_sem.at[j],
            device_id={"y": y}, device_id_type=MESH_ID,
        )
        pl.when(j != me)(recv.wait_recv)
    total = slots[0]
    for j in range(1, len(peers)):
        total = total + slots[j]
    out_ref[...] = total
    for j, desc in copies:
        pl.when(j != me)(desc.wait_send)


def reduce_bands(partial, col_count):
    rows, width = partial.shape
    band = rows // col_count
    parts = partial.reshape(col_count, band, width)
    return pl.pallas_call(
        reduce_kernel,
        out_shape=jax.ShapeDtypeStruct((band, width), partial.dtype),
        in_specs=[pl.BlockSpec(memory_space=pltpu.VMEM)],
        out_specs=pl.BlockSpec(memory_space=pltpu.VMEM),
        scratch_shapes=[
            pltpu.VMEM((col_count, band, width), partial.dtype),
            pltpu.SemaphoreType.DMA((col_count,)),
            pltpu.SemaphoreType.DMA((col_count,)),
        ],
        compiler_params=pltpu.CompilerParams(collective_id=1, has_side_effects=True),
    )(parts)


def per_device(traces, source_pos, receiver_pos, aperture_list, band_index, weight_tiles):
    samples, shot_count, recv_count = traces.shape
    col_count = axis_count(COL)
    row_count = axis_count(ROW)
    surface_count = recv_count * col_count
    image_panel_width = band_index.shape[0]
    depth_slab_samples = samples // col_count
    cosine, sine_table = phase_tables(samples)
    forward = (jnp.concatenate([cosine, -sine_table], 0) / math.sqrt(samples)).astype(jnp.bfloat16)
    spectra = jnp.dot(
        forward,
        traces.reshape(samples, shot_count * recv_count),
        preferred_element_type=jnp.float32,
    )
    spectra = spectra.astype(jnp.bfloat16).reshape(2, NF, shot_count, recv_count)

    colw, roww = gather_spectra(
        spectra.reshape(2 * NF, shot_count, recv_count), row_count, col_count
    )
    columns_whole = colw.reshape(2, NF, row_count * shot_count, recv_count)
    rows_whole = roww.reshape(2, NF, shot_count, surface_count)

    col_pos = axis_pos(COL)
    row_pos = axis_pos(ROW)
    columns = row_pos * image_panel_width + jnp.arange(image_panel_width, dtype=jnp.int32)
    spread_len = image_panel_width * row_count // 4
    stacking_weights = shot_weights(source_pos, columns, spread_len)
    my_receivers = lax.dynamic_slice_in_dim(receiver_pos, col_pos * recv_count, recv_count, 0)
    aperture = aperture_rows(
        aperture_list, my_receivers, columns, col_pos * recv_count, recv_count, spread_len
    )
    rows_whole, columns_whole, aperture, stacking_weights = lax.optimization_barrier(
        (rows_whole, columns_whole, aperture, stacking_weights)
    )

    summed = complex_product(rows_whole, columns_whole)
    multiples = -summed / math.sqrt(surface_count)
    inverse = jnp.concatenate([cosine, -sine_table], 0).T / math.sqrt(NF)
    wave_field = jnp.dot(
        inverse,
        multiples.reshape(2 * NF, shot_count * recv_count),
        precision=lax.Precision.HIGHEST,
        preferred_element_type=jnp.float32,
    )
    primaries = (
        traces.astype(jnp.float32) - wave_field.reshape(samples, shot_count, recv_count)
    ).astype(jnp.bfloat16)

    partial = jnp.dot(
        primaries.reshape(samples * shot_count, recv_count),
        aperture,
        preferred_element_type=jnp.float32,
    ).reshape(samples, shot_count, image_panel_width)
    partial = jnp.sum(partial * stacking_weights[None], axis=1)
    stacked = reduce_bands(partial, col_count)
    column_stack = (stacked / math.sqrt(shot_count)).astype(jnp.bfloat16)

    tile_kinds = weight_tiles.shape[0]
    select = band_index[None, :] == jnp.arange(tile_kinds, dtype=jnp.int32)[:, None]
    widened = jnp.where(select[:, None, :], column_stack[None], jnp.zeros((), jnp.bfloat16))
    image_out = jnp.einsum(
        "kz,kx->zx",
        weight_tiles.reshape(tile_kinds * depth_slab_samples, weight_tiles.shape[2]),
        widened.reshape(tile_kinds * depth_slab_samples, image_panel_width),
        preferred_element_type=jnp.float32,
    )
    return (primaries, image_out)


def solution(mesh):
    n_row = mesh.shape["row"]
    n_col = mesh.shape["col"]
    fine = Mesh(
        mesh.devices.reshape(4, n_row // 4, 4, n_col // 8, 2), ("x", "zl", "y", "zh", "c")
    )
    placed = (P(None, ROW, COL), P(ROW), P(), P(ROW, None), P(ROW), P())
    return jax.shard_map(
        per_device,
        mesh=fine,
        in_specs=placed,
        out_specs=(P(None, ROW, COL), P(COL, ROW)),
        check_vma=False,
    )
```

```python
import math

import jax
import jax.numpy as jnp
from jax import lax
from jax.experimental import pallas as pl
from jax.experimental.pallas import tpu as pltpu
from jax.sharding import Mesh
from jax.sharding import PartitionSpec as P

NFFT = 4096
NF = 4

ROW = ("x", "zl")
COL = ("y", "zh", "c")


def phase_tables(samples):
    freq_bins = (2 * jnp.arange(NF, dtype=jnp.int32) + 1) * (NFFT // (4 * NF))
    sample_ticks = jnp.arange(samples, dtype=jnp.int32)
    phase_turns = freq_bins[:, None] * sample_ticks[None, :] % NFFT
    phase_angle = phase_turns.astype(jnp.float32) * (2.0 * math.pi / NFFT)
    return (jnp.cos(phase_angle), jnp.sin(phase_angle))


def aperture_rows(tile_index_lists, positions, columns, first_row, row_count, spread_len):
    tile_count, listed = tile_index_lists.shape
    col_width = columns.shape[0]
    rows = first_row + jnp.arange(row_count, dtype=jnp.int32)
    hits = (tile_index_lists[:, :, None] == rows[None, None, :]).astype(jnp.float32)
    member = jnp.sum(hits, axis=1)
    widened = jnp.repeat(member.T, col_width // tile_count, axis=1)
    offset = (positions[:, None] - columns[None, :]).astype(jnp.float32) / spread_len
    taper_weight = 1.0 / (1.0 + offset * offset)
    return (widened * taper_weight * (2.0 / math.sqrt(listed))).astype(jnp.bfloat16)


def shot_weights(positions, columns, spread_len):
    offset = (positions[:, None] - columns[None, :]).astype(jnp.float32) / spread_len
    return 1.0 / (1.0 + offset * offset)


def complex_product(left_section, right_section):
    real_real = jnp.einsum(
        "qju,quy->qjy", left_section[0], right_section[0], preferred_element_type=jnp.float32
    )
    imag_imag = jnp.einsum(
        "qju,quy->qjy", left_section[1], right_section[1], preferred_element_type=jnp.float32
    )
    real_imag = jnp.einsum(
        "qju,quy->qjy", left_section[0], right_section[1], preferred_element_type=jnp.float32
    )
    imag_real = jnp.einsum(
        "qju,quy->qjy", left_section[1], right_section[0], preferred_element_type=jnp.float32
    )
    return jnp.stack([real_real - imag_imag, real_imag + imag_real])


def axis_pos(names):
    index = 0
    for name in names:
        index = index * lax.axis_size(name) + lax.axis_index(name)
    return index


def axis_count(names):
    count = 1
    for name in names:
        count *= lax.axis_size(name)
    return count


MESH_ID = pl.DeviceIdType.MESH
NX, NZ, NY = 4, 8, 4


def fused_kernel(spec_ref, traces_ref, aperture_ref, weights_ref, inverse_ref,
                 prim_ref, stack_ref,
                 colw_ref, roww_ref, mult_ref, partial_ref, slots_ref,
                 recv_row, recv_col, send_row, send_col, recv_red, send_red):
    x = lax.axis_index("x")
    z = lax.axis_index("zl")
    y = lax.axis_index("y")
    h = lax.axis_index("zh")
    c = lax.axis_index("c")
    xp = lax.rem(x + 1, NX)
    xm = lax.rem(x + NX - 1, NX)
    yp = lax.rem(y + 1, NY)
    ym = lax.rem(y + NY - 1, NY)
    me_row = x * NZ + z
    me_col = (y * 2 + h) * 2 + c

    col_peers = []
    for yy in range(NY):
        for hh in range(2):
            for cc in range(2):
                col_peers.append(((yy * 2 + hh) * 2 + cc, {"y": yy, "zh": hh, "c": cc}))

    barrier = pltpu.get_barrier_semaphore()
    for peer in ({"x": xp}, {"x": xm}):
        pl.semaphore_signal(barrier, 1, device_id=peer, device_id_type=MESH_ID)
    for j, peer in col_peers:
        pl.when(j != me_col)(
            lambda peer=peer: pl.semaphore_signal(
                barrier, 1, device_id=peer, device_id_type=MESH_ID
            )
        )

    @pl.when(z > 0)
    def _():
        pl.semaphore_signal(barrier, 1, device_id={"zl": z - 1}, device_id_type=MESH_ID)

    @pl.when(z < NZ - 1)
    def _():
        pl.semaphore_signal(barrier, 1, device_id={"zl": z + 1}, device_id_type=MESH_ID)

    peers_in = 2 + len(col_peers) - 1
    ends = jnp.logical_or(z == 0, z == NZ - 1)
    pl.when(ends)(lambda: pl.semaphore_wait(barrier, peers_in + 1))
    pl.when(jnp.logical_not(ends))(lambda: pl.semaphore_wait(barrier, peers_in + 2))

    started = []
    shots = spec_ref.shape[1]
    recvs = spec_ref.shape[2]
    half = spec_ref.shape[0] // 2
    parts = (0, 1)

    def planes(part):
        return pl.ds(part * half, half)

    def colw_blk(b, part):
        return colw_ref.at[planes(part), pl.ds(pl.multiple_of(b * shots, shots), shots), :]

    def roww_blk(j, part):
        return roww_ref.at[planes(part), :, pl.ds(pl.multiple_of(j * recvs, recvs), recvs)]

    def row_copy(b, part, d, peer, own=False):
        src = spec_ref.at[planes(part)] if own else colw_blk(b, part)
        return pltpu.make_async_remote_copy(
            src, colw_blk(b, part), send_row.at[b, part, d], recv_row.at[b, part],
            device_id=peer, device_id_type=MESH_ID,
        )

    def col_copy(j, part, d, peer, own=False):
        src = spec_ref.at[planes(part)] if own else roww_blk(j, part)
        return pltpu.make_async_remote_copy(
            src, roww_blk(j, part), send_col.at[j, part, d], recv_col.at[j, part],
            device_id=peer, device_id_type=MESH_ID,
        )

    def start(desc, cond=None):
        if cond is None:
            desc.start()
        else:
            pl.when(cond)(desc.start)
        started.append((desc, cond))

    def when(cond, fn):
        if cond is None:
            fn()
        else:
            pl.when(cond)(fn)

    def row_relay(b, sends, cond=None):
        for part in parts:
            when(cond, row_copy(b, part, 0, {"x": x}).wait_recv)
            for d, peer, extra in sends:
                c2 = cond if extra is None else (extra if cond is None else jnp.logical_and(cond, extra))
                start(row_copy(b, part, d, peer), c2)

    def col_relay(j, sends, cond=None):
        for part in parts:
            when(cond, col_copy(j, part, 0, {"y": y}).wait_recv)
            for d, peer in sends:
                start(col_copy(j, part, d, peer), cond)

    for part in parts:
        start(col_copy(me_col, part, 0, {"c": 1 - c}, own=True))
        start(col_copy(me_col, part, 1, {"zh": 1 - h}, own=True))
        start(row_copy(me_row, part, 0, {"zl": z + 1}, own=True), z < NZ - 1)
        start(row_copy(me_row, part, 1, {"zl": z - 1}, own=True), z > 0)
        start(row_copy(me_row, part, 2, {"x": xp}, own=True))
        start(row_copy(me_row, part, 3, {"x": xm}, own=True))
        start(col_copy(me_col, part, 2, {"y": yp}, own=True))
        start(col_copy(me_col, part, 3, {"y": ym}, own=True))
    colw_ref[:, pl.ds(pl.multiple_of(me_row * shots, shots), shots), :] = spec_ref[...]
    roww_ref[:, :, pl.ds(pl.multiple_of(me_col * recvs, recvs), recvs)] = spec_ref[...]

    j_h = (y * 2 + 1 - h) * 2 + c
    j_c = (y * 2 + h) * 2 + 1 - c
    j_hc = (y * 2 + 1 - h) * 2 + 1 - c
    y_sends = ((2, {"y": yp}), (3, {"y": ym}))
    col_relay(j_c, y_sends)

    def x_forward(zsrc, cond):
        even = lax.rem(zsrc, 2) == 0
        row_relay(xm * NZ + zsrc, ((2, {"x": xp}, None),), jnp.logical_and(cond, even))
        odd = jnp.logical_not(even)
        row_relay(xp * NZ + zsrc, ((3, {"x": xm}, None),), jnp.logical_and(cond, odd))

    def x_forward_at(dist):
        if dist == 0:
            x_forward(z, True)
        else:
            x_forward(z - dist, z >= dist)
            x_forward(z + dist, z + dist < NZ)

    lag = 2
    x_sends = ((2, {"x": xp}, None), (3, {"x": xm}, None))
    for k in range(1, NZ):
        row_relay(x * NZ + z - k, ((0, {"zl": z + 1}, z < NZ - 1),) + x_sends, z >= k)
        row_relay(x * NZ + z + k, ((1, {"zl": z - 1}, z > 0),) + x_sends, z + k < NZ)
        if k - lag >= 0:
            x_forward_at(k - lag)
        if k == 2:
            col_relay(j_h, ((0, {"c": 1 - c}),) + y_sends)
        if k == 3:
            col_relay(j_hc, y_sends)
        if k == 4:
            for cc in range(2):
                col_relay((ym * 2 + 0) * 2 + cc, ((2, {"y": yp}),))
                col_relay((yp * 2 + 1) * 2 + cc, ((3, {"y": ym}),))
    for dist in range(NZ - lag, NZ):
        x_forward_at(dist)

    x2 = lax.rem(x + 2, NX)
    for zz in range(NZ):
        row_relay(xm * NZ + zz if zz % 2 == 1 else xp * NZ + zz, ())
        row_relay(x2 * NZ + zz, ())
    y2 = lax.rem(y + 2, NY)
    for cc in range(2):
        col_relay((ym * 2 + 1) * 2 + cc, ())
        col_relay((yp * 2 + 0) * 2 + cc, ())
        for hh in range(2):
            col_relay((y2 * 2 + hh) * 2 + cc, ())
    nf = spec_ref.shape[0] // 2
    surface_root = math.sqrt(roww_ref.shape[2])
    for f in range(nf):
        lr = roww_ref[f]
        li = roww_ref[nf + f]
        rr = colw_ref[f]
        ri = colw_ref[nf + f]
        real_real = jnp.dot(lr, rr, preferred_element_type=jnp.float32)
        imag_imag = jnp.dot(li, ri, preferred_element_type=jnp.float32)
        real_imag = jnp.dot(lr, ri, preferred_element_type=jnp.float32)
        imag_real = jnp.dot(li, rr, preferred_element_type=jnp.float32)
        mult_ref[f] = -(real_real - imag_imag) / surface_root
        mult_ref[nf + f] = -(real_imag + imag_real) / surface_root

    def prim_body(t, carry):
        wave = inverse_ref[t, 0] * mult_ref[0]
        for p in range(1, 2 * nf):
            wave = wave + inverse_ref[t, p] * mult_ref[p]
        prim_ref[t] = (traces_ref[t].astype(jnp.float32) - wave).astype(prim_ref.dtype)
        return carry

    lax.fori_loop(0, traces_ref.shape[0], prim_body, 0)

    band = partial_ref.shape[1]

    def band_body(j, carry):
        rows = []
        for u in range(band):
            stacked = jnp.dot(
                prim_ref[j * band + u], aperture_ref[...], preferred_element_type=jnp.float32
            )
            rows.append(jnp.sum(stacked * weights_ref[...], axis=0, keepdims=True))
        partial_ref[j] = jnp.concatenate(rows, axis=0)
        return carry

    lax.fori_loop(0, partial_ref.shape[0], band_body, 0)

    reduce_sends = []
    for j, peer in col_peers:
        desc = pltpu.make_async_remote_copy(
            partial_ref.at[j], slots_ref.at[me_col], send_red.at[j], recv_red.at[me_col],
            device_id=peer, device_id_type=MESH_ID,
        )
        pl.when(j != me_col)(desc.start)
        reduce_sends.append((j, desc))
    slots_ref[me_col] = partial_ref[me_col]
    for j, peer in col_peers:
        recv = pltpu.make_async_remote_copy(
            partial_ref.at[j], slots_ref.at[j], send_red.at[j], recv_red.at[j],
            device_id=peer, device_id_type=MESH_ID,
        )
        pl.when(j != me_col)(recv.wait_recv)
    total = slots_ref[0]
    for j in range(1, len(col_peers)):
        total = total + slots_ref[j]
    stack_ref[...] = total

    for desc, cond in started:
        when(cond, desc.wait_send)
    for j, desc in reduce_sends:
        pl.when(j != me_col)(desc.wait_send)


def fused_call(spec, traces, aperture, weights, inverse, row_count, col_count):
    planes, shots, recvs = spec.shape
    samples = traces.shape[0]
    band = samples // col_count
    width = aperture.shape[1]
    vmem = pl.BlockSpec(memory_space=pltpu.VMEM)
    return pl.pallas_call(
        fused_kernel,
        out_shape=(
            jax.ShapeDtypeStruct(traces.shape, jnp.bfloat16),
            jax.ShapeDtypeStruct((band, width), jnp.float32),
        ),
        in_specs=[vmem, vmem, vmem, vmem, pl.BlockSpec(memory_space=pltpu.SMEM)],
        out_specs=(vmem, vmem),
        scratch_shapes=[
            pltpu.VMEM((planes, row_count * shots, recvs), spec.dtype),
            pltpu.VMEM((planes, shots, col_count * recvs), spec.dtype),
            pltpu.VMEM((planes, shots, recvs), jnp.float32),
            pltpu.VMEM((col_count, band, width), jnp.float32),
            pltpu.VMEM((col_count, band, width), jnp.float32),
            pltpu.SemaphoreType.DMA((row_count, 2)),
            pltpu.SemaphoreType.DMA((col_count, 2)),
            pltpu.SemaphoreType.DMA((row_count, 2, 4)),
            pltpu.SemaphoreType.DMA((col_count, 2, 4)),
            pltpu.SemaphoreType.DMA((col_count,)),
            pltpu.SemaphoreType.DMA((col_count,)),
        ],
        compiler_params=pltpu.CompilerParams(collective_id=0, has_side_effects=True),
    )(spec, traces, aperture, weights, inverse)


def per_device(traces, source_pos, receiver_pos, aperture_list, band_index, weight_tiles):
    samples, shot_count, recv_count = traces.shape
    col_count = axis_count(COL)
    row_count = axis_count(ROW)
    surface_count = recv_count * col_count
    image_panel_width = band_index.shape[0]
    depth_slab_samples = samples // col_count
    cosine, sine_table = phase_tables(samples)
    forward = (jnp.concatenate([cosine, -sine_table], 0) / math.sqrt(samples)).astype(jnp.bfloat16)
    spectra = jnp.dot(
        forward,
        traces.reshape(samples, shot_count * recv_count),
        preferred_element_type=jnp.float32,
    )
    spectra = spectra.astype(jnp.bfloat16)

    col_pos = axis_pos(COL)
    row_pos = axis_pos(ROW)
    columns = row_pos * image_panel_width + jnp.arange(image_panel_width, dtype=jnp.int32)
    spread_len = image_panel_width * row_count // 4
    stacking_weights = shot_weights(source_pos, columns, spread_len)
    my_receivers = lax.dynamic_slice_in_dim(receiver_pos, col_pos * recv_count, recv_count, 0)
    aperture = aperture_rows(
        aperture_list, my_receivers, columns, col_pos * recv_count, recv_count, spread_len
    )
    inverse = jnp.concatenate([cosine, -sine_table], 0).T / math.sqrt(NF)
    primaries, stacked = fused_call(
        spectra.reshape(2 * NF, shot_count, recv_count),
        traces,
        aperture,
        stacking_weights,
        inverse,
        row_count,
        col_count,
    )
    column_stack = (stacked / math.sqrt(shot_count)).astype(jnp.bfloat16)

    tile_kinds = weight_tiles.shape[0]
    select = band_index[None, :] == jnp.arange(tile_kinds, dtype=jnp.int32)[:, None]
    widened = jnp.where(select[:, None, :], column_stack[None], jnp.zeros((), jnp.bfloat16))
    image_out = jnp.einsum(
        "kz,kx->zx",
        weight_tiles.reshape(tile_kinds * depth_slab_samples, weight_tiles.shape[2]),
        widened.reshape(tile_kinds * depth_slab_samples, image_panel_width),
        preferred_element_type=jnp.float32,
    )
    return (primaries, image_out)


def solution(mesh):
    n_row = mesh.shape["row"]
    n_col = mesh.shape["col"]
    fine = Mesh(
        mesh.devices.reshape(4, n_row // 4, 4, n_col // 8, 2), ("x", "zl", "y", "zh", "c")
    )
    placed = (P(None, ROW, COL), P(ROW), P(), P(ROW, None), P(ROW), P())
    return jax.shard_map(
        per_device,
        mesh=fine,
        in_specs=placed,
        out_specs=(P(None, ROW, COL), P(COL, ROW)),
        check_vma=False,
    )
```

```python
import math

import jax
import jax.numpy as jnp
from jax import lax
from jax.experimental import pallas as pl
from jax.experimental.pallas import tpu as pltpu
from jax.sharding import Mesh
from jax.sharding import PartitionSpec as P

NFFT = 4096
NF = 4

ROW = ("x", "zl")
COL = ("y", "zh", "c")


def phase_tables(samples):
    freq_bins = (2 * jnp.arange(NF, dtype=jnp.int32) + 1) * (NFFT // (4 * NF))
    sample_ticks = jnp.arange(samples, dtype=jnp.int32)
    phase_turns = freq_bins[:, None] * sample_ticks[None, :] % NFFT
    phase_angle = phase_turns.astype(jnp.float32) * (2.0 * math.pi / NFFT)
    return (jnp.cos(phase_angle), jnp.sin(phase_angle))


def aperture_rows(tile_index_lists, positions, columns, first_row, row_count, spread_len):
    tile_count, listed = tile_index_lists.shape
    col_width = columns.shape[0]
    rows = first_row + jnp.arange(row_count, dtype=jnp.int32)
    hits = (tile_index_lists[:, :, None] == rows[None, None, :]).astype(jnp.float32)
    member = jnp.sum(hits, axis=1)
    widened = jnp.repeat(member.T, col_width // tile_count, axis=1)
    offset = (positions[:, None] - columns[None, :]).astype(jnp.float32) / spread_len
    taper_weight = 1.0 / (1.0 + offset * offset)
    return (widened * taper_weight * (2.0 / math.sqrt(listed))).astype(jnp.bfloat16)


def shot_weights(positions, columns, spread_len):
    offset = (positions[:, None] - columns[None, :]).astype(jnp.float32) / spread_len
    return 1.0 / (1.0 + offset * offset)


def complex_product(left_section, right_section):
    real_real = jnp.einsum(
        "qju,quy->qjy", left_section[0], right_section[0], preferred_element_type=jnp.float32
    )
    imag_imag = jnp.einsum(
        "qju,quy->qjy", left_section[1], right_section[1], preferred_element_type=jnp.float32
    )
    real_imag = jnp.einsum(
        "qju,quy->qjy", left_section[0], right_section[1], preferred_element_type=jnp.float32
    )
    imag_real = jnp.einsum(
        "qju,quy->qjy", left_section[1], right_section[0], preferred_element_type=jnp.float32
    )
    return jnp.stack([real_real - imag_imag, real_imag + imag_real])


def axis_pos(names):
    index = 0
    for name in names:
        index = index * lax.axis_size(name) + lax.axis_index(name)
    return index


def axis_count(names):
    count = 1
    for name in names:
        count *= lax.axis_size(name)
    return count


MESH_ID = pl.DeviceIdType.MESH
NX, NZ, NY = 4, 8, 4


def fused_kernel(spec_ref, traces_ref, aperture_ref, weights_ref, inverse_ref,
                 prim_ref, stack_ref,
                 colw_ref, roww_ref, mult_ref, partial_ref, slots_ref,
                 recv_row, recv_col, send_row, send_col, recv_red, send_red):
    x = lax.axis_index("x")
    z = lax.axis_index("zl")
    y = lax.axis_index("y")
    h = lax.axis_index("zh")
    c = lax.axis_index("c")
    xp = lax.rem(x + 1, NX)
    xm = lax.rem(x + NX - 1, NX)
    yp = lax.rem(y + 1, NY)
    ym = lax.rem(y + NY - 1, NY)
    me_row = x * NZ + z
    me_col = (y * 2 + h) * 2 + c

    col_peers = []
    for yy in range(NY):
        for hh in range(2):
            for cc in range(2):
                col_peers.append(((yy * 2 + hh) * 2 + cc, {"y": yy, "zh": hh, "c": cc}))

    barrier = pltpu.get_barrier_semaphore()
    for peer in ({"x": xp}, {"x": xm}):
        pl.semaphore_signal(barrier, 1, device_id=peer, device_id_type=MESH_ID)
    for j, peer in col_peers:
        pl.when(j != me_col)(
            lambda peer=peer: pl.semaphore_signal(
                barrier, 1, device_id=peer, device_id_type=MESH_ID
            )
        )

    @pl.when(z > 0)
    def _():
        pl.semaphore_signal(barrier, 1, device_id={"zl": z - 1}, device_id_type=MESH_ID)

    @pl.when(z < NZ - 1)
    def _():
        pl.semaphore_signal(barrier, 1, device_id={"zl": z + 1}, device_id_type=MESH_ID)

    peers_in = 2 + len(col_peers) - 1
    ends = jnp.logical_or(z == 0, z == NZ - 1)
    pl.when(ends)(lambda: pl.semaphore_wait(barrier, peers_in + 1))
    pl.when(jnp.logical_not(ends))(lambda: pl.semaphore_wait(barrier, peers_in + 2))

    started = []
    shots = spec_ref.shape[1]
    recvs = spec_ref.shape[2]
    half = spec_ref.shape[0] // 2
    parts = (0, 1)

    def planes(part):
        return pl.ds(part * half, half)

    def colw_blk(b, part):
        return colw_ref.at[planes(part), pl.ds(pl.multiple_of(b * shots, shots), shots), :]

    def roww_blk(j, part):
        return roww_ref.at[planes(part), :, pl.ds(pl.multiple_of(j * recvs, recvs), recvs)]

    def row_copy(b, part, d, peer, own=False):
        src = spec_ref.at[planes(part)] if own else colw_blk(b, part)
        return pltpu.make_async_remote_copy(
            src, colw_blk(b, part), send_row.at[b, part, d], recv_row.at[b, part],
            device_id=peer, device_id_type=MESH_ID,
        )

    def col_copy(j, part, d, peer, own=False):
        src = spec_ref.at[planes(part)] if own else roww_blk(j, part)
        return pltpu.make_async_remote_copy(
            src, roww_blk(j, part), send_col.at[j, part, d], recv_col.at[j, part],
            device_id=peer, device_id_type=MESH_ID,
        )

    def start(desc, cond=None):
        if cond is None:
            desc.start()
        else:
            pl.when(cond)(desc.start)
        started.append((desc, cond))

    def when(cond, fn):
        if cond is None:
            fn()
        else:
            pl.when(cond)(fn)

    def row_relay(b, sends, cond=None):
        for part in parts:
            when(cond, row_copy(b, part, 0, {"x": x}).wait_recv)
            for d, peer, extra in sends:
                c2 = cond if extra is None else (extra if cond is None else jnp.logical_and(cond, extra))
                start(row_copy(b, part, d, peer), c2)

    def col_relay(j, sends, cond=None):
        for part in parts:
            when(cond, col_copy(j, part, 0, {"y": y}).wait_recv)
            for d, peer in sends:
                start(col_copy(j, part, d, peer), cond)

    for part in parts:
        start(col_copy(me_col, part, 0, {"c": 1 - c}, own=True))
        start(row_copy(me_row, part, 0, {"zl": z + 1}, own=True), z < NZ - 1)
        start(row_copy(me_row, part, 1, {"zl": z - 1}, own=True), z > 0)
        start(row_copy(me_row, part, 2, {"x": xp}, own=True))
        start(row_copy(me_row, part, 3, {"x": xm}, own=True))
        start(col_copy(me_col, part, 2, {"y": yp}, own=True))
        start(col_copy(me_col, part, 3, {"y": ym}, own=True))
    colw_ref[:, pl.ds(pl.multiple_of(me_row * shots, shots), shots), :] = spec_ref[...]
    roww_ref[:, :, pl.ds(pl.multiple_of(me_col * recvs, recvs), recvs)] = spec_ref[...]

    j_h = (y * 2 + 1 - h) * 2 + c
    j_c = (y * 2 + h) * 2 + 1 - c
    j_hc = (y * 2 + 1 - h) * 2 + 1 - c
    y_sends = ((2, {"y": yp}), (3, {"y": ym}))
    col_relay(j_c, y_sends)

    def x_forward(zsrc, cond):
        even = lax.rem(zsrc, 2) == 0
        row_relay(xm * NZ + zsrc, ((2, {"x": xp}, None),), jnp.logical_and(cond, even))
        odd = jnp.logical_not(even)
        row_relay(xp * NZ + zsrc, ((3, {"x": xm}, None),), jnp.logical_and(cond, odd))

    def x_forward_at(dist):
        if dist == 0:
            x_forward(z, True)
        else:
            x_forward(z - dist, z >= dist)
            x_forward(z + dist, z + dist < NZ)

    lag = 2
    x_sends = ((2, {"x": xp}, None), (3, {"x": xm}, None))
    for k in range(1, NZ):
        row_relay(x * NZ + z - k, ((0, {"zl": z + 1}, z < NZ - 1),) + x_sends, z >= k)
        row_relay(x * NZ + z + k, ((1, {"zl": z - 1}, z > 0),) + x_sends, z + k < NZ)
        if k - lag >= 0:
            x_forward_at(k - lag)
        if k == 2:
            for part in parts:
                start(col_copy(me_col, part, 1, {"zh": 1 - h}, own=True))
        if k == 4:
            col_relay(j_h, ((0, {"c": 1 - c}),) + y_sends)
        if k == 5:
            col_relay(j_hc, y_sends)
        if k == 6:
            for cc in range(2):
                col_relay((ym * 2 + 0) * 2 + cc, ((2, {"y": yp}),))
                col_relay((yp * 2 + 1) * 2 + cc, ((3, {"y": ym}),))
    for dist in range(NZ - lag, NZ):
        x_forward_at(dist)

    x2 = lax.rem(x + 2, NX)
    for zz in range(NZ):
        row_relay(xm * NZ + zz if zz % 2 == 1 else xp * NZ + zz, ())
        row_relay(x2 * NZ + zz, ())
    y2 = lax.rem(y + 2, NY)
    for cc in range(2):
        col_relay((ym * 2 + 1) * 2 + cc, ())
        col_relay((yp * 2 + 0) * 2 + cc, ())
        for hh in range(2):
            col_relay((y2 * 2 + hh) * 2 + cc, ())
    nf = spec_ref.shape[0] // 2
    surface_root = math.sqrt(roww_ref.shape[2])
    for f in range(nf):
        lr = roww_ref[f]
        li = roww_ref[nf + f]
        rr = colw_ref[f]
        ri = colw_ref[nf + f]
        real_real = jnp.dot(lr, rr, preferred_element_type=jnp.float32)
        imag_imag = jnp.dot(li, ri, preferred_element_type=jnp.float32)
        real_imag = jnp.dot(lr, ri, preferred_element_type=jnp.float32)
        imag_real = jnp.dot(li, rr, preferred_element_type=jnp.float32)
        mult_ref[f] = -(real_real - imag_imag) / surface_root
        mult_ref[nf + f] = -(real_imag + imag_real) / surface_root

    def prim_body(t, carry):
        wave = inverse_ref[t, 0] * mult_ref[0]
        for p in range(1, 2 * nf):
            wave = wave + inverse_ref[t, p] * mult_ref[p]
        prim_ref[t] = (traces_ref[t].astype(jnp.float32) - wave).astype(prim_ref.dtype)
        return carry

    lax.fori_loop(0, traces_ref.shape[0], prim_body, 0)

    band = partial_ref.shape[1]

    def band_body(j, carry):
        rows = []
        for u in range(band):
            stacked = jnp.dot(
                prim_ref[j * band + u], aperture_ref[...], preferred_element_type=jnp.float32
            )
            rows.append(jnp.sum(stacked * weights_ref[...], axis=0, keepdims=True))
        partial_ref[j] = jnp.concatenate(rows, axis=0)
        return carry

    lax.fori_loop(0, partial_ref.shape[0], band_body, 0)

    reduce_sends = []
    for j, peer in col_peers:
        desc = pltpu.make_async_remote_copy(
            partial_ref.at[j], slots_ref.at[me_col], send_red.at[j], recv_red.at[me_col],
            device_id=peer, device_id_type=MESH_ID,
        )
        pl.when(j != me_col)(desc.start)
        reduce_sends.append((j, desc))
    slots_ref[me_col] = partial_ref[me_col]
    for j, peer in col_peers:
        recv = pltpu.make_async_remote_copy(
            partial_ref.at[j], slots_ref.at[j], send_red.at[j], recv_red.at[j],
            device_id=peer, device_id_type=MESH_ID,
        )
        pl.when(j != me_col)(recv.wait_recv)
    total = slots_ref[0]
    for j in range(1, len(col_peers)):
        total = total + slots_ref[j]
    stack_ref[...] = total

    for desc, cond in started:
        when(cond, desc.wait_send)
    for j, desc in reduce_sends:
        pl.when(j != me_col)(desc.wait_send)


def fused_call(spec, traces, aperture, weights, inverse, row_count, col_count):
    planes, shots, recvs = spec.shape
    samples = traces.shape[0]
    band = samples // col_count
    width = aperture.shape[1]
    vmem = pl.BlockSpec(memory_space=pltpu.VMEM)
    return pl.pallas_call(
        fused_kernel,
        out_shape=(
            jax.ShapeDtypeStruct(traces.shape, jnp.bfloat16),
            jax.ShapeDtypeStruct((band, width), jnp.float32),
        ),
        in_specs=[vmem, vmem, vmem, vmem, pl.BlockSpec(memory_space=pltpu.SMEM)],
        out_specs=(vmem, vmem),
        scratch_shapes=[
            pltpu.VMEM((planes, row_count * shots, recvs), spec.dtype),
            pltpu.VMEM((planes, shots, col_count * recvs), spec.dtype),
            pltpu.VMEM((planes, shots, recvs), jnp.float32),
            pltpu.VMEM((col_count, band, width), jnp.float32),
            pltpu.VMEM((col_count, band, width), jnp.float32),
            pltpu.SemaphoreType.DMA((row_count, 2)),
            pltpu.SemaphoreType.DMA((col_count, 2)),
            pltpu.SemaphoreType.DMA((row_count, 2, 4)),
            pltpu.SemaphoreType.DMA((col_count, 2, 4)),
            pltpu.SemaphoreType.DMA((col_count,)),
            pltpu.SemaphoreType.DMA((col_count,)),
        ],
        compiler_params=pltpu.CompilerParams(collective_id=0, has_side_effects=True),
    )(spec, traces, aperture, weights, inverse)


def per_device(traces, source_pos, receiver_pos, aperture_list, band_index, weight_tiles):
    samples, shot_count, recv_count = traces.shape
    col_count = axis_count(COL)
    row_count = axis_count(ROW)
    surface_count = recv_count * col_count
    image_panel_width = band_index.shape[0]
    depth_slab_samples = samples // col_count
    cosine, sine_table = phase_tables(samples)
    forward = (jnp.concatenate([cosine, -sine_table], 0) / math.sqrt(samples)).astype(jnp.bfloat16)
    spectra = jnp.dot(
        forward,
        traces.reshape(samples, shot_count * recv_count),
        preferred_element_type=jnp.float32,
    )
    spectra = spectra.astype(jnp.bfloat16)

    col_pos = axis_pos(COL)
    row_pos = axis_pos(ROW)
    columns = row_pos * image_panel_width + jnp.arange(image_panel_width, dtype=jnp.int32)
    spread_len = image_panel_width * row_count // 4
    stacking_weights = shot_weights(source_pos, columns, spread_len)
    my_receivers = lax.dynamic_slice_in_dim(receiver_pos, col_pos * recv_count, recv_count, 0)
    aperture = aperture_rows(
        aperture_list, my_receivers, columns, col_pos * recv_count, recv_count, spread_len
    )
    inverse = jnp.concatenate([cosine, -sine_table], 0).T / math.sqrt(NF)
    primaries, stacked = fused_call(
        spectra.reshape(2 * NF, shot_count, recv_count),
        traces,
        aperture,
        stacking_weights,
        inverse,
        row_count,
        col_count,
    )
    column_stack = (stacked / math.sqrt(shot_count)).astype(jnp.bfloat16)

    tile_kinds = weight_tiles.shape[0]
    select = band_index[None, :] == jnp.arange(tile_kinds, dtype=jnp.int32)[:, None]
    widened = jnp.where(select[:, None, :], column_stack[None], jnp.zeros((), jnp.bfloat16))
    image_out = jnp.einsum(
        "kz,kx->zx",
        weight_tiles.reshape(tile_kinds * depth_slab_samples, weight_tiles.shape[2]),
        widened.reshape(tile_kinds * depth_slab_samples, image_panel_width),
        preferred_element_type=jnp.float32,
    )
    return (primaries, image_out)


def solution(mesh):
    n_row = mesh.shape["row"]
    n_col = mesh.shape["col"]
    fine = Mesh(
        mesh.devices.reshape(4, n_row // 4, 4, n_col // 8, 2), ("x", "zl", "y", "zh", "c")
    )
    placed = (P(None, ROW, COL), P(ROW), P(), P(ROW, None), P(ROW), P())
    return jax.shard_map(
        per_device,
        mesh=fine,
        in_specs=placed,
        out_specs=(P(None, ROW, COL), P(COL, ROW)),
        check_vma=False,
    )
```

```python
import math

import jax
import jax.numpy as jnp
from jax import lax
from jax.experimental import pallas as pl
from jax.experimental.pallas import tpu as pltpu
from jax.sharding import Mesh
from jax.sharding import PartitionSpec as P

NFFT = 4096
NF = 4

ROW = ("x", "zl")
COL = ("y", "zh", "c")


def phase_tables(samples):
    freq_bins = (2 * jnp.arange(NF, dtype=jnp.int32) + 1) * (NFFT // (4 * NF))
    sample_ticks = jnp.arange(samples, dtype=jnp.int32)
    phase_turns = freq_bins[:, None] * sample_ticks[None, :] % NFFT
    phase_angle = phase_turns.astype(jnp.float32) * (2.0 * math.pi / NFFT)
    return (jnp.cos(phase_angle), jnp.sin(phase_angle))


def aperture_rows(tile_index_lists, positions, columns, first_row, row_count, spread_len):
    tile_count, listed = tile_index_lists.shape
    col_width = columns.shape[0]
    rows = first_row + jnp.arange(row_count, dtype=jnp.int32)
    hits = (tile_index_lists[:, :, None] == rows[None, None, :]).astype(jnp.float32)
    member = jnp.sum(hits, axis=1)
    widened = jnp.repeat(member.T, col_width // tile_count, axis=1)
    offset = (positions[:, None] - columns[None, :]).astype(jnp.float32) / spread_len
    taper_weight = 1.0 / (1.0 + offset * offset)
    return (widened * taper_weight * (2.0 / math.sqrt(listed))).astype(jnp.bfloat16)


def shot_weights(positions, columns, spread_len):
    offset = (positions[:, None] - columns[None, :]).astype(jnp.float32) / spread_len
    return 1.0 / (1.0 + offset * offset)


def complex_product(left_section, right_section):
    real_real = jnp.einsum(
        "qju,quy->qjy", left_section[0], right_section[0], preferred_element_type=jnp.float32
    )
    imag_imag = jnp.einsum(
        "qju,quy->qjy", left_section[1], right_section[1], preferred_element_type=jnp.float32
    )
    real_imag = jnp.einsum(
        "qju,quy->qjy", left_section[0], right_section[1], preferred_element_type=jnp.float32
    )
    imag_real = jnp.einsum(
        "qju,quy->qjy", left_section[1], right_section[0], preferred_element_type=jnp.float32
    )
    return jnp.stack([real_real - imag_imag, real_imag + imag_real])


def axis_pos(names):
    index = 0
    for name in names:
        index = index * lax.axis_size(name) + lax.axis_index(name)
    return index


def axis_count(names):
    count = 1
    for name in names:
        count *= lax.axis_size(name)
    return count


MESH_ID = pl.DeviceIdType.MESH
NX, NZ, NY = 4, 8, 4


def fused_kernel(spec_ref, traces_ref, aperture_ref, weights_ref, inverse_ref,
                 prim_ref, stack_ref,
                 colw_ref, roww_ref, mult_ref, partial_ref, slots_ref,
                 recv_row, recv_col, send_row, send_col, recv_red, send_red):
    x = lax.axis_index("x")
    z = lax.axis_index("zl")
    y = lax.axis_index("y")
    h = lax.axis_index("zh")
    c = lax.axis_index("c")
    xp = lax.rem(x + 1, NX)
    xm = lax.rem(x + NX - 1, NX)
    yp = lax.rem(y + 1, NY)
    ym = lax.rem(y + NY - 1, NY)
    x2 = lax.rem(x + 2, NX)
    me_row = x * NZ + z
    me_col = (y * 2 + h) * 2 + c

    col_peers = []
    for yy in range(NY):
        for hh in range(2):
            for cc in range(2):
                col_peers.append(((yy * 2 + hh) * 2 + cc, {"y": yy, "zh": hh, "c": cc}))

    barrier = pltpu.get_barrier_semaphore()
    for peer in ({"x": xp}, {"x": xm}, {"x": x2}):
        pl.semaphore_signal(barrier, 1, device_id=peer, device_id_type=MESH_ID)
    for j, peer in col_peers:
        pl.when(j != me_col)(
            lambda peer=peer: pl.semaphore_signal(
                barrier, 1, device_id=peer, device_id_type=MESH_ID
            )
        )

    @pl.when(z > 0)
    def _():
        pl.semaphore_signal(barrier, 1, device_id={"zl": z - 1}, device_id_type=MESH_ID)

    @pl.when(z < NZ - 1)
    def _():
        pl.semaphore_signal(barrier, 1, device_id={"zl": z + 1}, device_id_type=MESH_ID)

    peers_in = 3 + len(col_peers) - 1
    ends = jnp.logical_or(z == 0, z == NZ - 1)
    pl.when(ends)(lambda: pl.semaphore_wait(barrier, peers_in + 1))
    pl.when(jnp.logical_not(ends))(lambda: pl.semaphore_wait(barrier, peers_in + 2))

    started = []
    shots = spec_ref.shape[1]
    recvs = spec_ref.shape[2]
    half = spec_ref.shape[0] // 2
    parts = (0, 1)

    def planes(part):
        return pl.ds(part * half, half)

    def colw_blk(b, part):
        return colw_ref.at[planes(part), pl.ds(pl.multiple_of(b * shots, shots), shots), :]

    def roww_blk(j, part):
        return roww_ref.at[planes(part), :, pl.ds(pl.multiple_of(j * recvs, recvs), recvs)]

    def row_copy(b, part, d, peer, own=False):
        src = spec_ref.at[planes(part)] if own else colw_blk(b, part)
        return pltpu.make_async_remote_copy(
            src, colw_blk(b, part), send_row.at[b, part, d], recv_row.at[b, part],
            device_id=peer, device_id_type=MESH_ID,
        )

    def col_copy(j, part, d, peer, own=False):
        src = spec_ref.at[planes(part)] if own else roww_blk(j, part)
        return pltpu.make_async_remote_copy(
            src, roww_blk(j, part), send_col.at[j, part, d], recv_col.at[j, part],
            device_id=peer, device_id_type=MESH_ID,
        )

    def start(desc, cond=None):
        if cond is None:
            desc.start()
        else:
            pl.when(cond)(desc.start)
        started.append((desc, cond))

    def when(cond, fn):
        if cond is None:
            fn()
        else:
            pl.when(cond)(fn)

    def row_relay(b, sends, cond=None):
        for part in parts:
            when(cond, row_copy(b, part, 0, {"x": x}).wait_recv)
            for d, peer, extra in sends:
                c2 = cond if extra is None else (extra if cond is None else jnp.logical_and(cond, extra))
                start(row_copy(b, part, d, peer), c2)

    def col_relay(j, sends, cond=None):
        for part in parts:
            when(cond, col_copy(j, part, 0, {"y": y}).wait_recv)
            for d, peer in sends:
                start(col_copy(j, part, d, peer), cond)

    for part in parts:
        start(col_copy(me_col, part, 0, {"c": 1 - c}, own=True))
        start(row_copy(me_row, part, 0, {"zl": z + 1}, own=True), z < NZ - 1)
        start(row_copy(me_row, part, 1, {"zl": z - 1}, own=True), z > 0)
        start(row_copy(me_row, part, 2, {"x": xp}, own=True))
        start(row_copy(me_row, part, 3, {"x": xm}, own=True))
        start(row_copy(me_row, part, 4, {"x": x2}, own=True))
        start(col_copy(me_col, part, 2, {"y": yp}, own=True))
        start(col_copy(me_col, part, 3, {"y": ym}, own=True))
    colw_ref[:, pl.ds(pl.multiple_of(me_row * shots, shots), shots), :] = spec_ref[...]
    roww_ref[:, :, pl.ds(pl.multiple_of(me_col * recvs, recvs), recvs)] = spec_ref[...]

    j_h = (y * 2 + 1 - h) * 2 + c
    j_c = (y * 2 + h) * 2 + 1 - c
    j_hc = (y * 2 + 1 - h) * 2 + 1 - c
    y_sends = ((2, {"y": yp}), (3, {"y": ym}))
    col_relay(j_c, y_sends)

    x_sends = ((2, {"x": xp}, None), (3, {"x": xm}, None), (4, {"x": x2}, None))
    for k in range(1, NZ):
        row_relay(x * NZ + z - k, ((0, {"zl": z + 1}, z < NZ - 1),) + x_sends, z >= k)
        row_relay(x * NZ + z + k, ((1, {"zl": z - 1}, z > 0),) + x_sends, z + k < NZ)
        if k == 2:
            for part in parts:
                start(col_copy(me_col, part, 1, {"zh": 1 - h}, own=True))
        if k == 4:
            col_relay(j_h, ((0, {"c": 1 - c}),) + y_sends)
        if k == 5:
            col_relay(j_hc, y_sends)
        if k == 6:
            for cc in range(2):
                col_relay((ym * 2 + 0) * 2 + cc, ((2, {"y": yp}),))
                col_relay((yp * 2 + 1) * 2 + cc, ((3, {"y": ym}),))

    for zz in range(NZ):
        row_relay(xm * NZ + zz, ())
        row_relay(xp * NZ + zz, ())
        row_relay(x2 * NZ + zz, ())
    y2 = lax.rem(y + 2, NY)
    for cc in range(2):
        col_relay((ym * 2 + 1) * 2 + cc, ())
        col_relay((yp * 2 + 0) * 2 + cc, ())
        for hh in range(2):
            col_relay((y2 * 2 + hh) * 2 + cc, ())
    nf = spec_ref.shape[0] // 2
    surface_root = math.sqrt(roww_ref.shape[2])
    for f in range(nf):
        lr = roww_ref[f]
        li = roww_ref[nf + f]
        rr = colw_ref[f]
        ri = colw_ref[nf + f]
        real_real = jnp.dot(lr, rr, preferred_element_type=jnp.float32)
        imag_imag = jnp.dot(li, ri, preferred_element_type=jnp.float32)
        real_imag = jnp.dot(lr, ri, preferred_element_type=jnp.float32)
        imag_real = jnp.dot(li, rr, preferred_element_type=jnp.float32)
        mult_ref[f] = -(real_real - imag_imag) / surface_root
        mult_ref[nf + f] = -(real_imag + imag_real) / surface_root

    def prim_body(t, carry):
        wave = inverse_ref[t, 0] * mult_ref[0]
        for p in range(1, 2 * nf):
            wave = wave + inverse_ref[t, p] * mult_ref[p]
        prim_ref[t] = (traces_ref[t].astype(jnp.float32) - wave).astype(prim_ref.dtype)
        return carry

    lax.fori_loop(0, traces_ref.shape[0], prim_body, 0)

    band = partial_ref.shape[1]

    def band_body(j, carry):
        rows = []
        for u in range(band):
            stacked = jnp.dot(
                prim_ref[j * band + u], aperture_ref[...], preferred_element_type=jnp.float32
            )
            rows.append(jnp.sum(stacked * weights_ref[...], axis=0, keepdims=True))
        partial_ref[j] = jnp.concatenate(rows, axis=0)
        return carry

    lax.fori_loop(0, partial_ref.shape[0], band_body, 0)

    reduce_sends = []
    for j, peer in col_peers:
        desc = pltpu.make_async_remote_copy(
            partial_ref.at[j], slots_ref.at[me_col], send_red.at[j], recv_red.at[me_col],
            device_id=peer, device_id_type=MESH_ID,
        )
        pl.when(j != me_col)(desc.start)
        reduce_sends.append((j, desc))
    slots_ref[me_col] = partial_ref[me_col]
    for j, peer in col_peers:
        recv = pltpu.make_async_remote_copy(
            partial_ref.at[j], slots_ref.at[j], send_red.at[j], recv_red.at[j],
            device_id=peer, device_id_type=MESH_ID,
        )
        pl.when(j != me_col)(recv.wait_recv)
    total = slots_ref[0]
    for j in range(1, len(col_peers)):
        total = total + slots_ref[j]
    stack_ref[...] = total

    for desc, cond in started:
        when(cond, desc.wait_send)
    for j, desc in reduce_sends:
        pl.when(j != me_col)(desc.wait_send)


def fused_call(spec, traces, aperture, weights, inverse, row_count, col_count):
    planes, shots, recvs = spec.shape
    samples = traces.shape[0]
    band = samples // col_count
    width = aperture.shape[1]
    vmem = pl.BlockSpec(memory_space=pltpu.VMEM)
    return pl.pallas_call(
        fused_kernel,
        out_shape=(
            jax.ShapeDtypeStruct(traces.shape, jnp.bfloat16),
            jax.ShapeDtypeStruct((band, width), jnp.float32),
        ),
        in_specs=[vmem, vmem, vmem, vmem, pl.BlockSpec(memory_space=pltpu.SMEM)],
        out_specs=(vmem, vmem),
        scratch_shapes=[
            pltpu.VMEM((planes, row_count * shots, recvs), spec.dtype),
            pltpu.VMEM((planes, shots, col_count * recvs), spec.dtype),
            pltpu.VMEM((planes, shots, recvs), jnp.float32),
            pltpu.VMEM((col_count, band, width), jnp.float32),
            pltpu.VMEM((col_count, band, width), jnp.float32),
            pltpu.SemaphoreType.DMA((row_count, 2)),
            pltpu.SemaphoreType.DMA((col_count, 2)),
            pltpu.SemaphoreType.DMA((row_count, 2, 5)),
            pltpu.SemaphoreType.DMA((col_count, 2, 4)),
            pltpu.SemaphoreType.DMA((col_count,)),
            pltpu.SemaphoreType.DMA((col_count,)),
        ],
        compiler_params=pltpu.CompilerParams(collective_id=0, has_side_effects=True),
    )(spec, traces, aperture, weights, inverse)


def per_device(traces, source_pos, receiver_pos, aperture_list, band_index, weight_tiles):
    samples, shot_count, recv_count = traces.shape
    col_count = axis_count(COL)
    row_count = axis_count(ROW)
    surface_count = recv_count * col_count
    image_panel_width = band_index.shape[0]
    depth_slab_samples = samples // col_count
    cosine, sine_table = phase_tables(samples)
    forward = (jnp.concatenate([cosine, -sine_table], 0) / math.sqrt(samples)).astype(jnp.bfloat16)
    spectra = jnp.dot(
        forward,
        traces.reshape(samples, shot_count * recv_count),
        preferred_element_type=jnp.float32,
    )
    spectra = spectra.astype(jnp.bfloat16)

    col_pos = axis_pos(COL)
    row_pos = axis_pos(ROW)
    columns = row_pos * image_panel_width + jnp.arange(image_panel_width, dtype=jnp.int32)
    spread_len = image_panel_width * row_count // 4
    stacking_weights = shot_weights(source_pos, columns, spread_len)
    my_receivers = lax.dynamic_slice_in_dim(receiver_pos, col_pos * recv_count, recv_count, 0)
    aperture = aperture_rows(
        aperture_list, my_receivers, columns, col_pos * recv_count, recv_count, spread_len
    )
    inverse = jnp.concatenate([cosine, -sine_table], 0).T / math.sqrt(NF)
    primaries, stacked = fused_call(
        spectra.reshape(2 * NF, shot_count, recv_count),
        traces,
        aperture,
        stacking_weights,
        inverse,
        row_count,
        col_count,
    )
    column_stack = (stacked / math.sqrt(shot_count)).astype(jnp.bfloat16)

    tile_kinds = weight_tiles.shape[0]
    select = band_index[None, :] == jnp.arange(tile_kinds, dtype=jnp.int32)[:, None]
    widened = jnp.where(select[:, None, :], column_stack[None], jnp.zeros((), jnp.bfloat16))
    image_out = jnp.einsum(
        "kz,kx->zx",
        weight_tiles.reshape(tile_kinds * depth_slab_samples, weight_tiles.shape[2]),
        widened.reshape(tile_kinds * depth_slab_samples, image_panel_width),
        preferred_element_type=jnp.float32,
    )
    return (primaries, image_out)


def solution(mesh):
    n_row = mesh.shape["row"]
    n_col = mesh.shape["col"]
    fine = Mesh(
        mesh.devices.reshape(4, n_row // 4, 4, n_col // 8, 2), ("x", "zl", "y", "zh", "c")
    )
    placed = (P(None, ROW, COL), P(ROW), P(), P(ROW, None), P(ROW), P())
    return jax.shard_map(
        per_device,
        mesh=fine,
        in_specs=placed,
        out_specs=(P(None, ROW, COL), P(COL, ROW)),
        check_vma=False,
    )
```

```python
import math

import jax
import ml_dtypes
import numpy as np
import jax.numpy as jnp
from jax import lax
from jax.experimental import pallas as pl
from jax.experimental.pallas import tpu as pltpu
from jax.sharding import Mesh
from jax.sharding import PartitionSpec as P

NFFT = 4096
NF = 4

ROW = ("x", "zl")
COL = ("y", "zh", "c")


def phase_tables_np(samples):
    freq_bins = (2 * np.arange(NF, dtype=np.int32) + 1) * (NFFT // (4 * NF))
    sample_ticks = np.arange(samples, dtype=np.int32)
    phase_turns = freq_bins[:, None] * sample_ticks[None, :] % NFFT
    phase_angle = phase_turns.astype(np.float32) * np.float32(2.0 * math.pi / NFFT)
    angle = phase_angle.astype(np.float64)
    return (np.cos(angle).astype(np.float32), np.sin(angle).astype(np.float32))


def phase_tables(samples):
    freq_bins = (2 * jnp.arange(NF, dtype=jnp.int32) + 1) * (NFFT // (4 * NF))
    sample_ticks = jnp.arange(samples, dtype=jnp.int32)
    phase_turns = freq_bins[:, None] * sample_ticks[None, :] % NFFT
    phase_angle = phase_turns.astype(jnp.float32) * (2.0 * math.pi / NFFT)
    return (jnp.cos(phase_angle), jnp.sin(phase_angle))


def aperture_rows(tile_index_lists, positions, columns, first_row, row_count, spread_len):
    tile_count, listed = tile_index_lists.shape
    col_width = columns.shape[0]
    rows = first_row + jnp.arange(row_count, dtype=jnp.int32)
    hits = (tile_index_lists[:, :, None] == rows[None, None, :]).astype(jnp.float32)
    member = jnp.sum(hits, axis=1)
    widened = jnp.repeat(member.T, col_width // tile_count, axis=1)
    offset = (positions[:, None] - columns[None, :]).astype(jnp.float32) / spread_len
    taper_weight = 1.0 / (1.0 + offset * offset)
    return (widened * taper_weight * (2.0 / math.sqrt(listed))).astype(jnp.bfloat16)


def shot_weights(positions, columns, spread_len):
    offset = (positions[:, None] - columns[None, :]).astype(jnp.float32) / spread_len
    return 1.0 / (1.0 + offset * offset)


def complex_product(left_section, right_section):
    real_real = jnp.einsum(
        "qju,quy->qjy", left_section[0], right_section[0], preferred_element_type=jnp.float32
    )
    imag_imag = jnp.einsum(
        "qju,quy->qjy", left_section[1], right_section[1], preferred_element_type=jnp.float32
    )
    real_imag = jnp.einsum(
        "qju,quy->qjy", left_section[0], right_section[1], preferred_element_type=jnp.float32
    )
    imag_real = jnp.einsum(
        "qju,quy->qjy", left_section[1], right_section[0], preferred_element_type=jnp.float32
    )
    return jnp.stack([real_real - imag_imag, real_imag + imag_real])


def axis_pos(names):
    index = 0
    for name in names:
        index = index * lax.axis_size(name) + lax.axis_index(name)
    return index


def axis_count(names):
    count = 1
    for name in names:
        count *= lax.axis_size(name)
    return count


MESH_ID = pl.DeviceIdType.MESH
NX, NZ, NY = 4, 8, 4


def fused_kernel(spec_ref, traces_ref, aperture_ref, weights_ref, inverse_ref,
                 prim_ref, stack_ref,
                 colw_ref, roww_ref, mult_ref, partial_ref, slots_ref,
                 recv_row, recv_col, send_row, send_col, recv_red, send_red):
    x = lax.axis_index("x")
    z = lax.axis_index("zl")
    y = lax.axis_index("y")
    h = lax.axis_index("zh")
    c = lax.axis_index("c")
    xp = lax.rem(x + 1, NX)
    xm = lax.rem(x + NX - 1, NX)
    yp = lax.rem(y + 1, NY)
    ym = lax.rem(y + NY - 1, NY)
    me_row = x * NZ + z
    me_col = (y * 2 + h) * 2 + c

    col_peers = []
    for yy in range(NY):
        for hh in range(2):
            for cc in range(2):
                col_peers.append(((yy * 2 + hh) * 2 + cc, {"y": yy, "zh": hh, "c": cc}))

    barrier = pltpu.get_barrier_semaphore()
    for peer in ({"x": xp}, {"x": xm}):
        pl.semaphore_signal(barrier, 1, device_id=peer, device_id_type=MESH_ID)
    for j, peer in col_peers:
        pl.when(j != me_col)(
            lambda peer=peer: pl.semaphore_signal(
                barrier, 1, device_id=peer, device_id_type=MESH_ID
            )
        )

    @pl.when(z > 0)
    def _():
        pl.semaphore_signal(barrier, 1, device_id={"zl": z - 1}, device_id_type=MESH_ID)

    @pl.when(z < NZ - 1)
    def _():
        pl.semaphore_signal(barrier, 1, device_id={"zl": z + 1}, device_id_type=MESH_ID)

    peers_in = 2 + len(col_peers) - 1
    ends = jnp.logical_or(z == 0, z == NZ - 1)
    pl.when(ends)(lambda: pl.semaphore_wait(barrier, peers_in + 1))
    pl.when(jnp.logical_not(ends))(lambda: pl.semaphore_wait(barrier, peers_in + 2))

    started = []
    shots = spec_ref.shape[1]
    recvs = spec_ref.shape[2]
    half = spec_ref.shape[0] // 2
    parts = (0, 1)

    def planes(part):
        return pl.ds(part * half, half)

    def colw_blk(b, part):
        return colw_ref.at[planes(part), pl.ds(pl.multiple_of(b * shots, shots), shots), :]

    def roww_blk(j, part):
        return roww_ref.at[planes(part), :, pl.ds(pl.multiple_of(j * recvs, recvs), recvs)]

    def row_copy(b, part, d, peer, own=False):
        src = spec_ref.at[planes(part)] if own else colw_blk(b, part)
        return pltpu.make_async_remote_copy(
            src, colw_blk(b, part), send_row.at[b, part, d], recv_row.at[b, part],
            device_id=peer, device_id_type=MESH_ID,
        )

    def col_copy(j, part, d, peer, own=False):
        src = spec_ref.at[planes(part)] if own else roww_blk(j, part)
        return pltpu.make_async_remote_copy(
            src, roww_blk(j, part), send_col.at[j, part, d], recv_col.at[j, part],
            device_id=peer, device_id_type=MESH_ID,
        )

    def start(desc, cond=None):
        if cond is None:
            desc.start()
        else:
            pl.when(cond)(desc.start)
        started.append((desc, cond))

    def when(cond, fn):
        if cond is None:
            fn()
        else:
            pl.when(cond)(fn)

    def row_relay(b, sends, cond=None):
        for part in parts:
            when(cond, row_copy(b, part, 0, {"x": x}).wait_recv)
            for d, peer, extra in sends:
                c2 = cond if extra is None else (extra if cond is None else jnp.logical_and(cond, extra))
                start(row_copy(b, part, d, peer), c2)

    def col_relay(j, sends, cond=None):
        for part in parts:
            when(cond, col_copy(j, part, 0, {"y": y}).wait_recv)
            for d, peer in sends:
                start(col_copy(j, part, d, peer), cond)

    for part in parts:
        start(col_copy(me_col, part, 0, {"c": 1 - c}, own=True))
        start(row_copy(me_row, part, 0, {"zl": z + 1}, own=True), z < NZ - 1)
        start(row_copy(me_row, part, 1, {"zl": z - 1}, own=True), z > 0)
        start(row_copy(me_row, part, 2, {"x": xp}, own=True))
        start(row_copy(me_row, part, 3, {"x": xm}, own=True))
        start(col_copy(me_col, part, 2, {"y": yp}, own=True))
        start(col_copy(me_col, part, 3, {"y": ym}, own=True))
    colw_ref[:, pl.ds(pl.multiple_of(me_row * shots, shots), shots), :] = spec_ref[...]
    roww_ref[:, :, pl.ds(pl.multiple_of(me_col * recvs, recvs), recvs)] = spec_ref[...]

    j_h = (y * 2 + 1 - h) * 2 + c
    j_c = (y * 2 + h) * 2 + 1 - c
    j_hc = (y * 2 + 1 - h) * 2 + 1 - c
    y_sends = ((2, {"y": yp}), (3, {"y": ym}))
    col_relay(j_c, y_sends)

    def x_forward(zsrc, cond):
        even = lax.rem(zsrc, 2) == 0
        row_relay(xm * NZ + zsrc, ((2, {"x": xp}, None),), jnp.logical_and(cond, even))
        odd = jnp.logical_not(even)
        row_relay(xp * NZ + zsrc, ((3, {"x": xm}, None),), jnp.logical_and(cond, odd))

    def x_forward_at(dist):
        if dist == 0:
            x_forward(z, True)
        else:
            x_forward(z - dist, z >= dist)
            x_forward(z + dist, z + dist < NZ)

    lag = 2
    x_sends = ((2, {"x": xp}, None), (3, {"x": xm}, None))
    for k in range(1, NZ):
        row_relay(x * NZ + z - k, ((0, {"zl": z + 1}, z < NZ - 1),) + x_sends, z >= k)
        row_relay(x * NZ + z + k, ((1, {"zl": z - 1}, z > 0),) + x_sends, z + k < NZ)
        if k - lag >= 0:
            x_forward_at(k - lag)
        if k == 2:
            for part in parts:
                start(col_copy(me_col, part, 1, {"zh": 1 - h}, own=True))
        if k == 4:
            col_relay(j_h, ((0, {"c": 1 - c}),) + y_sends)
        if k == 5:
            col_relay(j_hc, y_sends)
        if k == 6:
            for cc in range(2):
                col_relay((ym * 2 + 0) * 2 + cc, ((2, {"y": yp}),))
                col_relay((yp * 2 + 1) * 2 + cc, ((3, {"y": ym}),))
    for dist in range(NZ - lag, NZ):
        x_forward_at(dist)

    x2 = lax.rem(x + 2, NX)
    for zz in range(NZ):
        row_relay(xm * NZ + zz if zz % 2 == 1 else xp * NZ + zz, ())
        row_relay(x2 * NZ + zz, ())
    y2 = lax.rem(y + 2, NY)
    for cc in range(2):
        col_relay((ym * 2 + 1) * 2 + cc, ())
        col_relay((yp * 2 + 0) * 2 + cc, ())
        for hh in range(2):
            col_relay((y2 * 2 + hh) * 2 + cc, ())
    nf = spec_ref.shape[0] // 2
    surface_root = math.sqrt(roww_ref.shape[2])
    for f in range(nf):
        lr = roww_ref[f]
        li = roww_ref[nf + f]
        rr = colw_ref[f]
        ri = colw_ref[nf + f]
        real_real = jnp.dot(lr, rr, preferred_element_type=jnp.float32)
        imag_imag = jnp.dot(li, ri, preferred_element_type=jnp.float32)
        real_imag = jnp.dot(lr, ri, preferred_element_type=jnp.float32)
        imag_real = jnp.dot(li, rr, preferred_element_type=jnp.float32)
        mult_ref[f] = -(real_real - imag_imag) / surface_root
        mult_ref[nf + f] = -(real_imag + imag_real) / surface_root

    def prim_body(t, carry):
        wave = inverse_ref[t, 0] * mult_ref[0]
        for p in range(1, 2 * nf):
            wave = wave + inverse_ref[t, p] * mult_ref[p]
        prim_ref[t] = (traces_ref[t].astype(jnp.float32) - wave).astype(prim_ref.dtype)
        return carry

    lax.fori_loop(0, traces_ref.shape[0], prim_body, 0)

    band = partial_ref.shape[1]

    def band_peer(i):
        hh = lax.rem(1 - h + i // 8, 2)
        yy = lax.rem(i, 8) // 2
        cc = lax.rem(i, 2)
        return (yy * 2 + hh) * 2 + cc, {"y": yy, "zh": hh, "c": cc}

    def reduce_copy(j, peer):
        return pltpu.make_async_remote_copy(
            partial_ref.at[j], slots_ref.at[me_col], send_red.at[j], recv_red.at[me_col],
            device_id=peer, device_id_type=MESH_ID,
        )

    def band_body(i, carry):
        j, peer = band_peer(i)
        rows = []
        for u in range(band):
            stacked = jnp.dot(
                prim_ref[j * band + u], aperture_ref[...], preferred_element_type=jnp.float32
            )
            rows.append(jnp.sum(stacked * weights_ref[...], axis=0, keepdims=True))
        partial_ref[j] = jnp.concatenate(rows, axis=0)
        pl.when(j != me_col)(reduce_copy(j, peer).start)
        return carry

    lax.fori_loop(0, partial_ref.shape[0], band_body, 0)

    slots_ref[me_col] = partial_ref[me_col]
    for j, peer in col_peers:
        recv = pltpu.make_async_remote_copy(
            partial_ref.at[j], slots_ref.at[j], send_red.at[j], recv_red.at[j],
            device_id=peer, device_id_type=MESH_ID,
        )
        pl.when(j != me_col)(recv.wait_recv)
    total = slots_ref[0]
    for j in range(1, len(col_peers)):
        total = total + slots_ref[j]
    stack_ref[...] = total

    for desc, cond in started:
        when(cond, desc.wait_send)
    for j, peer in col_peers:
        pl.when(j != me_col)(reduce_copy(j, peer).wait_send)


def fused_call(spec, traces, aperture, weights, inverse, row_count, col_count):
    planes, shots, recvs = spec.shape
    samples = traces.shape[0]
    band = samples // col_count
    width = aperture.shape[1]
    vmem = pl.BlockSpec(memory_space=pltpu.VMEM)
    return pl.pallas_call(
        fused_kernel,
        out_shape=(
            jax.ShapeDtypeStruct(traces.shape, jnp.bfloat16),
            jax.ShapeDtypeStruct((band, width), jnp.float32),
        ),
        in_specs=[vmem, vmem, vmem, vmem, pl.BlockSpec(memory_space=pltpu.SMEM)],
        out_specs=(vmem, vmem),
        scratch_shapes=[
            pltpu.VMEM((planes, row_count * shots, recvs), spec.dtype),
            pltpu.VMEM((planes, shots, col_count * recvs), spec.dtype),
            pltpu.VMEM((planes, shots, recvs), jnp.float32),
            pltpu.VMEM((col_count, band, width), jnp.float32),
            pltpu.VMEM((col_count, band, width), jnp.float32),
            pltpu.SemaphoreType.DMA((row_count, 2)),
            pltpu.SemaphoreType.DMA((col_count, 2)),
            pltpu.SemaphoreType.DMA((row_count, 2, 4)),
            pltpu.SemaphoreType.DMA((col_count, 2, 4)),
            pltpu.SemaphoreType.DMA((col_count,)),
            pltpu.SemaphoreType.DMA((col_count,)),
        ],
        compiler_params=pltpu.CompilerParams(collective_id=0, has_side_effects=True),
    )(spec, traces, aperture, weights, inverse)


def per_device(traces, source_pos, receiver_pos, aperture_list, band_index, weight_tiles):
    samples, shot_count, recv_count = traces.shape
    col_count = axis_count(COL)
    row_count = axis_count(ROW)
    surface_count = recv_count * col_count
    image_panel_width = band_index.shape[0]
    depth_slab_samples = samples // col_count
    cosine, sine_table = phase_tables_np(samples)
    forward = jnp.asarray(
        (np.concatenate([cosine, -sine_table], 0) / np.float32(math.sqrt(samples))).astype(
            ml_dtypes.bfloat16
        )
    )
    spectra = jnp.dot(
        forward,
        traces.reshape(samples, shot_count * recv_count),
        preferred_element_type=jnp.float32,
    )
    spectra = spectra.astype(jnp.bfloat16)

    col_pos = axis_pos(COL)
    row_pos = axis_pos(ROW)
    columns = row_pos * image_panel_width + jnp.arange(image_panel_width, dtype=jnp.int32)
    spread_len = image_panel_width * row_count // 4
    stacking_weights = shot_weights(source_pos, columns, spread_len)
    my_receivers = lax.dynamic_slice_in_dim(receiver_pos, col_pos * recv_count, recv_count, 0)
    aperture = aperture_rows(
        aperture_list, my_receivers, columns, col_pos * recv_count, recv_count, spread_len
    )
    inverse = jnp.asarray(np.concatenate([cosine, -sine_table], 0).T / np.float32(math.sqrt(NF)))
    primaries, stacked = fused_call(
        spectra.reshape(2 * NF, shot_count, recv_count),
        traces,
        aperture,
        stacking_weights,
        inverse,
        row_count,
        col_count,
    )
    column_stack = (stacked / math.sqrt(shot_count)).astype(jnp.bfloat16)

    tile_kinds = weight_tiles.shape[0]
    select = band_index[None, :] == jnp.arange(tile_kinds, dtype=jnp.int32)[:, None]
    widened = jnp.where(select[:, None, :], column_stack[None], jnp.zeros((), jnp.bfloat16))
    image_out = jnp.einsum(
        "kz,kx->zx",
        weight_tiles.reshape(tile_kinds * depth_slab_samples, weight_tiles.shape[2]),
        widened.reshape(tile_kinds * depth_slab_samples, image_panel_width),
        preferred_element_type=jnp.float32,
    )
    return (primaries, image_out)


def solution(mesh):
    n_row = mesh.shape["row"]
    n_col = mesh.shape["col"]
    fine = Mesh(
        mesh.devices.reshape(4, n_row // 4, 4, n_col // 8, 2), ("x", "zl", "y", "zh", "c")
    )
    placed = (P(None, ROW, COL), P(ROW), P(), P(ROW, None), P(ROW), P())
    return jax.shard_map(
        per_device,
        mesh=fine,
        in_specs=placed,
        out_specs=(P(None, ROW, COL), P(COL, ROW)),
        check_vma=False,
    )
```

```python
import math

import jax
import ml_dtypes
import numpy as np
import jax.numpy as jnp
from jax import lax
from jax.experimental import pallas as pl
from jax.experimental.pallas import tpu as pltpu
from jax.sharding import Mesh
from jax.sharding import PartitionSpec as P

NFFT = 4096
NF = 4

ROW = ("x", "zl")
COL = ("y", "zh", "c")


def phase_tables_np(samples):
    freq_bins = (2 * np.arange(NF, dtype=np.int32) + 1) * (NFFT // (4 * NF))
    sample_ticks = np.arange(samples, dtype=np.int32)
    phase_turns = freq_bins[:, None] * sample_ticks[None, :] % NFFT
    phase_angle = phase_turns.astype(np.float32) * np.float32(2.0 * math.pi / NFFT)
    angle = phase_angle.astype(np.float64)
    return (np.cos(angle).astype(np.float32), np.sin(angle).astype(np.float32))


def phase_tables(samples):
    freq_bins = (2 * jnp.arange(NF, dtype=jnp.int32) + 1) * (NFFT // (4 * NF))
    sample_ticks = jnp.arange(samples, dtype=jnp.int32)
    phase_turns = freq_bins[:, None] * sample_ticks[None, :] % NFFT
    phase_angle = phase_turns.astype(jnp.float32) * (2.0 * math.pi / NFFT)
    return (jnp.cos(phase_angle), jnp.sin(phase_angle))


def aperture_rows(tile_index_lists, positions, columns, first_row, row_count, spread_len):
    tile_count, listed = tile_index_lists.shape
    col_width = columns.shape[0]
    rows = first_row + jnp.arange(row_count, dtype=jnp.int32)
    hits = (tile_index_lists[:, :, None] == rows[None, None, :]).astype(jnp.float32)
    member = jnp.sum(hits, axis=1)
    widened = jnp.repeat(member.T, col_width // tile_count, axis=1)
    offset = (positions[:, None] - columns[None, :]).astype(jnp.float32) / spread_len
    taper_weight = 1.0 / (1.0 + offset * offset)
    return (widened * taper_weight * (2.0 / math.sqrt(listed))).astype(jnp.bfloat16)


def shot_weights(positions, columns, spread_len):
    offset = (positions[:, None] - columns[None, :]).astype(jnp.float32) / spread_len
    return 1.0 / (1.0 + offset * offset)


def complex_product(left_section, right_section):
    real_real = jnp.einsum(
        "qju,quy->qjy", left_section[0], right_section[0], preferred_element_type=jnp.float32
    )
    imag_imag = jnp.einsum(
        "qju,quy->qjy", left_section[1], right_section[1], preferred_element_type=jnp.float32
    )
    real_imag = jnp.einsum(
        "qju,quy->qjy", left_section[0], right_section[1], preferred_element_type=jnp.float32
    )
    imag_real = jnp.einsum(
        "qju,quy->qjy", left_section[1], right_section[0], preferred_element_type=jnp.float32
    )
    return jnp.stack([real_real - imag_imag, real_imag + imag_real])


def axis_pos(names):
    index = 0
    for name in names:
        index = index * lax.axis_size(name) + lax.axis_index(name)
    return index


def axis_count(names):
    count = 1
    for name in names:
        count *= lax.axis_size(name)
    return count


MESH_ID = pl.DeviceIdType.MESH
NX, NZ, NY = 4, 8, 4


def fused_kernel(spec_ref, traces_ref, lists_ref, rpos_ref, spos_ref, inverse_ref,
                 prim_ref, stack_ref,
                 colw_ref, roww_ref, mult_ref, partial_ref, slots_ref, aperture_ref, weights_ref,
                 recv_row, recv_col, send_row, send_col, recv_red, send_red):
    x = lax.axis_index("x")
    z = lax.axis_index("zl")
    y = lax.axis_index("y")
    h = lax.axis_index("zh")
    c = lax.axis_index("c")
    xp = lax.rem(x + 1, NX)
    xm = lax.rem(x + NX - 1, NX)
    yp = lax.rem(y + 1, NY)
    ym = lax.rem(y + NY - 1, NY)
    me_row = x * NZ + z
    me_col = (y * 2 + h) * 2 + c

    col_peers = []
    for yy in range(NY):
        for hh in range(2):
            for cc in range(2):
                col_peers.append(((yy * 2 + hh) * 2 + cc, {"y": yy, "zh": hh, "c": cc}))

    barrier = pltpu.get_barrier_semaphore()
    for peer in ({"x": xp}, {"x": xm}):
        pl.semaphore_signal(barrier, 1, device_id=peer, device_id_type=MESH_ID)
    for j, peer in col_peers:
        pl.when(j != me_col)(
            lambda peer=peer: pl.semaphore_signal(
                barrier, 1, device_id=peer, device_id_type=MESH_ID
            )
        )

    @pl.when(z > 0)
    def _():
        pl.semaphore_signal(barrier, 1, device_id={"zl": z - 1}, device_id_type=MESH_ID)

    @pl.when(z < NZ - 1)
    def _():
        pl.semaphore_signal(barrier, 1, device_id={"zl": z + 1}, device_id_type=MESH_ID)

    peers_in = 2 + len(col_peers) - 1
    ends = jnp.logical_or(z == 0, z == NZ - 1)
    pl.when(ends)(lambda: pl.semaphore_wait(barrier, peers_in + 1))
    pl.when(jnp.logical_not(ends))(lambda: pl.semaphore_wait(barrier, peers_in + 2))

    started = []
    shots = spec_ref.shape[1]
    recvs = spec_ref.shape[2]
    half = spec_ref.shape[0] // 2
    parts = (0, 1)

    def planes(part):
        return pl.ds(part * half, half)

    def colw_blk(b, part):
        return colw_ref.at[planes(part), pl.ds(pl.multiple_of(b * shots, shots), shots), :]

    def roww_blk(j, part):
        return roww_ref.at[planes(part), :, pl.ds(pl.multiple_of(j * recvs, recvs), recvs)]

    def row_copy(b, part, d, peer, own=False):
        src = spec_ref.at[planes(part)] if own else colw_blk(b, part)
        return pltpu.make_async_remote_copy(
            src, colw_blk(b, part), send_row.at[b, part, d], recv_row.at[b, part],
            device_id=peer, device_id_type=MESH_ID,
        )

    def col_copy(j, part, d, peer, own=False):
        src = spec_ref.at[planes(part)] if own else roww_blk(j, part)
        return pltpu.make_async_remote_copy(
            src, roww_blk(j, part), send_col.at[j, part, d], recv_col.at[j, part],
            device_id=peer, device_id_type=MESH_ID,
        )

    def start(desc, cond=None):
        if cond is None:
            desc.start()
        else:
            pl.when(cond)(desc.start)
        started.append((desc, cond))

    def when(cond, fn):
        if cond is None:
            fn()
        else:
            pl.when(cond)(fn)

    def row_relay(b, sends, cond=None):
        for part in parts:
            when(cond, row_copy(b, part, 0, {"x": x}).wait_recv)
            for d, peer, extra in sends:
                c2 = cond if extra is None else (extra if cond is None else jnp.logical_and(cond, extra))
                start(row_copy(b, part, d, peer), c2)

    def col_relay(j, sends, cond=None):
        for part in parts:
            when(cond, col_copy(j, part, 0, {"y": y}).wait_recv)
            for d, peer in sends:
                start(col_copy(j, part, d, peer), cond)

    for part in parts:
        start(col_copy(me_col, part, 0, {"c": 1 - c}, own=True))
        start(row_copy(me_row, part, 0, {"zl": z + 1}, own=True), z < NZ - 1)
        start(row_copy(me_row, part, 1, {"zl": z - 1}, own=True), z > 0)
        start(row_copy(me_row, part, 2, {"x": xp}, own=True))
        start(row_copy(me_row, part, 3, {"x": xm}, own=True))
        start(col_copy(me_col, part, 2, {"y": yp}, own=True))
        start(col_copy(me_col, part, 3, {"y": ym}, own=True))
    colw_ref[:, pl.ds(pl.multiple_of(me_row * shots, shots), shots), :] = spec_ref[...]
    roww_ref[:, :, pl.ds(pl.multiple_of(me_col * recvs, recvs), recvs)] = spec_ref[...]

    j_h = (y * 2 + 1 - h) * 2 + c
    j_c = (y * 2 + h) * 2 + 1 - c
    j_hc = (y * 2 + 1 - h) * 2 + 1 - c
    y_sends = ((2, {"y": yp}), (3, {"y": ym}))
    col_relay(j_c, y_sends)

    def x_forward(zsrc, cond):
        even = lax.rem(zsrc, 2) == 0
        row_relay(xm * NZ + zsrc, ((2, {"x": xp}, None),), jnp.logical_and(cond, even))
        odd = jnp.logical_not(even)
        row_relay(xp * NZ + zsrc, ((3, {"x": xm}, None),), jnp.logical_and(cond, odd))

    def x_forward_at(dist):
        if dist == 0:
            x_forward(z, True)
        else:
            x_forward(z - dist, z >= dist)
            x_forward(z + dist, z + dist < NZ)

    lag = 2
    x_sends = ((2, {"x": xp}, None), (3, {"x": xm}, None))
    for k in range(1, NZ):
        row_relay(x * NZ + z - k, ((0, {"zl": z + 1}, z < NZ - 1),) + x_sends, z >= k)
        row_relay(x * NZ + z + k, ((1, {"zl": z - 1}, z > 0),) + x_sends, z + k < NZ)
        if k - lag >= 0:
            x_forward_at(k - lag)
        if k == 2:
            for part in parts:
                start(col_copy(me_col, part, 1, {"zh": 1 - h}, own=True))
        if k == 4:
            col_relay(j_h, ((0, {"c": 1 - c}),) + y_sends)
        if k == 5:
            col_relay(j_hc, y_sends)
        if k == 6:
            for cc in range(2):
                col_relay((ym * 2 + 0) * 2 + cc, ((2, {"y": yp}),))
                col_relay((yp * 2 + 1) * 2 + cc, ((3, {"y": ym}),))
    for dist in range(NZ - lag, NZ):
        x_forward_at(dist)

    recvs_n = aperture_ref.shape[0]
    width = aperture_ref.shape[1]
    tiles, listed = lists_ref.shape
    tile_width = width // tiles
    spread_len = width * NX * NZ // 4
    first = me_col * recvs_n

    def as_column(row):
        n = row.shape[1]
        eye = lax.broadcasted_iota(jnp.int32, (n, n), 0) == lax.broadcasted_iota(jnp.int32, (n, n), 1)
        return jnp.sum(jnp.where(eye, row.astype(jnp.float32), 0.0), axis=1, keepdims=True)

    cols = (me_row * width + lax.broadcasted_iota(jnp.int32, (1, width), 1)).astype(jnp.float32)
    rpos = as_column(rpos_ref[:, pl.ds(pl.multiple_of(first, recvs_n), recvs_n)])
    offset = (rpos - cols) / spread_len
    taper = 1.0 / (1.0 + offset * offset)
    rows_here = first + lax.broadcasted_iota(jnp.int32, (recvs_n, listed), 0)
    for t in range(tiles):
        hits = (lists_ref[pl.ds(t, 1), :] == rows_here).astype(jnp.float32)
        member = jnp.sum(hits, axis=1, keepdims=True)
        part = taper[:, t * tile_width:(t + 1) * tile_width]
        aperture_ref[:, t * tile_width:(t + 1) * tile_width] = (
            member * part * (2.0 / math.sqrt(listed))
        ).astype(aperture_ref.dtype)
    spos = as_column(spos_ref[...])
    soffset = (spos - cols) / spread_len
    weights_ref[...] = 1.0 / (1.0 + soffset * soffset)

    x2 = lax.rem(x + 2, NX)
    for zz in range(NZ):
        row_relay(xm * NZ + zz if zz % 2 == 1 else xp * NZ + zz, ())
        row_relay(x2 * NZ + zz, ())
    y2 = lax.rem(y + 2, NY)
    for cc in range(2):
        col_relay((ym * 2 + 1) * 2 + cc, ())
        col_relay((yp * 2 + 0) * 2 + cc, ())
        for hh in range(2):
            col_relay((y2 * 2 + hh) * 2 + cc, ())
    nf = spec_ref.shape[0] // 2
    surface_root = math.sqrt(roww_ref.shape[2])
    for f in range(nf):
        lr = roww_ref[f]
        li = roww_ref[nf + f]
        rr = colw_ref[f]
        ri = colw_ref[nf + f]
        real_real = jnp.dot(lr, rr, preferred_element_type=jnp.float32)
        imag_imag = jnp.dot(li, ri, preferred_element_type=jnp.float32)
        real_imag = jnp.dot(lr, ri, preferred_element_type=jnp.float32)
        imag_real = jnp.dot(li, rr, preferred_element_type=jnp.float32)
        mult_ref[f] = -(real_real - imag_imag) / surface_root
        mult_ref[nf + f] = -(real_imag + imag_real) / surface_root

    def prim_body(t, carry):
        wave = inverse_ref[t, 0] * mult_ref[0]
        for p in range(1, 2 * nf):
            wave = wave + inverse_ref[t, p] * mult_ref[p]
        prim_ref[t] = (traces_ref[t].astype(jnp.float32) - wave).astype(prim_ref.dtype)
        return carry

    lax.fori_loop(0, traces_ref.shape[0], prim_body, 0)

    band = partial_ref.shape[1]

    def band_peer(i):
        hh = lax.rem(1 - h + i // 8, 2)
        yy = lax.rem(i, 8) // 2
        cc = lax.rem(i, 2)
        return (yy * 2 + hh) * 2 + cc, {"y": yy, "zh": hh, "c": cc}

    def reduce_copy(j, peer):
        return pltpu.make_async_remote_copy(
            partial_ref.at[j], slots_ref.at[me_col], send_red.at[j], recv_red.at[me_col],
            device_id=peer, device_id_type=MESH_ID,
        )

    def band_body(i, carry):
        j, peer = band_peer(i)
        rows = []
        for u in range(band):
            stacked = jnp.dot(
                prim_ref[j * band + u], aperture_ref[...], preferred_element_type=jnp.float32
            )
            rows.append(jnp.sum(stacked * weights_ref[...], axis=0, keepdims=True))
        partial_ref[j] = jnp.concatenate(rows, axis=0)
        pl.when(j != me_col)(reduce_copy(j, peer).start)
        return carry

    lax.fori_loop(0, partial_ref.shape[0], band_body, 0)

    slots_ref[me_col] = partial_ref[me_col]
    for j, peer in col_peers:
        recv = pltpu.make_async_remote_copy(
            partial_ref.at[j], slots_ref.at[j], send_red.at[j], recv_red.at[j],
            device_id=peer, device_id_type=MESH_ID,
        )
        pl.when(j != me_col)(recv.wait_recv)
    total = slots_ref[0]
    for j in range(1, len(col_peers)):
        total = total + slots_ref[j]
    stack_ref[...] = total

    for desc, cond in started:
        when(cond, desc.wait_send)
    for j, peer in col_peers:
        pl.when(j != me_col)(reduce_copy(j, peer).wait_send)


def fused_call(spec, traces, lists, rpos, spos, inverse, width, row_count, col_count):
    planes, shots, recvs = spec.shape
    samples = traces.shape[0]
    band = samples // col_count
    vmem = pl.BlockSpec(memory_space=pltpu.VMEM)
    return pl.pallas_call(
        fused_kernel,
        out_shape=(
            jax.ShapeDtypeStruct(traces.shape, jnp.bfloat16),
            jax.ShapeDtypeStruct((band, width), jnp.float32),
        ),
        in_specs=[vmem, vmem, vmem, vmem, vmem, pl.BlockSpec(memory_space=pltpu.SMEM)],
        out_specs=(vmem, vmem),
        scratch_shapes=[
            pltpu.VMEM((planes, row_count * shots, recvs), spec.dtype),
            pltpu.VMEM((planes, shots, col_count * recvs), spec.dtype),
            pltpu.VMEM((planes, shots, recvs), jnp.float32),
            pltpu.VMEM((col_count, band, width), jnp.float32),
            pltpu.VMEM((col_count, band, width), jnp.float32),
            pltpu.VMEM((recvs, width), jnp.bfloat16),
            pltpu.VMEM((shots, width), jnp.float32),
            pltpu.SemaphoreType.DMA((row_count, 2)),
            pltpu.SemaphoreType.DMA((col_count, 2)),
            pltpu.SemaphoreType.DMA((row_count, 2, 4)),
            pltpu.SemaphoreType.DMA((col_count, 2, 4)),
            pltpu.SemaphoreType.DMA((col_count,)),
            pltpu.SemaphoreType.DMA((col_count,)),
        ],
        compiler_params=pltpu.CompilerParams(collective_id=0, has_side_effects=True),
    )(spec, traces, lists, rpos, spos, inverse)


def per_device(traces, source_pos, receiver_pos, aperture_list, band_index, weight_tiles):
    samples, shot_count, recv_count = traces.shape
    col_count = axis_count(COL)
    row_count = axis_count(ROW)
    surface_count = recv_count * col_count
    image_panel_width = band_index.shape[0]
    depth_slab_samples = samples // col_count
    cosine, sine_table = phase_tables_np(samples)
    forward = jnp.asarray(
        (np.concatenate([cosine, -sine_table], 0) / np.float32(math.sqrt(samples))).astype(
            ml_dtypes.bfloat16
        )
    )
    spectra = jnp.einsum(
        "pt,tsr->psr", forward, traces, preferred_element_type=jnp.float32
    ).astype(jnp.bfloat16)

    inverse = jnp.asarray(np.concatenate([cosine, -sine_table], 0).T / np.float32(math.sqrt(NF)))
    primaries, stacked = fused_call(
        spectra,
        traces,
        aperture_list,
        receiver_pos.reshape(1, -1),
        source_pos.reshape(1, -1),
        inverse,
        image_panel_width,
        row_count,
        col_count,
    )
    column_stack = (stacked / math.sqrt(shot_count)).astype(jnp.bfloat16)

    tile_kinds = weight_tiles.shape[0]
    select = band_index[None, :] == jnp.arange(tile_kinds, dtype=jnp.int32)[:, None]
    widened = jnp.where(select[:, None, :], column_stack[None], jnp.zeros((), jnp.bfloat16))
    image_out = jnp.einsum(
        "kz,kx->zx",
        weight_tiles.reshape(tile_kinds * depth_slab_samples, weight_tiles.shape[2]),
        widened.reshape(tile_kinds * depth_slab_samples, image_panel_width),
        preferred_element_type=jnp.float32,
    )
    return (primaries, image_out)


def solution(mesh):
    n_row = mesh.shape["row"]
    n_col = mesh.shape["col"]
    fine = Mesh(
        mesh.devices.reshape(4, n_row // 4, 4, n_col // 8, 2), ("x", "zl", "y", "zh", "c")
    )
    placed = (P(None, ROW, COL), P(ROW), P(), P(ROW, None), P(ROW), P())
    return jax.shard_map(
        per_device,
        mesh=fine,
        in_specs=placed,
        out_specs=(P(None, ROW, COL), P(COL, ROW)),
        check_vma=False,
    )
```

```python
import math

import jax
import ml_dtypes
import numpy as np
import jax.numpy as jnp
from jax import lax
from jax.experimental import pallas as pl
from jax.experimental.pallas import tpu as pltpu
from jax.sharding import Mesh
from jax.sharding import PartitionSpec as P

NFFT = 4096
NF = 4

ROW = ("x", "zl")
COL = ("y", "zh", "c")


def phase_tables_np(samples):
    freq_bins = (2 * np.arange(NF, dtype=np.int32) + 1) * (NFFT // (4 * NF))
    sample_ticks = np.arange(samples, dtype=np.int32)
    phase_turns = freq_bins[:, None] * sample_ticks[None, :] % NFFT
    phase_angle = phase_turns.astype(np.float32) * np.float32(2.0 * math.pi / NFFT)
    angle = phase_angle.astype(np.float64)
    return (np.cos(angle).astype(np.float32), np.sin(angle).astype(np.float32))


def phase_tables(samples):
    freq_bins = (2 * jnp.arange(NF, dtype=jnp.int32) + 1) * (NFFT // (4 * NF))
    sample_ticks = jnp.arange(samples, dtype=jnp.int32)
    phase_turns = freq_bins[:, None] * sample_ticks[None, :] % NFFT
    phase_angle = phase_turns.astype(jnp.float32) * (2.0 * math.pi / NFFT)
    return (jnp.cos(phase_angle), jnp.sin(phase_angle))


def aperture_rows(tile_index_lists, positions, columns, first_row, row_count, spread_len):
    tile_count, listed = tile_index_lists.shape
    col_width = columns.shape[0]
    rows = first_row + jnp.arange(row_count, dtype=jnp.int32)
    hits = (tile_index_lists[:, :, None] == rows[None, None, :]).astype(jnp.float32)
    member = jnp.sum(hits, axis=1)
    widened = jnp.repeat(member.T, col_width // tile_count, axis=1)
    offset = (positions[:, None] - columns[None, :]).astype(jnp.float32) / spread_len
    taper_weight = 1.0 / (1.0 + offset * offset)
    return (widened * taper_weight * (2.0 / math.sqrt(listed))).astype(jnp.bfloat16)


def shot_weights(positions, columns, spread_len):
    offset = (positions[:, None] - columns[None, :]).astype(jnp.float32) / spread_len
    return 1.0 / (1.0 + offset * offset)


def complex_product(left_section, right_section):
    real_real = jnp.einsum(
        "qju,quy->qjy", left_section[0], right_section[0], preferred_element_type=jnp.float32
    )
    imag_imag = jnp.einsum(
        "qju,quy->qjy", left_section[1], right_section[1], preferred_element_type=jnp.float32
    )
    real_imag = jnp.einsum(
        "qju,quy->qjy", left_section[0], right_section[1], preferred_element_type=jnp.float32
    )
    imag_real = jnp.einsum(
        "qju,quy->qjy", left_section[1], right_section[0], preferred_element_type=jnp.float32
    )
    return jnp.stack([real_real - imag_imag, real_imag + imag_real])


def axis_pos(names):
    index = 0
    for name in names:
        index = index * lax.axis_size(name) + lax.axis_index(name)
    return index


def axis_count(names):
    count = 1
    for name in names:
        count *= lax.axis_size(name)
    return count


MESH_ID = pl.DeviceIdType.MESH
NX, NZ, NY = 4, 8, 4


def fused_kernel(spec_ref, traces_ref, lists_ref, rpos_ref, spos_ref, inverse_ref,
                 prim_ref, stack_ref,
                 colw_ref, roww_ref, mult_ref, partial_ref, slots_ref, aperture_ref, weights_ref,
                 recv_row, recv_col, send_row, send_col, recv_red, send_red):
    x = lax.axis_index("x")
    z = lax.axis_index("zl")
    y = lax.axis_index("y")
    h = lax.axis_index("zh")
    c = lax.axis_index("c")
    xp = lax.rem(x + 1, NX)
    xm = lax.rem(x + NX - 1, NX)
    yp = lax.rem(y + 1, NY)
    ym = lax.rem(y + NY - 1, NY)
    me_row = x * NZ + z
    me_col = (y * 2 + h) * 2 + c

    col_peers = []
    for yy in range(NY):
        for hh in range(2):
            for cc in range(2):
                col_peers.append(((yy * 2 + hh) * 2 + cc, {"y": yy, "zh": hh, "c": cc}))

    barrier = pltpu.get_barrier_semaphore()
    for peer in ({"x": xp}, {"x": xm}):
        pl.semaphore_signal(barrier, 1, device_id=peer, device_id_type=MESH_ID)
    for j, peer in col_peers:
        pl.when(j != me_col)(
            lambda peer=peer: pl.semaphore_signal(
                barrier, 1, device_id=peer, device_id_type=MESH_ID
            )
        )

    @pl.when(z > 0)
    def _():
        pl.semaphore_signal(barrier, 1, device_id={"zl": z - 1}, device_id_type=MESH_ID)

    @pl.when(z < NZ - 1)
    def _():
        pl.semaphore_signal(barrier, 1, device_id={"zl": z + 1}, device_id_type=MESH_ID)

    peers_in = 2 + len(col_peers) - 1
    ends = jnp.logical_or(z == 0, z == NZ - 1)
    pl.when(ends)(lambda: pl.semaphore_wait(barrier, peers_in + 1))
    pl.when(jnp.logical_not(ends))(lambda: pl.semaphore_wait(barrier, peers_in + 2))

    started = []
    shots = spec_ref.shape[1]
    recvs = spec_ref.shape[2]
    half = spec_ref.shape[0] // 2
    parts = (0, 1)

    def planes(part):
        return pl.ds(part * half, half)

    def colw_blk(b, part):
        return colw_ref.at[planes(part), pl.ds(pl.multiple_of(b * shots, shots), shots), :]

    def roww_blk(j, part):
        return roww_ref.at[planes(part), :, pl.ds(pl.multiple_of(j * recvs, recvs), recvs)]

    def row_copy(b, part, d, peer, own=False):
        src = spec_ref.at[planes(part)] if own else colw_blk(b, part)
        return pltpu.make_async_remote_copy(
            src, colw_blk(b, part), send_row.at[b, part, d], recv_row.at[b, part],
            device_id=peer, device_id_type=MESH_ID,
        )

    def col_copy(j, part, d, peer, own=False):
        src = spec_ref.at[planes(part)] if own else roww_blk(j, part)
        return pltpu.make_async_remote_copy(
            src, roww_blk(j, part), send_col.at[j, part, d], recv_col.at[j, part],
            device_id=peer, device_id_type=MESH_ID,
        )

    def start(desc, cond=None):
        if cond is None:
            desc.start()
        else:
            pl.when(cond)(desc.start)
        started.append((desc, cond))

    def when(cond, fn):
        if cond is None:
            fn()
        else:
            pl.when(cond)(fn)

    def row_relay(b, sends, cond=None):
        for part in parts:
            when(cond, row_copy(b, part, 0, {"x": x}).wait_recv)
            for d, peer, extra in sends:
                c2 = cond if extra is None else (extra if cond is None else jnp.logical_and(cond, extra))
                start(row_copy(b, part, d, peer), c2)

    def col_relay(j, sends, cond=None):
        for part in parts:
            when(cond, col_copy(j, part, 0, {"y": y}).wait_recv)
            for d, peer in sends:
                start(col_copy(j, part, d, peer), cond)

    for part in parts:
        start(col_copy(me_col, part, 0, {"c": 1 - c}, own=True))
        start(row_copy(me_row, part, 0, {"zl": z + 1}, own=True), z < NZ - 1)
        start(row_copy(me_row, part, 1, {"zl": z - 1}, own=True), z > 0)
        start(row_copy(me_row, part, 2, {"x": xp}, own=True))
        start(row_copy(me_row, part, 3, {"x": xm}, own=True))
        start(col_copy(me_col, part, 2, {"y": yp}, own=True))
        start(col_copy(me_col, part, 3, {"y": ym}, own=True))
    colw_ref[:, pl.ds(pl.multiple_of(me_row * shots, shots), shots), :] = spec_ref[...]
    roww_ref[:, :, pl.ds(pl.multiple_of(me_col * recvs, recvs), recvs)] = spec_ref[...]

    j_h = (y * 2 + 1 - h) * 2 + c
    j_c = (y * 2 + h) * 2 + 1 - c
    j_hc = (y * 2 + 1 - h) * 2 + 1 - c
    y_sends = ((2, {"y": yp}), (3, {"y": ym}))
    col_relay(j_c, y_sends)

    def x_forward(zsrc, cond):
        even = lax.rem(zsrc, 2) == 0
        row_relay(xm * NZ + zsrc, ((2, {"x": xp}, None),), jnp.logical_and(cond, even))
        odd = jnp.logical_not(even)
        row_relay(xp * NZ + zsrc, ((3, {"x": xm}, None),), jnp.logical_and(cond, odd))

    def x_forward_at(dist):
        if dist == 0:
            x_forward(z, True)
        else:
            x_forward(z - dist, z >= dist)
            x_forward(z + dist, z + dist < NZ)

    lag = 2
    x_sends = ((2, {"x": xp}, None), (3, {"x": xm}, None))
    for k in range(1, NZ):
        row_relay(x * NZ + z - k, ((0, {"zl": z + 1}, z < NZ - 1),) + x_sends, z >= k)
        row_relay(x * NZ + z + k, ((1, {"zl": z - 1}, z > 0),) + x_sends, z + k < NZ)
        if k - lag >= 0:
            x_forward_at(k - lag)
        if k == 4:
            for part in parts:
                start(col_copy(me_col, part, 1, {"zh": 1 - h}, own=True))
        if k == 6:
            col_relay(j_h, ((0, {"c": 1 - c}),) + y_sends)
        if k == 7:
            col_relay(j_hc, y_sends)
    for cc in range(2):
        col_relay((ym * 2 + 0) * 2 + cc, ((2, {"y": yp}),))
        col_relay((yp * 2 + 1) * 2 + cc, ((3, {"y": ym}),))
    for dist in range(NZ - lag, NZ):
        x_forward_at(dist)

    recvs_n = aperture_ref.shape[0]
    width = aperture_ref.shape[1]
    tiles, listed = lists_ref.shape
    tile_width = width // tiles
    spread_len = width * NX * NZ // 4
    first = me_col * recvs_n

    def as_column(row):
        n = row.shape[1]
        eye = lax.broadcasted_iota(jnp.int32, (n, n), 0) == lax.broadcasted_iota(jnp.int32, (n, n), 1)
        return jnp.sum(jnp.where(eye, row.astype(jnp.float32), 0.0), axis=1, keepdims=True)

    cols = (me_row * width + lax.broadcasted_iota(jnp.int32, (1, width), 1)).astype(jnp.float32)
    rpos = as_column(rpos_ref[:, pl.ds(pl.multiple_of(first, recvs_n), recvs_n)])
    offset = (rpos - cols) / spread_len
    taper = 1.0 / (1.0 + offset * offset)
    rows_here = first + lax.broadcasted_iota(jnp.int32, (recvs_n, listed), 0)
    for t in range(tiles):
        hits = (lists_ref[pl.ds(t, 1), :] == rows_here).astype(jnp.float32)
        member = jnp.sum(hits, axis=1, keepdims=True)
        part = taper[:, t * tile_width:(t + 1) * tile_width]
        aperture_ref[:, t * tile_width:(t + 1) * tile_width] = (
            member * part * (2.0 / math.sqrt(listed))
        ).astype(aperture_ref.dtype)
    spos = as_column(spos_ref[...])
    soffset = (spos - cols) / spread_len
    weights_ref[...] = 1.0 / (1.0 + soffset * soffset)

    x2 = lax.rem(x + 2, NX)
    for zz in range(NZ):
        row_relay(xm * NZ + zz if zz % 2 == 1 else xp * NZ + zz, ())
        row_relay(x2 * NZ + zz, ())
    y2 = lax.rem(y + 2, NY)
    for cc in range(2):
        col_relay((ym * 2 + 1) * 2 + cc, ())
        col_relay((yp * 2 + 0) * 2 + cc, ())
        for hh in range(2):
            col_relay((y2 * 2 + hh) * 2 + cc, ())
    nf = spec_ref.shape[0] // 2
    surface_root = math.sqrt(roww_ref.shape[2])
    for f in range(nf):
        lr = roww_ref[f]
        li = roww_ref[nf + f]
        rr = colw_ref[f]
        ri = colw_ref[nf + f]
        real_real = jnp.dot(lr, rr, preferred_element_type=jnp.float32)
        imag_imag = jnp.dot(li, ri, preferred_element_type=jnp.float32)
        real_imag = jnp.dot(lr, ri, preferred_element_type=jnp.float32)
        imag_real = jnp.dot(li, rr, preferred_element_type=jnp.float32)
        mult_ref[f] = -(real_real - imag_imag) / surface_root
        mult_ref[nf + f] = -(real_imag + imag_real) / surface_root

    def prim_body(t, carry):
        wave = inverse_ref[t, 0] * mult_ref[0]
        for p in range(1, 2 * nf):
            wave = wave + inverse_ref[t, p] * mult_ref[p]
        prim_ref[t] = (traces_ref[t].astype(jnp.float32) - wave).astype(prim_ref.dtype)
        return carry

    lax.fori_loop(0, traces_ref.shape[0], prim_body, 0)

    band = partial_ref.shape[1]

    def band_peer(i):
        hh = lax.rem(1 - h + i // 8, 2)
        yy = lax.rem(i, 8) // 2
        cc = lax.rem(i, 2)
        return (yy * 2 + hh) * 2 + cc, {"y": yy, "zh": hh, "c": cc}

    def reduce_copy(j, peer):
        return pltpu.make_async_remote_copy(
            partial_ref.at[j], slots_ref.at[me_col], send_red.at[j], recv_red.at[me_col],
            device_id=peer, device_id_type=MESH_ID,
        )

    def band_body(i, carry):
        j, peer = band_peer(i)
        rows = []
        for u in range(band):
            stacked = jnp.dot(
                prim_ref[j * band + u], aperture_ref[...], preferred_element_type=jnp.float32
            )
            rows.append(jnp.sum(stacked * weights_ref[...], axis=0, keepdims=True))
        partial_ref[j] = jnp.concatenate(rows, axis=0)
        pl.when(j != me_col)(reduce_copy(j, peer).start)
        return carry

    lax.fori_loop(0, partial_ref.shape[0], band_body, 0)

    slots_ref[me_col] = partial_ref[me_col]
    for j, peer in col_peers:
        recv = pltpu.make_async_remote_copy(
            partial_ref.at[j], slots_ref.at[j], send_red.at[j], recv_red.at[j],
            device_id=peer, device_id_type=MESH_ID,
        )
        pl.when(j != me_col)(recv.wait_recv)
    total = slots_ref[0]
    for j in range(1, len(col_peers)):
        total = total + slots_ref[j]
    stack_ref[...] = total

    for desc, cond in started:
        when(cond, desc.wait_send)
    for j, peer in col_peers:
        pl.when(j != me_col)(reduce_copy(j, peer).wait_send)


def fused_call(spec, traces, lists, rpos, spos, inverse, width, row_count, col_count):
    planes, shots, recvs = spec.shape
    samples = traces.shape[0]
    band = samples // col_count
    vmem = pl.BlockSpec(memory_space=pltpu.VMEM)
    return pl.pallas_call(
        fused_kernel,
        out_shape=(
            jax.ShapeDtypeStruct(traces.shape, jnp.bfloat16),
            jax.ShapeDtypeStruct((band, width), jnp.float32),
        ),
        in_specs=[vmem, vmem, vmem, vmem, vmem, pl.BlockSpec(memory_space=pltpu.SMEM)],
        out_specs=(vmem, vmem),
        scratch_shapes=[
            pltpu.VMEM((planes, row_count * shots, recvs), spec.dtype),
            pltpu.VMEM((planes, shots, col_count * recvs), spec.dtype),
            pltpu.VMEM((planes, shots, recvs), jnp.float32),
            pltpu.VMEM((col_count, band, width), jnp.float32),
            pltpu.VMEM((col_count, band, width), jnp.float32),
            pltpu.VMEM((recvs, width), jnp.bfloat16),
            pltpu.VMEM((shots, width), jnp.float32),
            pltpu.SemaphoreType.DMA((row_count, 2)),
            pltpu.SemaphoreType.DMA((col_count, 2)),
            pltpu.SemaphoreType.DMA((row_count, 2, 4)),
            pltpu.SemaphoreType.DMA((col_count, 2, 4)),
            pltpu.SemaphoreType.DMA((col_count,)),
            pltpu.SemaphoreType.DMA((col_count,)),
        ],
        compiler_params=pltpu.CompilerParams(collective_id=0, has_side_effects=True),
    )(spec, traces, lists, rpos, spos, inverse)


def per_device(traces, source_pos, receiver_pos, aperture_list, band_index, weight_tiles):
    samples, shot_count, recv_count = traces.shape
    col_count = axis_count(COL)
    row_count = axis_count(ROW)
    surface_count = recv_count * col_count
    image_panel_width = band_index.shape[0]
    depth_slab_samples = samples // col_count
    cosine, sine_table = phase_tables_np(samples)
    forward = jnp.asarray(
        (np.concatenate([cosine, -sine_table], 0) / np.float32(math.sqrt(samples))).astype(
            ml_dtypes.bfloat16
        )
    )
    spectra = jnp.einsum(
        "pt,tsr->psr", forward, traces, preferred_element_type=jnp.float32
    ).astype(jnp.bfloat16)

    inverse = jnp.asarray(np.concatenate([cosine, -sine_table], 0).T / np.float32(math.sqrt(NF)))
    primaries, stacked = fused_call(
        spectra,
        traces,
        aperture_list,
        receiver_pos.reshape(1, -1),
        source_pos.reshape(1, -1),
        inverse,
        image_panel_width,
        row_count,
        col_count,
    )
    column_stack = (stacked / math.sqrt(shot_count)).astype(jnp.bfloat16)

    tile_kinds = weight_tiles.shape[0]
    select = band_index[None, :] == jnp.arange(tile_kinds, dtype=jnp.int32)[:, None]
    widened = jnp.where(select[:, None, :], column_stack[None], jnp.zeros((), jnp.bfloat16))
    image_out = jnp.einsum(
        "kz,kx->zx",
        weight_tiles.reshape(tile_kinds * depth_slab_samples, weight_tiles.shape[2]),
        widened.reshape(tile_kinds * depth_slab_samples, image_panel_width),
        preferred_element_type=jnp.float32,
    )
    return (primaries, image_out)


def solution(mesh):
    n_row = mesh.shape["row"]
    n_col = mesh.shape["col"]
    fine = Mesh(
        mesh.devices.reshape(4, n_row // 4, 4, n_col // 8, 2), ("x", "zl", "y", "zh", "c")
    )
    placed = (P(None, ROW, COL), P(ROW), P(), P(ROW, None), P(ROW), P())
    return jax.shard_map(
        per_device,
        mesh=fine,
        in_specs=placed,
        out_specs=(P(None, ROW, COL), P(COL, ROW)),
        check_vma=False,
    )
```

```python
import math

import jax
import ml_dtypes
import numpy as np
import jax.numpy as jnp
from jax import lax
from jax.experimental import pallas as pl
from jax.experimental.pallas import tpu as pltpu
from jax.sharding import Mesh
from jax.sharding import PartitionSpec as P

NFFT = 4096
NF = 4

ROW = ("x", "zl")
COL = ("y", "zh", "c")


def phase_tables_np(samples):
    freq_bins = (2 * np.arange(NF, dtype=np.int32) + 1) * (NFFT // (4 * NF))
    sample_ticks = np.arange(samples, dtype=np.int32)
    phase_turns = freq_bins[:, None] * sample_ticks[None, :] % NFFT
    phase_angle = phase_turns.astype(np.float32) * np.float32(2.0 * math.pi / NFFT)
    angle = phase_angle.astype(np.float64)
    return (np.cos(angle).astype(np.float32), np.sin(angle).astype(np.float32))


def phase_tables(samples):
    freq_bins = (2 * jnp.arange(NF, dtype=jnp.int32) + 1) * (NFFT // (4 * NF))
    sample_ticks = jnp.arange(samples, dtype=jnp.int32)
    phase_turns = freq_bins[:, None] * sample_ticks[None, :] % NFFT
    phase_angle = phase_turns.astype(jnp.float32) * (2.0 * math.pi / NFFT)
    return (jnp.cos(phase_angle), jnp.sin(phase_angle))


def aperture_rows(tile_index_lists, positions, columns, first_row, row_count, spread_len):
    tile_count, listed = tile_index_lists.shape
    col_width = columns.shape[0]
    rows = first_row + jnp.arange(row_count, dtype=jnp.int32)
    hits = (tile_index_lists[:, :, None] == rows[None, None, :]).astype(jnp.float32)
    member = jnp.sum(hits, axis=1)
    widened = jnp.repeat(member.T, col_width // tile_count, axis=1)
    offset = (positions[:, None] - columns[None, :]).astype(jnp.float32) / spread_len
    taper_weight = 1.0 / (1.0 + offset * offset)
    return (widened * taper_weight * (2.0 / math.sqrt(listed))).astype(jnp.bfloat16)


def shot_weights(positions, columns, spread_len):
    offset = (positions[:, None] - columns[None, :]).astype(jnp.float32) / spread_len
    return 1.0 / (1.0 + offset * offset)


def complex_product(left_section, right_section):
    real_real = jnp.einsum(
        "qju,quy->qjy", left_section[0], right_section[0], preferred_element_type=jnp.float32
    )
    imag_imag = jnp.einsum(
        "qju,quy->qjy", left_section[1], right_section[1], preferred_element_type=jnp.float32
    )
    real_imag = jnp.einsum(
        "qju,quy->qjy", left_section[0], right_section[1], preferred_element_type=jnp.float32
    )
    imag_real = jnp.einsum(
        "qju,quy->qjy", left_section[1], right_section[0], preferred_element_type=jnp.float32
    )
    return jnp.stack([real_real - imag_imag, real_imag + imag_real])


def axis_pos(names):
    index = 0
    for name in names:
        index = index * lax.axis_size(name) + lax.axis_index(name)
    return index


def axis_count(names):
    count = 1
    for name in names:
        count *= lax.axis_size(name)
    return count


MESH_ID = pl.DeviceIdType.MESH
NX, NZ, NY = 4, 8, 4


def fused_kernel(spec_ref, traces_ref, lists_ref, rpos_ref, spos_ref, inverse_ref,
                 prim_ref, stack_ref,
                 colw_ref, roww_ref, mult_ref, partial_ref, slots_ref, aperture_ref, weights_ref,
                 recv_row, recv_col, send_row, send_col, recv_red, send_red):
    x = lax.axis_index("x")
    z = lax.axis_index("zl")
    y = lax.axis_index("y")
    h = lax.axis_index("zh")
    c = lax.axis_index("c")
    xp = lax.rem(x + 1, NX)
    xm = lax.rem(x + NX - 1, NX)
    yp = lax.rem(y + 1, NY)
    ym = lax.rem(y + NY - 1, NY)
    me_row = x * NZ + z
    me_col = (y * 2 + h) * 2 + c

    col_peers = []
    for yy in range(NY):
        for hh in range(2):
            for cc in range(2):
                col_peers.append(((yy * 2 + hh) * 2 + cc, {"y": yy, "zh": hh, "c": cc}))

    barrier = pltpu.get_barrier_semaphore()
    for peer in ({"x": xp}, {"x": xm}):
        pl.semaphore_signal(barrier, 1, device_id=peer, device_id_type=MESH_ID)
    for j, peer in col_peers:
        pl.when(j != me_col)(
            lambda peer=peer: pl.semaphore_signal(
                barrier, 1, device_id=peer, device_id_type=MESH_ID
            )
        )

    @pl.when(z > 0)
    def _():
        pl.semaphore_signal(barrier, 1, device_id={"zl": z - 1}, device_id_type=MESH_ID)

    @pl.when(z < NZ - 1)
    def _():
        pl.semaphore_signal(barrier, 1, device_id={"zl": z + 1}, device_id_type=MESH_ID)

    peers_in = 2 + len(col_peers) - 1
    ends = jnp.logical_or(z == 0, z == NZ - 1)
    pl.when(ends)(lambda: pl.semaphore_wait(barrier, peers_in + 1))
    pl.when(jnp.logical_not(ends))(lambda: pl.semaphore_wait(barrier, peers_in + 2))

    started = []
    shots = spec_ref.shape[1]
    recvs = spec_ref.shape[2]
    half = spec_ref.shape[0] // 2
    parts = (0, 1)

    def planes(part):
        return pl.ds(part * half, half)

    def colw_blk(b, part):
        return colw_ref.at[planes(part), pl.ds(pl.multiple_of(b * shots, shots), shots), :]

    def roww_blk(j, part):
        return roww_ref.at[planes(part), :, pl.ds(pl.multiple_of(j * recvs, recvs), recvs)]

    def row_copy(b, part, d, peer, own=False):
        src = spec_ref.at[planes(part)] if own else colw_blk(b, part)
        return pltpu.make_async_remote_copy(
            src, colw_blk(b, part), send_row.at[b, part, d], recv_row.at[b, part],
            device_id=peer, device_id_type=MESH_ID,
        )

    def col_copy(j, part, d, peer, own=False):
        src = spec_ref.at[planes(part)] if own else roww_blk(j, part)
        return pltpu.make_async_remote_copy(
            src, roww_blk(j, part), send_col.at[j, part, d], recv_col.at[j, part],
            device_id=peer, device_id_type=MESH_ID,
        )

    def start(desc, cond=None):
        if cond is None:
            desc.start()
        else:
            pl.when(cond)(desc.start)
        started.append((desc, cond))

    def when(cond, fn):
        if cond is None:
            fn()
        else:
            pl.when(cond)(fn)

    def row_relay(b, sends, cond=None, only=parts):
        for part in only:
            when(cond, row_copy(b, part, 0, {"x": x}).wait_recv)
            for d, peer, extra in sends:
                c2 = cond if extra is None else (extra if cond is None else jnp.logical_and(cond, extra))
                start(row_copy(b, part, d, peer), c2)

    def col_relay(j, sends, cond=None):
        for part in parts:
            when(cond, col_copy(j, part, 0, {"y": y}).wait_recv)
            for d, peer in sends:
                start(col_copy(j, part, d, peer), cond)

    for part in parts:
        start(col_copy(me_col, part, 0, {"c": 1 - c}, own=True))
        start(row_copy(me_row, part, 0, {"zl": z + 1}, own=True), z < NZ - 1)
        start(row_copy(me_row, part, 1, {"zl": z - 1}, own=True), z > 0)
        start(row_copy(me_row, part, 2, {"x": xp}, own=True))
        start(row_copy(me_row, part, 3, {"x": xm}, own=True))
        start(col_copy(me_col, part, 2, {"y": yp}, own=True))
        start(col_copy(me_col, part, 3, {"y": ym}, own=True))
    colw_ref[:, pl.ds(pl.multiple_of(me_row * shots, shots), shots), :] = spec_ref[...]
    roww_ref[:, :, pl.ds(pl.multiple_of(me_col * recvs, recvs), recvs)] = spec_ref[...]

    j_h = (y * 2 + 1 - h) * 2 + c
    j_c = (y * 2 + h) * 2 + 1 - c
    j_hc = (y * 2 + 1 - h) * 2 + 1 - c
    y_sends = ((2, {"y": yp}), (3, {"y": ym}))
    col_relay(j_c, y_sends)

    def x_forward(zsrc, cond):
        even = lax.rem(zsrc, 2) == 0
        row_relay(xm * NZ + zsrc, ((2, {"x": xp}, None),), jnp.logical_and(cond, even))
        odd = jnp.logical_not(even)
        row_relay(xp * NZ + zsrc, ((3, {"x": xm}, None),), jnp.logical_and(cond, odd))

    def x_forward_at(dist):
        if dist == 0:
            x_forward(z, True)
        else:
            x_forward(z - dist, z >= dist)
            x_forward(z + dist, z + dist < NZ)

    lag = 2
    x_sends = ((2, {"x": xp}, None), (3, {"x": xm}, None))
    for k in range(1, NZ):
        for part in parts:
            row_relay(x * NZ + z - k, ((0, {"zl": z + 1}, z < NZ - 1),) + x_sends, z >= k, (part,))
            row_relay(x * NZ + z + k, ((1, {"zl": z - 1}, z > 0),) + x_sends, z + k < NZ, (part,))
        if k - lag >= 0:
            x_forward_at(k - lag)
        if k == 2:
            for part in parts:
                start(col_copy(me_col, part, 1, {"zh": 1 - h}, own=True))
        if k == 4:
            col_relay(j_h, ((0, {"c": 1 - c}),) + y_sends)
        if k == 5:
            col_relay(j_hc, y_sends)
        if k == 6:
            for cc in range(2):
                col_relay((ym * 2 + 0) * 2 + cc, ((2, {"y": yp}),))
                col_relay((yp * 2 + 1) * 2 + cc, ((3, {"y": ym}),))
    for dist in range(NZ - lag, NZ):
        x_forward_at(dist)

    recvs_n = aperture_ref.shape[0]
    width = aperture_ref.shape[1]
    tiles, listed = lists_ref.shape
    tile_width = width // tiles
    spread_len = width * NX * NZ // 4
    first = me_col * recvs_n

    def as_column(row):
        n = row.shape[1]
        eye = lax.broadcasted_iota(jnp.int32, (n, n), 0) == lax.broadcasted_iota(jnp.int32, (n, n), 1)
        return jnp.sum(jnp.where(eye, row.astype(jnp.float32), 0.0), axis=1, keepdims=True)

    cols = (me_row * width + lax.broadcasted_iota(jnp.int32, (1, width), 1)).astype(jnp.float32)
    rpos = as_column(rpos_ref[:, pl.ds(pl.multiple_of(first, recvs_n), recvs_n)])
    offset = (rpos - cols) / spread_len
    taper = 1.0 / (1.0 + offset * offset)
    rows_here = first + lax.broadcasted_iota(jnp.int32, (recvs_n, listed), 0)
    for t in range(tiles):
        hits = (lists_ref[pl.ds(t, 1), :] == rows_here).astype(jnp.float32)
        member = jnp.sum(hits, axis=1, keepdims=True)
        part = taper[:, t * tile_width:(t + 1) * tile_width]
        aperture_ref[:, t * tile_width:(t + 1) * tile_width] = (
            member * part * (2.0 / math.sqrt(listed))
        ).astype(aperture_ref.dtype)
    spos = as_column(spos_ref[...])
    soffset = (spos - cols) / spread_len
    weights_ref[...] = 1.0 / (1.0 + soffset * soffset)

    x2 = lax.rem(x + 2, NX)
    for zz in range(NZ):
        row_relay(xm * NZ + zz if zz % 2 == 1 else xp * NZ + zz, ())
        row_relay(x2 * NZ + zz, ())
    y2 = lax.rem(y + 2, NY)
    for cc in range(2):
        col_relay((ym * 2 + 1) * 2 + cc, ())
        col_relay((yp * 2 + 0) * 2 + cc, ())
        for hh in range(2):
            col_relay((y2 * 2 + hh) * 2 + cc, ())
    nf = spec_ref.shape[0] // 2
    surface_root = math.sqrt(roww_ref.shape[2])
    for f in range(nf):
        lr = roww_ref[f]
        li = roww_ref[nf + f]
        rr = colw_ref[f]
        ri = colw_ref[nf + f]
        real_real = jnp.dot(lr, rr, preferred_element_type=jnp.float32)
        imag_imag = jnp.dot(li, ri, preferred_element_type=jnp.float32)
        real_imag = jnp.dot(lr, ri, preferred_element_type=jnp.float32)
        imag_real = jnp.dot(li, rr, preferred_element_type=jnp.float32)
        mult_ref[f] = -(real_real - imag_imag) / surface_root
        mult_ref[nf + f] = -(real_imag + imag_real) / surface_root

    def prim_body(t, carry):
        wave = inverse_ref[t, 0] * mult_ref[0]
        for p in range(1, 2 * nf):
            wave = wave + inverse_ref[t, p] * mult_ref[p]
        prim_ref[t] = (traces_ref[t].astype(jnp.float32) - wave).astype(prim_ref.dtype)
        return carry

    lax.fori_loop(0, traces_ref.shape[0], prim_body, 0)

    band = partial_ref.shape[1]

    def band_peer(i):
        hh = lax.rem(1 - h + i // 8, 2)
        yy = lax.rem(i, 8) // 2
        cc = lax.rem(i, 2)
        return (yy * 2 + hh) * 2 + cc, {"y": yy, "zh": hh, "c": cc}

    def reduce_copy(j, peer):
        return pltpu.make_async_remote_copy(
            partial_ref.at[j], slots_ref.at[me_col], send_red.at[j], recv_red.at[me_col],
            device_id=peer, device_id_type=MESH_ID,
        )

    def band_body(i, carry):
        j, peer = band_peer(i)
        rows = []
        for u in range(band):
            stacked = jnp.dot(
                prim_ref[j * band + u], aperture_ref[...], preferred_element_type=jnp.float32
            )
            rows.append(jnp.sum(stacked * weights_ref[...], axis=0, keepdims=True))
        partial_ref[j] = jnp.concatenate(rows, axis=0)
        pl.when(j != me_col)(reduce_copy(j, peer).start)
        return carry

    lax.fori_loop(0, partial_ref.shape[0], band_body, 0)

    slots_ref[me_col] = partial_ref[me_col]
    for j, peer in col_peers:
        recv = pltpu.make_async_remote_copy(
            partial_ref.at[j], slots_ref.at[j], send_red.at[j], recv_red.at[j],
            device_id=peer, device_id_type=MESH_ID,
        )
        pl.when(j != me_col)(recv.wait_recv)
    total = slots_ref[0]
    for j in range(1, len(col_peers)):
        total = total + slots_ref[j]
    stack_ref[...] = total

    for desc, cond in started:
        when(cond, desc.wait_send)
    for j, peer in col_peers:
        pl.when(j != me_col)(reduce_copy(j, peer).wait_send)


def fused_call(spec, traces, lists, rpos, spos, inverse, width, row_count, col_count):
    planes, shots, recvs = spec.shape
    samples = traces.shape[0]
    band = samples // col_count
    vmem = pl.BlockSpec(memory_space=pltpu.VMEM)
    return pl.pallas_call(
        fused_kernel,
        out_shape=(
            jax.ShapeDtypeStruct(traces.shape, jnp.bfloat16),
            jax.ShapeDtypeStruct((band, width), jnp.float32),
        ),
        in_specs=[vmem, vmem, vmem, vmem, vmem, pl.BlockSpec(memory_space=pltpu.SMEM)],
        out_specs=(vmem, vmem),
        scratch_shapes=[
            pltpu.VMEM((planes, row_count * shots, recvs), spec.dtype),
            pltpu.VMEM((planes, shots, col_count * recvs), spec.dtype),
            pltpu.VMEM((planes, shots, recvs), jnp.float32),
            pltpu.VMEM((col_count, band, width), jnp.float32),
            pltpu.VMEM((col_count, band, width), jnp.float32),
            pltpu.VMEM((recvs, width), jnp.bfloat16),
            pltpu.VMEM((shots, width), jnp.float32),
            pltpu.SemaphoreType.DMA((row_count, 2)),
            pltpu.SemaphoreType.DMA((col_count, 2)),
            pltpu.SemaphoreType.DMA((row_count, 2, 4)),
            pltpu.SemaphoreType.DMA((col_count, 2, 4)),
            pltpu.SemaphoreType.DMA((col_count,)),
            pltpu.SemaphoreType.DMA((col_count,)),
        ],
        compiler_params=pltpu.CompilerParams(collective_id=0, has_side_effects=True),
    )(spec, traces, lists, rpos, spos, inverse)


def per_device(traces, source_pos, receiver_pos, aperture_list, band_index, weight_tiles):
    samples, shot_count, recv_count = traces.shape
    col_count = axis_count(COL)
    row_count = axis_count(ROW)
    surface_count = recv_count * col_count
    image_panel_width = band_index.shape[0]
    depth_slab_samples = samples // col_count
    cosine, sine_table = phase_tables_np(samples)
    forward = jnp.asarray(
        (np.concatenate([cosine, -sine_table], 0) / np.float32(math.sqrt(samples))).astype(
            ml_dtypes.bfloat16
        )
    )
    spectra = jnp.einsum(
        "pt,tsr->psr", forward, traces, preferred_element_type=jnp.float32
    ).astype(jnp.bfloat16)

    inverse = jnp.asarray(np.concatenate([cosine, -sine_table], 0).T / np.float32(math.sqrt(NF)))
    primaries, stacked = fused_call(
        spectra,
        traces,
        aperture_list,
        receiver_pos.reshape(1, -1),
        source_pos.reshape(1, -1),
        inverse,
        image_panel_width,
        row_count,
        col_count,
    )
    column_stack = (stacked / math.sqrt(shot_count)).astype(jnp.bfloat16)

    tile_kinds = weight_tiles.shape[0]
    select = band_index[None, :] == jnp.arange(tile_kinds, dtype=jnp.int32)[:, None]
    widened = jnp.where(select[:, None, :], column_stack[None], jnp.zeros((), jnp.bfloat16))
    image_out = jnp.einsum(
        "kz,kx->zx",
        weight_tiles.reshape(tile_kinds * depth_slab_samples, weight_tiles.shape[2]),
        widened.reshape(tile_kinds * depth_slab_samples, image_panel_width),
        preferred_element_type=jnp.float32,
    )
    return (primaries, image_out)


def solution(mesh):
    n_row = mesh.shape["row"]
    n_col = mesh.shape["col"]
    fine = Mesh(
        mesh.devices.reshape(4, n_row // 4, 4, n_col // 8, 2), ("x", "zl", "y", "zh", "c")
    )
    placed = (P(None, ROW, COL), P(ROW), P(), P(ROW, None), P(ROW), P())
    return jax.shard_map(
        per_device,
        mesh=fine,
        in_specs=placed,
        out_specs=(P(None, ROW, COL), P(COL, ROW)),
        check_vma=False,
    )
```

```python
import math

import jax
import ml_dtypes
import numpy as np
import jax.numpy as jnp
from jax import lax
from jax.experimental import pallas as pl
from jax.experimental.pallas import tpu as pltpu
from jax.sharding import Mesh
from jax.sharding import PartitionSpec as P

NFFT = 4096
NF = 4

ROW = ("x", "zl")
COL = ("y", "zh", "c")


def phase_tables_np(samples):
    freq_bins = (2 * np.arange(NF, dtype=np.int32) + 1) * (NFFT // (4 * NF))
    sample_ticks = np.arange(samples, dtype=np.int32)
    phase_turns = freq_bins[:, None] * sample_ticks[None, :] % NFFT
    phase_angle = phase_turns.astype(np.float32) * np.float32(2.0 * math.pi / NFFT)
    angle = phase_angle.astype(np.float64)
    return (np.cos(angle).astype(np.float32), np.sin(angle).astype(np.float32))


def phase_tables(samples):
    freq_bins = (2 * jnp.arange(NF, dtype=jnp.int32) + 1) * (NFFT // (4 * NF))
    sample_ticks = jnp.arange(samples, dtype=jnp.int32)
    phase_turns = freq_bins[:, None] * sample_ticks[None, :] % NFFT
    phase_angle = phase_turns.astype(jnp.float32) * (2.0 * math.pi / NFFT)
    return (jnp.cos(phase_angle), jnp.sin(phase_angle))


def aperture_rows(tile_index_lists, positions, columns, first_row, row_count, spread_len):
    tile_count, listed = tile_index_lists.shape
    col_width = columns.shape[0]
    rows = first_row + jnp.arange(row_count, dtype=jnp.int32)
    hits = (tile_index_lists[:, :, None] == rows[None, None, :]).astype(jnp.float32)
    member = jnp.sum(hits, axis=1)
    widened = jnp.repeat(member.T, col_width // tile_count, axis=1)
    offset = (positions[:, None] - columns[None, :]).astype(jnp.float32) / spread_len
    taper_weight = 1.0 / (1.0 + offset * offset)
    return (widened * taper_weight * (2.0 / math.sqrt(listed))).astype(jnp.bfloat16)


def shot_weights(positions, columns, spread_len):
    offset = (positions[:, None] - columns[None, :]).astype(jnp.float32) / spread_len
    return 1.0 / (1.0 + offset * offset)


def complex_product(left_section, right_section):
    real_real = jnp.einsum(
        "qju,quy->qjy", left_section[0], right_section[0], preferred_element_type=jnp.float32
    )
    imag_imag = jnp.einsum(
        "qju,quy->qjy", left_section[1], right_section[1], preferred_element_type=jnp.float32
    )
    real_imag = jnp.einsum(
        "qju,quy->qjy", left_section[0], right_section[1], preferred_element_type=jnp.float32
    )
    imag_real = jnp.einsum(
        "qju,quy->qjy", left_section[1], right_section[0], preferred_element_type=jnp.float32
    )
    return jnp.stack([real_real - imag_imag, real_imag + imag_real])


def axis_pos(names):
    index = 0
    for name in names:
        index = index * lax.axis_size(name) + lax.axis_index(name)
    return index


def axis_count(names):
    count = 1
    for name in names:
        count *= lax.axis_size(name)
    return count


MESH_ID = pl.DeviceIdType.MESH
NX, NZ, NY = 4, 8, 4


def fused_kernel(spec_ref, traces_ref, lists_ref, rpos_ref, spos_ref, inverse_ref,
                 prim_ref, stack_ref,
                 colw_ref, roww_ref, mult_ref, partial_ref, slots_ref, aperture_ref, weights_ref,
                 recv_row, recv_col, send_row, send_col, recv_red, send_red):
    x = lax.axis_index("x")
    z = lax.axis_index("zl")
    y = lax.axis_index("y")
    h = lax.axis_index("zh")
    c = lax.axis_index("c")
    xp = lax.rem(x + 1, NX)
    xm = lax.rem(x + NX - 1, NX)
    yp = lax.rem(y + 1, NY)
    ym = lax.rem(y + NY - 1, NY)
    me_row = x * NZ + z
    me_col = (y * 2 + h) * 2 + c

    col_peers = []
    for yy in range(NY):
        for hh in range(2):
            for cc in range(2):
                col_peers.append(((yy * 2 + hh) * 2 + cc, {"y": yy, "zh": hh, "c": cc}))

    barrier = pltpu.get_barrier_semaphore()
    for peer in ({"x": xp}, {"x": xm}):
        pl.semaphore_signal(barrier, 1, device_id=peer, device_id_type=MESH_ID)
    for j, peer in col_peers:
        pl.when(j != me_col)(
            lambda peer=peer: pl.semaphore_signal(
                barrier, 1, device_id=peer, device_id_type=MESH_ID
            )
        )

    @pl.when(z > 0)
    def _():
        pl.semaphore_signal(barrier, 1, device_id={"zl": z - 1}, device_id_type=MESH_ID)

    @pl.when(z < NZ - 1)
    def _():
        pl.semaphore_signal(barrier, 1, device_id={"zl": z + 1}, device_id_type=MESH_ID)

    peers_in = 2 + len(col_peers) - 1
    ends = jnp.logical_or(z == 0, z == NZ - 1)
    pl.when(ends)(lambda: pl.semaphore_wait(barrier, peers_in + 1))
    pl.when(jnp.logical_not(ends))(lambda: pl.semaphore_wait(barrier, peers_in + 2))

    started = []
    shots = spec_ref.shape[1]
    recvs = spec_ref.shape[2]
    half = spec_ref.shape[0] // 2
    parts = (0, 1)

    def planes(part):
        return pl.ds(part * half, half)

    def colw_blk(b, part):
        return colw_ref.at[planes(part), pl.ds(pl.multiple_of(b * shots, shots), shots), :]

    def roww_blk(j, part):
        return roww_ref.at[planes(part), :, pl.ds(pl.multiple_of(j * recvs, recvs), recvs)]

    def row_copy(b, part, d, peer, own=False):
        src = spec_ref.at[planes(part)] if own else colw_blk(b, part)
        return pltpu.make_async_remote_copy(
            src, colw_blk(b, part), send_row.at[b, part, d], recv_row.at[b, part],
            device_id=peer, device_id_type=MESH_ID,
        )

    def col_copy(j, part, d, peer, own=False):
        src = spec_ref.at[planes(part)] if own else roww_blk(j, part)
        return pltpu.make_async_remote_copy(
            src, roww_blk(j, part), send_col.at[j, part, d], recv_col.at[j, part],
            device_id=peer, device_id_type=MESH_ID,
        )

    def start(desc, cond=None):
        if cond is None:
            desc.start()
        else:
            pl.when(cond)(desc.start)
        started.append((desc, cond))

    def when(cond, fn):
        if cond is None:
            fn()
        else:
            pl.when(cond)(fn)

    def row_relay(b, sends, cond=None, only=parts):
        for part in only:
            when(cond, row_copy(b, part, 0, {"x": x}).wait_recv)
            for d, peer, extra in sends:
                c2 = cond if extra is None else (extra if cond is None else jnp.logical_and(cond, extra))
                start(row_copy(b, part, d, peer), c2)

    def col_relay(j, sends, cond=None):
        for part in parts:
            when(cond, col_copy(j, part, 0, {"y": y}).wait_recv)
            for d, peer in sends:
                start(col_copy(j, part, d, peer), cond)

    for part in parts:
        start(col_copy(me_col, part, 0, {"c": 1 - c}, own=True))
        start(row_copy(me_row, part, 0, {"zl": z + 1}, own=True), z < NZ - 1)
        start(row_copy(me_row, part, 1, {"zl": z - 1}, own=True), z > 0)
        start(row_copy(me_row, part, 2, {"x": xp}, own=True))
        start(row_copy(me_row, part, 3, {"x": xm}, own=True))
        start(col_copy(me_col, part, 2, {"y": yp}, own=True))
        start(col_copy(me_col, part, 3, {"y": ym}, own=True))
    colw_ref[:, pl.ds(pl.multiple_of(me_row * shots, shots), shots), :] = spec_ref[...]
    roww_ref[:, :, pl.ds(pl.multiple_of(me_col * recvs, recvs), recvs)] = spec_ref[...]

    j_h = (y * 2 + 1 - h) * 2 + c
    j_c = (y * 2 + h) * 2 + 1 - c
    j_hc = (y * 2 + 1 - h) * 2 + 1 - c
    y_sends = ((2, {"y": yp}), (3, {"y": ym}))
    col_relay(j_c, y_sends)

    def x_forward(zsrc, cond):
        even = lax.rem(zsrc, 2) == 0
        row_relay(xm * NZ + zsrc, ((2, {"x": xp}, None),), jnp.logical_and(cond, even))
        odd = jnp.logical_not(even)
        row_relay(xp * NZ + zsrc, ((3, {"x": xm}, None),), jnp.logical_and(cond, odd))

    def x_forward_at(dist):
        if dist == 0:
            x_forward(z, True)
        else:
            x_forward(z - dist, z >= dist)
            x_forward(z + dist, z + dist < NZ)

    lag = 3
    x_sends = ((2, {"x": xp}, None), (3, {"x": xm}, None))

    def send_across(items):
        for b, part, cond in items:
            for d, peer, _ in x_sends:
                start(row_copy(b, part, d, peer), cond)

    pending = []
    for k in range(1, NZ):
        arrived = []
        for part in parts:
            b_lo = x * NZ + z - k
            row_relay(b_lo, ((0, {"zl": z + 1}, z < NZ - 1),), z >= k, (part,))
            arrived.append((b_lo, part, z >= k))
            b_hi = x * NZ + z + k
            row_relay(b_hi, ((1, {"zl": z - 1}, z > 0),), z + k < NZ, (part,))
            arrived.append((b_hi, part, z + k < NZ))
        send_across(pending)
        pending = arrived
        if k - lag >= 0:
            x_forward_at(k - lag)
        if k == 2:
            for part in parts:
                start(col_copy(me_col, part, 1, {"zh": 1 - h}, own=True))
        if k == 4:
            col_relay(j_h, ((0, {"c": 1 - c}),) + y_sends)
        if k == 5:
            col_relay(j_hc, y_sends)
        if k == 6:
            for cc in range(2):
                col_relay((ym * 2 + 0) * 2 + cc, ((2, {"y": yp}),))
                col_relay((yp * 2 + 1) * 2 + cc, ((3, {"y": ym}),))
    send_across(pending)
    for dist in range(NZ - lag, NZ):
        x_forward_at(dist)

    recvs_n = aperture_ref.shape[0]
    width = aperture_ref.shape[1]
    tiles, listed = lists_ref.shape
    tile_width = width // tiles
    spread_len = width * NX * NZ // 4
    first = me_col * recvs_n

    def as_column(row):
        n = row.shape[1]
        eye = lax.broadcasted_iota(jnp.int32, (n, n), 0) == lax.broadcasted_iota(jnp.int32, (n, n), 1)
        return jnp.sum(jnp.where(eye, row.astype(jnp.float32), 0.0), axis=1, keepdims=True)

    cols = (me_row * width + lax.broadcasted_iota(jnp.int32, (1, width), 1)).astype(jnp.float32)
    rpos = as_column(rpos_ref[:, pl.ds(pl.multiple_of(first, recvs_n), recvs_n)])
    offset = (rpos - cols) / spread_len
    taper = 1.0 / (1.0 + offset * offset)
    rows_here = first + lax.broadcasted_iota(jnp.int32, (recvs_n, listed), 0)
    for t in range(tiles):
        hits = (lists_ref[pl.ds(t, 1), :] == rows_here).astype(jnp.float32)
        member = jnp.sum(hits, axis=1, keepdims=True)
        part = taper[:, t * tile_width:(t + 1) * tile_width]
        aperture_ref[:, t * tile_width:(t + 1) * tile_width] = (
            member * part * (2.0 / math.sqrt(listed))
        ).astype(aperture_ref.dtype)
    spos = as_column(spos_ref[...])
    soffset = (spos - cols) / spread_len
    weights_ref[...] = 1.0 / (1.0 + soffset * soffset)

    x2 = lax.rem(x + 2, NX)
    for zz in range(NZ):
        row_relay(xm * NZ + zz if zz % 2 == 1 else xp * NZ + zz, ())
        row_relay(x2 * NZ + zz, ())
    y2 = lax.rem(y + 2, NY)
    for cc in range(2):
        col_relay((ym * 2 + 1) * 2 + cc, ())
        col_relay((yp * 2 + 0) * 2 + cc, ())
        for hh in range(2):
            col_relay((y2 * 2 + hh) * 2 + cc, ())
    nf = spec_ref.shape[0] // 2
    surface_root = math.sqrt(roww_ref.shape[2])
    for f in range(nf):
        lr = roww_ref[f]
        li = roww_ref[nf + f]
        rr = colw_ref[f]
        ri = colw_ref[nf + f]
        real_real = jnp.dot(lr, rr, preferred_element_type=jnp.float32)
        imag_imag = jnp.dot(li, ri, preferred_element_type=jnp.float32)
        real_imag = jnp.dot(lr, ri, preferred_element_type=jnp.float32)
        imag_real = jnp.dot(li, rr, preferred_element_type=jnp.float32)
        mult_ref[f] = -(real_real - imag_imag) / surface_root
        mult_ref[nf + f] = -(real_imag + imag_real) / surface_root

    def prim_body(t, carry):
        wave = inverse_ref[t, 0] * mult_ref[0]
        for p in range(1, 2 * nf):
            wave = wave + inverse_ref[t, p] * mult_ref[p]
        prim_ref[t] = (traces_ref[t].astype(jnp.float32) - wave).astype(prim_ref.dtype)
        return carry

    lax.fori_loop(0, traces_ref.shape[0], prim_body, 0)

    band = partial_ref.shape[1]

    def band_peer(i):
        hh = lax.rem(1 - h + i // 8, 2)
        yy = lax.rem(i, 8) // 2
        cc = lax.rem(i, 2)
        return (yy * 2 + hh) * 2 + cc, {"y": yy, "zh": hh, "c": cc}

    def reduce_copy(j, peer):
        return pltpu.make_async_remote_copy(
            partial_ref.at[j], slots_ref.at[me_col], send_red.at[j], recv_red.at[me_col],
            device_id=peer, device_id_type=MESH_ID,
        )

    def band_body(i, carry):
        j, peer = band_peer(i)
        rows = []
        for u in range(band):
            stacked = jnp.dot(
                prim_ref[j * band + u], aperture_ref[...], preferred_element_type=jnp.float32
            )
            rows.append(jnp.sum(stacked * weights_ref[...], axis=0, keepdims=True))
        partial_ref[j] = jnp.concatenate(rows, axis=0)
        pl.when(j != me_col)(reduce_copy(j, peer).start)
        return carry

    lax.fori_loop(0, partial_ref.shape[0], band_body, 0)

    slots_ref[me_col] = partial_ref[me_col]
    for j, peer in col_peers:
        recv = pltpu.make_async_remote_copy(
            partial_ref.at[j], slots_ref.at[j], send_red.at[j], recv_red.at[j],
            device_id=peer, device_id_type=MESH_ID,
        )
        pl.when(j != me_col)(recv.wait_recv)
    total = slots_ref[0]
    for j in range(1, len(col_peers)):
        total = total + slots_ref[j]
    stack_ref[...] = total

    for desc, cond in started:
        when(cond, desc.wait_send)
    for j, peer in col_peers:
        pl.when(j != me_col)(reduce_copy(j, peer).wait_send)


def fused_call(spec, traces, lists, rpos, spos, inverse, width, row_count, col_count):
    planes, shots, recvs = spec.shape
    samples = traces.shape[0]
    band = samples // col_count
    vmem = pl.BlockSpec(memory_space=pltpu.VMEM)
    return pl.pallas_call(
        fused_kernel,
        out_shape=(
            jax.ShapeDtypeStruct(traces.shape, jnp.bfloat16),
            jax.ShapeDtypeStruct((band, width), jnp.float32),
        ),
        in_specs=[vmem, vmem, vmem, vmem, vmem, pl.BlockSpec(memory_space=pltpu.SMEM)],
        out_specs=(vmem, vmem),
        scratch_shapes=[
            pltpu.VMEM((planes, row_count * shots, recvs), spec.dtype),
            pltpu.VMEM((planes, shots, col_count * recvs), spec.dtype),
            pltpu.VMEM((planes, shots, recvs), jnp.float32),
            pltpu.VMEM((col_count, band, width), jnp.float32),
            pltpu.VMEM((col_count, band, width), jnp.float32),
            pltpu.VMEM((recvs, width), jnp.bfloat16),
            pltpu.VMEM((shots, width), jnp.float32),
            pltpu.SemaphoreType.DMA((row_count, 2)),
            pltpu.SemaphoreType.DMA((col_count, 2)),
            pltpu.SemaphoreType.DMA((row_count, 2, 4)),
            pltpu.SemaphoreType.DMA((col_count, 2, 4)),
            pltpu.SemaphoreType.DMA((col_count,)),
            pltpu.SemaphoreType.DMA((col_count,)),
        ],
        compiler_params=pltpu.CompilerParams(collective_id=0, has_side_effects=True),
    )(spec, traces, lists, rpos, spos, inverse)


def per_device(traces, source_pos, receiver_pos, aperture_list, band_index, weight_tiles):
    samples, shot_count, recv_count = traces.shape
    col_count = axis_count(COL)
    row_count = axis_count(ROW)
    surface_count = recv_count * col_count
    image_panel_width = band_index.shape[0]
    depth_slab_samples = samples // col_count
    cosine, sine_table = phase_tables_np(samples)
    forward = jnp.asarray(
        (np.concatenate([cosine, -sine_table], 0) / np.float32(math.sqrt(samples))).astype(
            ml_dtypes.bfloat16
        )
    )
    spectra = jnp.einsum(
        "pt,tsr->psr", forward, traces, preferred_element_type=jnp.float32
    ).astype(jnp.bfloat16)

    inverse = jnp.asarray(np.concatenate([cosine, -sine_table], 0).T / np.float32(math.sqrt(NF)))
    primaries, stacked = fused_call(
        spectra,
        traces,
        aperture_list,
        receiver_pos.reshape(1, -1),
        source_pos.reshape(1, -1),
        inverse,
        image_panel_width,
        row_count,
        col_count,
    )
    column_stack = (stacked / math.sqrt(shot_count)).astype(jnp.bfloat16)

    tile_kinds = weight_tiles.shape[0]
    select = band_index[None, :] == jnp.arange(tile_kinds, dtype=jnp.int32)[:, None]
    widened = jnp.where(select[:, None, :], column_stack[None], jnp.zeros((), jnp.bfloat16))
    image_out = jnp.einsum(
        "kz,kx->zx",
        weight_tiles.reshape(tile_kinds * depth_slab_samples, weight_tiles.shape[2]),
        widened.reshape(tile_kinds * depth_slab_samples, image_panel_width),
        preferred_element_type=jnp.float32,
    )
    return (primaries, image_out)


def solution(mesh):
    n_row = mesh.shape["row"]
    n_col = mesh.shape["col"]
    fine = Mesh(
        mesh.devices.reshape(4, n_row // 4, 4, n_col // 8, 2), ("x", "zl", "y", "zh", "c")
    )
    placed = (P(None, ROW, COL), P(ROW), P(), P(ROW, None), P(ROW), P())
    return jax.shard_map(
        per_device,
        mesh=fine,
        in_specs=placed,
        out_specs=(P(None, ROW, COL), P(COL, ROW)),
        check_vma=False,
    )
```

```python
import math

import jax
import ml_dtypes
import numpy as np
import jax.numpy as jnp
from jax import lax
from jax.experimental import pallas as pl
from jax.experimental.pallas import tpu as pltpu
from jax.sharding import Mesh
from jax.sharding import PartitionSpec as P

NFFT = 4096
NF = 4

ROW = ("x", "zl")
COL = ("y", "zh", "c")


def phase_tables_np(samples):
    freq_bins = (2 * np.arange(NF, dtype=np.int32) + 1) * (NFFT // (4 * NF))
    sample_ticks = np.arange(samples, dtype=np.int32)
    phase_turns = freq_bins[:, None] * sample_ticks[None, :] % NFFT
    phase_angle = phase_turns.astype(np.float32) * np.float32(2.0 * math.pi / NFFT)
    angle = phase_angle.astype(np.float64)
    return (np.cos(angle).astype(np.float32), np.sin(angle).astype(np.float32))


def phase_tables(samples):
    freq_bins = (2 * jnp.arange(NF, dtype=jnp.int32) + 1) * (NFFT // (4 * NF))
    sample_ticks = jnp.arange(samples, dtype=jnp.int32)
    phase_turns = freq_bins[:, None] * sample_ticks[None, :] % NFFT
    phase_angle = phase_turns.astype(jnp.float32) * (2.0 * math.pi / NFFT)
    return (jnp.cos(phase_angle), jnp.sin(phase_angle))


def aperture_rows(tile_index_lists, positions, columns, first_row, row_count, spread_len):
    tile_count, listed = tile_index_lists.shape
    col_width = columns.shape[0]
    rows = first_row + jnp.arange(row_count, dtype=jnp.int32)
    hits = (tile_index_lists[:, :, None] == rows[None, None, :]).astype(jnp.float32)
    member = jnp.sum(hits, axis=1)
    widened = jnp.repeat(member.T, col_width // tile_count, axis=1)
    offset = (positions[:, None] - columns[None, :]).astype(jnp.float32) / spread_len
    taper_weight = 1.0 / (1.0 + offset * offset)
    return (widened * taper_weight * (2.0 / math.sqrt(listed))).astype(jnp.bfloat16)


def shot_weights(positions, columns, spread_len):
    offset = (positions[:, None] - columns[None, :]).astype(jnp.float32) / spread_len
    return 1.0 / (1.0 + offset * offset)


def complex_product(left_section, right_section):
    real_real = jnp.einsum(
        "qju,quy->qjy", left_section[0], right_section[0], preferred_element_type=jnp.float32
    )
    imag_imag = jnp.einsum(
        "qju,quy->qjy", left_section[1], right_section[1], preferred_element_type=jnp.float32
    )
    real_imag = jnp.einsum(
        "qju,quy->qjy", left_section[0], right_section[1], preferred_element_type=jnp.float32
    )
    imag_real = jnp.einsum(
        "qju,quy->qjy", left_section[1], right_section[0], preferred_element_type=jnp.float32
    )
    return jnp.stack([real_real - imag_imag, real_imag + imag_real])


def axis_pos(names):
    index = 0
    for name in names:
        index = index * lax.axis_size(name) + lax.axis_index(name)
    return index


def axis_count(names):
    count = 1
    for name in names:
        count *= lax.axis_size(name)
    return count


MESH_ID = pl.DeviceIdType.MESH
NX, NZ, NY = 4, 8, 4


def fused_kernel(spec_ref, traces_ref, lists_ref, rpos_ref, spos_ref, inverse_ref,
                 prim_ref, stack_ref,
                 colw_ref, roww_ref, mult_ref, partial_ref, slots_ref, aperture_ref, weights_ref,
                 recv_row, recv_col, send_row, send_col, recv_red, send_red):
    x = lax.axis_index("x")
    z = lax.axis_index("zl")
    y = lax.axis_index("y")
    h = lax.axis_index("zh")
    c = lax.axis_index("c")
    xp = lax.rem(x + 1, NX)
    xm = lax.rem(x + NX - 1, NX)
    yp = lax.rem(y + 1, NY)
    ym = lax.rem(y + NY - 1, NY)
    me_row = x * NZ + z
    me_col = (y * 2 + h) * 2 + c

    col_peers = []
    for yy in range(NY):
        for hh in range(2):
            for cc in range(2):
                col_peers.append(((yy * 2 + hh) * 2 + cc, {"y": yy, "zh": hh, "c": cc}))

    barrier = pltpu.get_barrier_semaphore()
    for peer in ({"x": xp}, {"x": xm}):
        pl.semaphore_signal(barrier, 1, device_id=peer, device_id_type=MESH_ID)
    for j, peer in col_peers:
        pl.when(j != me_col)(
            lambda peer=peer: pl.semaphore_signal(
                barrier, 1, device_id=peer, device_id_type=MESH_ID
            )
        )

    @pl.when(z > 0)
    def _():
        pl.semaphore_signal(barrier, 1, device_id={"zl": z - 1}, device_id_type=MESH_ID)

    @pl.when(z < NZ - 1)
    def _():
        pl.semaphore_signal(barrier, 1, device_id={"zl": z + 1}, device_id_type=MESH_ID)

    peers_in = 2 + len(col_peers) - 1
    ends = jnp.logical_or(z == 0, z == NZ - 1)
    pl.when(ends)(lambda: pl.semaphore_wait(barrier, peers_in + 1))
    pl.when(jnp.logical_not(ends))(lambda: pl.semaphore_wait(barrier, peers_in + 2))

    started = []
    shots = spec_ref.shape[1]
    recvs = spec_ref.shape[2]
    half = spec_ref.shape[0] // 2
    parts = (0, 1)

    def planes(part):
        return pl.ds(part * half, half)

    def colw_blk(b, part):
        return colw_ref.at[planes(part), pl.ds(pl.multiple_of(b * shots, shots), shots), :]

    def roww_blk(j, part):
        return roww_ref.at[planes(part), :, pl.ds(pl.multiple_of(j * recvs, recvs), recvs)]

    def row_copy(b, part, d, peer, own=False):
        src = spec_ref.at[planes(part)] if own else colw_blk(b, part)
        return pltpu.make_async_remote_copy(
            src, colw_blk(b, part), send_row.at[b, part, d], recv_row.at[b, part],
            device_id=peer, device_id_type=MESH_ID,
        )

    def col_copy(j, part, d, peer, own=False):
        src = spec_ref.at[planes(part)] if own else roww_blk(j, part)
        return pltpu.make_async_remote_copy(
            src, roww_blk(j, part), send_col.at[j, part, d], recv_col.at[j, part],
            device_id=peer, device_id_type=MESH_ID,
        )

    def start(desc, cond=None):
        if cond is None:
            desc.start()
        else:
            pl.when(cond)(desc.start)
        started.append((desc, cond))

    def when(cond, fn):
        if cond is None:
            fn()
        else:
            pl.when(cond)(fn)

    def row_relay(b, sends, cond=None, only=parts):
        for part in only:
            when(cond, row_copy(b, part, 0, {"x": x}).wait_recv)
            for d, peer, extra in sends:
                c2 = cond if extra is None else (extra if cond is None else jnp.logical_and(cond, extra))
                start(row_copy(b, part, d, peer), c2)

    def col_relay(j, sends, cond=None):
        for part in parts:
            when(cond, col_copy(j, part, 0, {"y": y}).wait_recv)
            for d, peer in sends:
                start(col_copy(j, part, d, peer), cond)

    for part in parts:
        start(col_copy(me_col, part, 0, {"c": 1 - c}, own=True))
        start(row_copy(me_row, part, 0, {"zl": z + 1}, own=True), z < NZ - 1)
        start(row_copy(me_row, part, 1, {"zl": z - 1}, own=True), z > 0)
        start(row_copy(me_row, part, 2, {"x": xp}, own=True))
        start(row_copy(me_row, part, 3, {"x": xm}, own=True))
        start(col_copy(me_col, part, 2, {"y": yp}, own=True))
        start(col_copy(me_col, part, 3, {"y": ym}, own=True))
    colw_ref[:, pl.ds(pl.multiple_of(me_row * shots, shots), shots), :] = spec_ref[...]
    roww_ref[:, :, pl.ds(pl.multiple_of(me_col * recvs, recvs), recvs)] = spec_ref[...]

    j_h = (y * 2 + 1 - h) * 2 + c
    j_c = (y * 2 + h) * 2 + 1 - c
    j_hc = (y * 2 + 1 - h) * 2 + 1 - c
    y_sends = ((2, {"y": yp}), (3, {"y": ym}))
    col_relay(j_c, y_sends)

    def x_forward(zsrc, cond):
        even = lax.rem(zsrc, 2) == 0
        row_relay(xm * NZ + zsrc, ((2, {"x": xp}, None),), jnp.logical_and(cond, even))
        odd = jnp.logical_not(even)
        row_relay(xp * NZ + zsrc, ((3, {"x": xm}, None),), jnp.logical_and(cond, odd))

    def x_forward_at(dist):
        if dist == 0:
            x_forward(z, True)
        else:
            x_forward(z - dist, z >= dist)
            x_forward(z + dist, z + dist < NZ)

    lag = 2
    x_sends = ((2, {"x": xp}, None), (3, {"x": xm}, None))
    for k in range(1, NZ):
        for part in parts:
            row_relay(x * NZ + z - k, x_sends + ((0, {"zl": z + 1}, z < NZ - 1),), z >= k, (part,))
            row_relay(x * NZ + z + k, x_sends + ((1, {"zl": z - 1}, z > 0),), z + k < NZ, (part,))
        if k - lag >= 0:
            x_forward_at(k - lag)
        if k == 2:
            for part in parts:
                start(col_copy(me_col, part, 1, {"zh": 1 - h}, own=True))
        if k == 4:
            col_relay(j_h, ((0, {"c": 1 - c}),) + y_sends)
        if k == 5:
            col_relay(j_hc, y_sends)
        if k == 6:
            for cc in range(2):
                col_relay((ym * 2 + 0) * 2 + cc, ((2, {"y": yp}),))
                col_relay((yp * 2 + 1) * 2 + cc, ((3, {"y": ym}),))
    for dist in range(NZ - lag, NZ):
        x_forward_at(dist)

    recvs_n = aperture_ref.shape[0]
    width = aperture_ref.shape[1]
    tiles, listed = lists_ref.shape
    tile_width = width // tiles
    spread_len = width * NX * NZ // 4
    first = me_col * recvs_n

    def as_column(row):
        n = row.shape[1]
        eye = lax.broadcasted_iota(jnp.int32, (n, n), 0) == lax.broadcasted_iota(jnp.int32, (n, n), 1)
        return jnp.sum(jnp.where(eye, row.astype(jnp.float32), 0.0), axis=1, keepdims=True)

    cols = (me_row * width + lax.broadcasted_iota(jnp.int32, (1, width), 1)).astype(jnp.float32)
    rpos = as_column(rpos_ref[:, pl.ds(pl.multiple_of(first, recvs_n), recvs_n)])
    offset = (rpos - cols) / spread_len
    taper = 1.0 / (1.0 + offset * offset)
    rows_here = first + lax.broadcasted_iota(jnp.int32, (recvs_n, listed), 0)
    for t in range(tiles):
        hits = (lists_ref[pl.ds(t, 1), :] == rows_here).astype(jnp.float32)
        member = jnp.sum(hits, axis=1, keepdims=True)
        part = taper[:, t * tile_width:(t + 1) * tile_width]
        aperture_ref[:, t * tile_width:(t + 1) * tile_width] = (
            member * part * (2.0 / math.sqrt(listed))
        ).astype(aperture_ref.dtype)
    spos = as_column(spos_ref[...])
    soffset = (spos - cols) / spread_len
    weights_ref[...] = 1.0 / (1.0 + soffset * soffset)

    x2 = lax.rem(x + 2, NX)
    for zz in range(NZ):
        row_relay(xm * NZ + zz if zz % 2 == 1 else xp * NZ + zz, ())
        row_relay(x2 * NZ + zz, ())
    y2 = lax.rem(y + 2, NY)
    for cc in range(2):
        col_relay((ym * 2 + 1) * 2 + cc, ())
        col_relay((yp * 2 + 0) * 2 + cc, ())
        for hh in range(2):
            col_relay((y2 * 2 + hh) * 2 + cc, ())
    nf = spec_ref.shape[0] // 2
    surface_root = math.sqrt(roww_ref.shape[2])
    for f in range(nf):
        lr = roww_ref[f]
        li = roww_ref[nf + f]
        rr = colw_ref[f]
        ri = colw_ref[nf + f]
        real_real = jnp.dot(lr, rr, preferred_element_type=jnp.float32)
        imag_imag = jnp.dot(li, ri, preferred_element_type=jnp.float32)
        real_imag = jnp.dot(lr, ri, preferred_element_type=jnp.float32)
        imag_real = jnp.dot(li, rr, preferred_element_type=jnp.float32)
        mult_ref[f] = -(real_real - imag_imag) / surface_root
        mult_ref[nf + f] = -(real_imag + imag_real) / surface_root

    def prim_body(t, carry):
        wave = inverse_ref[t, 0] * mult_ref[0]
        for p in range(1, 2 * nf):
            wave = wave + inverse_ref[t, p] * mult_ref[p]
        prim_ref[t] = (traces_ref[t].astype(jnp.float32) - wave).astype(prim_ref.dtype)
        return carry

    lax.fori_loop(0, traces_ref.shape[0], prim_body, 0)

    band = partial_ref.shape[1]

    def band_peer(i):
        hh = lax.rem(1 - h + i // 8, 2)
        yy = lax.rem(i, 8) // 2
        cc = lax.rem(i, 2)
        return (yy * 2 + hh) * 2 + cc, {"y": yy, "zh": hh, "c": cc}

    def reduce_copy(j, peer):
        return pltpu.make_async_remote_copy(
            partial_ref.at[j], slots_ref.at[me_col], send_red.at[j], recv_red.at[me_col],
            device_id=peer, device_id_type=MESH_ID,
        )

    def band_body(i, carry):
        j, peer = band_peer(i)
        rows = []
        for u in range(band):
            stacked = jnp.dot(
                prim_ref[j * band + u], aperture_ref[...], preferred_element_type=jnp.float32
            )
            rows.append(jnp.sum(stacked * weights_ref[...], axis=0, keepdims=True))
        partial_ref[j] = jnp.concatenate(rows, axis=0)
        pl.when(j != me_col)(reduce_copy(j, peer).start)
        return carry

    lax.fori_loop(0, partial_ref.shape[0], band_body, 0)

    slots_ref[me_col] = partial_ref[me_col]
    for j, peer in col_peers:
        recv = pltpu.make_async_remote_copy(
            partial_ref.at[j], slots_ref.at[j], send_red.at[j], recv_red.at[j],
            device_id=peer, device_id_type=MESH_ID,
        )
        pl.when(j != me_col)(recv.wait_recv)
    total = slots_ref[0]
    for j in range(1, len(col_peers)):
        total = total + slots_ref[j]
    stack_ref[...] = total

    for desc, cond in started:
        when(cond, desc.wait_send)
    for j, peer in col_peers:
        pl.when(j != me_col)(reduce_copy(j, peer).wait_send)


def fused_call(spec, traces, lists, rpos, spos, inverse, width, row_count, col_count):
    planes, shots, recvs = spec.shape
    samples = traces.shape[0]
    band = samples // col_count
    vmem = pl.BlockSpec(memory_space=pltpu.VMEM)
    return pl.pallas_call(
        fused_kernel,
        out_shape=(
            jax.ShapeDtypeStruct(traces.shape, jnp.bfloat16),
            jax.ShapeDtypeStruct((band, width), jnp.float32),
        ),
        in_specs=[vmem, vmem, vmem, vmem, vmem, pl.BlockSpec(memory_space=pltpu.SMEM)],
        out_specs=(vmem, vmem),
        scratch_shapes=[
            pltpu.VMEM((planes, row_count * shots, recvs), spec.dtype),
            pltpu.VMEM((planes, shots, col_count * recvs), spec.dtype),
            pltpu.VMEM((planes, shots, recvs), jnp.float32),
            pltpu.VMEM((col_count, band, width), jnp.float32),
            pltpu.VMEM((col_count, band, width), jnp.float32),
            pltpu.VMEM((recvs, width), jnp.bfloat16),
            pltpu.VMEM((shots, width), jnp.float32),
            pltpu.SemaphoreType.DMA((row_count, 2)),
            pltpu.SemaphoreType.DMA((col_count, 2)),
            pltpu.SemaphoreType.DMA((row_count, 2, 4)),
            pltpu.SemaphoreType.DMA((col_count, 2, 4)),
            pltpu.SemaphoreType.DMA((col_count,)),
            pltpu.SemaphoreType.DMA((col_count,)),
        ],
        compiler_params=pltpu.CompilerParams(collective_id=0, has_side_effects=True),
    )(spec, traces, lists, rpos, spos, inverse)


def per_device(traces, source_pos, receiver_pos, aperture_list, band_index, weight_tiles):
    samples, shot_count, recv_count = traces.shape
    col_count = axis_count(COL)
    row_count = axis_count(ROW)
    surface_count = recv_count * col_count
    image_panel_width = band_index.shape[0]
    depth_slab_samples = samples // col_count
    cosine, sine_table = phase_tables_np(samples)
    forward = jnp.asarray(
        (np.concatenate([cosine, -sine_table], 0) / np.float32(math.sqrt(samples))).astype(
            ml_dtypes.bfloat16
        )
    )
    spectra = jnp.einsum(
        "pt,tsr->psr", forward, traces, preferred_element_type=jnp.float32
    ).astype(jnp.bfloat16)

    inverse = jnp.asarray(np.concatenate([cosine, -sine_table], 0).T / np.float32(math.sqrt(NF)))
    primaries, stacked = fused_call(
        spectra,
        traces,
        aperture_list,
        receiver_pos.reshape(1, -1),
        source_pos.reshape(1, -1),
        inverse,
        image_panel_width,
        row_count,
        col_count,
    )
    column_stack = (stacked / math.sqrt(shot_count)).astype(jnp.bfloat16)

    tile_kinds = weight_tiles.shape[0]
    select = band_index[None, :] == jnp.arange(tile_kinds, dtype=jnp.int32)[:, None]
    widened = jnp.where(select[:, None, :], column_stack[None], jnp.zeros((), jnp.bfloat16))
    image_out = jnp.einsum(
        "kz,kx->zx",
        weight_tiles.reshape(tile_kinds * depth_slab_samples, weight_tiles.shape[2]),
        widened.reshape(tile_kinds * depth_slab_samples, image_panel_width),
        preferred_element_type=jnp.float32,
    )
    return (primaries, image_out)


def solution(mesh):
    n_row = mesh.shape["row"]
    n_col = mesh.shape["col"]
    fine = Mesh(
        mesh.devices.reshape(4, n_row // 4, 4, n_col // 8, 2), ("x", "zl", "y", "zh", "c")
    )
    placed = (P(None, ROW, COL), P(ROW), P(), P(ROW, None), P(ROW), P())
    return jax.shard_map(
        per_device,
        mesh=fine,
        in_specs=placed,
        out_specs=(P(None, ROW, COL), P(COL, ROW)),
        check_vma=False,
    )
```

```python
import math

import jax
import ml_dtypes
import numpy as np
import jax.numpy as jnp
from jax import lax
from jax.experimental import pallas as pl
from jax.experimental.pallas import tpu as pltpu
from jax.sharding import Mesh
from jax.sharding import PartitionSpec as P

NFFT = 4096
NF = 4

ROW = ("x", "zl")
COL = ("y", "zh", "c")


def phase_tables_np(samples):
    freq_bins = (2 * np.arange(NF, dtype=np.int32) + 1) * (NFFT // (4 * NF))
    sample_ticks = np.arange(samples, dtype=np.int32)
    phase_turns = freq_bins[:, None] * sample_ticks[None, :] % NFFT
    phase_angle = phase_turns.astype(np.float32) * np.float32(2.0 * math.pi / NFFT)
    angle = phase_angle.astype(np.float64)
    return (np.cos(angle).astype(np.float32), np.sin(angle).astype(np.float32))


def phase_tables(samples):
    freq_bins = (2 * jnp.arange(NF, dtype=jnp.int32) + 1) * (NFFT // (4 * NF))
    sample_ticks = jnp.arange(samples, dtype=jnp.int32)
    phase_turns = freq_bins[:, None] * sample_ticks[None, :] % NFFT
    phase_angle = phase_turns.astype(jnp.float32) * (2.0 * math.pi / NFFT)
    return (jnp.cos(phase_angle), jnp.sin(phase_angle))


def aperture_rows(tile_index_lists, positions, columns, first_row, row_count, spread_len):
    tile_count, listed = tile_index_lists.shape
    col_width = columns.shape[0]
    rows = first_row + jnp.arange(row_count, dtype=jnp.int32)
    hits = (tile_index_lists[:, :, None] == rows[None, None, :]).astype(jnp.float32)
    member = jnp.sum(hits, axis=1)
    widened = jnp.repeat(member.T, col_width // tile_count, axis=1)
    offset = (positions[:, None] - columns[None, :]).astype(jnp.float32) / spread_len
    taper_weight = 1.0 / (1.0 + offset * offset)
    return (widened * taper_weight * (2.0 / math.sqrt(listed))).astype(jnp.bfloat16)


def shot_weights(positions, columns, spread_len):
    offset = (positions[:, None] - columns[None, :]).astype(jnp.float32) / spread_len
    return 1.0 / (1.0 + offset * offset)


def complex_product(left_section, right_section):
    real_real = jnp.einsum(
        "qju,quy->qjy", left_section[0], right_section[0], preferred_element_type=jnp.float32
    )
    imag_imag = jnp.einsum(
        "qju,quy->qjy", left_section[1], right_section[1], preferred_element_type=jnp.float32
    )
    real_imag = jnp.einsum(
        "qju,quy->qjy", left_section[0], right_section[1], preferred_element_type=jnp.float32
    )
    imag_real = jnp.einsum(
        "qju,quy->qjy", left_section[1], right_section[0], preferred_element_type=jnp.float32
    )
    return jnp.stack([real_real - imag_imag, real_imag + imag_real])


def axis_pos(names):
    index = 0
    for name in names:
        index = index * lax.axis_size(name) + lax.axis_index(name)
    return index


def axis_count(names):
    count = 1
    for name in names:
        count *= lax.axis_size(name)
    return count


MESH_ID = pl.DeviceIdType.MESH
NX, NZ, NY = 4, 8, 4


def fused_kernel(spec_ref, traces_ref, lists_ref, rpos_ref, spos_ref, inverse_ref,
                 prim_ref, stack_ref,
                 colw_ref, roww_ref, mult_ref, partial_ref, slots_ref, aperture_ref, weights_ref,
                 recv_row, recv_col, send_row, send_col, recv_red, send_red):
    x = lax.axis_index("x")
    z = lax.axis_index("zl")
    y = lax.axis_index("y")
    h = lax.axis_index("zh")
    c = lax.axis_index("c")
    xp = lax.rem(x + 1, NX)
    xm = lax.rem(x + NX - 1, NX)
    yp = lax.rem(y + 1, NY)
    ym = lax.rem(y + NY - 1, NY)
    me_row = x * NZ + z
    me_col = (y * 2 + h) * 2 + c

    col_peers = []
    for yy in range(NY):
        for hh in range(2):
            for cc in range(2):
                col_peers.append(((yy * 2 + hh) * 2 + cc, {"y": yy, "zh": hh, "c": cc}))

    barrier = pltpu.get_barrier_semaphore()
    for peer in ({"x": xp}, {"x": xm}):
        pl.semaphore_signal(barrier, 1, device_id=peer, device_id_type=MESH_ID)
    for j, peer in col_peers:
        pl.when(j != me_col)(
            lambda peer=peer: pl.semaphore_signal(
                barrier, 1, device_id=peer, device_id_type=MESH_ID
            )
        )

    @pl.when(z > 0)
    def _():
        pl.semaphore_signal(barrier, 1, device_id={"zl": z - 1}, device_id_type=MESH_ID)

    @pl.when(z < NZ - 1)
    def _():
        pl.semaphore_signal(barrier, 1, device_id={"zl": z + 1}, device_id_type=MESH_ID)

    peers_in = 2 + len(col_peers) - 1
    ends = jnp.logical_or(z == 0, z == NZ - 1)
    pl.when(ends)(lambda: pl.semaphore_wait(barrier, peers_in + 1))
    pl.when(jnp.logical_not(ends))(lambda: pl.semaphore_wait(barrier, peers_in + 2))

    started = []
    shots = spec_ref.shape[1]
    recvs = spec_ref.shape[2]
    half = spec_ref.shape[0] // 2
    parts = (0, 1)

    def planes(part):
        return pl.ds(part * half, half)

    def colw_blk(b, part):
        return colw_ref.at[planes(part), pl.ds(pl.multiple_of(b * shots, shots), shots), :]

    def roww_blk(j, part):
        return roww_ref.at[planes(part), :, pl.ds(pl.multiple_of(j * recvs, recvs), recvs)]

    def row_copy(b, part, d, peer, own=False):
        src = spec_ref.at[planes(part)] if own else colw_blk(b, part)
        return pltpu.make_async_remote_copy(
            src, colw_blk(b, part), send_row.at[b, part, d], recv_row.at[b, part],
            device_id=peer, device_id_type=MESH_ID,
        )

    def col_copy(j, part, d, peer, own=False):
        src = spec_ref.at[planes(part)] if own else roww_blk(j, part)
        return pltpu.make_async_remote_copy(
            src, roww_blk(j, part), send_col.at[j, part, d], recv_col.at[j, part],
            device_id=peer, device_id_type=MESH_ID,
        )

    def start(desc, cond=None):
        if cond is None:
            desc.start()
        else:
            pl.when(cond)(desc.start)
        started.append((desc, cond))

    def when(cond, fn):
        if cond is None:
            fn()
        else:
            pl.when(cond)(fn)

    def row_relay(b, sends, cond=None, only=parts):
        for part in only:
            when(cond, row_copy(b, part, 0, {"x": x}).wait_recv)
            for d, peer, extra in sends:
                c2 = cond if extra is None else (extra if cond is None else jnp.logical_and(cond, extra))
                start(row_copy(b, part, d, peer), c2)

    def col_relay(j, sends, cond=None):
        for part in parts:
            when(cond, col_copy(j, part, 0, {"y": y}).wait_recv)
            for d, peer in sends:
                start(col_copy(j, part, d, peer), cond)

    for part in parts:
        start(col_copy(me_col, part, 0, {"c": 1 - c}, own=True))
        start(row_copy(me_row, part, 0, {"zl": z + 1}, own=True), z < NZ - 1)
        start(row_copy(me_row, part, 1, {"zl": z - 1}, own=True), z > 0)
        start(row_copy(me_row, part, 2, {"x": xp}, own=True))
        start(row_copy(me_row, part, 3, {"x": xm}, own=True))
        start(col_copy(me_col, part, 2, {"y": yp}, own=True))
        start(col_copy(me_col, part, 3, {"y": ym}, own=True))
    colw_ref[:, pl.ds(pl.multiple_of(me_row * shots, shots), shots), :] = spec_ref[...]
    roww_ref[:, :, pl.ds(pl.multiple_of(me_col * recvs, recvs), recvs)] = spec_ref[...]

    j_h = (y * 2 + 1 - h) * 2 + c
    j_c = (y * 2 + h) * 2 + 1 - c
    j_hc = (y * 2 + 1 - h) * 2 + 1 - c
    y_sends = ((2, {"y": yp}), (3, {"y": ym}))
    col_relay(j_c, y_sends)

    def x_forward(zsrc, cond):
        even = lax.rem(zsrc, 2) == 0
        row_relay(xm * NZ + zsrc, ((2, {"x": xp}, None),), jnp.logical_and(cond, even))
        odd = jnp.logical_not(even)
        row_relay(xp * NZ + zsrc, ((3, {"x": xm}, None),), jnp.logical_and(cond, odd))

    def x_forward_at(dist):
        if dist == 0:
            x_forward(z, True)
        else:
            x_forward(z - dist, z >= dist)
            x_forward(z + dist, z + dist < NZ)

    lag = 1
    x_sends = ((2, {"x": xp}, None), (3, {"x": xm}, None))
    for k in range(1, NZ):
        for part in parts:
            row_relay(x * NZ + z - k, x_sends + ((0, {"zl": z + 1}, z < NZ - 1),), z >= k, (part,))
            row_relay(x * NZ + z + k, x_sends + ((1, {"zl": z - 1}, z > 0),), z + k < NZ, (part,))
        if k - lag >= 0:
            x_forward_at(k - lag)
        if k == 2:
            for part in parts:
                start(col_copy(me_col, part, 1, {"zh": 1 - h}, own=True))
        if k == 4:
            col_relay(j_h, ((0, {"c": 1 - c}),) + y_sends)
        if k == 5:
            col_relay(j_hc, y_sends)
        if k == 6:
            for cc in range(2):
                col_relay((ym * 2 + 0) * 2 + cc, ((2, {"y": yp}),))
                col_relay((yp * 2 + 1) * 2 + cc, ((3, {"y": ym}),))
    for dist in range(NZ - lag, NZ):
        x_forward_at(dist)

    recvs_n = aperture_ref.shape[0]
    width = aperture_ref.shape[1]
    tiles, listed = lists_ref.shape
    tile_width = width // tiles
    spread_len = width * NX * NZ // 4
    first = me_col * recvs_n

    def as_column(row):
        n = row.shape[1]
        eye = lax.broadcasted_iota(jnp.int32, (n, n), 0) == lax.broadcasted_iota(jnp.int32, (n, n), 1)
        return jnp.sum(jnp.where(eye, row.astype(jnp.float32), 0.0), axis=1, keepdims=True)

    cols = (me_row * width + lax.broadcasted_iota(jnp.int32, (1, width), 1)).astype(jnp.float32)
    rpos = as_column(rpos_ref[:, pl.ds(pl.multiple_of(first, recvs_n), recvs_n)])
    offset = (rpos - cols) / spread_len
    taper = 1.0 / (1.0 + offset * offset)
    rows_here = first + lax.broadcasted_iota(jnp.int32, (recvs_n, listed), 0)
    for t in range(tiles):
        hits = (lists_ref[pl.ds(t, 1), :] == rows_here).astype(jnp.float32)
        member = jnp.sum(hits, axis=1, keepdims=True)
        part = taper[:, t * tile_width:(t + 1) * tile_width]
        aperture_ref[:, t * tile_width:(t + 1) * tile_width] = (
            member * part * (2.0 / math.sqrt(listed))
        ).astype(aperture_ref.dtype)
    spos = as_column(spos_ref[...])
    soffset = (spos - cols) / spread_len
    weights_ref[...] = 1.0 / (1.0 + soffset * soffset)

    x2 = lax.rem(x + 2, NX)
    for zz in range(NZ):
        row_relay(xm * NZ + zz if zz % 2 == 1 else xp * NZ + zz, ())
        row_relay(x2 * NZ + zz, ())
    y2 = lax.rem(y + 2, NY)
    for cc in range(2):
        col_relay((ym * 2 + 1) * 2 + cc, ())
        col_relay((yp * 2 + 0) * 2 + cc, ())
        for hh in range(2):
            col_relay((y2 * 2 + hh) * 2 + cc, ())
    nf = spec_ref.shape[0] // 2
    surface_root = math.sqrt(roww_ref.shape[2])
    for f in range(nf):
        lr = roww_ref[f]
        li = roww_ref[nf + f]
        rr = colw_ref[f]
        ri = colw_ref[nf + f]
        real_real = jnp.dot(lr, rr, preferred_element_type=jnp.float32)
        imag_imag = jnp.dot(li, ri, preferred_element_type=jnp.float32)
        real_imag = jnp.dot(lr, ri, preferred_element_type=jnp.float32)
        imag_real = jnp.dot(li, rr, preferred_element_type=jnp.float32)
        mult_ref[f] = -(real_real - imag_imag) / surface_root
        mult_ref[nf + f] = -(real_imag + imag_real) / surface_root

    def prim_body(t, carry):
        wave = inverse_ref[t, 0] * mult_ref[0]
        for p in range(1, 2 * nf):
            wave = wave + inverse_ref[t, p] * mult_ref[p]
        prim_ref[t] = (traces_ref[t].astype(jnp.float32) - wave).astype(prim_ref.dtype)
        return carry

    lax.fori_loop(0, traces_ref.shape[0], prim_body, 0)

    band = partial_ref.shape[1]

    def band_peer(i):
        hh = lax.rem(1 - h + i // 8, 2)
        yy = lax.rem(i, 8) // 2
        cc = lax.rem(i, 2)
        return (yy * 2 + hh) * 2 + cc, {"y": yy, "zh": hh, "c": cc}

    def reduce_copy(j, peer):
        return pltpu.make_async_remote_copy(
            partial_ref.at[j], slots_ref.at[me_col], send_red.at[j], recv_red.at[me_col],
            device_id=peer, device_id_type=MESH_ID,
        )

    def band_body(i, carry):
        j, peer = band_peer(i)
        rows = []
        for u in range(band):
            stacked = jnp.dot(
                prim_ref[j * band + u], aperture_ref[...], preferred_element_type=jnp.float32
            )
            rows.append(jnp.sum(stacked * weights_ref[...], axis=0, keepdims=True))
        partial_ref[j] = jnp.concatenate(rows, axis=0)
        pl.when(j != me_col)(reduce_copy(j, peer).start)
        return carry

    lax.fori_loop(0, partial_ref.shape[0], band_body, 0)

    slots_ref[me_col] = partial_ref[me_col]
    for j, peer in col_peers:
        recv = pltpu.make_async_remote_copy(
            partial_ref.at[j], slots_ref.at[j], send_red.at[j], recv_red.at[j],
            device_id=peer, device_id_type=MESH_ID,
        )
        pl.when(j != me_col)(recv.wait_recv)
    total = slots_ref[0]
    for j in range(1, len(col_peers)):
        total = total + slots_ref[j]
    stack_ref[...] = total

    for desc, cond in started:
        when(cond, desc.wait_send)
    for j, peer in col_peers:
        pl.when(j != me_col)(reduce_copy(j, peer).wait_send)


def fused_call(spec, traces, lists, rpos, spos, inverse, width, row_count, col_count):
    planes, shots, recvs = spec.shape
    samples = traces.shape[0]
    band = samples // col_count
    vmem = pl.BlockSpec(memory_space=pltpu.VMEM)
    return pl.pallas_call(
        fused_kernel,
        out_shape=(
            jax.ShapeDtypeStruct(traces.shape, jnp.bfloat16),
            jax.ShapeDtypeStruct((band, width), jnp.float32),
        ),
        in_specs=[vmem, vmem, vmem, vmem, vmem, pl.BlockSpec(memory_space=pltpu.SMEM)],
        out_specs=(vmem, vmem),
        scratch_shapes=[
            pltpu.VMEM((planes, row_count * shots, recvs), spec.dtype),
            pltpu.VMEM((planes, shots, col_count * recvs), spec.dtype),
            pltpu.VMEM((planes, shots, recvs), jnp.float32),
            pltpu.VMEM((col_count, band, width), jnp.float32),
            pltpu.VMEM((col_count, band, width), jnp.float32),
            pltpu.VMEM((recvs, width), jnp.bfloat16),
            pltpu.VMEM((shots, width), jnp.float32),
            pltpu.SemaphoreType.DMA((row_count, 2)),
            pltpu.SemaphoreType.DMA((col_count, 2)),
            pltpu.SemaphoreType.DMA((row_count, 2, 4)),
            pltpu.SemaphoreType.DMA((col_count, 2, 4)),
            pltpu.SemaphoreType.DMA((col_count,)),
            pltpu.SemaphoreType.DMA((col_count,)),
        ],
        compiler_params=pltpu.CompilerParams(collective_id=0, has_side_effects=True),
    )(spec, traces, lists, rpos, spos, inverse)


def per_device(traces, source_pos, receiver_pos, aperture_list, band_index, weight_tiles):
    samples, shot_count, recv_count = traces.shape
    col_count = axis_count(COL)
    row_count = axis_count(ROW)
    surface_count = recv_count * col_count
    image_panel_width = band_index.shape[0]
    depth_slab_samples = samples // col_count
    cosine, sine_table = phase_tables_np(samples)
    forward = jnp.asarray(
        (np.concatenate([cosine, -sine_table], 0) / np.float32(math.sqrt(samples))).astype(
            ml_dtypes.bfloat16
        )
    )
    spectra = jnp.einsum(
        "pt,tsr->psr", forward, traces, preferred_element_type=jnp.float32
    ).astype(jnp.bfloat16)

    inverse = jnp.asarray(np.concatenate([cosine, -sine_table], 0).T / np.float32(math.sqrt(NF)))
    primaries, stacked = fused_call(
        spectra,
        traces,
        aperture_list,
        receiver_pos.reshape(1, -1),
        source_pos.reshape(1, -1),
        inverse,
        image_panel_width,
        row_count,
        col_count,
    )
    column_stack = (stacked / math.sqrt(shot_count)).astype(jnp.bfloat16)

    tile_kinds = weight_tiles.shape[0]
    select = band_index[None, :] == jnp.arange(tile_kinds, dtype=jnp.int32)[:, None]
    widened = jnp.where(select[:, None, :], column_stack[None], jnp.zeros((), jnp.bfloat16))
    image_out = jnp.einsum(
        "kz,kx->zx",
        weight_tiles.reshape(tile_kinds * depth_slab_samples, weight_tiles.shape[2]),
        widened.reshape(tile_kinds * depth_slab_samples, image_panel_width),
        preferred_element_type=jnp.float32,
    )
    return (primaries, image_out)


def solution(mesh):
    n_row = mesh.shape["row"]
    n_col = mesh.shape["col"]
    fine = Mesh(
        mesh.devices.reshape(4, n_row // 4, 4, n_col // 8, 2), ("x", "zl", "y", "zh", "c")
    )
    placed = (P(None, ROW, COL), P(ROW), P(), P(ROW, None), P(ROW), P())
    return jax.shard_map(
        per_device,
        mesh=fine,
        in_specs=placed,
        out_specs=(P(None, ROW, COL), P(COL, ROW)),
        check_vma=False,
    )
```

```python
import math

import jax
import ml_dtypes
import numpy as np
import jax.numpy as jnp
from jax import lax
from jax.experimental import pallas as pl
from jax.experimental.pallas import tpu as pltpu
from jax.sharding import Mesh
from jax.sharding import PartitionSpec as P

NFFT = 4096
NF = 4

ROW = ("x", "zl")
COL = ("y", "zh", "c")


def phase_tables_np(samples):
    freq_bins = (2 * np.arange(NF, dtype=np.int32) + 1) * (NFFT // (4 * NF))
    sample_ticks = np.arange(samples, dtype=np.int32)
    phase_turns = freq_bins[:, None] * sample_ticks[None, :] % NFFT
    phase_angle = phase_turns.astype(np.float32) * np.float32(2.0 * math.pi / NFFT)
    angle = phase_angle.astype(np.float64)
    return (np.cos(angle).astype(np.float32), np.sin(angle).astype(np.float32))


def phase_tables(samples):
    freq_bins = (2 * jnp.arange(NF, dtype=jnp.int32) + 1) * (NFFT // (4 * NF))
    sample_ticks = jnp.arange(samples, dtype=jnp.int32)
    phase_turns = freq_bins[:, None] * sample_ticks[None, :] % NFFT
    phase_angle = phase_turns.astype(jnp.float32) * (2.0 * math.pi / NFFT)
    return (jnp.cos(phase_angle), jnp.sin(phase_angle))


def aperture_rows(tile_index_lists, positions, columns, first_row, row_count, spread_len):
    tile_count, listed = tile_index_lists.shape
    col_width = columns.shape[0]
    rows = first_row + jnp.arange(row_count, dtype=jnp.int32)
    hits = (tile_index_lists[:, :, None] == rows[None, None, :]).astype(jnp.float32)
    member = jnp.sum(hits, axis=1)
    widened = jnp.repeat(member.T, col_width // tile_count, axis=1)
    offset = (positions[:, None] - columns[None, :]).astype(jnp.float32) / spread_len
    taper_weight = 1.0 / (1.0 + offset * offset)
    return (widened * taper_weight * (2.0 / math.sqrt(listed))).astype(jnp.bfloat16)


def shot_weights(positions, columns, spread_len):
    offset = (positions[:, None] - columns[None, :]).astype(jnp.float32) / spread_len
    return 1.0 / (1.0 + offset * offset)


def complex_product(left_section, right_section):
    real_real = jnp.einsum(
        "qju,quy->qjy", left_section[0], right_section[0], preferred_element_type=jnp.float32
    )
    imag_imag = jnp.einsum(
        "qju,quy->qjy", left_section[1], right_section[1], preferred_element_type=jnp.float32
    )
    real_imag = jnp.einsum(
        "qju,quy->qjy", left_section[0], right_section[1], preferred_element_type=jnp.float32
    )
    imag_real = jnp.einsum(
        "qju,quy->qjy", left_section[1], right_section[0], preferred_element_type=jnp.float32
    )
    return jnp.stack([real_real - imag_imag, real_imag + imag_real])


def axis_pos(names):
    index = 0
    for name in names:
        index = index * lax.axis_size(name) + lax.axis_index(name)
    return index


def axis_count(names):
    count = 1
    for name in names:
        count *= lax.axis_size(name)
    return count


MESH_ID = pl.DeviceIdType.MESH
NX, NZ, NY = 4, 8, 4


def fused_kernel(spec_ref, traces_ref, lists_ref, rpos_ref, spos_ref, inverse_ref,
                 prim_ref, stack_ref,
                 colw_ref, roww_ref, mult_ref, partial_ref, slots_ref, aperture_ref, weights_ref,
                 recv_row, recv_col, send_row, send_col, recv_red, send_red):
    x = lax.axis_index("x")
    z = lax.axis_index("zl")
    y = lax.axis_index("y")
    h = lax.axis_index("zh")
    c = lax.axis_index("c")
    xp = lax.rem(x + 1, NX)
    xm = lax.rem(x + NX - 1, NX)
    yp = lax.rem(y + 1, NY)
    ym = lax.rem(y + NY - 1, NY)
    me_row = x * NZ + z
    me_col = (y * 2 + h) * 2 + c

    col_peers = []
    for yy in range(NY):
        for hh in range(2):
            for cc in range(2):
                col_peers.append(((yy * 2 + hh) * 2 + cc, {"y": yy, "zh": hh, "c": cc}))

    barrier = pltpu.get_barrier_semaphore()
    for peer in ({"x": xp}, {"x": xm}):
        pl.semaphore_signal(barrier, 1, device_id=peer, device_id_type=MESH_ID)
    for j, peer in col_peers:
        pl.when(j != me_col)(
            lambda peer=peer: pl.semaphore_signal(
                barrier, 1, device_id=peer, device_id_type=MESH_ID
            )
        )

    @pl.when(z > 0)
    def _():
        pl.semaphore_signal(barrier, 1, device_id={"zl": z - 1}, device_id_type=MESH_ID)

    @pl.when(z < NZ - 1)
    def _():
        pl.semaphore_signal(barrier, 1, device_id={"zl": z + 1}, device_id_type=MESH_ID)

    peers_in = 2 + len(col_peers) - 1
    ends = jnp.logical_or(z == 0, z == NZ - 1)
    pl.when(ends)(lambda: pl.semaphore_wait(barrier, peers_in + 1))
    pl.when(jnp.logical_not(ends))(lambda: pl.semaphore_wait(barrier, peers_in + 2))

    started = []
    shots = spec_ref.shape[1]
    recvs = spec_ref.shape[2]
    half = spec_ref.shape[0] // 2
    parts = (0, 1)

    def planes(part):
        return pl.ds(part * half, half)

    def colw_blk(b, part):
        return colw_ref.at[planes(part), pl.ds(pl.multiple_of(b * shots, shots), shots), :]

    def roww_blk(j, part):
        return roww_ref.at[planes(part), :, pl.ds(pl.multiple_of(j * recvs, recvs), recvs)]

    def row_copy(b, part, d, peer, own=False):
        src = spec_ref.at[planes(part)] if own else colw_blk(b, part)
        return pltpu.make_async_remote_copy(
            src, colw_blk(b, part), send_row.at[b, part, d], recv_row.at[b, part],
            device_id=peer, device_id_type=MESH_ID,
        )

    def col_copy(j, part, d, peer, own=False):
        src = spec_ref.at[planes(part)] if own else roww_blk(j, part)
        return pltpu.make_async_remote_copy(
            src, roww_blk(j, part), send_col.at[j, part, d], recv_col.at[j, part],
            device_id=peer, device_id_type=MESH_ID,
        )

    def start(desc, cond=None):
        if cond is None:
            desc.start()
        else:
            pl.when(cond)(desc.start)
        started.append((desc, cond))

    def when(cond, fn):
        if cond is None:
            fn()
        else:
            pl.when(cond)(fn)

    def row_relay(b, sends, cond=None, only=parts):
        for part in only:
            when(cond, row_copy(b, part, 0, {"x": x}).wait_recv)
            for d, peer, extra in sends:
                c2 = cond if extra is None else (extra if cond is None else jnp.logical_and(cond, extra))
                start(row_copy(b, part, d, peer), c2)

    def col_relay(j, sends, cond=None):
        for part in parts:
            when(cond, col_copy(j, part, 0, {"y": y}).wait_recv)
            for d, peer in sends:
                start(col_copy(j, part, d, peer), cond)

    for part in parts:
        start(col_copy(me_col, part, 0, {"c": 1 - c}, own=True))
        start(row_copy(me_row, part, 0, {"zl": z + 1}, own=True), z < NZ - 1)
        start(row_copy(me_row, part, 1, {"zl": z - 1}, own=True), z > 0)
        start(row_copy(me_row, part, 2, {"x": xp}, own=True))
        start(row_copy(me_row, part, 3, {"x": xm}, own=True))
        start(col_copy(me_col, part, 2, {"y": yp}, own=True))
        start(col_copy(me_col, part, 3, {"y": ym}, own=True))
    colw_ref[:, pl.ds(pl.multiple_of(me_row * shots, shots), shots), :] = spec_ref[...]
    roww_ref[:, :, pl.ds(pl.multiple_of(me_col * recvs, recvs), recvs)] = spec_ref[...]

    j_h = (y * 2 + 1 - h) * 2 + c
    j_c = (y * 2 + h) * 2 + 1 - c
    j_hc = (y * 2 + 1 - h) * 2 + 1 - c
    y_sends = ((2, {"y": yp}), (3, {"y": ym}))
    col_relay(j_c, y_sends)

    def x_forward(zsrc, cond):
        even = lax.rem(zsrc, 2) == 0
        row_relay(xm * NZ + zsrc, ((2, {"x": xp}, None),), jnp.logical_and(cond, even))
        odd = jnp.logical_not(even)
        row_relay(xp * NZ + zsrc, ((3, {"x": xm}, None),), jnp.logical_and(cond, odd))

    def x_forward_at(dist):
        if dist == 0:
            x_forward(z, True)
        else:
            x_forward(z - dist, z >= dist)
            x_forward(z + dist, z + dist < NZ)

    lag = 3
    x_sends = ((2, {"x": xp}, None), (3, {"x": xm}, None))
    for k in range(1, NZ):
        for part in parts:
            row_relay(x * NZ + z - k, x_sends + ((0, {"zl": z + 1}, z < NZ - 1),), z >= k, (part,))
            row_relay(x * NZ + z + k, x_sends + ((1, {"zl": z - 1}, z > 0),), z + k < NZ, (part,))
        if k - lag >= 0:
            x_forward_at(k - lag)
        if k == 2:
            for part in parts:
                start(col_copy(me_col, part, 1, {"zh": 1 - h}, own=True))
        if k == 4:
            col_relay(j_h, ((0, {"c": 1 - c}),) + y_sends)
        if k == 5:
            col_relay(j_hc, y_sends)
        if k == 6:
            for cc in range(2):
                col_relay((ym * 2 + 0) * 2 + cc, ((2, {"y": yp}),))
                col_relay((yp * 2 + 1) * 2 + cc, ((3, {"y": ym}),))
    for dist in range(NZ - lag, NZ):
        x_forward_at(dist)

    recvs_n = aperture_ref.shape[0]
    width = aperture_ref.shape[1]
    tiles, listed = lists_ref.shape
    tile_width = width // tiles
    spread_len = width * NX * NZ // 4
    first = me_col * recvs_n

    def as_column(row):
        n = row.shape[1]
        eye = lax.broadcasted_iota(jnp.int32, (n, n), 0) == lax.broadcasted_iota(jnp.int32, (n, n), 1)
        return jnp.sum(jnp.where(eye, row.astype(jnp.float32), 0.0), axis=1, keepdims=True)

    cols = (me_row * width + lax.broadcasted_iota(jnp.int32, (1, width), 1)).astype(jnp.float32)
    rpos = as_column(rpos_ref[:, pl.ds(pl.multiple_of(first, recvs_n), recvs_n)])
    offset = (rpos - cols) / spread_len
    taper = 1.0 / (1.0 + offset * offset)
    rows_here = first + lax.broadcasted_iota(jnp.int32, (recvs_n, listed), 0)
    for t in range(tiles):
        hits = (lists_ref[pl.ds(t, 1), :] == rows_here).astype(jnp.float32)
        member = jnp.sum(hits, axis=1, keepdims=True)
        part = taper[:, t * tile_width:(t + 1) * tile_width]
        aperture_ref[:, t * tile_width:(t + 1) * tile_width] = (
            member * part * (2.0 / math.sqrt(listed))
        ).astype(aperture_ref.dtype)
    spos = as_column(spos_ref[...])
    soffset = (spos - cols) / spread_len
    weights_ref[...] = 1.0 / (1.0 + soffset * soffset)

    x2 = lax.rem(x + 2, NX)
    for zz in range(NZ):
        row_relay(xm * NZ + zz if zz % 2 == 1 else xp * NZ + zz, ())
        row_relay(x2 * NZ + zz, ())
    y2 = lax.rem(y + 2, NY)
    for cc in range(2):
        col_relay((ym * 2 + 1) * 2 + cc, ())
        col_relay((yp * 2 + 0) * 2 + cc, ())
        for hh in range(2):
            col_relay((y2 * 2 + hh) * 2 + cc, ())
    nf = spec_ref.shape[0] // 2
    surface_root = math.sqrt(roww_ref.shape[2])
    for f in range(nf):
        lr = roww_ref[f]
        li = roww_ref[nf + f]
        rr = colw_ref[f]
        ri = colw_ref[nf + f]
        real_real = jnp.dot(lr, rr, preferred_element_type=jnp.float32)
        imag_imag = jnp.dot(li, ri, preferred_element_type=jnp.float32)
        real_imag = jnp.dot(lr, ri, preferred_element_type=jnp.float32)
        imag_real = jnp.dot(li, rr, preferred_element_type=jnp.float32)
        mult_ref[f] = -(real_real - imag_imag) / surface_root
        mult_ref[nf + f] = -(real_imag + imag_real) / surface_root

    def prim_body(t, carry):
        wave = inverse_ref[t, 0] * mult_ref[0]
        for p in range(1, 2 * nf):
            wave = wave + inverse_ref[t, p] * mult_ref[p]
        prim_ref[t] = (traces_ref[t].astype(jnp.float32) - wave).astype(prim_ref.dtype)
        return carry

    lax.fori_loop(0, traces_ref.shape[0], prim_body, 0)

    band = partial_ref.shape[1]

    def band_peer(i):
        hh = lax.rem(1 - h + i // 8, 2)
        yy = lax.rem(i, 8) // 2
        cc = lax.rem(i, 2)
        return (yy * 2 + hh) * 2 + cc, {"y": yy, "zh": hh, "c": cc}

    def reduce_copy(j, peer):
        return pltpu.make_async_remote_copy(
            partial_ref.at[j], slots_ref.at[me_col], send_red.at[j], recv_red.at[me_col],
            device_id=peer, device_id_type=MESH_ID,
        )

    def band_body(i, carry):
        j, peer = band_peer(i)
        rows = []
        for u in range(band):
            stacked = jnp.dot(
                prim_ref[j * band + u], aperture_ref[...], preferred_element_type=jnp.float32
            )
            rows.append(jnp.sum(stacked * weights_ref[...], axis=0, keepdims=True))
        partial_ref[j] = jnp.concatenate(rows, axis=0)
        pl.when(j != me_col)(reduce_copy(j, peer).start)
        return carry

    lax.fori_loop(0, partial_ref.shape[0], band_body, 0)

    slots_ref[me_col] = partial_ref[me_col]
    for j, peer in col_peers:
        recv = pltpu.make_async_remote_copy(
            partial_ref.at[j], slots_ref.at[j], send_red.at[j], recv_red.at[j],
            device_id=peer, device_id_type=MESH_ID,
        )
        pl.when(j != me_col)(recv.wait_recv)
    total = slots_ref[0]
    for j in range(1, len(col_peers)):
        total = total + slots_ref[j]
    stack_ref[...] = total

    for desc, cond in started:
        when(cond, desc.wait_send)
    for j, peer in col_peers:
        pl.when(j != me_col)(reduce_copy(j, peer).wait_send)


def fused_call(spec, traces, lists, rpos, spos, inverse, width, row_count, col_count):
    planes, shots, recvs = spec.shape
    samples = traces.shape[0]
    band = samples // col_count
    vmem = pl.BlockSpec(memory_space=pltpu.VMEM)
    return pl.pallas_call(
        fused_kernel,
        out_shape=(
            jax.ShapeDtypeStruct(traces.shape, jnp.bfloat16),
            jax.ShapeDtypeStruct((band, width), jnp.float32),
        ),
        in_specs=[vmem, vmem, vmem, vmem, vmem, pl.BlockSpec(memory_space=pltpu.SMEM)],
        out_specs=(vmem, vmem),
        scratch_shapes=[
            pltpu.VMEM((planes, row_count * shots, recvs), spec.dtype),
            pltpu.VMEM((planes, shots, col_count * recvs), spec.dtype),
            pltpu.VMEM((planes, shots, recvs), jnp.float32),
            pltpu.VMEM((col_count, band, width), jnp.float32),
            pltpu.VMEM((col_count, band, width), jnp.float32),
            pltpu.VMEM((recvs, width), jnp.bfloat16),
            pltpu.VMEM((shots, width), jnp.float32),
            pltpu.SemaphoreType.DMA((row_count, 2)),
            pltpu.SemaphoreType.DMA((col_count, 2)),
            pltpu.SemaphoreType.DMA((row_count, 2, 4)),
            pltpu.SemaphoreType.DMA((col_count, 2, 4)),
            pltpu.SemaphoreType.DMA((col_count,)),
            pltpu.SemaphoreType.DMA((col_count,)),
        ],
        compiler_params=pltpu.CompilerParams(collective_id=0, has_side_effects=True),
    )(spec, traces, lists, rpos, spos, inverse)


def per_device(traces, source_pos, receiver_pos, aperture_list, band_index, weight_tiles):
    samples, shot_count, recv_count = traces.shape
    col_count = axis_count(COL)
    row_count = axis_count(ROW)
    surface_count = recv_count * col_count
    image_panel_width = band_index.shape[0]
    depth_slab_samples = samples // col_count
    cosine, sine_table = phase_tables_np(samples)
    forward = jnp.asarray(
        (np.concatenate([cosine, -sine_table], 0) / np.float32(math.sqrt(samples))).astype(
            ml_dtypes.bfloat16
        )
    )
    spectra = jnp.einsum(
        "pt,tsr->psr", forward, traces, preferred_element_type=jnp.float32
    ).astype(jnp.bfloat16)

    inverse = jnp.asarray(np.concatenate([cosine, -sine_table], 0).T / np.float32(math.sqrt(NF)))
    primaries, stacked = fused_call(
        spectra,
        traces,
        aperture_list,
        receiver_pos.reshape(1, -1),
        source_pos.reshape(1, -1),
        inverse,
        image_panel_width,
        row_count,
        col_count,
    )
    column_stack = (stacked / math.sqrt(shot_count)).astype(jnp.bfloat16)

    tile_kinds = weight_tiles.shape[0]
    select = band_index[None, :] == jnp.arange(tile_kinds, dtype=jnp.int32)[:, None]
    widened = jnp.where(select[:, None, :], column_stack[None], jnp.zeros((), jnp.bfloat16))
    image_out = jnp.einsum(
        "kz,kx->zx",
        weight_tiles.reshape(tile_kinds * depth_slab_samples, weight_tiles.shape[2]),
        widened.reshape(tile_kinds * depth_slab_samples, image_panel_width),
        preferred_element_type=jnp.float32,
    )
    return (primaries, image_out)


def solution(mesh):
    n_row = mesh.shape["row"]
    n_col = mesh.shape["col"]
    fine = Mesh(
        mesh.devices.reshape(4, n_row // 4, 4, n_col // 8, 2), ("x", "zl", "y", "zh", "c")
    )
    placed = (P(None, ROW, COL), P(ROW), P(), P(ROW, None), P(ROW), P())
    return jax.shard_map(
        per_device,
        mesh=fine,
        in_specs=placed,
        out_specs=(P(None, ROW, COL), P(COL, ROW)),
        check_vma=False,
    )
```

```python
import math

import jax
import ml_dtypes
import numpy as np
import jax.numpy as jnp
from jax import lax
from jax.experimental import pallas as pl
from jax.experimental.pallas import tpu as pltpu
from jax.sharding import Mesh
from jax.sharding import PartitionSpec as P

NFFT = 4096
NF = 4

ROW = ("x", "zl")
COL = ("y", "zh", "c")


def phase_tables_np(samples):
    freq_bins = (2 * np.arange(NF, dtype=np.int32) + 1) * (NFFT // (4 * NF))
    sample_ticks = np.arange(samples, dtype=np.int32)
    phase_turns = freq_bins[:, None] * sample_ticks[None, :] % NFFT
    phase_angle = phase_turns.astype(np.float32) * np.float32(2.0 * math.pi / NFFT)
    angle = phase_angle.astype(np.float64)
    return (np.cos(angle).astype(np.float32), np.sin(angle).astype(np.float32))


def phase_tables(samples):
    freq_bins = (2 * jnp.arange(NF, dtype=jnp.int32) + 1) * (NFFT // (4 * NF))
    sample_ticks = jnp.arange(samples, dtype=jnp.int32)
    phase_turns = freq_bins[:, None] * sample_ticks[None, :] % NFFT
    phase_angle = phase_turns.astype(jnp.float32) * (2.0 * math.pi / NFFT)
    return (jnp.cos(phase_angle), jnp.sin(phase_angle))


def aperture_rows(tile_index_lists, positions, columns, first_row, row_count, spread_len):
    tile_count, listed = tile_index_lists.shape
    col_width = columns.shape[0]
    rows = first_row + jnp.arange(row_count, dtype=jnp.int32)
    hits = (tile_index_lists[:, :, None] == rows[None, None, :]).astype(jnp.float32)
    member = jnp.sum(hits, axis=1)
    widened = jnp.repeat(member.T, col_width // tile_count, axis=1)
    offset = (positions[:, None] - columns[None, :]).astype(jnp.float32) / spread_len
    taper_weight = 1.0 / (1.0 + offset * offset)
    return (widened * taper_weight * (2.0 / math.sqrt(listed))).astype(jnp.bfloat16)


def shot_weights(positions, columns, spread_len):
    offset = (positions[:, None] - columns[None, :]).astype(jnp.float32) / spread_len
    return 1.0 / (1.0 + offset * offset)


def complex_product(left_section, right_section):
    real_real = jnp.einsum(
        "qju,quy->qjy", left_section[0], right_section[0], preferred_element_type=jnp.float32
    )
    imag_imag = jnp.einsum(
        "qju,quy->qjy", left_section[1], right_section[1], preferred_element_type=jnp.float32
    )
    real_imag = jnp.einsum(
        "qju,quy->qjy", left_section[0], right_section[1], preferred_element_type=jnp.float32
    )
    imag_real = jnp.einsum(
        "qju,quy->qjy", left_section[1], right_section[0], preferred_element_type=jnp.float32
    )
    return jnp.stack([real_real - imag_imag, real_imag + imag_real])


def axis_pos(names):
    index = 0
    for name in names:
        index = index * lax.axis_size(name) + lax.axis_index(name)
    return index


def axis_count(names):
    count = 1
    for name in names:
        count *= lax.axis_size(name)
    return count


MESH_ID = pl.DeviceIdType.MESH
NX, NZ, NY = 4, 8, 4


def fused_kernel(spec_ref, traces_ref, lists_ref, rpos_ref, spos_ref, inverse_ref,
                 prim_ref, stack_ref,
                 colw_ref, roww_ref, mult_ref, partial_ref, slots_ref, aperture_ref, weights_ref,
                 recv_row, recv_col, send_row, send_col, recv_red, send_red):
    x = lax.axis_index("x")
    z = lax.axis_index("zl")
    y = lax.axis_index("y")
    h = lax.axis_index("zh")
    c = lax.axis_index("c")
    xp = lax.rem(x + 1, NX)
    xm = lax.rem(x + NX - 1, NX)
    yp = lax.rem(y + 1, NY)
    ym = lax.rem(y + NY - 1, NY)
    me_row = x * NZ + z
    me_col = (y * 2 + h) * 2 + c

    col_peers = []
    for yy in range(NY):
        for hh in range(2):
            for cc in range(2):
                col_peers.append(((yy * 2 + hh) * 2 + cc, {"y": yy, "zh": hh, "c": cc}))

    barrier = pltpu.get_barrier_semaphore()
    for peer in ({"x": xp}, {"x": xm}):
        pl.semaphore_signal(barrier, 1, device_id=peer, device_id_type=MESH_ID)
    for j, peer in col_peers:
        pl.when(j != me_col)(
            lambda peer=peer: pl.semaphore_signal(
                barrier, 1, device_id=peer, device_id_type=MESH_ID
            )
        )

    @pl.when(z > 0)
    def _():
        pl.semaphore_signal(barrier, 1, device_id={"zl": z - 1}, device_id_type=MESH_ID)

    @pl.when(z < NZ - 1)
    def _():
        pl.semaphore_signal(barrier, 1, device_id={"zl": z + 1}, device_id_type=MESH_ID)

    peers_in = 2 + len(col_peers) - 1
    ends = jnp.logical_or(z == 0, z == NZ - 1)
    pl.when(ends)(lambda: pl.semaphore_wait(barrier, peers_in + 1))
    pl.when(jnp.logical_not(ends))(lambda: pl.semaphore_wait(barrier, peers_in + 2))

    started = []
    shots = spec_ref.shape[1]
    recvs = spec_ref.shape[2]
    half = spec_ref.shape[0] // 2
    parts = (0, 1)

    def planes(part):
        return pl.ds(part * half, half)

    def colw_blk(b, part):
        return colw_ref.at[planes(part), pl.ds(pl.multiple_of(b * shots, shots), shots), :]

    def roww_blk(j, part):
        return roww_ref.at[planes(part), :, pl.ds(pl.multiple_of(j * recvs, recvs), recvs)]

    def row_copy(b, part, d, peer, own=False):
        src = spec_ref.at[planes(part)] if own else colw_blk(b, part)
        return pltpu.make_async_remote_copy(
            src, colw_blk(b, part), send_row.at[b, part, d], recv_row.at[b, part],
            device_id=peer, device_id_type=MESH_ID,
        )

    def col_copy(j, part, d, peer, own=False):
        src = spec_ref.at[planes(part)] if own else roww_blk(j, part)
        return pltpu.make_async_remote_copy(
            src, roww_blk(j, part), send_col.at[j, part, d], recv_col.at[j, part],
            device_id=peer, device_id_type=MESH_ID,
        )

    def start(desc, cond=None):
        if cond is None:
            desc.start()
        else:
            pl.when(cond)(desc.start)
        started.append((desc, cond))

    def when(cond, fn):
        if cond is None:
            fn()
        else:
            pl.when(cond)(fn)

    def row_relay(b, sends, cond=None, only=parts):
        for part in only:
            when(cond, row_copy(b, part, 0, {"x": x}).wait_recv)
            for d, peer, extra in sends:
                c2 = cond if extra is None else (extra if cond is None else jnp.logical_and(cond, extra))
                start(row_copy(b, part, d, peer), c2)

    def col_relay(j, sends, cond=None):
        for part in parts:
            when(cond, col_copy(j, part, 0, {"y": y}).wait_recv)
            for d, peer in sends:
                start(col_copy(j, part, d, peer), cond)

    for part in parts:
        start(col_copy(me_col, part, 0, {"c": 1 - c}, own=True))
        start(row_copy(me_row, part, 0, {"zl": z + 1}, own=True), z < NZ - 1)
        start(row_copy(me_row, part, 1, {"zl": z - 1}, own=True), z > 0)
        start(row_copy(me_row, part, 2, {"x": xp}, own=True))
        start(row_copy(me_row, part, 3, {"x": xm}, own=True))
        start(col_copy(me_col, part, 2, {"y": yp}, own=True))
        start(col_copy(me_col, part, 3, {"y": ym}, own=True))
    colw_ref[:, pl.ds(pl.multiple_of(me_row * shots, shots), shots), :] = spec_ref[...]
    roww_ref[:, :, pl.ds(pl.multiple_of(me_col * recvs, recvs), recvs)] = spec_ref[...]

    j_h = (y * 2 + 1 - h) * 2 + c
    j_c = (y * 2 + h) * 2 + 1 - c
    j_hc = (y * 2 + 1 - h) * 2 + 1 - c
    y_sends = ((2, {"y": yp}), (3, {"y": ym}))
    col_relay(j_c, y_sends)

    def x_forward(zsrc, cond):
        even = lax.rem(zsrc, 2) == 0
        row_relay(xm * NZ + zsrc, ((2, {"x": xp}, None),), jnp.logical_and(cond, even))
        odd = jnp.logical_not(even)
        row_relay(xp * NZ + zsrc, ((3, {"x": xm}, None),), jnp.logical_and(cond, odd))

    def x_forward_at(dist):
        if dist == 0:
            x_forward(z, True)
        else:
            x_forward(z - dist, z >= dist)
            x_forward(z + dist, z + dist < NZ)

    lag = 2
    x_sends = ((2, {"x": xp}, None), (3, {"x": xm}, None))
    for k in range(1, NZ):
        for part in parts:
            row_relay(x * NZ + z - k, x_sends + ((0, {"zl": z + 1}, z < NZ - 1),), z >= k, (part,))
            row_relay(x * NZ + z + k, x_sends + ((1, {"zl": z - 1}, z > 0),), z + k < NZ, (part,))
        if k - lag >= 0:
            x_forward_at(k - lag)
        if k == 2:
            for part in parts:
                start(col_copy(me_col, part, 1, {"zh": 1 - h}, own=True))
        if k == 4:
            col_relay(j_h, ((0, {"c": 1 - c}),) + y_sends)
        if k == 5:
            col_relay(j_hc, y_sends)
        if k == 6:
            for cc in range(2):
                col_relay((ym * 2 + 0) * 2 + cc, ((2, {"y": yp}),))
                col_relay((yp * 2 + 1) * 2 + cc, ((3, {"y": ym}),))
    for dist in range(NZ - lag, NZ):
        x_forward_at(dist)

    recvs_n = aperture_ref.shape[0]
    width = aperture_ref.shape[1]
    tiles, listed = lists_ref.shape
    tile_width = width // tiles
    spread_len = width * NX * NZ // 4
    first = me_col * recvs_n

    def as_column(row):
        n = row.shape[1]
        eye = lax.broadcasted_iota(jnp.int32, (n, n), 0) == lax.broadcasted_iota(jnp.int32, (n, n), 1)
        return jnp.sum(jnp.where(eye, row.astype(jnp.float32), 0.0), axis=1, keepdims=True)

    cols = (me_row * width + lax.broadcasted_iota(jnp.int32, (1, width), 1)).astype(jnp.float32)
    rpos = as_column(rpos_ref[:, pl.ds(pl.multiple_of(first, recvs_n), recvs_n)])
    offset = (rpos - cols) / spread_len
    taper = 1.0 / (1.0 + offset * offset)
    rows_here = first + lax.broadcasted_iota(jnp.int32, (recvs_n, listed), 0)
    for t in range(tiles):
        hits = (lists_ref[pl.ds(t, 1), :] == rows_here).astype(jnp.float32)
        member = jnp.sum(hits, axis=1, keepdims=True)
        part = taper[:, t * tile_width:(t + 1) * tile_width]
        aperture_ref[:, t * tile_width:(t + 1) * tile_width] = (
            member * part * (2.0 / math.sqrt(listed))
        ).astype(aperture_ref.dtype)
    spos = as_column(spos_ref[...])
    soffset = (spos - cols) / spread_len
    weights_ref[...] = 1.0 / (1.0 + soffset * soffset)

    y2 = lax.rem(y + 2, NY)
    for cc in range(2):
        col_relay((ym * 2 + 1) * 2 + cc, ())
        col_relay((yp * 2 + 0) * 2 + cc, ())
        for hh in range(2):
            col_relay((y2 * 2 + hh) * 2 + cc, ())
    for zz in range(NZ):
        row_relay(xm * NZ + zz if zz % 2 == 1 else xp * NZ + zz, ())

    nf = spec_ref.shape[0] // 2
    surface_root = math.sqrt(roww_ref.shape[2])
    span = NZ * shots
    mult_ref[...] = jnp.zeros(mult_ref.shape, mult_ref.dtype)

    def product_part(xc):
        u = pl.ds(pl.multiple_of(xc * span, span), span)
        for f in range(nf):
            lr = roww_ref[f, :, u]
            li = roww_ref[nf + f, :, u]
            rr = colw_ref[f, u, :]
            ri = colw_ref[nf + f, u, :]
            real_real = jnp.dot(lr, rr, preferred_element_type=jnp.float32)
            imag_imag = jnp.dot(li, ri, preferred_element_type=jnp.float32)
            real_imag = jnp.dot(lr, ri, preferred_element_type=jnp.float32)
            imag_real = jnp.dot(li, rr, preferred_element_type=jnp.float32)
            mult_ref[f] += real_real - imag_imag
            mult_ref[nf + f] += real_imag + imag_real

    product_part(x)
    product_part(xm)
    product_part(xp)
    x2 = lax.rem(x + 2, NX)
    for zz in range(NZ):
        row_relay(x2 * NZ + zz, ())
    product_part(x2)
    for p in range(2 * nf):
        mult_ref[p] = -mult_ref[p] / surface_root

    def prim_body(t, carry):
        wave = inverse_ref[t, 0] * mult_ref[0]
        for p in range(1, 2 * nf):
            wave = wave + inverse_ref[t, p] * mult_ref[p]
        prim_ref[t] = (traces_ref[t].astype(jnp.float32) - wave).astype(prim_ref.dtype)
        return carry

    lax.fori_loop(0, traces_ref.shape[0], prim_body, 0)

    band = partial_ref.shape[1]

    def band_peer(i):
        hh = lax.rem(1 - h + i // 8, 2)
        yy = lax.rem(i, 8) // 2
        cc = lax.rem(i, 2)
        return (yy * 2 + hh) * 2 + cc, {"y": yy, "zh": hh, "c": cc}

    def reduce_copy(j, peer):
        return pltpu.make_async_remote_copy(
            partial_ref.at[j], slots_ref.at[me_col], send_red.at[j], recv_red.at[me_col],
            device_id=peer, device_id_type=MESH_ID,
        )

    def band_body(i, carry):
        j, peer = band_peer(i)
        rows = []
        for u in range(band):
            stacked = jnp.dot(
                prim_ref[j * band + u], aperture_ref[...], preferred_element_type=jnp.float32
            )
            rows.append(jnp.sum(stacked * weights_ref[...], axis=0, keepdims=True))
        partial_ref[j] = jnp.concatenate(rows, axis=0)
        pl.when(j != me_col)(reduce_copy(j, peer).start)
        return carry

    lax.fori_loop(0, partial_ref.shape[0], band_body, 0)

    slots_ref[me_col] = partial_ref[me_col]
    for j, peer in col_peers:
        recv = pltpu.make_async_remote_copy(
            partial_ref.at[j], slots_ref.at[j], send_red.at[j], recv_red.at[j],
            device_id=peer, device_id_type=MESH_ID,
        )
        pl.when(j != me_col)(recv.wait_recv)
    total = slots_ref[0]
    for j in range(1, len(col_peers)):
        total = total + slots_ref[j]
    stack_ref[...] = total

    for desc, cond in started:
        when(cond, desc.wait_send)
    for j, peer in col_peers:
        pl.when(j != me_col)(reduce_copy(j, peer).wait_send)


def fused_call(spec, traces, lists, rpos, spos, inverse, width, row_count, col_count):
    planes, shots, recvs = spec.shape
    samples = traces.shape[0]
    band = samples // col_count
    vmem = pl.BlockSpec(memory_space=pltpu.VMEM)
    return pl.pallas_call(
        fused_kernel,
        out_shape=(
            jax.ShapeDtypeStruct(traces.shape, jnp.bfloat16),
            jax.ShapeDtypeStruct((band, width), jnp.float32),
        ),
        in_specs=[vmem, vmem, vmem, vmem, vmem, pl.BlockSpec(memory_space=pltpu.SMEM)],
        out_specs=(vmem, vmem),
        scratch_shapes=[
            pltpu.VMEM((planes, row_count * shots, recvs), spec.dtype),
            pltpu.VMEM((planes, shots, col_count * recvs), spec.dtype),
            pltpu.VMEM((planes, shots, recvs), jnp.float32),
            pltpu.VMEM((col_count, band, width), jnp.float32),
            pltpu.VMEM((col_count, band, width), jnp.float32),
            pltpu.VMEM((recvs, width), jnp.bfloat16),
            pltpu.VMEM((shots, width), jnp.float32),
            pltpu.SemaphoreType.DMA((row_count, 2)),
            pltpu.SemaphoreType.DMA((col_count, 2)),
            pltpu.SemaphoreType.DMA((row_count, 2, 4)),
            pltpu.SemaphoreType.DMA((col_count, 2, 4)),
            pltpu.SemaphoreType.DMA((col_count,)),
            pltpu.SemaphoreType.DMA((col_count,)),
        ],
        compiler_params=pltpu.CompilerParams(collective_id=0, has_side_effects=True),
    )(spec, traces, lists, rpos, spos, inverse)


def per_device(traces, source_pos, receiver_pos, aperture_list, band_index, weight_tiles):
    samples, shot_count, recv_count = traces.shape
    col_count = axis_count(COL)
    row_count = axis_count(ROW)
    surface_count = recv_count * col_count
    image_panel_width = band_index.shape[0]
    depth_slab_samples = samples // col_count
    cosine, sine_table = phase_tables_np(samples)
    forward = jnp.asarray(
        (np.concatenate([cosine, -sine_table], 0) / np.float32(math.sqrt(samples))).astype(
            ml_dtypes.bfloat16
        )
    )
    spectra = jnp.einsum(
        "pt,tsr->psr", forward, traces, preferred_element_type=jnp.float32
    ).astype(jnp.bfloat16)

    inverse = jnp.asarray(np.concatenate([cosine, -sine_table], 0).T / np.float32(math.sqrt(NF)))
    primaries, stacked = fused_call(
        spectra,
        traces,
        aperture_list,
        receiver_pos.reshape(1, -1),
        source_pos.reshape(1, -1),
        inverse,
        image_panel_width,
        row_count,
        col_count,
    )
    column_stack = (stacked / math.sqrt(shot_count)).astype(jnp.bfloat16)

    tile_kinds = weight_tiles.shape[0]
    select = band_index[None, :] == jnp.arange(tile_kinds, dtype=jnp.int32)[:, None]
    widened = jnp.where(select[:, None, :], column_stack[None], jnp.zeros((), jnp.bfloat16))
    image_out = jnp.einsum(
        "kz,kx->zx",
        weight_tiles.reshape(tile_kinds * depth_slab_samples, weight_tiles.shape[2]),
        widened.reshape(tile_kinds * depth_slab_samples, image_panel_width),
        preferred_element_type=jnp.float32,
    )
    return (primaries, image_out)


def solution(mesh):
    n_row = mesh.shape["row"]
    n_col = mesh.shape["col"]
    fine = Mesh(
        mesh.devices.reshape(4, n_row // 4, 4, n_col // 8, 2), ("x", "zl", "y", "zh", "c")
    )
    placed = (P(None, ROW, COL), P(ROW), P(), P(ROW, None), P(ROW), P())
    return jax.shard_map(
        per_device,
        mesh=fine,
        in_specs=placed,
        out_specs=(P(None, ROW, COL), P(COL, ROW)),
        check_vma=False,
    )
```

```python
import math

import jax
import ml_dtypes
import numpy as np
import jax.numpy as jnp
from jax import lax
from jax.experimental import pallas as pl
from jax.experimental.pallas import tpu as pltpu
from jax.sharding import Mesh
from jax.sharding import PartitionSpec as P

NFFT = 4096
NF = 4

ROW = ("x", "zl")
COL = ("y", "zh", "c")


def phase_tables_np(samples):
    freq_bins = (2 * np.arange(NF, dtype=np.int32) + 1) * (NFFT // (4 * NF))
    sample_ticks = np.arange(samples, dtype=np.int32)
    phase_turns = freq_bins[:, None] * sample_ticks[None, :] % NFFT
    phase_angle = phase_turns.astype(np.float32) * np.float32(2.0 * math.pi / NFFT)
    angle = phase_angle.astype(np.float64)
    return (np.cos(angle).astype(np.float32), np.sin(angle).astype(np.float32))


def phase_tables(samples):
    freq_bins = (2 * jnp.arange(NF, dtype=jnp.int32) + 1) * (NFFT // (4 * NF))
    sample_ticks = jnp.arange(samples, dtype=jnp.int32)
    phase_turns = freq_bins[:, None] * sample_ticks[None, :] % NFFT
    phase_angle = phase_turns.astype(jnp.float32) * (2.0 * math.pi / NFFT)
    return (jnp.cos(phase_angle), jnp.sin(phase_angle))


def aperture_rows(tile_index_lists, positions, columns, first_row, row_count, spread_len):
    tile_count, listed = tile_index_lists.shape
    col_width = columns.shape[0]
    rows = first_row + jnp.arange(row_count, dtype=jnp.int32)
    hits = (tile_index_lists[:, :, None] == rows[None, None, :]).astype(jnp.float32)
    member = jnp.sum(hits, axis=1)
    widened = jnp.repeat(member.T, col_width // tile_count, axis=1)
    offset = (positions[:, None] - columns[None, :]).astype(jnp.float32) / spread_len
    taper_weight = 1.0 / (1.0 + offset * offset)
    return (widened * taper_weight * (2.0 / math.sqrt(listed))).astype(jnp.bfloat16)


def shot_weights(positions, columns, spread_len):
    offset = (positions[:, None] - columns[None, :]).astype(jnp.float32) / spread_len
    return 1.0 / (1.0 + offset * offset)


def complex_product(left_section, right_section):
    real_real = jnp.einsum(
        "qju,quy->qjy", left_section[0], right_section[0], preferred_element_type=jnp.float32
    )
    imag_imag = jnp.einsum(
        "qju,quy->qjy", left_section[1], right_section[1], preferred_element_type=jnp.float32
    )
    real_imag = jnp.einsum(
        "qju,quy->qjy", left_section[0], right_section[1], preferred_element_type=jnp.float32
    )
    imag_real = jnp.einsum(
        "qju,quy->qjy", left_section[1], right_section[0], preferred_element_type=jnp.float32
    )
    return jnp.stack([real_real - imag_imag, real_imag + imag_real])


def axis_pos(names):
    index = 0
    for name in names:
        index = index * lax.axis_size(name) + lax.axis_index(name)
    return index


def axis_count(names):
    count = 1
    for name in names:
        count *= lax.axis_size(name)
    return count


MESH_ID = pl.DeviceIdType.MESH
NX, NZ, NY = 4, 8, 4


def fused_kernel(spec_ref, traces_ref, lists_ref, rpos_ref, spos_ref, inverse_ref,
                 prim_ref, stack_ref,
                 colw_ref, roww_ref, mult_ref, partial_ref, slots_ref, aperture_ref, weights_ref,
                 recv_row, recv_col, send_row, send_col, recv_red, send_red):
    x = lax.axis_index("x")
    z = lax.axis_index("zl")
    y = lax.axis_index("y")
    h = lax.axis_index("zh")
    c = lax.axis_index("c")
    xp = lax.rem(x + 1, NX)
    xm = lax.rem(x + NX - 1, NX)
    yp = lax.rem(y + 1, NY)
    ym = lax.rem(y + NY - 1, NY)
    me_row = x * NZ + z
    me_col = (y * 2 + h) * 2 + c

    col_peers = []
    for yy in range(NY):
        for hh in range(2):
            for cc in range(2):
                col_peers.append(((yy * 2 + hh) * 2 + cc, {"y": yy, "zh": hh, "c": cc}))

    barrier = pltpu.get_barrier_semaphore()
    for peer in ({"x": xp}, {"x": xm}):
        pl.semaphore_signal(barrier, 1, device_id=peer, device_id_type=MESH_ID)
    for j, peer in col_peers:
        pl.when(j != me_col)(
            lambda peer=peer: pl.semaphore_signal(
                barrier, 1, device_id=peer, device_id_type=MESH_ID
            )
        )

    @pl.when(z > 0)
    def _():
        pl.semaphore_signal(barrier, 1, device_id={"zl": z - 1}, device_id_type=MESH_ID)

    @pl.when(z < NZ - 1)
    def _():
        pl.semaphore_signal(barrier, 1, device_id={"zl": z + 1}, device_id_type=MESH_ID)

    peers_in = 2 + len(col_peers) - 1
    ends = jnp.logical_or(z == 0, z == NZ - 1)
    pl.when(ends)(lambda: pl.semaphore_wait(barrier, peers_in + 1))
    pl.when(jnp.logical_not(ends))(lambda: pl.semaphore_wait(barrier, peers_in + 2))

    started = []
    shots = spec_ref.shape[1]
    recvs = spec_ref.shape[2]
    half = spec_ref.shape[0] // 2
    parts = (0, 1)

    def planes(part):
        return pl.ds(part * half, half)

    def colw_blk(b, part):
        return colw_ref.at[planes(part), pl.ds(pl.multiple_of(b * shots, shots), shots), :]

    def roww_blk(j, part):
        return roww_ref.at[planes(part), :, pl.ds(pl.multiple_of(j * recvs, recvs), recvs)]

    def row_copy(b, part, d, peer, own=False):
        src = spec_ref.at[planes(part)] if own else colw_blk(b, part)
        return pltpu.make_async_remote_copy(
            src, colw_blk(b, part), send_row.at[b, part, d], recv_row.at[b, part],
            device_id=peer, device_id_type=MESH_ID,
        )

    def col_copy(j, part, d, peer, own=False):
        src = spec_ref.at[planes(part)] if own else roww_blk(j, part)
        return pltpu.make_async_remote_copy(
            src, roww_blk(j, part), send_col.at[j, part, d], recv_col.at[j, part],
            device_id=peer, device_id_type=MESH_ID,
        )

    def start(desc, cond=None):
        if cond is None:
            desc.start()
        else:
            pl.when(cond)(desc.start)
        started.append((desc, cond))

    def when(cond, fn):
        if cond is None:
            fn()
        else:
            pl.when(cond)(fn)

    def row_relay(b, sends, cond=None, only=parts):
        for part in only:
            when(cond, row_copy(b, part, 0, {"x": x}).wait_recv)
            for d, peer, extra in sends:
                c2 = cond if extra is None else (extra if cond is None else jnp.logical_and(cond, extra))
                start(row_copy(b, part, d, peer), c2)

    def col_relay(j, sends, cond=None):
        for part in parts:
            when(cond, col_copy(j, part, 0, {"y": y}).wait_recv)
            for d, peer in sends:
                start(col_copy(j, part, d, peer), cond)

    for part in parts:
        start(col_copy(me_col, part, 0, {"c": 1 - c}, own=True))
        start(row_copy(me_row, part, 0, {"zl": z + 1}, own=True), z < NZ - 1)
        start(row_copy(me_row, part, 1, {"zl": z - 1}, own=True), z > 0)
        start(row_copy(me_row, part, 2, {"x": xp}, own=True))
        start(row_copy(me_row, part, 3, {"x": xm}, own=True))
        start(col_copy(me_col, part, 2, {"y": yp}, own=True))
        start(col_copy(me_col, part, 3, {"y": ym}, own=True))
    colw_ref[:, pl.ds(pl.multiple_of(me_row * shots, shots), shots), :] = spec_ref[...]
    roww_ref[:, :, pl.ds(pl.multiple_of(me_col * recvs, recvs), recvs)] = spec_ref[...]

    j_h = (y * 2 + 1 - h) * 2 + c
    j_c = (y * 2 + h) * 2 + 1 - c
    j_hc = (y * 2 + 1 - h) * 2 + 1 - c
    y_sends = ((2, {"y": yp}), (3, {"y": ym}))
    to_partner = (0, {"c": 1 - c})
    col_relay(j_c, ())

    def x_forward(zsrc, cond):
        even = lax.rem(zsrc, 2) == 0
        row_relay(xm * NZ + zsrc, ((2, {"x": xp}, None),), jnp.logical_and(cond, even))
        odd = jnp.logical_not(even)
        row_relay(xp * NZ + zsrc, ((3, {"x": xm}, None),), jnp.logical_and(cond, odd))

    def x_forward_at(dist):
        if dist == 0:
            x_forward(z, True)
        else:
            x_forward(z - dist, z >= dist)
            x_forward(z + dist, z + dist < NZ)

    lag = 2
    x_sends = ((2, {"x": xp}, None), (3, {"x": xm}, None))
    for k in range(1, NZ):
        for part in parts:
            row_relay(x * NZ + z - k, x_sends + ((0, {"zl": z + 1}, z < NZ - 1),), z >= k, (part,))
            row_relay(x * NZ + z + k, x_sends + ((1, {"zl": z - 1}, z > 0),), z + k < NZ, (part,))
        if k - lag >= 0:
            x_forward_at(k - lag)
        if k == 2:
            for part in parts:
                start(col_copy(me_col, part, 1, {"zh": 1 - h}, own=True))
        if k == 4:
            col_relay(j_h, ((0, {"c": 1 - c}),) + y_sends)
        if k == 5:
            col_relay(j_hc, ())
        if k == 6:
            col_relay((ym * 2 + 0) * 2 + c, ((2, {"y": yp}), to_partner))
            col_relay((yp * 2 + 1) * 2 + c, ((3, {"y": ym}), to_partner))
    for dist in range(NZ - lag, NZ):
        x_forward_at(dist)

    recvs_n = aperture_ref.shape[0]
    width = aperture_ref.shape[1]
    tiles, listed = lists_ref.shape
    tile_width = width // tiles
    spread_len = width * NX * NZ // 4
    first = me_col * recvs_n

    def as_column(row):
        n = row.shape[1]
        eye = lax.broadcasted_iota(jnp.int32, (n, n), 0) == lax.broadcasted_iota(jnp.int32, (n, n), 1)
        return jnp.sum(jnp.where(eye, row.astype(jnp.float32), 0.0), axis=1, keepdims=True)

    cols = (me_row * width + lax.broadcasted_iota(jnp.int32, (1, width), 1)).astype(jnp.float32)
    rpos = as_column(rpos_ref[:, pl.ds(pl.multiple_of(first, recvs_n), recvs_n)])
    offset = (rpos - cols) / spread_len
    taper = 1.0 / (1.0 + offset * offset)
    rows_here = first + lax.broadcasted_iota(jnp.int32, (recvs_n, listed), 0)
    for t in range(tiles):
        hits = (lists_ref[pl.ds(t, 1), :] == rows_here).astype(jnp.float32)
        member = jnp.sum(hits, axis=1, keepdims=True)
        part = taper[:, t * tile_width:(t + 1) * tile_width]
        aperture_ref[:, t * tile_width:(t + 1) * tile_width] = (
            member * part * (2.0 / math.sqrt(listed))
        ).astype(aperture_ref.dtype)
    spos = as_column(spos_ref[...])
    soffset = (spos - cols) / spread_len
    weights_ref[...] = 1.0 / (1.0 + soffset * soffset)

    y2 = lax.rem(y + 2, NY)
    col_relay((ym * 2 + 1) * 2 + c, (to_partner,))
    col_relay((yp * 2 + 0) * 2 + c, (to_partner,))
    for hh in range(2):
        col_relay((y2 * 2 + hh) * 2 + c, (to_partner,))
    for plane in (ym, yp, y2):
        for hh in range(2):
            col_relay((plane * 2 + hh) * 2 + 1 - c, ())
    for zz in range(NZ):
        row_relay(xm * NZ + zz if zz % 2 == 1 else xp * NZ + zz, ())

    nf = spec_ref.shape[0] // 2
    surface_root = math.sqrt(roww_ref.shape[2])
    span = NZ * shots
    mult_ref[...] = jnp.zeros(mult_ref.shape, mult_ref.dtype)

    def product_part(xc):
        u = pl.ds(pl.multiple_of(xc * span, span), span)
        for f in range(nf):
            lr = roww_ref[f, :, u]
            li = roww_ref[nf + f, :, u]
            rr = colw_ref[f, u, :]
            ri = colw_ref[nf + f, u, :]
            real_real = jnp.dot(lr, rr, preferred_element_type=jnp.float32)
            imag_imag = jnp.dot(li, ri, preferred_element_type=jnp.float32)
            real_imag = jnp.dot(lr, ri, preferred_element_type=jnp.float32)
            imag_real = jnp.dot(li, rr, preferred_element_type=jnp.float32)
            mult_ref[f] += real_real - imag_imag
            mult_ref[nf + f] += real_imag + imag_real

    product_part(x)
    product_part(xm)
    product_part(xp)
    x2 = lax.rem(x + 2, NX)
    for zz in range(NZ):
        row_relay(x2 * NZ + zz, ())
    product_part(x2)
    for p in range(2 * nf):
        mult_ref[p] = -mult_ref[p] / surface_root

    def prim_body(t, carry):
        wave = inverse_ref[t, 0] * mult_ref[0]
        for p in range(1, 2 * nf):
            wave = wave + inverse_ref[t, p] * mult_ref[p]
        prim_ref[t] = (traces_ref[t].astype(jnp.float32) - wave).astype(prim_ref.dtype)
        return carry

    lax.fori_loop(0, traces_ref.shape[0], prim_body, 0)

    band = partial_ref.shape[1]

    def band_peer(i):
        hh = lax.rem(1 - h + i // 8, 2)
        yy = lax.rem(i, 8) // 2
        cc = lax.rem(i, 2)
        return (yy * 2 + hh) * 2 + cc, {"y": yy, "zh": hh, "c": cc}

    def reduce_copy(j, peer):
        return pltpu.make_async_remote_copy(
            partial_ref.at[j], slots_ref.at[me_col], send_red.at[j], recv_red.at[me_col],
            device_id=peer, device_id_type=MESH_ID,
        )

    def band_body(i, carry):
        j, peer = band_peer(i)
        rows = []
        for u in range(band):
            stacked = jnp.dot(
                prim_ref[j * band + u], aperture_ref[...], preferred_element_type=jnp.float32
            )
            rows.append(jnp.sum(stacked * weights_ref[...], axis=0, keepdims=True))
        partial_ref[j] = jnp.concatenate(rows, axis=0)
        pl.when(j != me_col)(reduce_copy(j, peer).start)
        return carry

    lax.fori_loop(0, partial_ref.shape[0], band_body, 0)

    slots_ref[me_col] = partial_ref[me_col]
    for j, peer in col_peers:
        recv = pltpu.make_async_remote_copy(
            partial_ref.at[j], slots_ref.at[j], send_red.at[j], recv_red.at[j],
            device_id=peer, device_id_type=MESH_ID,
        )
        pl.when(j != me_col)(recv.wait_recv)
    total = slots_ref[0]
    for j in range(1, len(col_peers)):
        total = total + slots_ref[j]
    stack_ref[...] = total

    for desc, cond in started:
        when(cond, desc.wait_send)
    for j, peer in col_peers:
        pl.when(j != me_col)(reduce_copy(j, peer).wait_send)


def fused_call(spec, traces, lists, rpos, spos, inverse, width, row_count, col_count):
    planes, shots, recvs = spec.shape
    samples = traces.shape[0]
    band = samples // col_count
    vmem = pl.BlockSpec(memory_space=pltpu.VMEM)
    return pl.pallas_call(
        fused_kernel,
        out_shape=(
            jax.ShapeDtypeStruct(traces.shape, jnp.bfloat16),
            jax.ShapeDtypeStruct((band, width), jnp.float32),
        ),
        in_specs=[vmem, vmem, vmem, vmem, vmem, pl.BlockSpec(memory_space=pltpu.SMEM)],
        out_specs=(vmem, vmem),
        scratch_shapes=[
            pltpu.VMEM((planes, row_count * shots, recvs), spec.dtype),
            pltpu.VMEM((planes, shots, col_count * recvs), spec.dtype),
            pltpu.VMEM((planes, shots, recvs), jnp.float32),
            pltpu.VMEM((col_count, band, width), jnp.float32),
            pltpu.VMEM((col_count, band, width), jnp.float32),
            pltpu.VMEM((recvs, width), jnp.bfloat16),
            pltpu.VMEM((shots, width), jnp.float32),
            pltpu.SemaphoreType.DMA((row_count, 2)),
            pltpu.SemaphoreType.DMA((col_count, 2)),
            pltpu.SemaphoreType.DMA((row_count, 2, 4)),
            pltpu.SemaphoreType.DMA((col_count, 2, 4)),
            pltpu.SemaphoreType.DMA((col_count,)),
            pltpu.SemaphoreType.DMA((col_count,)),
        ],
        compiler_params=pltpu.CompilerParams(collective_id=0, has_side_effects=True),
    )(spec, traces, lists, rpos, spos, inverse)


def per_device(traces, source_pos, receiver_pos, aperture_list, band_index, weight_tiles):
    samples, shot_count, recv_count = traces.shape
    col_count = axis_count(COL)
    row_count = axis_count(ROW)
    surface_count = recv_count * col_count
    image_panel_width = band_index.shape[0]
    depth_slab_samples = samples // col_count
    cosine, sine_table = phase_tables_np(samples)
    forward = jnp.asarray(
        (np.concatenate([cosine, -sine_table], 0) / np.float32(math.sqrt(samples))).astype(
            ml_dtypes.bfloat16
        )
    )
    spectra = jnp.einsum(
        "pt,tsr->psr", forward, traces, preferred_element_type=jnp.float32
    ).astype(jnp.bfloat16)

    inverse = jnp.asarray(np.concatenate([cosine, -sine_table], 0).T / np.float32(math.sqrt(NF)))
    primaries, stacked = fused_call(
        spectra,
        traces,
        aperture_list,
        receiver_pos.reshape(1, -1),
        source_pos.reshape(1, -1),
        inverse,
        image_panel_width,
        row_count,
        col_count,
    )
    column_stack = (stacked / math.sqrt(shot_count)).astype(jnp.bfloat16)

    tile_kinds = weight_tiles.shape[0]
    select = band_index[None, :] == jnp.arange(tile_kinds, dtype=jnp.int32)[:, None]
    widened = jnp.where(select[:, None, :], column_stack[None], jnp.zeros((), jnp.bfloat16))
    image_out = jnp.einsum(
        "kz,kx->zx",
        weight_tiles.reshape(tile_kinds * depth_slab_samples, weight_tiles.shape[2]),
        widened.reshape(tile_kinds * depth_slab_samples, image_panel_width),
        preferred_element_type=jnp.float32,
    )
    return (primaries, image_out)


def solution(mesh):
    n_row = mesh.shape["row"]
    n_col = mesh.shape["col"]
    fine = Mesh(
        mesh.devices.reshape(4, n_row // 4, 4, n_col // 8, 2), ("x", "zl", "y", "zh", "c")
    )
    placed = (P(None, ROW, COL), P(ROW), P(), P(ROW, None), P(ROW), P())
    return jax.shard_map(
        per_device,
        mesh=fine,
        in_specs=placed,
        out_specs=(P(None, ROW, COL), P(COL, ROW)),
        check_vma=False,
    )
```

```python
import math

import jax
import ml_dtypes
import numpy as np
import jax.numpy as jnp
from jax import lax
from jax.experimental import pallas as pl
from jax.experimental.pallas import tpu as pltpu
from jax.sharding import Mesh
from jax.sharding import PartitionSpec as P

NFFT = 4096
NF = 4

ROW = ("x", "zl")
COL = ("y", "zh", "c")


def phase_tables_np(samples):
    freq_bins = (2 * np.arange(NF, dtype=np.int32) + 1) * (NFFT // (4 * NF))
    sample_ticks = np.arange(samples, dtype=np.int32)
    phase_turns = freq_bins[:, None] * sample_ticks[None, :] % NFFT
    phase_angle = phase_turns.astype(np.float32) * np.float32(2.0 * math.pi / NFFT)
    angle = phase_angle.astype(np.float64)
    return (np.cos(angle).astype(np.float32), np.sin(angle).astype(np.float32))


def phase_tables(samples):
    freq_bins = (2 * jnp.arange(NF, dtype=jnp.int32) + 1) * (NFFT // (4 * NF))
    sample_ticks = jnp.arange(samples, dtype=jnp.int32)
    phase_turns = freq_bins[:, None] * sample_ticks[None, :] % NFFT
    phase_angle = phase_turns.astype(jnp.float32) * (2.0 * math.pi / NFFT)
    return (jnp.cos(phase_angle), jnp.sin(phase_angle))


def aperture_rows(tile_index_lists, positions, columns, first_row, row_count, spread_len):
    tile_count, listed = tile_index_lists.shape
    col_width = columns.shape[0]
    rows = first_row + jnp.arange(row_count, dtype=jnp.int32)
    hits = (tile_index_lists[:, :, None] == rows[None, None, :]).astype(jnp.float32)
    member = jnp.sum(hits, axis=1)
    widened = jnp.repeat(member.T, col_width // tile_count, axis=1)
    offset = (positions[:, None] - columns[None, :]).astype(jnp.float32) / spread_len
    taper_weight = 1.0 / (1.0 + offset * offset)
    return (widened * taper_weight * (2.0 / math.sqrt(listed))).astype(jnp.bfloat16)


def shot_weights(positions, columns, spread_len):
    offset = (positions[:, None] - columns[None, :]).astype(jnp.float32) / spread_len
    return 1.0 / (1.0 + offset * offset)


def complex_product(left_section, right_section):
    real_real = jnp.einsum(
        "qju,quy->qjy", left_section[0], right_section[0], preferred_element_type=jnp.float32
    )
    imag_imag = jnp.einsum(
        "qju,quy->qjy", left_section[1], right_section[1], preferred_element_type=jnp.float32
    )
    real_imag = jnp.einsum(
        "qju,quy->qjy", left_section[0], right_section[1], preferred_element_type=jnp.float32
    )
    imag_real = jnp.einsum(
        "qju,quy->qjy", left_section[1], right_section[0], preferred_element_type=jnp.float32
    )
    return jnp.stack([real_real - imag_imag, real_imag + imag_real])


def axis_pos(names):
    index = 0
    for name in names:
        index = index * lax.axis_size(name) + lax.axis_index(name)
    return index


def axis_count(names):
    count = 1
    for name in names:
        count *= lax.axis_size(name)
    return count


MESH_ID = pl.DeviceIdType.MESH
NX, NZ, NY = 4, 8, 4


def fused_kernel(traces_ref, forward_ref, lists_ref, rpos_ref, spos_ref, inverse_ref,
                 prim_ref, stack_ref,
                 spec_ref, colw_ref, roww_ref, mult_ref, partial_ref, slots_ref, aperture_ref, weights_ref,
                 recv_row, recv_col, send_row, send_col, recv_red, send_red):
    x = lax.axis_index("x")
    z = lax.axis_index("zl")
    y = lax.axis_index("y")
    h = lax.axis_index("zh")
    c = lax.axis_index("c")
    xp = lax.rem(x + 1, NX)
    xm = lax.rem(x + NX - 1, NX)
    yp = lax.rem(y + 1, NY)
    ym = lax.rem(y + NY - 1, NY)
    me_row = x * NZ + z
    me_col = (y * 2 + h) * 2 + c

    col_peers = []
    for yy in range(NY):
        for hh in range(2):
            for cc in range(2):
                col_peers.append(((yy * 2 + hh) * 2 + cc, {"y": yy, "zh": hh, "c": cc}))

    barrier = pltpu.get_barrier_semaphore()
    for peer in ({"x": xp}, {"x": xm}):
        pl.semaphore_signal(barrier, 1, device_id=peer, device_id_type=MESH_ID)
    for j, peer in col_peers:
        pl.when(j != me_col)(
            lambda peer=peer: pl.semaphore_signal(
                barrier, 1, device_id=peer, device_id_type=MESH_ID
            )
        )

    @pl.when(z > 0)
    def _():
        pl.semaphore_signal(barrier, 1, device_id={"zl": z - 1}, device_id_type=MESH_ID)

    @pl.when(z < NZ - 1)
    def _():
        pl.semaphore_signal(barrier, 1, device_id={"zl": z + 1}, device_id_type=MESH_ID)

    samples = traces_ref.shape[0]
    group = 4
    for p0 in range(0, spec_ref.shape[0], group):
        def spectra_body(t, accs, p0=p0):
            sample = traces_ref[t].astype(jnp.float32)
            return tuple(acc + forward_ref[p0 + g, t] * sample for g, acc in enumerate(accs))

        zero = jnp.zeros(spec_ref.shape[1:], jnp.float32)
        accs = lax.fori_loop(0, samples, spectra_body, (zero,) * group)
        for g in range(group):
            spec_ref[p0 + g] = accs[g].astype(spec_ref.dtype)

    peers_in = 2 + len(col_peers) - 1
    ends = jnp.logical_or(z == 0, z == NZ - 1)
    pl.when(ends)(lambda: pl.semaphore_wait(barrier, peers_in + 1))
    pl.when(jnp.logical_not(ends))(lambda: pl.semaphore_wait(barrier, peers_in + 2))

    started = []
    shots = spec_ref.shape[1]
    recvs = spec_ref.shape[2]
    half = spec_ref.shape[0] // 2
    parts = (0, 1)

    def planes(part):
        return pl.ds(part * half, half)

    def colw_blk(b, part):
        return colw_ref.at[planes(part), pl.ds(pl.multiple_of(b * shots, shots), shots), :]

    def roww_blk(j, part):
        return roww_ref.at[planes(part), :, pl.ds(pl.multiple_of(j * recvs, recvs), recvs)]

    def row_copy(b, part, d, peer, own=False):
        src = spec_ref.at[planes(part)] if own else colw_blk(b, part)
        return pltpu.make_async_remote_copy(
            src, colw_blk(b, part), send_row.at[b, part, d], recv_row.at[b, part],
            device_id=peer, device_id_type=MESH_ID,
        )

    def col_copy(j, part, d, peer, own=False):
        src = spec_ref.at[planes(part)] if own else roww_blk(j, part)
        return pltpu.make_async_remote_copy(
            src, roww_blk(j, part), send_col.at[j, part, d], recv_col.at[j, part],
            device_id=peer, device_id_type=MESH_ID,
        )

    def start(desc, cond=None):
        if cond is None:
            desc.start()
        else:
            pl.when(cond)(desc.start)
        started.append((desc, cond))

    def when(cond, fn):
        if cond is None:
            fn()
        else:
            pl.when(cond)(fn)

    def row_relay(b, sends, cond=None, only=parts):
        for part in only:
            when(cond, row_copy(b, part, 0, {"x": x}).wait_recv)
            for d, peer, extra in sends:
                c2 = cond if extra is None else (extra if cond is None else jnp.logical_and(cond, extra))
                start(row_copy(b, part, d, peer), c2)

    def col_relay(j, sends, cond=None):
        for part in parts:
            when(cond, col_copy(j, part, 0, {"y": y}).wait_recv)
            for d, peer in sends:
                start(col_copy(j, part, d, peer), cond)

    for part in parts:
        start(col_copy(me_col, part, 0, {"c": 1 - c}, own=True))
        start(row_copy(me_row, part, 0, {"zl": z + 1}, own=True), z < NZ - 1)
        start(row_copy(me_row, part, 1, {"zl": z - 1}, own=True), z > 0)
        start(row_copy(me_row, part, 2, {"x": xp}, own=True))
        start(row_copy(me_row, part, 3, {"x": xm}, own=True))
        start(col_copy(me_col, part, 2, {"y": yp}, own=True))
        start(col_copy(me_col, part, 3, {"y": ym}, own=True))
    colw_ref[:, pl.ds(pl.multiple_of(me_row * shots, shots), shots), :] = spec_ref[...]
    roww_ref[:, :, pl.ds(pl.multiple_of(me_col * recvs, recvs), recvs)] = spec_ref[...]

    j_h = (y * 2 + 1 - h) * 2 + c
    j_c = (y * 2 + h) * 2 + 1 - c
    j_hc = (y * 2 + 1 - h) * 2 + 1 - c
    y_sends = ((2, {"y": yp}), (3, {"y": ym}))
    to_partner = (0, {"c": 1 - c})
    col_relay(j_c, ())

    def x_forward(zsrc, cond):
        even = lax.rem(zsrc, 2) == 0
        row_relay(xm * NZ + zsrc, ((2, {"x": xp}, None),), jnp.logical_and(cond, even))
        odd = jnp.logical_not(even)
        row_relay(xp * NZ + zsrc, ((3, {"x": xm}, None),), jnp.logical_and(cond, odd))

    def x_forward_at(dist):
        if dist == 0:
            x_forward(z, True)
        else:
            x_forward(z - dist, z >= dist)
            x_forward(z + dist, z + dist < NZ)

    lag = 2
    x_sends = ((2, {"x": xp}, None), (3, {"x": xm}, None))
    for k in range(1, NZ):
        for part in parts:
            row_relay(x * NZ + z - k, x_sends + ((0, {"zl": z + 1}, z < NZ - 1),), z >= k, (part,))
            row_relay(x * NZ + z + k, x_sends + ((1, {"zl": z - 1}, z > 0),), z + k < NZ, (part,))
        if k - lag >= 0:
            x_forward_at(k - lag)
        if k == 2:
            for part in parts:
                start(col_copy(me_col, part, 1, {"zh": 1 - h}, own=True))
        if k == 4:
            col_relay(j_h, ((0, {"c": 1 - c}),) + y_sends)
        if k == 5:
            col_relay(j_hc, ())
        if k == 6:
            col_relay((ym * 2 + 0) * 2 + c, ((2, {"y": yp}), to_partner))
            col_relay((yp * 2 + 1) * 2 + c, ((3, {"y": ym}), to_partner))
    for dist in range(NZ - lag, NZ):
        x_forward_at(dist)

    recvs_n = aperture_ref.shape[0]
    width = aperture_ref.shape[1]
    tiles, listed = lists_ref.shape
    tile_width = width // tiles
    spread_len = width * NX * NZ // 4
    first = me_col * recvs_n

    def as_column(row):
        n = row.shape[1]
        eye = lax.broadcasted_iota(jnp.int32, (n, n), 0) == lax.broadcasted_iota(jnp.int32, (n, n), 1)
        return jnp.sum(jnp.where(eye, row.astype(jnp.float32), 0.0), axis=1, keepdims=True)

    cols = (me_row * width + lax.broadcasted_iota(jnp.int32, (1, width), 1)).astype(jnp.float32)
    rpos = as_column(rpos_ref[:, pl.ds(pl.multiple_of(first, recvs_n), recvs_n)])
    offset = (rpos - cols) / spread_len
    taper = 1.0 / (1.0 + offset * offset)
    rows_here = first + lax.broadcasted_iota(jnp.int32, (recvs_n, listed), 0)
    for t in range(tiles):
        hits = (lists_ref[pl.ds(t, 1), :] == rows_here).astype(jnp.float32)
        member = jnp.sum(hits, axis=1, keepdims=True)
        part = taper[:, t * tile_width:(t + 1) * tile_width]
        aperture_ref[:, t * tile_width:(t + 1) * tile_width] = (
            member * part * (2.0 / math.sqrt(listed))
        ).astype(aperture_ref.dtype)
    spos = as_column(spos_ref[...])
    soffset = (spos - cols) / spread_len
    weights_ref[...] = 1.0 / (1.0 + soffset * soffset)

    y2 = lax.rem(y + 2, NY)
    col_relay((ym * 2 + 1) * 2 + c, (to_partner,))
    col_relay((yp * 2 + 0) * 2 + c, (to_partner,))
    for hh in range(2):
        col_relay((y2 * 2 + hh) * 2 + c, (to_partner,))
    for plane in (ym, yp, y2):
        for hh in range(2):
            col_relay((plane * 2 + hh) * 2 + 1 - c, ())
    for zz in range(NZ):
        row_relay(xm * NZ + zz if zz % 2 == 1 else xp * NZ + zz, ())

    nf = spec_ref.shape[0] // 2
    surface_root = math.sqrt(roww_ref.shape[2])
    span = NZ * shots
    mult_ref[...] = jnp.zeros(mult_ref.shape, mult_ref.dtype)

    def product_part(xc):
        u = pl.ds(pl.multiple_of(xc * span, span), span)
        for f in range(nf):
            lr = roww_ref[f, :, u]
            li = roww_ref[nf + f, :, u]
            rr = colw_ref[f, u, :]
            ri = colw_ref[nf + f, u, :]
            real_real = jnp.dot(lr, rr, preferred_element_type=jnp.float32)
            imag_imag = jnp.dot(li, ri, preferred_element_type=jnp.float32)
            real_imag = jnp.dot(lr, ri, preferred_element_type=jnp.float32)
            imag_real = jnp.dot(li, rr, preferred_element_type=jnp.float32)
            mult_ref[f] += real_real - imag_imag
            mult_ref[nf + f] += real_imag + imag_real

    product_part(x)
    product_part(xm)
    product_part(xp)
    x2 = lax.rem(x + 2, NX)
    for zz in range(NZ):
        row_relay(x2 * NZ + zz, ())
    product_part(x2)
    for p in range(2 * nf):
        mult_ref[p] = -mult_ref[p] / surface_root

    def prim_body(t, carry):
        wave = inverse_ref[t, 0] * mult_ref[0]
        for p in range(1, 2 * nf):
            wave = wave + inverse_ref[t, p] * mult_ref[p]
        prim_ref[t] = (traces_ref[t].astype(jnp.float32) - wave).astype(prim_ref.dtype)
        return carry

    lax.fori_loop(0, traces_ref.shape[0], prim_body, 0)

    band = partial_ref.shape[1]

    def band_peer(i):
        hh = lax.rem(1 - h + i // 8, 2)
        yy = lax.rem(i, 8) // 2
        cc = lax.rem(i, 2)
        return (yy * 2 + hh) * 2 + cc, {"y": yy, "zh": hh, "c": cc}

    def reduce_copy(j, peer):
        return pltpu.make_async_remote_copy(
            partial_ref.at[j], slots_ref.at[me_col], send_red.at[j], recv_red.at[me_col],
            device_id=peer, device_id_type=MESH_ID,
        )

    def band_body(i, carry):
        j, peer = band_peer(i)
        rows = []
        for u in range(band):
            stacked = jnp.dot(
                prim_ref[j * band + u], aperture_ref[...], preferred_element_type=jnp.float32
            )
            rows.append(jnp.sum(stacked * weights_ref[...], axis=0, keepdims=True))
        partial_ref[j] = jnp.concatenate(rows, axis=0)
        pl.when(j != me_col)(reduce_copy(j, peer).start)
        return carry

    lax.fori_loop(0, partial_ref.shape[0], band_body, 0)

    slots_ref[me_col] = partial_ref[me_col]
    for j, peer in col_peers:
        recv = pltpu.make_async_remote_copy(
            partial_ref.at[j], slots_ref.at[j], send_red.at[j], recv_red.at[j],
            device_id=peer, device_id_type=MESH_ID,
        )
        pl.when(j != me_col)(recv.wait_recv)
    total = slots_ref[0]
    for j in range(1, len(col_peers)):
        total = total + slots_ref[j]
    stack_ref[...] = total

    for desc, cond in started:
        when(cond, desc.wait_send)
    for j, peer in col_peers:
        pl.when(j != me_col)(reduce_copy(j, peer).wait_send)


def fused_call(traces, forward, lists, rpos, spos, inverse, width, row_count, col_count):
    samples, shots, recvs = traces.shape
    planes = forward.shape[0]
    band = samples // col_count
    vmem = pl.BlockSpec(memory_space=pltpu.VMEM)
    return pl.pallas_call(
        fused_kernel,
        out_shape=(
            jax.ShapeDtypeStruct(traces.shape, jnp.bfloat16),
            jax.ShapeDtypeStruct((band, width), jnp.float32),
        ),
        in_specs=[
            vmem,
            pl.BlockSpec(memory_space=pltpu.SMEM),
            vmem,
            vmem,
            vmem,
            pl.BlockSpec(memory_space=pltpu.SMEM),
        ],
        out_specs=(vmem, vmem),
        scratch_shapes=[
            pltpu.VMEM((planes, shots, recvs), jnp.bfloat16),
            pltpu.VMEM((planes, row_count * shots, recvs), jnp.bfloat16),
            pltpu.VMEM((planes, shots, col_count * recvs), jnp.bfloat16),
            pltpu.VMEM((planes, shots, recvs), jnp.float32),
            pltpu.VMEM((col_count, band, width), jnp.float32),
            pltpu.VMEM((col_count, band, width), jnp.float32),
            pltpu.VMEM((recvs, width), jnp.bfloat16),
            pltpu.VMEM((shots, width), jnp.float32),
            pltpu.SemaphoreType.DMA((row_count, 2)),
            pltpu.SemaphoreType.DMA((col_count, 2)),
            pltpu.SemaphoreType.DMA((row_count, 2, 4)),
            pltpu.SemaphoreType.DMA((col_count, 2, 4)),
            pltpu.SemaphoreType.DMA((col_count,)),
            pltpu.SemaphoreType.DMA((col_count,)),
        ],
        compiler_params=pltpu.CompilerParams(collective_id=0, has_side_effects=True),
    )(traces, forward, lists, rpos, spos, inverse)


def per_device(traces, source_pos, receiver_pos, aperture_list, band_index, weight_tiles):
    samples, shot_count, recv_count = traces.shape
    col_count = axis_count(COL)
    row_count = axis_count(ROW)
    surface_count = recv_count * col_count
    image_panel_width = band_index.shape[0]
    depth_slab_samples = samples // col_count
    cosine, sine_table = phase_tables_np(samples)
    forward = jnp.asarray(
        (np.concatenate([cosine, -sine_table], 0) / np.float32(math.sqrt(samples)))
        .astype(ml_dtypes.bfloat16)
        .astype(np.float32)
    )

    inverse = jnp.asarray(np.concatenate([cosine, -sine_table], 0).T / np.float32(math.sqrt(NF)))
    primaries, stacked = fused_call(
        traces,
        forward,
        aperture_list,
        receiver_pos.reshape(1, -1),
        source_pos.reshape(1, -1),
        inverse,
        image_panel_width,
        row_count,
        col_count,
    )
    column_stack = (stacked / math.sqrt(shot_count)).astype(jnp.bfloat16)

    tile_kinds = weight_tiles.shape[0]
    select = band_index[None, :] == jnp.arange(tile_kinds, dtype=jnp.int32)[:, None]
    widened = jnp.where(select[:, None, :], column_stack[None], jnp.zeros((), jnp.bfloat16))
    image_out = jnp.einsum(
        "kz,kx->zx",
        weight_tiles.reshape(tile_kinds * depth_slab_samples, weight_tiles.shape[2]),
        widened.reshape(tile_kinds * depth_slab_samples, image_panel_width),
        preferred_element_type=jnp.float32,
    )
    return (primaries, image_out)


def solution(mesh):
    n_row = mesh.shape["row"]
    n_col = mesh.shape["col"]
    fine = Mesh(
        mesh.devices.reshape(4, n_row // 4, 4, n_col // 8, 2), ("x", "zl", "y", "zh", "c")
    )
    placed = (P(None, ROW, COL), P(ROW), P(), P(ROW, None), P(ROW), P())
    return jax.shard_map(
        per_device,
        mesh=fine,
        in_specs=placed,
        out_specs=(P(None, ROW, COL), P(COL, ROW)),
        check_vma=False,
    )
```

```python
import math

import jax
import ml_dtypes
import numpy as np
import jax.numpy as jnp
from jax import lax
from jax.experimental import pallas as pl
from jax.experimental.pallas import tpu as pltpu
from jax.sharding import Mesh
from jax.sharding import PartitionSpec as P

NFFT = 4096
NF = 4

ROW = ("x", "zl")
COL = ("y", "zh", "c")


def phase_tables_np(samples):
    freq_bins = (2 * np.arange(NF, dtype=np.int32) + 1) * (NFFT // (4 * NF))
    sample_ticks = np.arange(samples, dtype=np.int32)
    phase_turns = freq_bins[:, None] * sample_ticks[None, :] % NFFT
    phase_angle = phase_turns.astype(np.float32) * np.float32(2.0 * math.pi / NFFT)
    angle = phase_angle.astype(np.float64)
    return (np.cos(angle).astype(np.float32), np.sin(angle).astype(np.float32))


def phase_tables(samples):
    freq_bins = (2 * jnp.arange(NF, dtype=jnp.int32) + 1) * (NFFT // (4 * NF))
    sample_ticks = jnp.arange(samples, dtype=jnp.int32)
    phase_turns = freq_bins[:, None] * sample_ticks[None, :] % NFFT
    phase_angle = phase_turns.astype(jnp.float32) * (2.0 * math.pi / NFFT)
    return (jnp.cos(phase_angle), jnp.sin(phase_angle))


def aperture_rows(tile_index_lists, positions, columns, first_row, row_count, spread_len):
    tile_count, listed = tile_index_lists.shape
    col_width = columns.shape[0]
    rows = first_row + jnp.arange(row_count, dtype=jnp.int32)
    hits = (tile_index_lists[:, :, None] == rows[None, None, :]).astype(jnp.float32)
    member = jnp.sum(hits, axis=1)
    widened = jnp.repeat(member.T, col_width // tile_count, axis=1)
    offset = (positions[:, None] - columns[None, :]).astype(jnp.float32) / spread_len
    taper_weight = 1.0 / (1.0 + offset * offset)
    return (widened * taper_weight * (2.0 / math.sqrt(listed))).astype(jnp.bfloat16)


def shot_weights(positions, columns, spread_len):
    offset = (positions[:, None] - columns[None, :]).astype(jnp.float32) / spread_len
    return 1.0 / (1.0 + offset * offset)


def complex_product(left_section, right_section):
    real_real = jnp.einsum(
        "qju,quy->qjy", left_section[0], right_section[0], preferred_element_type=jnp.float32
    )
    imag_imag = jnp.einsum(
        "qju,quy->qjy", left_section[1], right_section[1], preferred_element_type=jnp.float32
    )
    real_imag = jnp.einsum(
        "qju,quy->qjy", left_section[0], right_section[1], preferred_element_type=jnp.float32
    )
    imag_real = jnp.einsum(
        "qju,quy->qjy", left_section[1], right_section[0], preferred_element_type=jnp.float32
    )
    return jnp.stack([real_real - imag_imag, real_imag + imag_real])


def axis_pos(names):
    index = 0
    for name in names:
        index = index * lax.axis_size(name) + lax.axis_index(name)
    return index


def axis_count(names):
    count = 1
    for name in names:
        count *= lax.axis_size(name)
    return count


MESH_ID = pl.DeviceIdType.MESH
NX, NZ, NY = 4, 8, 4


def fused_kernel(traces_ref, forward_ref, lists_ref, rpos_ref, spos_ref, inverse_ref,
                 prim_ref, stack_ref,
                 spec_ref, colw_ref, roww_ref, mult_ref, partial_ref, slots_ref, aperture_ref, weights_ref,
                 recv_row, recv_col, send_row, send_col, recv_red, send_red):
    x = lax.axis_index("x")
    z = lax.axis_index("zl")
    y = lax.axis_index("y")
    h = lax.axis_index("zh")
    c = lax.axis_index("c")
    xp = lax.rem(x + 1, NX)
    xm = lax.rem(x + NX - 1, NX)
    yp = lax.rem(y + 1, NY)
    ym = lax.rem(y + NY - 1, NY)
    me_row = x * NZ + z
    me_col = (y * 2 + h) * 2 + c

    col_peers = []
    for yy in range(NY):
        for hh in range(2):
            for cc in range(2):
                col_peers.append(((yy * 2 + hh) * 2 + cc, {"y": yy, "zh": hh, "c": cc}))

    barrier = pltpu.get_barrier_semaphore()
    for peer in ({"x": xp}, {"x": xm}):
        pl.semaphore_signal(barrier, 1, device_id=peer, device_id_type=MESH_ID)
    for j, peer in col_peers:
        pl.when(j != me_col)(
            lambda peer=peer: pl.semaphore_signal(
                barrier, 1, device_id=peer, device_id_type=MESH_ID
            )
        )

    @pl.when(z > 0)
    def _():
        pl.semaphore_signal(barrier, 1, device_id={"zl": z - 1}, device_id_type=MESH_ID)

    @pl.when(z < NZ - 1)
    def _():
        pl.semaphore_signal(barrier, 1, device_id={"zl": z + 1}, device_id_type=MESH_ID)

    samples = traces_ref.shape[0]
    group = 4
    for p0 in range(0, spec_ref.shape[0], group):
        def spectra_body(t, accs, p0=p0):
            sample = traces_ref[t].astype(jnp.float32)
            return tuple(acc + forward_ref[p0 + g, t] * sample for g, acc in enumerate(accs))

        zero = jnp.zeros(spec_ref.shape[1:], jnp.float32)
        accs = lax.fori_loop(0, samples, spectra_body, (zero,) * group)
        for g in range(group):
            spec_ref[p0 + g] = accs[g].astype(spec_ref.dtype)

    peers_in = 2 + len(col_peers) - 1
    ends = jnp.logical_or(z == 0, z == NZ - 1)
    pl.when(ends)(lambda: pl.semaphore_wait(barrier, peers_in + 1))
    pl.when(jnp.logical_not(ends))(lambda: pl.semaphore_wait(barrier, peers_in + 2))

    started = []
    shots = spec_ref.shape[1]
    recvs = spec_ref.shape[2]
    half = spec_ref.shape[0] // 2
    parts = (0, 1)

    def planes(part):
        return pl.ds(part * half, half)

    def colw_blk(b, part):
        return colw_ref.at[planes(part), pl.ds(pl.multiple_of(b * shots, shots), shots), :]

    def roww_blk(j, part):
        return roww_ref.at[planes(part), :, pl.ds(pl.multiple_of(j * recvs, recvs), recvs)]

    def row_copy(b, part, d, peer, own=False):
        src = spec_ref.at[planes(part)] if own else colw_blk(b, part)
        return pltpu.make_async_remote_copy(
            src, colw_blk(b, part), send_row.at[b, part, d], recv_row.at[b, part],
            device_id=peer, device_id_type=MESH_ID,
        )

    def col_copy(j, part, d, peer, own=False):
        whole = roww_ref.at[:, :, pl.ds(pl.multiple_of(j * recvs, recvs), recvs)]
        src = spec_ref if own else whole
        return pltpu.make_async_remote_copy(
            src, whole, send_col.at[j, part, d], recv_col.at[j, part],
            device_id=peer, device_id_type=MESH_ID,
        )

    def start(desc, cond=None):
        if cond is None:
            desc.start()
        else:
            pl.when(cond)(desc.start)
        started.append((desc, cond))

    def when(cond, fn):
        if cond is None:
            fn()
        else:
            pl.when(cond)(fn)

    def row_relay(b, sends, cond=None, only=parts):
        for part in only:
            when(cond, row_copy(b, part, 0, {"x": x}).wait_recv)
            for d, peer, extra in sends:
                c2 = cond if extra is None else (extra if cond is None else jnp.logical_and(cond, extra))
                start(row_copy(b, part, d, peer), c2)

    def col_relay(j, sends, cond=None):
        for part in (0,):
            when(cond, col_copy(j, part, 0, {"y": y}).wait_recv)
            for d, peer in sends:
                start(col_copy(j, part, d, peer), cond)

    start(col_copy(me_col, 0, 0, {"c": 1 - c}, own=True))
    for part in parts:
        start(row_copy(me_row, part, 0, {"zl": z + 1}, own=True), z < NZ - 1)
        start(row_copy(me_row, part, 1, {"zl": z - 1}, own=True), z > 0)
        start(row_copy(me_row, part, 2, {"x": xp}, own=True))
        start(row_copy(me_row, part, 3, {"x": xm}, own=True))
    start(col_copy(me_col, 0, 2, {"y": yp}, own=True))
    start(col_copy(me_col, 0, 3, {"y": ym}, own=True))
    colw_ref[:, pl.ds(pl.multiple_of(me_row * shots, shots), shots), :] = spec_ref[...]
    roww_ref[:, :, pl.ds(pl.multiple_of(me_col * recvs, recvs), recvs)] = spec_ref[...]

    j_h = (y * 2 + 1 - h) * 2 + c
    j_c = (y * 2 + h) * 2 + 1 - c
    j_hc = (y * 2 + 1 - h) * 2 + 1 - c
    y_sends = ((2, {"y": yp}), (3, {"y": ym}))
    to_partner = (0, {"c": 1 - c})
    col_relay(j_c, ())

    def x_forward(zsrc, cond):
        even = lax.rem(zsrc, 2) == 0
        row_relay(xm * NZ + zsrc, ((2, {"x": xp}, None),), jnp.logical_and(cond, even))
        odd = jnp.logical_not(even)
        row_relay(xp * NZ + zsrc, ((3, {"x": xm}, None),), jnp.logical_and(cond, odd))

    def x_forward_at(dist):
        if dist == 0:
            x_forward(z, True)
        else:
            x_forward(z - dist, z >= dist)
            x_forward(z + dist, z + dist < NZ)

    lag = 2
    x_sends = ((2, {"x": xp}, None), (3, {"x": xm}, None))
    for k in range(1, NZ):
        for part in parts:
            row_relay(x * NZ + z - k, x_sends + ((0, {"zl": z + 1}, z < NZ - 1),), z >= k, (part,))
            row_relay(x * NZ + z + k, x_sends + ((1, {"zl": z - 1}, z > 0),), z + k < NZ, (part,))
        if k - lag >= 0:
            x_forward_at(k - lag)
        if k == 2:
            start(col_copy(me_col, 0, 1, {"zh": 1 - h}, own=True))
        if k == 4:
            col_relay(j_h, ((0, {"c": 1 - c}),) + y_sends)
        if k == 5:
            col_relay(j_hc, ())
        if k == 6:
            col_relay((ym * 2 + 0) * 2 + c, ((2, {"y": yp}), to_partner))
            col_relay((yp * 2 + 1) * 2 + c, ((3, {"y": ym}), to_partner))
    for dist in range(NZ - lag, NZ):
        x_forward_at(dist)

    recvs_n = aperture_ref.shape[0]
    width = aperture_ref.shape[1]
    tiles, listed = lists_ref.shape
    tile_width = width // tiles
    spread_len = width * NX * NZ // 4
    first = me_col * recvs_n

    def as_column(row):
        n = row.shape[1]
        eye = lax.broadcasted_iota(jnp.int32, (n, n), 0) == lax.broadcasted_iota(jnp.int32, (n, n), 1)
        return jnp.sum(jnp.where(eye, row.astype(jnp.float32), 0.0), axis=1, keepdims=True)

    cols = (me_row * width + lax.broadcasted_iota(jnp.int32, (1, width), 1)).astype(jnp.float32)
    rpos = as_column(rpos_ref[:, pl.ds(pl.multiple_of(first, recvs_n), recvs_n)])
    offset = (rpos - cols) / spread_len
    taper = 1.0 / (1.0 + offset * offset)
    rows_here = first + lax.broadcasted_iota(jnp.int32, (recvs_n, listed), 0)
    for t in range(tiles):
        hits = (lists_ref[pl.ds(t, 1), :] == rows_here).astype(jnp.float32)
        member = jnp.sum(hits, axis=1, keepdims=True)
        part = taper[:, t * tile_width:(t + 1) * tile_width]
        aperture_ref[:, t * tile_width:(t + 1) * tile_width] = (
            member * part * (2.0 / math.sqrt(listed))
        ).astype(aperture_ref.dtype)
    spos = as_column(spos_ref[...])
    soffset = (spos - cols) / spread_len
    weights_ref[...] = 1.0 / (1.0 + soffset * soffset)

    y2 = lax.rem(y + 2, NY)
    col_relay((ym * 2 + 1) * 2 + c, (to_partner,))
    col_relay((yp * 2 + 0) * 2 + c, (to_partner,))
    for hh in range(2):
        col_relay((y2 * 2 + hh) * 2 + c, (to_partner,))
    for plane in (ym, yp, y2):
        for hh in range(2):
            col_relay((plane * 2 + hh) * 2 + 1 - c, ())
    for zz in range(NZ):
        row_relay(xm * NZ + zz if zz % 2 == 1 else xp * NZ + zz, ())

    nf = spec_ref.shape[0] // 2
    surface_root = math.sqrt(roww_ref.shape[2])
    span = NZ * shots
    mult_ref[...] = jnp.zeros(mult_ref.shape, mult_ref.dtype)

    def product_part(xc):
        u = pl.ds(pl.multiple_of(xc * span, span), span)
        for f in range(nf):
            lr = roww_ref[f, :, u]
            li = roww_ref[nf + f, :, u]
            rr = colw_ref[f, u, :]
            ri = colw_ref[nf + f, u, :]
            real_real = jnp.dot(lr, rr, preferred_element_type=jnp.float32)
            imag_imag = jnp.dot(li, ri, preferred_element_type=jnp.float32)
            real_imag = jnp.dot(lr, ri, preferred_element_type=jnp.float32)
            imag_real = jnp.dot(li, rr, preferred_element_type=jnp.float32)
            mult_ref[f] += real_real - imag_imag
            mult_ref[nf + f] += real_imag + imag_real

    product_part(x)
    product_part(xm)
    product_part(xp)
    x2 = lax.rem(x + 2, NX)
    for zz in range(NZ):
        row_relay(x2 * NZ + zz, ())
    product_part(x2)
    for p in range(2 * nf):
        mult_ref[p] = -mult_ref[p] / surface_root

    def prim_body(t, carry):
        wave = inverse_ref[t, 0] * mult_ref[0]
        for p in range(1, 2 * nf):
            wave = wave + inverse_ref[t, p] * mult_ref[p]
        prim_ref[t] = (traces_ref[t].astype(jnp.float32) - wave).astype(prim_ref.dtype)
        return carry

    lax.fori_loop(0, traces_ref.shape[0], prim_body, 0)

    band = partial_ref.shape[1]

    def band_peer(i):
        hh = lax.rem(1 - h + i // 8, 2)
        yy = lax.rem(i, 8) // 2
        cc = lax.rem(i, 2)
        return (yy * 2 + hh) * 2 + cc, {"y": yy, "zh": hh, "c": cc}

    def reduce_copy(j, peer):
        return pltpu.make_async_remote_copy(
            partial_ref.at[j], slots_ref.at[me_col], send_red.at[j], recv_red.at[me_col],
            device_id=peer, device_id_type=MESH_ID,
        )

    def band_body(i, carry):
        j, peer = band_peer(i)
        rows = []
        for u in range(band):
            stacked = jnp.dot(
                prim_ref[j * band + u], aperture_ref[...], preferred_element_type=jnp.float32
            )
            rows.append(jnp.sum(stacked * weights_ref[...], axis=0, keepdims=True))
        partial_ref[j] = jnp.concatenate(rows, axis=0)
        pl.when(j != me_col)(reduce_copy(j, peer).start)
        return carry

    lax.fori_loop(0, partial_ref.shape[0], band_body, 0)

    slots_ref[me_col] = partial_ref[me_col]
    for j, peer in col_peers:
        recv = pltpu.make_async_remote_copy(
            partial_ref.at[j], slots_ref.at[j], send_red.at[j], recv_red.at[j],
            device_id=peer, device_id_type=MESH_ID,
        )
        pl.when(j != me_col)(recv.wait_recv)
    total = slots_ref[0]
    for j in range(1, len(col_peers)):
        total = total + slots_ref[j]
    stack_ref[...] = total

    for desc, cond in started:
        when(cond, desc.wait_send)
    for j, peer in col_peers:
        pl.when(j != me_col)(reduce_copy(j, peer).wait_send)


def fused_call(traces, forward, lists, rpos, spos, inverse, width, row_count, col_count):
    samples, shots, recvs = traces.shape
    planes = forward.shape[0]
    band = samples // col_count
    vmem = pl.BlockSpec(memory_space=pltpu.VMEM)
    return pl.pallas_call(
        fused_kernel,
        out_shape=(
            jax.ShapeDtypeStruct(traces.shape, jnp.bfloat16),
            jax.ShapeDtypeStruct((band, width), jnp.float32),
        ),
        in_specs=[
            vmem,
            pl.BlockSpec(memory_space=pltpu.SMEM),
            vmem,
            vmem,
            vmem,
            pl.BlockSpec(memory_space=pltpu.SMEM),
        ],
        out_specs=(vmem, vmem),
        scratch_shapes=[
            pltpu.VMEM((planes, shots, recvs), jnp.bfloat16),
            pltpu.VMEM((planes, row_count * shots, recvs), jnp.bfloat16),
            pltpu.VMEM((planes, shots, col_count * recvs), jnp.bfloat16),
            pltpu.VMEM((planes, shots, recvs), jnp.float32),
            pltpu.VMEM((col_count, band, width), jnp.float32),
            pltpu.VMEM((col_count, band, width), jnp.float32),
            pltpu.VMEM((recvs, width), jnp.bfloat16),
            pltpu.VMEM((shots, width), jnp.float32),
            pltpu.SemaphoreType.DMA((row_count, 2)),
            pltpu.SemaphoreType.DMA((col_count, 2)),
            pltpu.SemaphoreType.DMA((row_count, 2, 4)),
            pltpu.SemaphoreType.DMA((col_count, 2, 4)),
            pltpu.SemaphoreType.DMA((col_count,)),
            pltpu.SemaphoreType.DMA((col_count,)),
        ],
        compiler_params=pltpu.CompilerParams(collective_id=0, has_side_effects=True),
    )(traces, forward, lists, rpos, spos, inverse)


def per_device(traces, source_pos, receiver_pos, aperture_list, band_index, weight_tiles):
    samples, shot_count, recv_count = traces.shape
    col_count = axis_count(COL)
    row_count = axis_count(ROW)
    surface_count = recv_count * col_count
    image_panel_width = band_index.shape[0]
    depth_slab_samples = samples // col_count
    cosine, sine_table = phase_tables_np(samples)
    forward = jnp.asarray(
        (np.concatenate([cosine, -sine_table], 0) / np.float32(math.sqrt(samples)))
        .astype(ml_dtypes.bfloat16)
        .astype(np.float32)
    )

    inverse = jnp.asarray(np.concatenate([cosine, -sine_table], 0).T / np.float32(math.sqrt(NF)))
    primaries, stacked = fused_call(
        traces,
        forward,
        aperture_list,
        receiver_pos.reshape(1, -1),
        source_pos.reshape(1, -1),
        inverse,
        image_panel_width,
        row_count,
        col_count,
    )
    column_stack = (stacked / math.sqrt(shot_count)).astype(jnp.bfloat16)

    tile_kinds = weight_tiles.shape[0]
    select = band_index[None, :] == jnp.arange(tile_kinds, dtype=jnp.int32)[:, None]
    widened = jnp.where(select[:, None, :], column_stack[None], jnp.zeros((), jnp.bfloat16))
    image_out = jnp.einsum(
        "kz,kx->zx",
        weight_tiles.reshape(tile_kinds * depth_slab_samples, weight_tiles.shape[2]),
        widened.reshape(tile_kinds * depth_slab_samples, image_panel_width),
        preferred_element_type=jnp.float32,
    )
    return (primaries, image_out)


def solution(mesh):
    n_row = mesh.shape["row"]
    n_col = mesh.shape["col"]
    fine = Mesh(
        mesh.devices.reshape(4, n_row // 4, 4, n_col // 8, 2), ("x", "zl", "y", "zh", "c")
    )
    placed = (P(None, ROW, COL), P(ROW), P(), P(ROW, None), P(ROW), P())
    return jax.shard_map(
        per_device,
        mesh=fine,
        in_specs=placed,
        out_specs=(P(None, ROW, COL), P(COL, ROW)),
        check_vma=False,
    )
```

```python
import math

import jax
import ml_dtypes
import numpy as np
import jax.numpy as jnp
from jax import lax
from jax.experimental import pallas as pl
from jax.experimental.pallas import tpu as pltpu
from jax.sharding import Mesh
from jax.sharding import PartitionSpec as P

NFFT = 4096
NF = 4

ROW = ("x", "zl")
COL = ("y", "zh", "c")


def phase_tables_np(samples):
    freq_bins = (2 * np.arange(NF, dtype=np.int32) + 1) * (NFFT // (4 * NF))
    sample_ticks = np.arange(samples, dtype=np.int32)
    phase_turns = freq_bins[:, None] * sample_ticks[None, :] % NFFT
    phase_angle = phase_turns.astype(np.float32) * np.float32(2.0 * math.pi / NFFT)
    angle = phase_angle.astype(np.float64)
    return (np.cos(angle).astype(np.float32), np.sin(angle).astype(np.float32))


def phase_tables(samples):
    freq_bins = (2 * jnp.arange(NF, dtype=jnp.int32) + 1) * (NFFT // (4 * NF))
    sample_ticks = jnp.arange(samples, dtype=jnp.int32)
    phase_turns = freq_bins[:, None] * sample_ticks[None, :] % NFFT
    phase_angle = phase_turns.astype(jnp.float32) * (2.0 * math.pi / NFFT)
    return (jnp.cos(phase_angle), jnp.sin(phase_angle))


def aperture_rows(tile_index_lists, positions, columns, first_row, row_count, spread_len):
    tile_count, listed = tile_index_lists.shape
    col_width = columns.shape[0]
    rows = first_row + jnp.arange(row_count, dtype=jnp.int32)
    hits = (tile_index_lists[:, :, None] == rows[None, None, :]).astype(jnp.float32)
    member = jnp.sum(hits, axis=1)
    widened = jnp.repeat(member.T, col_width // tile_count, axis=1)
    offset = (positions[:, None] - columns[None, :]).astype(jnp.float32) / spread_len
    taper_weight = 1.0 / (1.0 + offset * offset)
    return (widened * taper_weight * (2.0 / math.sqrt(listed))).astype(jnp.bfloat16)


def shot_weights(positions, columns, spread_len):
    offset = (positions[:, None] - columns[None, :]).astype(jnp.float32) / spread_len
    return 1.0 / (1.0 + offset * offset)


def complex_product(left_section, right_section):
    real_real = jnp.einsum(
        "qju,quy->qjy", left_section[0], right_section[0], preferred_element_type=jnp.float32
    )
    imag_imag = jnp.einsum(
        "qju,quy->qjy", left_section[1], right_section[1], preferred_element_type=jnp.float32
    )
    real_imag = jnp.einsum(
        "qju,quy->qjy", left_section[0], right_section[1], preferred_element_type=jnp.float32
    )
    imag_real = jnp.einsum(
        "qju,quy->qjy", left_section[1], right_section[0], preferred_element_type=jnp.float32
    )
    return jnp.stack([real_real - imag_imag, real_imag + imag_real])


def axis_pos(names):
    index = 0
    for name in names:
        index = index * lax.axis_size(name) + lax.axis_index(name)
    return index


def axis_count(names):
    count = 1
    for name in names:
        count *= lax.axis_size(name)
    return count


MESH_ID = pl.DeviceIdType.MESH
NX, NZ, NY = 4, 8, 4


def fused_kernel(traces_ref, forward_ref, lists_ref, rpos_ref, spos_ref, inverse_ref,
                 prim_ref, stack_ref,
                 spec_ref, colw_ref, roww_ref, mult_ref, partial_ref, slots_ref, aperture_ref, weights_ref,
                 recv_row, recv_col, send_row, send_col, recv_red, send_red):
    x = lax.axis_index("x")
    z = lax.axis_index("zl")
    y = lax.axis_index("y")
    h = lax.axis_index("zh")
    c = lax.axis_index("c")
    xp = lax.rem(x + 1, NX)
    xm = lax.rem(x + NX - 1, NX)
    yp = lax.rem(y + 1, NY)
    ym = lax.rem(y + NY - 1, NY)
    me_row = x * NZ + z
    me_col = (y * 2 + h) * 2 + c

    col_peers = []
    for yy in range(NY):
        for hh in range(2):
            for cc in range(2):
                col_peers.append(((yy * 2 + hh) * 2 + cc, {"y": yy, "zh": hh, "c": cc}))

    barrier = pltpu.get_barrier_semaphore()
    for peer in ({"x": xp}, {"x": xm}):
        pl.semaphore_signal(barrier, 1, device_id=peer, device_id_type=MESH_ID)
    for j, peer in col_peers:
        pl.when(j != me_col)(
            lambda peer=peer: pl.semaphore_signal(
                barrier, 1, device_id=peer, device_id_type=MESH_ID
            )
        )

    @pl.when(z > 0)
    def _():
        pl.semaphore_signal(barrier, 1, device_id={"zl": z - 1}, device_id_type=MESH_ID)

    @pl.when(z < NZ - 1)
    def _():
        pl.semaphore_signal(barrier, 1, device_id={"zl": z + 1}, device_id_type=MESH_ID)

    samples = traces_ref.shape[0]
    group = 4
    for p0 in range(0, spec_ref.shape[0], group):
        def spectra_body(t, accs, p0=p0):
            sample = traces_ref[t].astype(jnp.float32)
            return tuple(acc + forward_ref[p0 + g, t] * sample for g, acc in enumerate(accs))

        zero = jnp.zeros(spec_ref.shape[1:], jnp.float32)
        accs = lax.fori_loop(0, samples, spectra_body, (zero,) * group)
        for g in range(group):
            spec_ref[p0 + g] = accs[g].astype(spec_ref.dtype)

    peers_in = 2 + len(col_peers) - 1
    ends = jnp.logical_or(z == 0, z == NZ - 1)
    pl.when(ends)(lambda: pl.semaphore_wait(barrier, peers_in + 1))
    pl.when(jnp.logical_not(ends))(lambda: pl.semaphore_wait(barrier, peers_in + 2))

    started = []
    shots = spec_ref.shape[1]
    recvs = spec_ref.shape[2]
    half = spec_ref.shape[0] // 2
    parts = (0, 1)

    def planes(part):
        return pl.ds(part * half, half)

    def colw_blk(b, part):
        return colw_ref.at[planes(part), pl.ds(pl.multiple_of(b * shots, shots), shots), :]

    def roww_blk(j, part):
        return roww_ref.at[planes(part), :, pl.ds(pl.multiple_of(j * recvs, recvs), recvs)]

    def row_copy(b, part, d, peer, own=False):
        src = spec_ref.at[planes(part)] if own else colw_blk(b, part)
        return pltpu.make_async_remote_copy(
            src, colw_blk(b, part), send_row.at[b, part, d], recv_row.at[b, part],
            device_id=peer, device_id_type=MESH_ID,
        )

    def col_copy(j, part, d, peer, own=False):
        whole = roww_ref.at[:, :, pl.ds(pl.multiple_of(j * recvs, recvs), recvs)]
        src = spec_ref if own else whole
        return pltpu.make_async_remote_copy(
            src, whole, send_col.at[j, part, d], recv_col.at[j, part],
            device_id=peer, device_id_type=MESH_ID,
        )

    def start(desc, cond=None):
        if cond is None:
            desc.start()
        else:
            pl.when(cond)(desc.start)
        started.append((desc, cond))

    def when(cond, fn):
        if cond is None:
            fn()
        else:
            pl.when(cond)(fn)

    def row_relay(b, sends, cond=None, only=parts):
        for part in only:
            when(cond, row_copy(b, part, 0, {"x": x}).wait_recv)
            for d, peer, extra in sends:
                c2 = cond if extra is None else (extra if cond is None else jnp.logical_and(cond, extra))
                start(row_copy(b, part, d, peer), c2)

    def col_relay(j, sends, cond=None):
        for part in (0,):
            when(cond, col_copy(j, part, 0, {"y": y}).wait_recv)
            for d, peer in sends:
                start(col_copy(j, part, d, peer), cond)

    start(col_copy(me_col, 0, 0, {"c": 1 - c}, own=True))
    for part in parts:
        start(row_copy(me_row, part, 0, {"zl": z + 1}, own=True), z < NZ - 1)
        start(row_copy(me_row, part, 1, {"zl": z - 1}, own=True), z > 0)
        start(row_copy(me_row, part, 2, {"x": xp}, own=True))
        start(row_copy(me_row, part, 3, {"x": xm}, own=True))
    start(col_copy(me_col, 0, 2, {"y": yp}, own=True))
    start(col_copy(me_col, 0, 3, {"y": ym}, own=True))
    colw_ref[:, pl.ds(pl.multiple_of(me_row * shots, shots), shots), :] = spec_ref[...]
    roww_ref[:, :, pl.ds(pl.multiple_of(me_col * recvs, recvs), recvs)] = spec_ref[...]

    j_h = (y * 2 + 1 - h) * 2 + c
    j_c = (y * 2 + h) * 2 + 1 - c
    j_hc = (y * 2 + 1 - h) * 2 + 1 - c
    y_sends = ((2, {"y": yp}), (3, {"y": ym}))
    to_partner = (0, {"c": 1 - c})
    col_relay(j_c, ())

    def x_forward(zsrc, cond):
        even = lax.rem(zsrc, 2) == 0
        row_relay(xm * NZ + zsrc, ((2, {"x": xp}, None),), jnp.logical_and(cond, even))
        odd = jnp.logical_not(even)
        row_relay(xp * NZ + zsrc, ((3, {"x": xm}, None),), jnp.logical_and(cond, odd))

    def x_forward_at(dist):
        if dist == 0:
            x_forward(z, True)
        else:
            x_forward(z - dist, z >= dist)
            x_forward(z + dist, z + dist < NZ)

    lag = 2
    x_sends = ((2, {"x": xp}, None), (3, {"x": xm}, None))
    for k in range(1, NZ):
        for part in parts:
            row_relay(x * NZ + z - k, x_sends + ((0, {"zl": z + 1}, z < NZ - 1),), z >= k, (part,))
            row_relay(x * NZ + z + k, x_sends + ((1, {"zl": z - 1}, z > 0),), z + k < NZ, (part,))
        if k - lag >= 0:
            x_forward_at(k - lag)
        if k == 2:
            start(col_copy(me_col, 0, 1, {"zh": 1 - h}, own=True))
        if k == 4:
            col_relay(j_h, ((0, {"c": 1 - c}),) + y_sends)
        if k == 5:
            col_relay(j_hc, ())
        if k == 6:
            col_relay((ym * 2 + 0) * 2 + c, ((2, {"y": yp}), to_partner))
            col_relay((yp * 2 + 1) * 2 + c, ((3, {"y": ym}), to_partner))
    for dist in range(NZ - lag, NZ):
        x_forward_at(dist)

    recvs_n = aperture_ref.shape[0]
    width = aperture_ref.shape[1]
    tiles, listed = lists_ref.shape
    tile_width = width // tiles
    spread_len = width * NX * NZ // 4
    first = me_col * recvs_n

    def as_column(row):
        n = row.shape[1]
        eye = lax.broadcasted_iota(jnp.int32, (n, n), 0) == lax.broadcasted_iota(jnp.int32, (n, n), 1)
        return jnp.sum(jnp.where(eye, row.astype(jnp.float32), 0.0), axis=1, keepdims=True)

    cols = (me_row * width + lax.broadcasted_iota(jnp.int32, (1, width), 1)).astype(jnp.float32)
    rpos = as_column(rpos_ref[:, pl.ds(pl.multiple_of(first, recvs_n), recvs_n)])
    offset = (rpos - cols) / spread_len
    taper = 1.0 / (1.0 + offset * offset)
    rows_here = first + lax.broadcasted_iota(jnp.int32, (recvs_n, listed), 0)
    for t in range(tiles):
        hits = (lists_ref[pl.ds(t, 1), :] == rows_here).astype(jnp.float32)
        member = jnp.sum(hits, axis=1, keepdims=True)
        part = taper[:, t * tile_width:(t + 1) * tile_width]
        aperture_ref[:, t * tile_width:(t + 1) * tile_width] = (
            member * part * (2.0 / math.sqrt(listed))
        ).astype(aperture_ref.dtype)
    spos = as_column(spos_ref[...])
    soffset = (spos - cols) / spread_len
    weights_ref[...] = 1.0 / (1.0 + soffset * soffset)

    y2 = lax.rem(y + 2, NY)
    col_relay((ym * 2 + 1) * 2 + c, (to_partner,))
    col_relay((yp * 2 + 0) * 2 + c, (to_partner,))
    for hh in range(2):
        col_relay((y2 * 2 + hh) * 2 + c, (to_partner,))
    for plane in (ym, yp, y2):
        for hh in range(2):
            col_relay((plane * 2 + hh) * 2 + 1 - c, ())
    for zz in range(NZ):
        row_relay(xm * NZ + zz if zz % 2 == 1 else xp * NZ + zz, ())

    nf = spec_ref.shape[0] // 2
    surface_root = math.sqrt(roww_ref.shape[2])
    span = NZ * shots
    mult_ref[...] = jnp.zeros(mult_ref.shape, mult_ref.dtype)

    def product_part(xc):
        u = pl.ds(pl.multiple_of(xc * span, span), span)
        for f in range(nf):
            lr = roww_ref[f, :, u]
            li = roww_ref[nf + f, :, u]
            rr = colw_ref[f, u, :]
            ri = colw_ref[nf + f, u, :]
            real_real = jnp.dot(lr, rr, preferred_element_type=jnp.float32)
            imag_imag = jnp.dot(li, ri, preferred_element_type=jnp.float32)
            real_imag = jnp.dot(lr, ri, preferred_element_type=jnp.float32)
            imag_real = jnp.dot(li, rr, preferred_element_type=jnp.float32)
            mult_ref[f] += real_real - imag_imag
            mult_ref[nf + f] += real_imag + imag_real

    product_part(x)
    product_part(xm)
    product_part(xp)
    x2 = lax.rem(x + 2, NX)
    for zz in range(NZ):
        row_relay(x2 * NZ + zz, ())
    product_part(x2)
    for p in range(2 * nf):
        mult_ref[p] = -mult_ref[p] / surface_root

    def prim_body(t, carry):
        wave = inverse_ref[t, 0] * mult_ref[0]
        for p in range(1, 2 * nf):
            wave = wave + inverse_ref[t, p] * mult_ref[p]
        prim_ref[t] = (traces_ref[t].astype(jnp.float32) - wave).astype(prim_ref.dtype)
        return carry

    lax.fori_loop(0, traces_ref.shape[0], prim_body, 0, unroll=True)

    band = partial_ref.shape[1]

    def band_peer(i):
        hh = lax.rem(1 - h + i // 8, 2)
        yy = lax.rem(i, 8) // 2
        cc = lax.rem(i, 2)
        return (yy * 2 + hh) * 2 + cc, {"y": yy, "zh": hh, "c": cc}

    def reduce_copy(j, peer):
        return pltpu.make_async_remote_copy(
            partial_ref.at[j], slots_ref.at[me_col], send_red.at[j], recv_red.at[me_col],
            device_id=peer, device_id_type=MESH_ID,
        )

    def band_body(i, carry):
        j, peer = band_peer(i)
        rows = []
        for u in range(band):
            stacked = jnp.dot(
                prim_ref[j * band + u], aperture_ref[...], preferred_element_type=jnp.float32
            )
            rows.append(jnp.sum(stacked * weights_ref[...], axis=0, keepdims=True))
        partial_ref[j] = jnp.concatenate(rows, axis=0)
        pl.when(j != me_col)(reduce_copy(j, peer).start)
        return carry

    lax.fori_loop(0, partial_ref.shape[0], band_body, 0, unroll=True)

    slots_ref[me_col] = partial_ref[me_col]
    for j, peer in col_peers:
        recv = pltpu.make_async_remote_copy(
            partial_ref.at[j], slots_ref.at[j], send_red.at[j], recv_red.at[j],
            device_id=peer, device_id_type=MESH_ID,
        )
        pl.when(j != me_col)(recv.wait_recv)
    total = slots_ref[0]
    for j in range(1, len(col_peers)):
        total = total + slots_ref[j]
    stack_ref[...] = total

    for desc, cond in started:
        when(cond, desc.wait_send)
    for j, peer in col_peers:
        pl.when(j != me_col)(reduce_copy(j, peer).wait_send)


def fused_call(traces, forward, lists, rpos, spos, inverse, width, row_count, col_count):
    samples, shots, recvs = traces.shape
    planes = forward.shape[0]
    band = samples // col_count
    vmem = pl.BlockSpec(memory_space=pltpu.VMEM)
    return pl.pallas_call(
        fused_kernel,
        out_shape=(
            jax.ShapeDtypeStruct(traces.shape, jnp.bfloat16),
            jax.ShapeDtypeStruct((band, width), jnp.float32),
        ),
        in_specs=[
            vmem,
            pl.BlockSpec(memory_space=pltpu.SMEM),
            vmem,
            vmem,
            vmem,
            pl.BlockSpec(memory_space=pltpu.SMEM),
        ],
        out_specs=(vmem, vmem),
        scratch_shapes=[
            pltpu.VMEM((planes, shots, recvs), jnp.bfloat16),
            pltpu.VMEM((planes, row_count * shots, recvs), jnp.bfloat16),
            pltpu.VMEM((planes, shots, col_count * recvs), jnp.bfloat16),
            pltpu.VMEM((planes, shots, recvs), jnp.float32),
            pltpu.VMEM((col_count, band, width), jnp.float32),
            pltpu.VMEM((col_count, band, width), jnp.float32),
            pltpu.VMEM((recvs, width), jnp.bfloat16),
            pltpu.VMEM((shots, width), jnp.float32),
            pltpu.SemaphoreType.DMA((row_count, 2)),
            pltpu.SemaphoreType.DMA((col_count, 2)),
            pltpu.SemaphoreType.DMA((row_count, 2, 4)),
            pltpu.SemaphoreType.DMA((col_count, 2, 4)),
            pltpu.SemaphoreType.DMA((col_count,)),
            pltpu.SemaphoreType.DMA((col_count,)),
        ],
        compiler_params=pltpu.CompilerParams(collective_id=0, has_side_effects=True),
    )(traces, forward, lists, rpos, spos, inverse)


def per_device(traces, source_pos, receiver_pos, aperture_list, band_index, weight_tiles):
    samples, shot_count, recv_count = traces.shape
    col_count = axis_count(COL)
    row_count = axis_count(ROW)
    surface_count = recv_count * col_count
    image_panel_width = band_index.shape[0]
    depth_slab_samples = samples // col_count
    cosine, sine_table = phase_tables_np(samples)
    forward = jnp.asarray(
        (np.concatenate([cosine, -sine_table], 0) / np.float32(math.sqrt(samples)))
        .astype(ml_dtypes.bfloat16)
        .astype(np.float32)
    )

    inverse = jnp.asarray(np.concatenate([cosine, -sine_table], 0).T / np.float32(math.sqrt(NF)))
    primaries, stacked = fused_call(
        traces,
        forward,
        aperture_list,
        receiver_pos.reshape(1, -1),
        source_pos.reshape(1, -1),
        inverse,
        image_panel_width,
        row_count,
        col_count,
    )
    column_stack = (stacked / math.sqrt(shot_count)).astype(jnp.bfloat16)

    tile_kinds = weight_tiles.shape[0]
    select = band_index[None, :] == jnp.arange(tile_kinds, dtype=jnp.int32)[:, None]
    widened = jnp.where(select[:, None, :], column_stack[None], jnp.zeros((), jnp.bfloat16))
    image_out = jnp.einsum(
        "kz,kx->zx",
        weight_tiles.reshape(tile_kinds * depth_slab_samples, weight_tiles.shape[2]),
        widened.reshape(tile_kinds * depth_slab_samples, image_panel_width),
        preferred_element_type=jnp.float32,
    )
    return (primaries, image_out)


def solution(mesh):
    n_row = mesh.shape["row"]
    n_col = mesh.shape["col"]
    fine = Mesh(
        mesh.devices.reshape(4, n_row // 4, 4, n_col // 8, 2), ("x", "zl", "y", "zh", "c")
    )
    placed = (P(None, ROW, COL), P(ROW), P(), P(ROW, None), P(ROW), P())
    return jax.shard_map(
        per_device,
        mesh=fine,
        in_specs=placed,
        out_specs=(P(None, ROW, COL), P(COL, ROW)),
        check_vma=False,
    )
```

```python
import math

import jax
import ml_dtypes
import numpy as np
import jax.numpy as jnp
from jax import lax
from jax.experimental import pallas as pl
from jax.experimental.pallas import tpu as pltpu
from jax.sharding import Mesh
from jax.sharding import PartitionSpec as P

NFFT = 4096
NF = 4

ROW = ("x", "zl")
COL = ("y", "zh", "c")


def phase_tables_np(samples):
    freq_bins = (2 * np.arange(NF, dtype=np.int32) + 1) * (NFFT // (4 * NF))
    sample_ticks = np.arange(samples, dtype=np.int32)
    phase_turns = freq_bins[:, None] * sample_ticks[None, :] % NFFT
    phase_angle = phase_turns.astype(np.float32) * np.float32(2.0 * math.pi / NFFT)
    angle = phase_angle.astype(np.float64)
    return (np.cos(angle).astype(np.float32), np.sin(angle).astype(np.float32))


def phase_tables(samples):
    freq_bins = (2 * jnp.arange(NF, dtype=jnp.int32) + 1) * (NFFT // (4 * NF))
    sample_ticks = jnp.arange(samples, dtype=jnp.int32)
    phase_turns = freq_bins[:, None] * sample_ticks[None, :] % NFFT
    phase_angle = phase_turns.astype(jnp.float32) * (2.0 * math.pi / NFFT)
    return (jnp.cos(phase_angle), jnp.sin(phase_angle))


def aperture_rows(tile_index_lists, positions, columns, first_row, row_count, spread_len):
    tile_count, listed = tile_index_lists.shape
    col_width = columns.shape[0]
    rows = first_row + jnp.arange(row_count, dtype=jnp.int32)
    hits = (tile_index_lists[:, :, None] == rows[None, None, :]).astype(jnp.float32)
    member = jnp.sum(hits, axis=1)
    widened = jnp.repeat(member.T, col_width // tile_count, axis=1)
    offset = (positions[:, None] - columns[None, :]).astype(jnp.float32) / spread_len
    taper_weight = 1.0 / (1.0 + offset * offset)
    return (widened * taper_weight * (2.0 / math.sqrt(listed))).astype(jnp.bfloat16)


def shot_weights(positions, columns, spread_len):
    offset = (positions[:, None] - columns[None, :]).astype(jnp.float32) / spread_len
    return 1.0 / (1.0 + offset * offset)


def complex_product(left_section, right_section):
    real_real = jnp.einsum(
        "qju,quy->qjy", left_section[0], right_section[0], preferred_element_type=jnp.float32
    )
    imag_imag = jnp.einsum(
        "qju,quy->qjy", left_section[1], right_section[1], preferred_element_type=jnp.float32
    )
    real_imag = jnp.einsum(
        "qju,quy->qjy", left_section[0], right_section[1], preferred_element_type=jnp.float32
    )
    imag_real = jnp.einsum(
        "qju,quy->qjy", left_section[1], right_section[0], preferred_element_type=jnp.float32
    )
    return jnp.stack([real_real - imag_imag, real_imag + imag_real])


def axis_pos(names):
    index = 0
    for name in names:
        index = index * lax.axis_size(name) + lax.axis_index(name)
    return index


def axis_count(names):
    count = 1
    for name in names:
        count *= lax.axis_size(name)
    return count


MESH_ID = pl.DeviceIdType.MESH
NX, NZ, NY = 4, 8, 4


def fused_kernel(traces_ref, forward_ref, lists_ref, rpos_ref, spos_ref, inverse_ref,
                 prim_ref, stack_ref,
                 spec_ref, colw_ref, roww_ref, mult_ref, partial_ref, slots_ref, aperture_ref, weights_ref,
                 recv_row, recv_col, send_row, send_col, recv_red, send_red):
    x = lax.axis_index("x")
    z = lax.axis_index("zl")
    y = lax.axis_index("y")
    h = lax.axis_index("zh")
    c = lax.axis_index("c")
    xp = lax.rem(x + 1, NX)
    xm = lax.rem(x + NX - 1, NX)
    yp = lax.rem(y + 1, NY)
    ym = lax.rem(y + NY - 1, NY)
    me_row = x * NZ + z
    me_col = (y * 2 + h) * 2 + c

    col_peers = []
    for yy in range(NY):
        for hh in range(2):
            for cc in range(2):
                col_peers.append(((yy * 2 + hh) * 2 + cc, {"y": yy, "zh": hh, "c": cc}))

    barrier = pltpu.get_barrier_semaphore()
    for peer in ({"x": xp}, {"x": xm}):
        pl.semaphore_signal(barrier, 1, device_id=peer, device_id_type=MESH_ID)
    for j, peer in col_peers:
        pl.when(j != me_col)(
            lambda peer=peer: pl.semaphore_signal(
                barrier, 1, device_id=peer, device_id_type=MESH_ID
            )
        )

    @pl.when(z > 0)
    def _():
        pl.semaphore_signal(barrier, 1, device_id={"zl": z - 1}, device_id_type=MESH_ID)

    @pl.when(z < NZ - 1)
    def _():
        pl.semaphore_signal(barrier, 1, device_id={"zl": z + 1}, device_id_type=MESH_ID)

    samples = traces_ref.shape[0]
    group = 4
    for p0 in range(0, spec_ref.shape[0], group):
        def spectra_body(t, accs, p0=p0):
            sample = traces_ref[t].astype(jnp.float32)
            return tuple(acc + forward_ref[p0 + g, t] * sample for g, acc in enumerate(accs))

        zero = jnp.zeros(spec_ref.shape[1:], jnp.float32)
        accs = lax.fori_loop(0, samples, spectra_body, (zero,) * group)
        for g in range(group):
            spec_ref[p0 + g] = accs[g].astype(spec_ref.dtype)

    peers_in = 2 + len(col_peers) - 1
    ends = jnp.logical_or(z == 0, z == NZ - 1)
    pl.when(ends)(lambda: pl.semaphore_wait(barrier, peers_in + 1))
    pl.when(jnp.logical_not(ends))(lambda: pl.semaphore_wait(barrier, peers_in + 2))

    started = []
    shots = spec_ref.shape[1]
    recvs = spec_ref.shape[2]
    half = spec_ref.shape[0] // 2
    parts = (0, 1)

    def planes(part):
        return pl.ds(part * half, half)

    def colw_blk(b, part):
        return colw_ref.at[planes(part), pl.ds(pl.multiple_of(b * shots, shots), shots), :]

    def roww_blk(j, part):
        return roww_ref.at[planes(part), :, pl.ds(pl.multiple_of(j * recvs, recvs), recvs)]

    def row_copy(b, part, d, peer, own=False):
        src = spec_ref.at[planes(part)] if own else colw_blk(b, part)
        return pltpu.make_async_remote_copy(
            src, colw_blk(b, part), send_row.at[b, part, d], recv_row.at[b, part],
            device_id=peer, device_id_type=MESH_ID,
        )

    def col_copy(j, part, d, peer, own=False):
        whole = roww_ref.at[:, :, pl.ds(pl.multiple_of(j * recvs, recvs), recvs)]
        src = spec_ref if own else whole
        return pltpu.make_async_remote_copy(
            src, whole, send_col.at[j, part, d], recv_col.at[j, part],
            device_id=peer, device_id_type=MESH_ID,
        )

    def start(desc, cond=None):
        if cond is None:
            desc.start()
        else:
            pl.when(cond)(desc.start)
        started.append((desc, cond))

    def when(cond, fn):
        if cond is None:
            fn()
        else:
            pl.when(cond)(fn)

    def row_relay(b, sends, cond=None, only=parts):
        for part in only:
            when(cond, row_copy(b, part, 0, {"x": x}).wait_recv)
            for d, peer, extra in sends:
                c2 = cond if extra is None else (extra if cond is None else jnp.logical_and(cond, extra))
                start(row_copy(b, part, d, peer), c2)

    def col_relay(j, sends, cond=None):
        for part in (0,):
            when(cond, col_copy(j, part, 0, {"y": y}).wait_recv)
            for d, peer in sends:
                start(col_copy(j, part, d, peer), cond)

    start(col_copy(me_col, 0, 0, {"c": 1 - c}, own=True))
    for part in parts:
        start(row_copy(me_row, part, 0, {"zl": z + 1}, own=True), z < NZ - 1)
        start(row_copy(me_row, part, 1, {"zl": z - 1}, own=True), z > 0)
        start(row_copy(me_row, part, 2, {"x": xp}, own=True))
        start(row_copy(me_row, part, 3, {"x": xm}, own=True))
    start(col_copy(me_col, 0, 2, {"y": yp}, own=True))
    start(col_copy(me_col, 0, 3, {"y": ym}, own=True))
    colw_ref[:, pl.ds(pl.multiple_of(me_row * shots, shots), shots), :] = spec_ref[...]
    roww_ref[:, :, pl.ds(pl.multiple_of(me_col * recvs, recvs), recvs)] = spec_ref[...]

    j_h = (y * 2 + 1 - h) * 2 + c
    j_c = (y * 2 + h) * 2 + 1 - c
    j_hc = (y * 2 + 1 - h) * 2 + 1 - c
    y_sends = ((2, {"y": yp}), (3, {"y": ym}))
    to_partner = (0, {"c": 1 - c})
    col_relay(j_c, ())

    def x_forward(zsrc, cond):
        even = lax.rem(zsrc, 2) == 0
        row_relay(xm * NZ + zsrc, ((2, {"x": xp}, None),), jnp.logical_and(cond, even))
        odd = jnp.logical_not(even)
        row_relay(xp * NZ + zsrc, ((3, {"x": xm}, None),), jnp.logical_and(cond, odd))

    def x_forward_at(dist):
        if dist == 0:
            x_forward(z, True)
        else:
            x_forward(z - dist, z >= dist)
            x_forward(z + dist, z + dist < NZ)

    lag = 2
    x_sends = ((2, {"x": xp}, None), (3, {"x": xm}, None))
    for k in range(1, NZ):
        for part in parts:
            row_relay(x * NZ + z - k, x_sends + ((0, {"zl": z + 1}, z < NZ - 1),), z >= k, (part,))
            row_relay(x * NZ + z + k, x_sends + ((1, {"zl": z - 1}, z > 0),), z + k < NZ, (part,))
        if k - lag >= 0:
            x_forward_at(k - lag)
        if k == 1:
            start(col_copy(me_col, 0, 1, {"zh": 1 - h}, own=True))
        if k == 4:
            col_relay(j_h, ((0, {"c": 1 - c}),) + y_sends)
        if k == 5:
            col_relay(j_hc, ())
        if k == 6:
            col_relay((ym * 2 + 0) * 2 + c, ((2, {"y": yp}), to_partner))
            col_relay((yp * 2 + 1) * 2 + c, ((3, {"y": ym}), to_partner))
    for dist in range(NZ - lag, NZ):
        x_forward_at(dist)

    recvs_n = aperture_ref.shape[0]
    width = aperture_ref.shape[1]
    tiles, listed = lists_ref.shape
    tile_width = width // tiles
    spread_len = width * NX * NZ // 4
    first = me_col * recvs_n

    def as_column(row):
        n = row.shape[1]
        eye = lax.broadcasted_iota(jnp.int32, (n, n), 0) == lax.broadcasted_iota(jnp.int32, (n, n), 1)
        return jnp.sum(jnp.where(eye, row.astype(jnp.float32), 0.0), axis=1, keepdims=True)

    cols = (me_row * width + lax.broadcasted_iota(jnp.int32, (1, width), 1)).astype(jnp.float32)
    rpos = as_column(rpos_ref[:, pl.ds(pl.multiple_of(first, recvs_n), recvs_n)])
    offset = (rpos - cols) / spread_len
    taper = 1.0 / (1.0 + offset * offset)
    rows_here = first + lax.broadcasted_iota(jnp.int32, (recvs_n, listed), 0)
    for t in range(tiles):
        hits = (lists_ref[pl.ds(t, 1), :] == rows_here).astype(jnp.float32)
        member = jnp.sum(hits, axis=1, keepdims=True)
        part = taper[:, t * tile_width:(t + 1) * tile_width]
        aperture_ref[:, t * tile_width:(t + 1) * tile_width] = (
            member * part * (2.0 / math.sqrt(listed))
        ).astype(aperture_ref.dtype)
    spos = as_column(spos_ref[...])
    soffset = (spos - cols) / spread_len
    weights_ref[...] = 1.0 / (1.0 + soffset * soffset)

    y2 = lax.rem(y + 2, NY)
    col_relay((ym * 2 + 1) * 2 + c, (to_partner,))
    col_relay((yp * 2 + 0) * 2 + c, (to_partner,))
    for hh in range(2):
        col_relay((y2 * 2 + hh) * 2 + c, (to_partner,))
    for plane in (ym, yp, y2):
        for hh in range(2):
            col_relay((plane * 2 + hh) * 2 + 1 - c, ())
    for zz in range(NZ):
        row_relay(xm * NZ + zz if zz % 2 == 1 else xp * NZ + zz, ())

    nf = spec_ref.shape[0] // 2
    surface_root = math.sqrt(roww_ref.shape[2])
    span = NZ * shots
    mult_ref[...] = jnp.zeros(mult_ref.shape, mult_ref.dtype)

    def product_part(xc):
        u = pl.ds(pl.multiple_of(xc * span, span), span)
        for f in range(nf):
            lr = roww_ref[f, :, u]
            li = roww_ref[nf + f, :, u]
            rr = colw_ref[f, u, :]
            ri = colw_ref[nf + f, u, :]
            real_real = jnp.dot(lr, rr, preferred_element_type=jnp.float32)
            imag_imag = jnp.dot(li, ri, preferred_element_type=jnp.float32)
            real_imag = jnp.dot(lr, ri, preferred_element_type=jnp.float32)
            imag_real = jnp.dot(li, rr, preferred_element_type=jnp.float32)
            mult_ref[f] += real_real - imag_imag
            mult_ref[nf + f] += real_imag + imag_real

    product_part(x)
    product_part(xm)
    product_part(xp)
    x2 = lax.rem(x + 2, NX)
    for zz in range(NZ):
        row_relay(x2 * NZ + zz, ())
    product_part(x2)
    for p in range(2 * nf):
        mult_ref[p] = -mult_ref[p] / surface_root

    def prim_body(t, carry):
        wave = inverse_ref[t, 0] * mult_ref[0]
        for p in range(1, 2 * nf):
            wave = wave + inverse_ref[t, p] * mult_ref[p]
        prim_ref[t] = (traces_ref[t].astype(jnp.float32) - wave).astype(prim_ref.dtype)
        return carry

    lax.fori_loop(0, traces_ref.shape[0], prim_body, 0, unroll=True)

    band = partial_ref.shape[1]

    def band_peer(i):
        hh = lax.rem(1 - h + i // 8, 2)
        yy = lax.rem(i, 8) // 2
        cc = lax.rem(i, 2)
        return (yy * 2 + hh) * 2 + cc, {"y": yy, "zh": hh, "c": cc}

    def reduce_copy(j, peer):
        return pltpu.make_async_remote_copy(
            partial_ref.at[j], slots_ref.at[me_col], send_red.at[j], recv_red.at[me_col],
            device_id=peer, device_id_type=MESH_ID,
        )

    def band_body(i, carry):
        j, peer = band_peer(i)
        rows = []
        for u in range(band):
            stacked = jnp.dot(
                prim_ref[j * band + u], aperture_ref[...], preferred_element_type=jnp.float32
            )
            rows.append(jnp.sum(stacked * weights_ref[...], axis=0, keepdims=True))
        partial_ref[j] = jnp.concatenate(rows, axis=0)
        pl.when(j != me_col)(reduce_copy(j, peer).start)
        return carry

    lax.fori_loop(0, partial_ref.shape[0], band_body, 0, unroll=True)

    slots_ref[me_col] = partial_ref[me_col]
    for j, peer in col_peers:
        recv = pltpu.make_async_remote_copy(
            partial_ref.at[j], slots_ref.at[j], send_red.at[j], recv_red.at[j],
            device_id=peer, device_id_type=MESH_ID,
        )
        pl.when(j != me_col)(recv.wait_recv)
    total = slots_ref[0]
    for j in range(1, len(col_peers)):
        total = total + slots_ref[j]
    stack_ref[...] = total

    for desc, cond in started:
        when(cond, desc.wait_send)
    for j, peer in col_peers:
        pl.when(j != me_col)(reduce_copy(j, peer).wait_send)


def fused_call(traces, forward, lists, rpos, spos, inverse, width, row_count, col_count):
    samples, shots, recvs = traces.shape
    planes = forward.shape[0]
    band = samples // col_count
    vmem = pl.BlockSpec(memory_space=pltpu.VMEM)
    return pl.pallas_call(
        fused_kernel,
        out_shape=(
            jax.ShapeDtypeStruct(traces.shape, jnp.bfloat16),
            jax.ShapeDtypeStruct((band, width), jnp.float32),
        ),
        in_specs=[
            vmem,
            pl.BlockSpec(memory_space=pltpu.SMEM),
            vmem,
            vmem,
            vmem,
            pl.BlockSpec(memory_space=pltpu.SMEM),
        ],
        out_specs=(vmem, vmem),
        scratch_shapes=[
            pltpu.VMEM((planes, shots, recvs), jnp.bfloat16),
            pltpu.VMEM((planes, row_count * shots, recvs), jnp.bfloat16),
            pltpu.VMEM((planes, shots, col_count * recvs), jnp.bfloat16),
            pltpu.VMEM((planes, shots, recvs), jnp.float32),
            pltpu.VMEM((col_count, band, width), jnp.float32),
            pltpu.VMEM((col_count, band, width), jnp.float32),
            pltpu.VMEM((recvs, width), jnp.bfloat16),
            pltpu.VMEM((shots, width), jnp.float32),
            pltpu.SemaphoreType.DMA((row_count, 2)),
            pltpu.SemaphoreType.DMA((col_count, 2)),
            pltpu.SemaphoreType.DMA((row_count, 2, 4)),
            pltpu.SemaphoreType.DMA((col_count, 2, 4)),
            pltpu.SemaphoreType.DMA((col_count,)),
            pltpu.SemaphoreType.DMA((col_count,)),
        ],
        compiler_params=pltpu.CompilerParams(collective_id=0, has_side_effects=True),
    )(traces, forward, lists, rpos, spos, inverse)


def per_device(traces, source_pos, receiver_pos, aperture_list, band_index, weight_tiles):
    samples, shot_count, recv_count = traces.shape
    col_count = axis_count(COL)
    row_count = axis_count(ROW)
    surface_count = recv_count * col_count
    image_panel_width = band_index.shape[0]
    depth_slab_samples = samples // col_count
    cosine, sine_table = phase_tables_np(samples)
    forward = jnp.asarray(
        (np.concatenate([cosine, -sine_table], 0) / np.float32(math.sqrt(samples)))
        .astype(ml_dtypes.bfloat16)
        .astype(np.float32)
    )

    inverse = jnp.asarray(np.concatenate([cosine, -sine_table], 0).T / np.float32(math.sqrt(NF)))
    primaries, stacked = fused_call(
        traces,
        forward,
        aperture_list,
        receiver_pos.reshape(1, -1),
        source_pos.reshape(1, -1),
        inverse,
        image_panel_width,
        row_count,
        col_count,
    )
    column_stack = (stacked / math.sqrt(shot_count)).astype(jnp.bfloat16)

    tile_kinds = weight_tiles.shape[0]
    select = band_index[None, :] == jnp.arange(tile_kinds, dtype=jnp.int32)[:, None]
    widened = jnp.where(select[:, None, :], column_stack[None], jnp.zeros((), jnp.bfloat16))
    image_out = jnp.einsum(
        "kz,kx->zx",
        weight_tiles.reshape(tile_kinds * depth_slab_samples, weight_tiles.shape[2]),
        widened.reshape(tile_kinds * depth_slab_samples, image_panel_width),
        preferred_element_type=jnp.float32,
    )
    return (primaries, image_out)


def solution(mesh):
    n_row = mesh.shape["row"]
    n_col = mesh.shape["col"]
    fine = Mesh(
        mesh.devices.reshape(4, n_row // 4, 4, n_col // 8, 2), ("x", "zl", "y", "zh", "c")
    )
    placed = (P(None, ROW, COL), P(ROW), P(), P(ROW, None), P(ROW), P())
    return jax.shard_map(
        per_device,
        mesh=fine,
        in_specs=placed,
        out_specs=(P(None, ROW, COL), P(COL, ROW)),
        check_vma=False,
    )
```

```python
import math

import jax
import ml_dtypes
import numpy as np
import jax.numpy as jnp
from jax import lax
from jax.experimental import pallas as pl
from jax.experimental.pallas import tpu as pltpu
from jax.sharding import Mesh
from jax.sharding import PartitionSpec as P

NFFT = 4096
NF = 4

ROW = ("x", "zl")
COL = ("y", "zh", "c")


def phase_tables_np(samples):
    freq_bins = (2 * np.arange(NF, dtype=np.int32) + 1) * (NFFT // (4 * NF))
    sample_ticks = np.arange(samples, dtype=np.int32)
    phase_turns = freq_bins[:, None] * sample_ticks[None, :] % NFFT
    phase_angle = phase_turns.astype(np.float32) * np.float32(2.0 * math.pi / NFFT)
    angle = phase_angle.astype(np.float64)
    return (np.cos(angle).astype(np.float32), np.sin(angle).astype(np.float32))


def phase_tables(samples):
    freq_bins = (2 * jnp.arange(NF, dtype=jnp.int32) + 1) * (NFFT // (4 * NF))
    sample_ticks = jnp.arange(samples, dtype=jnp.int32)
    phase_turns = freq_bins[:, None] * sample_ticks[None, :] % NFFT
    phase_angle = phase_turns.astype(jnp.float32) * (2.0 * math.pi / NFFT)
    return (jnp.cos(phase_angle), jnp.sin(phase_angle))


def aperture_rows(tile_index_lists, positions, columns, first_row, row_count, spread_len):
    tile_count, listed = tile_index_lists.shape
    col_width = columns.shape[0]
    rows = first_row + jnp.arange(row_count, dtype=jnp.int32)
    hits = (tile_index_lists[:, :, None] == rows[None, None, :]).astype(jnp.float32)
    member = jnp.sum(hits, axis=1)
    widened = jnp.repeat(member.T, col_width // tile_count, axis=1)
    offset = (positions[:, None] - columns[None, :]).astype(jnp.float32) / spread_len
    taper_weight = 1.0 / (1.0 + offset * offset)
    return (widened * taper_weight * (2.0 / math.sqrt(listed))).astype(jnp.bfloat16)


def shot_weights(positions, columns, spread_len):
    offset = (positions[:, None] - columns[None, :]).astype(jnp.float32) / spread_len
    return 1.0 / (1.0 + offset * offset)


def complex_product(left_section, right_section):
    real_real = jnp.einsum(
        "qju,quy->qjy", left_section[0], right_section[0], preferred_element_type=jnp.float32
    )
    imag_imag = jnp.einsum(
        "qju,quy->qjy", left_section[1], right_section[1], preferred_element_type=jnp.float32
    )
    real_imag = jnp.einsum(
        "qju,quy->qjy", left_section[0], right_section[1], preferred_element_type=jnp.float32
    )
    imag_real = jnp.einsum(
        "qju,quy->qjy", left_section[1], right_section[0], preferred_element_type=jnp.float32
    )
    return jnp.stack([real_real - imag_imag, real_imag + imag_real])


def axis_pos(names):
    index = 0
    for name in names:
        index = index * lax.axis_size(name) + lax.axis_index(name)
    return index


def axis_count(names):
    count = 1
    for name in names:
        count *= lax.axis_size(name)
    return count


MESH_ID = pl.DeviceIdType.MESH
NX, NZ, NY = 4, 8, 4


def fused_kernel(traces_ref, forward_ref, lists_ref, rpos_ref, spos_ref, inverse_ref,
                 prim_ref, stack_ref,
                 spec_ref, colw_ref, roww_ref, mult_ref, partial_ref, slots_ref, aperture_ref, weights_ref,
                 recv_row, recv_col, send_row, send_col, recv_red, send_red):
    x = lax.axis_index("x")
    z = lax.axis_index("zl")
    y = lax.axis_index("y")
    h = lax.axis_index("zh")
    c = lax.axis_index("c")
    xp = lax.rem(x + 1, NX)
    xm = lax.rem(x + NX - 1, NX)
    yp = lax.rem(y + 1, NY)
    ym = lax.rem(y + NY - 1, NY)
    me_row = x * NZ + z
    me_col = (y * 2 + h) * 2 + c

    col_peers = []
    for yy in range(NY):
        for hh in range(2):
            for cc in range(2):
                col_peers.append(((yy * 2 + hh) * 2 + cc, {"y": yy, "zh": hh, "c": cc}))

    barrier = pltpu.get_barrier_semaphore()
    for peer in ({"x": xp}, {"x": xm}):
        pl.semaphore_signal(barrier, 1, device_id=peer, device_id_type=MESH_ID)
    for j, peer in col_peers:
        pl.when(j != me_col)(
            lambda peer=peer: pl.semaphore_signal(
                barrier, 1, device_id=peer, device_id_type=MESH_ID
            )
        )

    @pl.when(z > 0)
    def _():
        pl.semaphore_signal(barrier, 1, device_id={"zl": z - 1}, device_id_type=MESH_ID)

    @pl.when(z < NZ - 1)
    def _():
        pl.semaphore_signal(barrier, 1, device_id={"zl": z + 1}, device_id_type=MESH_ID)

    samples = traces_ref.shape[0]
    group = 4
    for p0 in range(0, spec_ref.shape[0], group):
        def spectra_body(t, accs, p0=p0):
            sample = traces_ref[t].astype(jnp.float32)
            return tuple(acc + forward_ref[p0 + g, t] * sample for g, acc in enumerate(accs))

        zero = jnp.zeros(spec_ref.shape[1:], jnp.float32)
        accs = lax.fori_loop(0, samples, spectra_body, (zero,) * group)
        for g in range(group):
            spec_ref[p0 + g] = accs[g].astype(spec_ref.dtype)

    peers_in = 2 + len(col_peers) - 1
    ends = jnp.logical_or(z == 0, z == NZ - 1)
    pl.when(ends)(lambda: pl.semaphore_wait(barrier, peers_in + 1))
    pl.when(jnp.logical_not(ends))(lambda: pl.semaphore_wait(barrier, peers_in + 2))

    started = []
    shots = spec_ref.shape[1]
    recvs = spec_ref.shape[2]
    half = spec_ref.shape[0]
    parts = (0,)

    def planes(part):
        return pl.ds(part * half, half)

    def colw_blk(b, part):
        return colw_ref.at[planes(part), pl.ds(pl.multiple_of(b * shots, shots), shots), :]

    def roww_blk(j, part):
        return roww_ref.at[planes(part), :, pl.ds(pl.multiple_of(j * recvs, recvs), recvs)]

    def row_copy(b, part, d, peer, own=False):
        src = spec_ref.at[planes(part)] if own else colw_blk(b, part)
        return pltpu.make_async_remote_copy(
            src, colw_blk(b, part), send_row.at[b, part, d], recv_row.at[b, part],
            device_id=peer, device_id_type=MESH_ID,
        )

    def col_copy(j, part, d, peer, own=False):
        whole = roww_ref.at[:, :, pl.ds(pl.multiple_of(j * recvs, recvs), recvs)]
        src = spec_ref if own else whole
        return pltpu.make_async_remote_copy(
            src, whole, send_col.at[j, part, d], recv_col.at[j, part],
            device_id=peer, device_id_type=MESH_ID,
        )

    def start(desc, cond=None):
        if cond is None:
            desc.start()
        else:
            pl.when(cond)(desc.start)
        started.append((desc, cond))

    def when(cond, fn):
        if cond is None:
            fn()
        else:
            pl.when(cond)(fn)

    def row_relay(b, sends, cond=None, only=parts):
        for part in only:
            when(cond, row_copy(b, part, 0, {"x": x}).wait_recv)
            for d, peer, extra in sends:
                c2 = cond if extra is None else (extra if cond is None else jnp.logical_and(cond, extra))
                start(row_copy(b, part, d, peer), c2)

    def col_relay(j, sends, cond=None):
        for part in (0,):
            when(cond, col_copy(j, part, 0, {"y": y}).wait_recv)
            for d, peer in sends:
                start(col_copy(j, part, d, peer), cond)

    start(col_copy(me_col, 0, 0, {"c": 1 - c}, own=True))
    for part in parts:
        start(row_copy(me_row, part, 0, {"zl": z + 1}, own=True), z < NZ - 1)
        start(row_copy(me_row, part, 1, {"zl": z - 1}, own=True), z > 0)
        start(row_copy(me_row, part, 2, {"x": xp}, own=True))
        start(row_copy(me_row, part, 3, {"x": xm}, own=True))
    start(col_copy(me_col, 0, 2, {"y": yp}, own=True))
    start(col_copy(me_col, 0, 3, {"y": ym}, own=True))
    colw_ref[:, pl.ds(pl.multiple_of(me_row * shots, shots), shots), :] = spec_ref[...]
    roww_ref[:, :, pl.ds(pl.multiple_of(me_col * recvs, recvs), recvs)] = spec_ref[...]

    j_h = (y * 2 + 1 - h) * 2 + c
    j_c = (y * 2 + h) * 2 + 1 - c
    j_hc = (y * 2 + 1 - h) * 2 + 1 - c
    y_sends = ((2, {"y": yp}), (3, {"y": ym}))
    to_partner = (0, {"c": 1 - c})
    col_relay(j_c, ())

    def x_forward(zsrc, cond):
        even = lax.rem(zsrc, 2) == 0
        row_relay(xm * NZ + zsrc, ((2, {"x": xp}, None),), jnp.logical_and(cond, even))
        odd = jnp.logical_not(even)
        row_relay(xp * NZ + zsrc, ((3, {"x": xm}, None),), jnp.logical_and(cond, odd))

    def x_forward_at(dist):
        if dist == 0:
            x_forward(z, True)
        else:
            x_forward(z - dist, z >= dist)
            x_forward(z + dist, z + dist < NZ)

    lag = 2
    x_sends = ((2, {"x": xp}, None), (3, {"x": xm}, None))
    for k in range(1, NZ):
        for part in parts:
            row_relay(x * NZ + z - k, x_sends + ((0, {"zl": z + 1}, z < NZ - 1),), z >= k, (part,))
            row_relay(x * NZ + z + k, x_sends + ((1, {"zl": z - 1}, z > 0),), z + k < NZ, (part,))
        if k - lag >= 0:
            x_forward_at(k - lag)
        if k == 2:
            start(col_copy(me_col, 0, 1, {"zh": 1 - h}, own=True))
        if k == 4:
            col_relay(j_h, ((0, {"c": 1 - c}),) + y_sends)
        if k == 5:
            col_relay(j_hc, ())
        if k == 6:
            col_relay((ym * 2 + 0) * 2 + c, ((2, {"y": yp}), to_partner))
            col_relay((yp * 2 + 1) * 2 + c, ((3, {"y": ym}), to_partner))
    for dist in range(NZ - lag, NZ):
        x_forward_at(dist)

    recvs_n = aperture_ref.shape[0]
    width = aperture_ref.shape[1]
    tiles, listed = lists_ref.shape
    tile_width = width // tiles
    spread_len = width * NX * NZ // 4
    first = me_col * recvs_n

    def as_column(row):
        n = row.shape[1]
        eye = lax.broadcasted_iota(jnp.int32, (n, n), 0) == lax.broadcasted_iota(jnp.int32, (n, n), 1)
        return jnp.sum(jnp.where(eye, row.astype(jnp.float32), 0.0), axis=1, keepdims=True)

    cols = (me_row * width + lax.broadcasted_iota(jnp.int32, (1, width), 1)).astype(jnp.float32)
    rpos = as_column(rpos_ref[:, pl.ds(pl.multiple_of(first, recvs_n), recvs_n)])
    offset = (rpos - cols) / spread_len
    taper = 1.0 / (1.0 + offset * offset)
    rows_here = first + lax.broadcasted_iota(jnp.int32, (recvs_n, listed), 0)
    for t in range(tiles):
        hits = (lists_ref[pl.ds(t, 1), :] == rows_here).astype(jnp.float32)
        member = jnp.sum(hits, axis=1, keepdims=True)
        part = taper[:, t * tile_width:(t + 1) * tile_width]
        aperture_ref[:, t * tile_width:(t + 1) * tile_width] = (
            member * part * (2.0 / math.sqrt(listed))
        ).astype(aperture_ref.dtype)
    spos = as_column(spos_ref[...])
    soffset = (spos - cols) / spread_len
    weights_ref[...] = 1.0 / (1.0 + soffset * soffset)

    y2 = lax.rem(y + 2, NY)
    col_relay((ym * 2 + 1) * 2 + c, (to_partner,))
    col_relay((yp * 2 + 0) * 2 + c, (to_partner,))
    for hh in range(2):
        col_relay((y2 * 2 + hh) * 2 + c, (to_partner,))
    for plane in (ym, yp, y2):
        for hh in range(2):
            col_relay((plane * 2 + hh) * 2 + 1 - c, ())
    for zz in range(NZ):
        row_relay(xm * NZ + zz if zz % 2 == 1 else xp * NZ + zz, ())

    nf = spec_ref.shape[0] // 2
    surface_root = math.sqrt(roww_ref.shape[2])
    span = NZ * shots
    mult_ref[...] = jnp.zeros(mult_ref.shape, mult_ref.dtype)

    def product_part(xc):
        u = pl.ds(pl.multiple_of(xc * span, span), span)
        for f in range(nf):
            lr = roww_ref[f, :, u]
            li = roww_ref[nf + f, :, u]
            rr = colw_ref[f, u, :]
            ri = colw_ref[nf + f, u, :]
            real_real = jnp.dot(lr, rr, preferred_element_type=jnp.float32)
            imag_imag = jnp.dot(li, ri, preferred_element_type=jnp.float32)
            real_imag = jnp.dot(lr, ri, preferred_element_type=jnp.float32)
            imag_real = jnp.dot(li, rr, preferred_element_type=jnp.float32)
            mult_ref[f] += real_real - imag_imag
            mult_ref[nf + f] += real_imag + imag_real

    product_part(x)
    product_part(xm)
    product_part(xp)
    x2 = lax.rem(x + 2, NX)
    for zz in range(NZ):
        row_relay(x2 * NZ + zz, ())
    product_part(x2)
    for p in range(2 * nf):
        mult_ref[p] = -mult_ref[p] / surface_root

    def prim_body(t, carry):
        wave = inverse_ref[t, 0] * mult_ref[0]
        for p in range(1, 2 * nf):
            wave = wave + inverse_ref[t, p] * mult_ref[p]
        prim_ref[t] = (traces_ref[t].astype(jnp.float32) - wave).astype(prim_ref.dtype)
        return carry

    lax.fori_loop(0, traces_ref.shape[0], prim_body, 0, unroll=True)

    band = partial_ref.shape[1]

    def band_peer(i):
        hh = lax.rem(1 - h + i // 8, 2)
        yy = lax.rem(i, 8) // 2
        cc = lax.rem(i, 2)
        return (yy * 2 + hh) * 2 + cc, {"y": yy, "zh": hh, "c": cc}

    def reduce_copy(j, peer):
        return pltpu.make_async_remote_copy(
            partial_ref.at[j], slots_ref.at[me_col], send_red.at[j], recv_red.at[me_col],
            device_id=peer, device_id_type=MESH_ID,
        )

    def band_body(i, carry):
        j, peer = band_peer(i)
        rows = []
        for u in range(band):
            stacked = jnp.dot(
                prim_ref[j * band + u], aperture_ref[...], preferred_element_type=jnp.float32
            )
            rows.append(jnp.sum(stacked * weights_ref[...], axis=0, keepdims=True))
        partial_ref[j] = jnp.concatenate(rows, axis=0)
        pl.when(j != me_col)(reduce_copy(j, peer).start)
        return carry

    lax.fori_loop(0, partial_ref.shape[0], band_body, 0, unroll=True)

    slots_ref[me_col] = partial_ref[me_col]
    for j, peer in col_peers:
        recv = pltpu.make_async_remote_copy(
            partial_ref.at[j], slots_ref.at[j], send_red.at[j], recv_red.at[j],
            device_id=peer, device_id_type=MESH_ID,
        )
        pl.when(j != me_col)(recv.wait_recv)
    total = slots_ref[0]
    for j in range(1, len(col_peers)):
        total = total + slots_ref[j]
    stack_ref[...] = total

    for desc, cond in started:
        when(cond, desc.wait_send)
    for j, peer in col_peers:
        pl.when(j != me_col)(reduce_copy(j, peer).wait_send)


def fused_call(traces, forward, lists, rpos, spos, inverse, width, row_count, col_count):
    samples, shots, recvs = traces.shape
    planes = forward.shape[0]
    band = samples // col_count
    vmem = pl.BlockSpec(memory_space=pltpu.VMEM)
    return pl.pallas_call(
        fused_kernel,
        out_shape=(
            jax.ShapeDtypeStruct(traces.shape, jnp.bfloat16),
            jax.ShapeDtypeStruct((band, width), jnp.float32),
        ),
        in_specs=[
            vmem,
            pl.BlockSpec(memory_space=pltpu.SMEM),
            vmem,
            vmem,
            vmem,
            pl.BlockSpec(memory_space=pltpu.SMEM),
        ],
        out_specs=(vmem, vmem),
        scratch_shapes=[
            pltpu.VMEM((planes, shots, recvs), jnp.bfloat16),
            pltpu.VMEM((planes, row_count * shots, recvs), jnp.bfloat16),
            pltpu.VMEM((planes, shots, col_count * recvs), jnp.bfloat16),
            pltpu.VMEM((planes, shots, recvs), jnp.float32),
            pltpu.VMEM((col_count, band, width), jnp.float32),
            pltpu.VMEM((col_count, band, width), jnp.float32),
            pltpu.VMEM((recvs, width), jnp.bfloat16),
            pltpu.VMEM((shots, width), jnp.float32),
            pltpu.SemaphoreType.DMA((row_count, 2)),
            pltpu.SemaphoreType.DMA((col_count, 2)),
            pltpu.SemaphoreType.DMA((row_count, 2, 4)),
            pltpu.SemaphoreType.DMA((col_count, 2, 4)),
            pltpu.SemaphoreType.DMA((col_count,)),
            pltpu.SemaphoreType.DMA((col_count,)),
        ],
        compiler_params=pltpu.CompilerParams(collective_id=0, has_side_effects=True),
    )(traces, forward, lists, rpos, spos, inverse)


def per_device(traces, source_pos, receiver_pos, aperture_list, band_index, weight_tiles):
    samples, shot_count, recv_count = traces.shape
    col_count = axis_count(COL)
    row_count = axis_count(ROW)
    surface_count = recv_count * col_count
    image_panel_width = band_index.shape[0]
    depth_slab_samples = samples // col_count
    cosine, sine_table = phase_tables_np(samples)
    forward = jnp.asarray(
        (np.concatenate([cosine, -sine_table], 0) / np.float32(math.sqrt(samples)))
        .astype(ml_dtypes.bfloat16)
        .astype(np.float32)
    )

    inverse = jnp.asarray(np.concatenate([cosine, -sine_table], 0).T / np.float32(math.sqrt(NF)))
    primaries, stacked = fused_call(
        traces,
        forward,
        aperture_list,
        receiver_pos.reshape(1, -1),
        source_pos.reshape(1, -1),
        inverse,
        image_panel_width,
        row_count,
        col_count,
    )
    column_stack = (stacked / math.sqrt(shot_count)).astype(jnp.bfloat16)

    tile_kinds = weight_tiles.shape[0]
    select = band_index[None, :] == jnp.arange(tile_kinds, dtype=jnp.int32)[:, None]
    widened = jnp.where(select[:, None, :], column_stack[None], jnp.zeros((), jnp.bfloat16))
    image_out = jnp.einsum(
        "kz,kx->zx",
        weight_tiles.reshape(tile_kinds * depth_slab_samples, weight_tiles.shape[2]),
        widened.reshape(tile_kinds * depth_slab_samples, image_panel_width),
        preferred_element_type=jnp.float32,
    )
    return (primaries, image_out)


def solution(mesh):
    n_row = mesh.shape["row"]
    n_col = mesh.shape["col"]
    fine = Mesh(
        mesh.devices.reshape(4, n_row // 4, 4, n_col // 8, 2), ("x", "zl", "y", "zh", "c")
    )
    placed = (P(None, ROW, COL), P(ROW), P(), P(ROW, None), P(ROW), P())
    return jax.shard_map(
        per_device,
        mesh=fine,
        in_specs=placed,
        out_specs=(P(None, ROW, COL), P(COL, ROW)),
        check_vma=False,
    )
```
